32 devices in a mesh: dp: 8 (over z, y), tensor: 4 (over x, core).
Axes of the slice: x: 2, y: 2, z: 4, core: 2. Of those that a mesh axis runs over, the one named last changes fastest.
Arguments:
- block_input: bfloat16 [2048, 8, 768], P('tensor', 'dp'), may hold values from -6 to 6
- condition: bfloat16 [8, 128], P('dp'), may hold values from -6 to 6
- modulation_weight: bfloat16 [128, 4608], P(None, 'dp'), may hold values from -0.25 to 0.25
- modulation_bias: bfloat16 [4608], P('dp'), may hold values from -3 to 3
- first_gain: bfloat16 [768], P('dp'), may hold values from 0.5 to 1.5
- qkv_weight: bfloat16 [3, 768, 768], P(None, 'dp', 'tensor'), may hold values from -0.3125 to 0.3125
- out_weight: bfloat16 [768, 768], P('tensor', 'dp'), may hold values from -0.875 to 0.875
- second_gain: bfloat16 [768], P('dp'), may hold values from 0.5 to 1.5
- up_weight: bfloat16 [768, 3072], P('dp', 'tensor'), may hold values from -0.21875 to 0.21875
- up_bias: bfloat16 [3072], P('dp'), may hold values from -3 to 3
- down_weight: bfloat16 [3072, 768], P('tensor', 'dp'), may hold values from -0.109375 to 0.109375
- down_bias: bfloat16 [768], P('dp'), may hold values from -2 to 2
- grad_output: bfloat16 [2048, 8, 768], P('tensor', 'dp'), may hold values from -6 to 6
Outputs:
- block_output: bfloat16 [2048, 8, 768], P('tensor', 'dp')
- grad_input: float32 [2048, 8, 768], P('tensor', 'dp')
- grad_condition: float32 [8, 128], P('dp')
- grad_modulation_weight: float32 [128, 4608], replicated
- grad_modulation_bias: float32 [4608], replicated
- grad_first_gain: float32 [768], replicated
- grad_qkv_weight: float32 [3, 768, 768], P(None, 'dp', 'tensor')
- grad_out_weight: float32 [768, 768], P('tensor', 'dp')
- grad_second_gain: float32 [768], replicated
- grad_up_weight: float32 [768, 3072], P('dp', 'tensor')
- grad_up_bias: float32 [3072], replicated
- grad_down_weight: float32 [3072, 768], P('tensor', 'dp')
- grad_down_bias: float32 [768], replicated
- root_means: float32 [3], replicated
The draws below stay inside these ranges and needn't reach their ends.
All inputs are finite; a program needn't handle non-finite values.
Results may differ from the reference program's by a relative error of at most 0.014.
The reference program's roundings to bfloat16 on the way count: a program that leaves them out, or rounds other values in their place, can miss the bound.
Values may be sent and summed in bfloat16 or wider, within the bound.
A program may use at most 128 MiB of HBM per device.

```python
import jax
import jax.numpy as jnp
from jax import lax

D = 768
HEADS = 12
HEAD_DIM = 64
FF = 3072
COND = 128
LENGTH = 2048
BATCH = 8


def rising(total_rows):
    return jnp.exp(jnp.log(3.0) * jnp.arange(total_rows, dtype=jnp.float32) / max(total_rows - 1, 1))


def draw_block_input(key, part):
    dims_all = (LENGTH, BATCH, D)
    sample = jax.random.normal(key, dims_all, jnp.float32)
    sample = jnp.clip(sample, -4.0, 4.0)
    return (sample * 0.5 * rising(BATCH)[None, :, None]).astype(jnp.bfloat16)


def draw_condition(key, part):
    dims_all = (BATCH, COND)
    sample = jax.random.normal(key, dims_all, jnp.float32)
    sample = jnp.clip(sample, -4.0, 4.0)
    return (sample * 0.5 * rising(BATCH)[:, None]).astype(jnp.bfloat16)


def steps_of(key, extent, pieces, low, top_value):
    loudness, own = 1.0, jax.random.fold_in(key, 6)
    for axis_at, parts in pieces:
        steps = jnp.exp(jax.random.uniform(jax.random.fold_in(own, axis_at), (parts,), jnp.float32, low / len(pieces), top_value / len(pieces)))
        loudness = loudness * jnp.repeat(steps, extent[axis_at] // parts).reshape([-1 if axis == axis_at else 1 for axis in range(len(extent))])
    return loudness


def scatter_about(stream_key, dims, deviation, bound, cuts=(), held_as=jnp.bfloat16):
    level = steps_of(stream_key, dims, cuts, -0.22, 0.18) if cuts else 1.0
    values = jax.random.normal(stream_key, dims, jnp.float32) * deviation * level
    return jnp.minimum(jnp.maximum(values, -bound), bound).astype(held_as)


def setup_inputs(seed: int = 0) -> dict:
    seeds = jax.random.split(jax.random.key(seed), 14)
    block_input = draw_block_input(jax.random.fold_in(seeds[13], 71), 0)
    condition = draw_condition(jax.random.fold_in(seeds[13], 71), 0)
    modulation_weight = scatter_about(seeds[2], (COND, 6 * D), (4 * COND) ** -0.5, 0.25, ((1, 8),))
    modulation_bias = scatter_about(seeds[3], (6 * D,), 0.5, 3.0, ((0, 8),))
    first_gain = jnp.clip(1.0 + 0.1 * jax.random.normal(seeds[4], (D,), jnp.float32), 0.5, 1.5).astype(jnp.bfloat16)
    qkv_weight = scatter_about(seeds[5], (3, D, D), (D // 2) ** -0.5, 0.3125, ((1, 8), (2, 4)))
    out_weight = scatter_about(seeds[6], (D, D), (D // 16) ** -0.5, 0.875, ((0, 4), (1, 8)))
    second_gain = jnp.clip(1.0 + 0.1 * jax.random.normal(seeds[7], (D,), jnp.float32), 0.5, 1.5).astype(jnp.bfloat16)
    up_weight = scatter_about(seeds[8], (D, FF), D ** -0.5, 0.21875, ((0, 8), (1, 4)))
    up_bias = scatter_about(seeds[9], (FF,), 0.5, 3.0, ((0, 8),))
    down_weight = scatter_about(seeds[10], (FF, D), FF ** -0.5, 0.109375, ((0, 4), (1, 8)))
    down_bias = scatter_about(seeds[11], (D,), 0.3, 2.0, ((0, 8),))
    grad_output = scatter_about(seeds[12], (LENGTH, BATCH, D), 1.0, 6.0, ((0, 4), (1, 8)))
    return {"block_input": block_input, "condition": condition, "modulation_weight": modulation_weight, "modulation_bias": modulation_bias, "first_gain": first_gain, "qkv_weight": qkv_weight, "out_weight": out_weight, "second_gain": second_gain, "up_weight": up_weight, "up_bias": up_bias, "down_weight": down_weight, "down_bias": down_bias, "grad_output": grad_output}


PRECISE = lax.Precision.HIGHEST
EPSILON = 1e-05

@jax.custom_vjp
def low(v):
    return lax.optimization_barrier(v.astype(jnp.bfloat16)).astype(jnp.float32)

@jax.custom_vjp
def low_back(v):
    return v

def low_keep(v):
    return (low(v), None)

def low_pass(kept, grad):
    return (grad,)

def back_keep(v):
    return (v, None)

def back_low(kept, grad):
    return (low(grad),)
low.defvjp(low_keep, low_pass)
low_back.defvjp(back_keep, back_low)

def norm_mod(stream, gain_vec, shift_vec, scale_vec):
    row_mean = lax.optimization_barrier(jnp.mean(stream, axis=-1, keepdims=True))
    centred = stream - row_mean
    variance = lax.optimization_barrier(jnp.mean(centred * centred, axis=-1, keepdims=True))
    normed = centred * lax.rsqrt(variance + EPSILON) * gain_vec
    return normed * (1.0 + scale_vec) + shift_vec

def rotary_tables(length, head_width):
    half_dim = head_width // 2
    inverse = 1.0 / 10000.0 ** (jnp.arange(half_dim, dtype=jnp.float32) * 2.0 / head_width)
    angles = jnp.arange(length, dtype=jnp.float32)[:, None] * inverse[None, :]
    angles = jnp.concatenate([angles, angles], axis=-1)
    return (jnp.cos(angles), jnp.sin(angles))

def rotate(vector, cos_table, sine_table):
    half_dim = vector.shape[-1] // 2
    turned = jnp.concatenate([-vector[..., half_dim:], vector[..., :half_dim]], axis=-1)
    return vector * cos_table[:, None, None, :] + turned * sine_table[:, None, None, :]

def attend_one(operands):
    query_seq, key_seq, value_seq = operands
    scores = low_back(jnp.einsum('qhe,khe->hqk', query_seq, key_seq, precision=PRECISE))
    probs = jax.nn.softmax(scores, axis=-1)
    return jnp.einsum('hqk,khe->qhe', low(probs), value_seq, precision=PRECISE)

def layer_forward(stream, cond_f, ada_w, ada_b, gain_one, qkv_w, out_w, gain_two, up_w, up_b, down_w, down_b):
    modulation = jnp.dot(cond_f, ada_w, precision=PRECISE) + ada_b
    shift_attn, scale_attn, gate_attn, shift_mlp, scale_mlp, gate_mlp = jnp.split(modulation, 6, axis=-1)
    attn_in = low(norm_mod(stream, gain_one, shift_attn, scale_attn))
    projected = low_back(jnp.einsum('lbd,jde->lbje', attn_in, qkv_w, precision=PRECISE))
    cos_table, sine_table = rotary_tables(LENGTH, HEAD_DIM)
    head_shape = (LENGTH, BATCH, HEADS, HEAD_DIM)
    query_rot = low(rotate(projected[:, :, 0].reshape(head_shape), cos_table, sine_table) * HEAD_DIM ** (-0.5))
    key_rot = low(rotate(projected[:, :, 1].reshape(head_shape), cos_table, sine_table))
    value_low = low(projected[:, :, 2].reshape(head_shape))
    mixed_all = lax.map(jax.checkpoint(attend_one), (query_rot.transpose(1, 0, 2, 3), key_rot.transpose(1, 0, 2, 3), value_low.transpose(1, 0, 2, 3)))
    mixed_all = low(low_back(mixed_all.transpose(1, 0, 2, 3).reshape(LENGTH, BATCH, D)))
    attn_out = low_back(jnp.einsum('lbd,de->lbe', mixed_all, out_w, precision=PRECISE))
    attn_branch = gate_attn * attn_out
    middle = stream + attn_branch
    mlp_in = low(norm_mod(middle, gain_two, shift_mlp, scale_mlp))
    hidden = low_back(jnp.einsum('lbd,df->lbf', mlp_in, up_w, precision=PRECISE) + up_b)
    active = low(jax.nn.gelu(hidden, approximate=True))
    mlp_out = low_back(jnp.einsum('lbf,fd->lbd', active, down_w, precision=PRECISE) + down_b)
    mlp_branch = gate_mlp * mlp_out
    result = middle + mlp_branch
    squares = jnp.stack([jnp.sum(attn_branch * attn_branch), jnp.sum(mlp_branch * mlp_branch), jnp.sum(result * result)])
    return (result, squares)

def reference(block_input, condition, modulation_weight, modulation_bias, first_gain, qkv_weight, out_weight, second_gain, up_weight, up_bias, down_weight, down_bias, grad_output):
    floats = [array.astype(jnp.float32) for array in (block_input, condition, modulation_weight, modulation_bias, first_gain, qkv_weight, out_weight, second_gain, up_weight, up_bias, down_weight, down_bias)]
    result, pull_back, squares = jax.vjp(layer_forward, *floats, has_aux=True)
    grads = pull_back(grad_output.astype(jnp.float32))
    root_means = jnp.sqrt(squares / (LENGTH * BATCH * D))
    return (result.astype(jnp.bfloat16), grads[0], grads[1], grads[2], grads[3], grads[4], grads[5], grads[6], grads[7], grads[8], grads[9], grads[10], grads[11], root_means)
```

```python
from functools import partial

import jax
import jax.numpy as jnp
import numpy as np
from jax import lax
from jax.experimental import pallas as pl
from jax.experimental.pallas import tpu as pltpu
from jax.sharding import PartitionSpec as P

HEAD_DIM = 64
EPSILON = 1e-05
CORES = 2
INNER = 2
MESH = pl.DeviceIdType.MESH
VMEM_LIMIT = 58 << 20
GELU_C = float(np.sqrt(2.0 / np.pi))
GELU_A = 0.044715
F32 = jnp.float32
BF16 = jnp.bfloat16
ANY = pl.BlockSpec(memory_space=pl.ANY)
VMEM = pl.BlockSpec(memory_space=pltpu.VMEM)
DMA = pltpu.SemaphoreType.DMA


def dot(lhs, rhs, lhs_dim, rhs_dim):
    return lax.dot_general(
        lhs, rhs, (((lhs_dim,), (rhs_dim,)), ((), ())), preferred_element_type=F32
    )


def params(collective_id=None, **more):
    if collective_id is not None:
        more.update(collective_id=collective_id, has_side_effects=True)
    return pltpu.CompilerParams(vmem_limit_bytes=VMEM_LIMIT, **more)


def cost(flops, moved, special=0):
    return pl.CostEstimate(flops=int(flops), bytes_accessed=int(moved), transcendentals=int(special))


def struct(shape, dtype):
    return jax.ShapeDtypeStruct(shape, dtype)


def mean_rows(values):
    return jnp.mean(values, axis=-1, keepdims=True)


def sum_tokens(values):
    return jnp.sum(values, axis=0, keepdims=True)


def greet(n_d, n_t):
    d, t = lax.axis_index("dp"), lax.axis_index("tensor")
    barrier = pltpu.get_barrier_semaphore()
    for r in range(1, n_t):
        pl.semaphore_signal(
            barrier, 1, device_id=(d, lax.rem(t + r, n_t)), device_id_type=MESH
        )
    for r in range(1, n_d):
        pl.semaphore_signal(
            barrier, 1, device_id=(lax.rem(d + r, n_d), t), device_id_type=MESH
        )
    pl.semaphore_wait(barrier, n_t - 1 + n_d - 1)


def remote(src, dst, send, recv, d, t):
    return pltpu.make_async_remote_copy(
        src_ref=src, dst_ref=dst, send_sem=send, recv_sem=recv, device_id=(d, t), device_id_type=MESH
    )


def gather_kernel(
    n_d, n_t, parts, cond_at,
    x_ref, w_ref, small_ref, ada_ref, ada_b_ref,
    x_all, w_all, small_all, mod_all, mod_rows,
    s_x, r_x, s_c, r_c, s_f, r_f, s_z, r_z, s_y, r_y, s_s, r_s, s_m, r_m, s_l,
):
    d, t = lax.axis_index("dp"), lax.axis_index("tensor")
    nx, no = n_t // CORES, n_d // INNER
    xi, ci = t // CORES, lax.rem(t, CORES)
    oi, ii = d // INNER, lax.rem(d, INNER)
    other = xi * CORES + (1 - ci)
    rows = x_ref.shape[0] // parts
    greet(n_d, n_t)
    local = [
        pltpu.make_async_copy(x_ref, x_all.at[t], s_l.at[0]),
        pltpu.make_async_copy(w_ref, w_all.at[d], s_l.at[1]),
        pltpu.make_async_copy(small_ref, small_all.at[d], s_l.at[2]),
    ]
    for copy in local:
        copy.start()
    sends = []
    for r in range(1, n_d):
        copy = remote(
            small_ref, small_all.at[d], s_s.at[r - 1], r_s.at[r - 1], lax.rem(d + r, n_d), t
        )
        copy.start()
        sends.append(copy)
    x_copies = []
    for r in range(1, nx):
        peer = lax.rem(xi + r, nx) * CORES + ci
        for p in range(parts):
            part = pl.ds(p * rows, rows)
            copy = remote(
                x_ref.at[part], x_all.at[t, part], s_x.at[r - 1, p], r_x.at[r - 1, p], d, peer
            )
            copy.start()
            x_copies.append((r, p, copy))
    z_copies = []
    for r in range(1, no):
        copy = remote(
            w_ref, w_all.at[d], s_z.at[r - 1], r_z.at[r - 1], lax.rem(oi + r, no) * INNER + ii, t
        )
        copy.start()
        z_copies.append(copy)
    y_copies = []
    for q in range(1, INNER):
        copy = remote(
            w_ref, w_all.at[d], s_y.at[q - 1, 0], r_y.at[q - 1, 0],
            oi * INNER + lax.rem(ii + q, INNER), t,
        )
        copy.start()
        y_copies.append(copy)
    core_copy = remote(x_ref, x_all.at[t], s_c, r_c, d, other)
    core_copy.start()
    local[2].wait()
    for copy in sends:
        copy.wait()
    cond = small_all[:, 0, cond_at:].astype(BF16)
    mod_rows[:, 0, :] = dot(cond, ada_ref[...], 1, 0) + ada_b_ref[...].astype(F32)
    own_mod = pltpu.make_async_copy(mod_rows.at[d], mod_all.at[d], s_l.at[3])
    own_mod.start()
    m_copies = []
    for r in range(1, n_d):
        peer = lax.rem(d + r, n_d)
        copy = remote(mod_rows.at[peer], mod_all.at[d], s_m.at[r - 1], r_m.at[r - 1], peer, t)
        copy.start()
        m_copies.append(copy)
    for r in range(1, no):
        z_copies[r - 1].wait()
        origin = lax.rem(oi + no - r, no) * INNER + ii
        for q in range(1, INNER):
            copy = remote(
                w_all.at[origin], w_all.at[origin], s_y.at[q - 1, r], r_y.at[q - 1, r],
                oi * INNER + lax.rem(ii + q, INNER), t,
            )
            copy.start()
            y_copies.append(copy)
    f_copies = []
    for r, p, copy in x_copies:
        copy.wait()
        origin = lax.rem(xi + nx - r, nx) * CORES + ci
        part = pl.ds(p * rows, rows)
        copy = remote(
            x_all.at[origin, part], x_all.at[origin, part],
            s_f.at[r - 1, p], r_f.at[r - 1, p], d, other,
        )
        copy.start()
        f_copies.append(copy)
    core_copy.wait()
    for copy in m_copies + y_copies + f_copies + [local[0], local[1], own_mod]:
        copy.wait()


def gather_call(x, w, small, ada, ada_b, cond_at, n_d, n_t):
    parts = 4
    nx, no = n_t // CORES, n_d // INNER
    cols = ada.shape[1]
    return pl.pallas_call(
        partial(gather_kernel, n_d, n_t, parts, cond_at),
        name="gather_tokens",
        out_shape=[
            struct((n_t,) + x.shape, BF16),
            struct((n_d,) + w.shape, BF16),
            struct((n_d,) + small.shape, F32),
            struct((n_d, 1, cols), F32),
        ],
        in_specs=[ANY, ANY, VMEM, VMEM, VMEM],
        out_specs=[ANY, ANY, VMEM, VMEM],
        scratch_shapes=[
            pltpu.VMEM((n_d, 1, cols), F32),
            DMA((nx - 1, parts)), DMA((nx - 1, parts)), DMA, DMA,
            DMA((nx - 1, parts)), DMA((nx - 1, parts)),
            DMA((no - 1,)), DMA((no - 1,)),
            DMA((INNER - 1, no)), DMA((INNER - 1, no)),
            DMA((n_d - 1,)), DMA((n_d - 1,)), DMA((n_d - 1,)), DMA((n_d - 1,)),
            DMA((4,)),
        ],
        compiler_params=params(0),
        cost_estimate=cost(1e6, 60e6),
    )(x, w, small, ada, ada_b)


def project_kernel(x_ref, w_ref, vec_ref, cos_ref, sin_ref, in_ref, out_ref):
    x = x_ref[0].astype(F32)
    gain, shift, scale = vec_ref[0:1], vec_ref[1:2], vec_ref[2:3]
    centred = x - mean_rows(x)
    normed = centred * lax.rsqrt(mean_rows(centred * centred) + EPSILON) * gain
    low = (normed * (1.0 + scale) + shift).astype(BF16)
    in_ref[0] = low
    proj = dot(w_ref[...], low, 0, 1)
    width = proj.shape[0] // 3
    half = HEAD_DIM // 2
    cos, sin = cos_ref[...], sin_ref[...]
    for j in range(2):
        factor = HEAD_DIM**-0.5 if j == 0 else 1.0
        for h in range(width // HEAD_DIM):
            at = j * width + h * HEAD_DIM
            a, b = proj[at : at + half], proj[at + half : at + HEAD_DIM]
            out_ref[0, at : at + half] = ((a * cos - b * sin) * factor).astype(BF16)
            out_ref[0, at + half : at + HEAD_DIM] = ((b * cos + a * sin) * factor).astype(BF16)
    out_ref[0, 2 * width :] = proj[2 * width :].astype(BF16)


def project_call(x_all, w, vecs, cos, sin):
    n_t, rows, features = x_all.shape
    width = w.shape[1]
    return pl.pallas_call(
        project_kernel,
        name="project",
        grid=(n_t,),
        in_specs=[
            pl.BlockSpec((1, rows, features), lambda i: (i, 0, 0)),
            pl.BlockSpec((features, width), lambda i: (0, 0)),
            pl.BlockSpec(vecs.shape, lambda i: (0, 0)),
            pl.BlockSpec((HEAD_DIM // 2, rows), lambda i: (0, i)),
            pl.BlockSpec((HEAD_DIM // 2, rows), lambda i: (0, i)),
        ],
        out_specs=[
            pl.BlockSpec((1, rows, features), lambda i: (i, 0, 0)),
            pl.BlockSpec((1, width, rows), lambda i: (i, 0, 0)),
        ],
        out_shape=[
            struct((n_t, rows, features), BF16),
            struct((n_t, width, rows), BF16),
        ],
        compiler_params=params(),
        cost_estimate=cost(2 * n_t * rows * features * width, 12e6),
    )(x_all, w, vecs, cos, sin)


def attend_kernel(heads, proj_ref, mix_ref, lse_ref, key_ref, val_ref):
    i = pl.program_id(0)
    blocks, total, rows = proj_ref.shape
    width = total // 3

    @pl.when(i == 0)
    def _():
        for b in range(blocks):
            for h in range(heads):
                at = width + h * HEAD_DIM
                key_ref[h, b * rows : (b + 1) * rows] = proj_ref[b, at : at + HEAD_DIM].T
            val_ref[:, b * rows : (b + 1) * rows] = proj_ref[b, 2 * width :]

    for h in range(heads):
        at = h * HEAD_DIM
        scores = dot(key_ref[h], proj_ref[i, at : at + HEAD_DIM], 1, 0)
        top = jnp.max(scores, axis=0, keepdims=True)
        grown = jnp.exp(scores - top)
        total_row = jnp.sum(grown, axis=0, keepdims=True)
        mixed = dot(val_ref[at : at + HEAD_DIM], grown.astype(BF16), 1, 0)
        mix_ref[0, at : at + HEAD_DIM] = (mixed / total_row).astype(BF16)
        lse_ref[0, h : h + 1] = top + jnp.log(total_row)


def attend_call(proj):
    blocks, total, rows = proj.shape
    width = total // 3
    heads = width // HEAD_DIM
    length = blocks * rows
    return pl.pallas_call(
        partial(attend_kernel, heads),
        name="attend",
        grid=(blocks,),
        in_specs=[pl.BlockSpec(proj.shape, lambda i: (0, 0, 0))],
        out_specs=[
            pl.BlockSpec((1, width, rows), lambda i: (i, 0, 0)),
            pl.BlockSpec((1, heads, rows), lambda i: (i, 0, 0)),
        ],
        out_shape=[struct((blocks, width, rows), BF16), struct((blocks, heads, rows), F32)],
        scratch_shapes=[
            pltpu.VMEM((heads, length, HEAD_DIM), BF16),
            pltpu.VMEM((width, length), BF16),
        ],
        compiler_params=params(),
        cost_estimate=cost(16 * heads * length * length * HEAD_DIM, 4e6, heads * length * length),
    )(proj)


def swap_kernel(n_t, src_ref, dst_ref, send, recv, own):
    d, t = lax.axis_index("dp"), lax.axis_index("tensor")
    barrier = pltpu.get_barrier_semaphore()
    for r in range(1, n_t):
        pl.semaphore_signal(barrier, 1, device_id=(d, lax.rem(t + r, n_t)), device_id_type=MESH)
    pl.semaphore_wait(barrier, n_t - 1)
    copies = [pltpu.make_async_copy(src_ref.at[t], dst_ref.at[t], own)]
    copies[0].start()
    for r in range(1, n_t):
        peer = lax.rem(t + r, n_t)
        copy = remote(src_ref.at[peer], dst_ref.at[t], send.at[r - 1], recv.at[r - 1], d, peer)
        copy.start()
        copies.append(copy)
    for copy in copies:
        copy.wait()


def swap_call(blocks, n_t, collective_id):
    return pl.pallas_call(
        partial(swap_kernel, n_t),
        name="swap_blocks",
        out_shape=struct(blocks.shape, blocks.dtype),
        in_specs=[ANY],
        out_specs=ANY,
        scratch_shapes=[DMA((n_t - 1,)), DMA((n_t - 1,)), DMA],
        compiler_params=params(collective_id),
        cost_estimate=cost(0, 30e6),
    )(blocks)


GAIN1, SHIFT_A, SCALE_A, GATE_A, GAIN2, SHIFT_M, SCALE_M, GATE_M, B_DOWN, B_UP = range(10)
S_SHIFT_A, S_SCALE_A, S_GATE_A, S_SHIFT_M, S_SCALE_M, S_GATE_M = range(6)
S_GAIN2, S_B_DOWN, S_SQ_A, S_SQ_M, S_SQ_R, S_GAIN1, S_B_UP = range(6, 13)


def middle_kernel(
    n_d, n_t,
    mix_ref, x_ref, g_ref, vec_ref, w_ref,
    out_ref, dmid_ref, dmix_ref, stat_ref, grad_ref,
    w_buf, o_buf, g_buf, go_buf, mid_ref, low_ref, lowt_ref, dlt_ref, dl_ref, acc_out, acc_in, s_w, s_o, s_g,
):
    rows, features = x_ref.shape
    width = mix_ref.shape[1]
    units = w_buf.shape[3] // 2
    loads = [
        pltpu.make_async_copy(w_ref.at[:, :, :, pl.ds(2 * units, o_buf.shape[3])], o_buf, s_o)
    ]
    for b in range(n_t):
        loads.append(
            pltpu.make_async_copy(
                w_ref.at[:, b, :, pl.ds(0, 2 * units)], w_buf.at[b], s_w.at[b]
            )
        )
    for copy in loads:
        copy.start()
    vec = lambda row: vec_ref[row : row + 1]
    x = x_ref[...].astype(F32)
    cot = g_ref[...].astype(F32)
    d_mlp = (vec(GATE_M) * cot).astype(BF16)
    dl_ref[...] = d_mlp
    dlt_ref[...] = d_mlp.T
    stat_ref[S_B_DOWN : S_B_DOWN + 1] = sum_tokens(d_mlp.astype(F32))
    loads[0].wait()
    attn_out = jnp.zeros((rows, features), F32)
    for b in range(n_t):
        w_out = o_buf[:, b].reshape(features, o_buf.shape[3])[:, :width]
        attn_out += dot(mix_ref[b].T, w_out, 1, 1)
    branch = vec(GATE_A) * attn_out
    stat_ref[S_SQ_A : S_SQ_A + 1] = sum_tokens(branch * branch)
    middle = x + branch
    mid_ref[...] = middle
    centred = middle - mean_rows(middle)
    inv = lax.rsqrt(mean_rows(centred * centred) + EPSILON)
    low = (centred * inv * vec(GAIN2) * (1.0 + vec(SCALE_M)) + vec(SHIFT_M)).astype(BF16)
    low_ref[...] = low
    lowt_ref[...] = low.T
    acc_out[...] = jnp.zeros_like(acc_out)
    acc_in[...] = jnp.zeros_like(acc_in)
    stores = []
    for b in range(n_t):
        loads[1 + b].wait()
        up = w_buf[b, :, :, :units].reshape(features, units)
        down = w_buf[b, :, :, units:].reshape(features, units)
        hidden = dot(low_ref[...], up, 1, 0) + vec(B_UP + b)
        square = hidden * hidden
        bent = jnp.tanh(GELU_C * hidden * (1.0 + GELU_A * square))
        half = 0.5 * (1.0 + bent)
        active = (hidden * half).astype(BF16)
        slope = half + (0.5 * GELU_C) * hidden * (1.0 - bent * bent) * (
            1.0 + (3.0 * GELU_A) * square
        )
        acc_out[...] += dot(active, down, 1, 1)
        g_buf[b, :, :, units:] = (
            dot(dlt_ref[...], active, 1, 0).astype(BF16).reshape(n_d, -1, units)
        )
        d_hidden = (dot(dl_ref[...], down, 1, 0) * slope).astype(BF16)
        stat_ref[S_B_UP + b : S_B_UP + b + 1] = sum_tokens(d_hidden.astype(F32))
        g_buf[b, :, :, :units] = (
            dot(lowt_ref[...], d_hidden, 1, 0).astype(BF16).reshape(n_d, -1, units)
        )
        copy = pltpu.make_async_copy(
            g_buf.at[b], grad_ref.at[:, b, :, pl.ds(0, 2 * units)], s_g.at[b]
        )
        copy.start()
        stores.append(copy)
        acc_in[...] += dot(d_hidden, up, 1, 1)
    middle = mid_ref[...]
    cot = g_ref[...].astype(F32)
    mlp_out = acc_out[...] + vec(B_DOWN)
    mlp_branch = vec(GATE_M) * mlp_out
    result = middle + mlp_branch
    out_ref[...] = result.astype(BF16)
    stat_ref[S_SQ_M : S_SQ_M + 1] = sum_tokens(mlp_branch * mlp_branch)
    stat_ref[S_SQ_R : S_SQ_R + 1] = sum_tokens(result * result)
    stat_ref[S_GATE_M : S_GATE_M + 1] = sum_tokens(cot * mlp_out)
    e = acc_in[...]
    centred = middle - mean_rows(middle)
    inv = lax.rsqrt(mean_rows(centred * centred) + EPSILON)
    nhat = centred * inv
    gain, scale = vec(GAIN2), 1.0 + vec(SCALE_M)
    by_nhat = sum_tokens(e * nhat)
    stat_ref[S_SHIFT_M : S_SHIFT_M + 1] = sum_tokens(e)
    stat_ref[S_SCALE_M : S_SCALE_M + 1] = by_nhat * gain
    stat_ref[S_GAIN2 : S_GAIN2 + 1] = by_nhat * scale
    dn = e * (scale * gain)
    d_middle = cot + inv * (dn - mean_rows(dn) - nhat * mean_rows(dn * nhat))
    dmid_ref[...] = d_middle
    attn_out = jnp.zeros((rows, features), F32)
    for b in range(n_t):
        w_out = o_buf[:, b].reshape(features, o_buf.shape[3])[:, :width]
        attn_out += dot(mix_ref[b].T, w_out, 1, 1)
    stat_ref[S_GATE_A : S_GATE_A + 1] = sum_tokens(d_middle * attn_out)
    d_attn = (vec(GATE_A) * d_middle).astype(BF16)
    d_attn_t = d_attn.T
    go_buf[...] = jnp.zeros_like(go_buf)
    for b in range(n_t):
        w_out = o_buf[:, b].reshape(features, o_buf.shape[3])[:, :width]
        dmix_ref[b] = dot(d_attn, w_out, 1, 0).astype(BF16).T
        go_buf[:, b, :, :width] = dot(d_attn_t, mix_ref[b], 1, 1).astype(BF16).reshape(n_d, -1, width)
    stat_ref[S_GAIN1 : S_GAIN1 + 1] = jnp.zeros((1, features), F32)
    stat_ref[S_SHIFT_A : S_SCALE_A + 1] = jnp.zeros((2, features), F32)
    if stat_ref.shape[0] > S_B_UP + n_t:
        stat_ref[S_B_UP + n_t :] = jnp.zeros((stat_ref.shape[0] - S_B_UP - n_t, features), F32)
    copy = pltpu.make_async_copy(
        go_buf, grad_ref.at[:, :, :, pl.ds(2 * units, o_buf.shape[3])], s_o
    )
    copy.start()
    for copy in stores + [copy]:
        copy.wait()


def middle_call(mix, x, g, vecs, w, n_d, n_t, stat_rows):
    rows, features = x.shape
    part, columns = w.shape[2], w.shape[3]
    width = mix.shape[1]
    units = features
    extra = columns - 2 * units
    return pl.pallas_call(
        partial(middle_kernel, n_d, n_t),
        name="middle",
        out_shape=[
            struct((rows, features), BF16),
            struct((rows, features), F32),
            struct((n_t, width, rows), BF16),
            struct((stat_rows, features), F32),
            struct(w.shape, BF16),
        ],
        in_specs=[VMEM, VMEM, VMEM, VMEM, ANY],
        out_specs=[VMEM, VMEM, VMEM, VMEM, ANY],
        scratch_shapes=[
            pltpu.VMEM((n_t, n_d, part, 2 * units), BF16),
            pltpu.VMEM((n_d, n_t, part, extra), BF16),
            pltpu.VMEM((n_t, n_d, part, 2 * units), BF16),
            pltpu.VMEM((n_d, n_t, part, extra), BF16),
            pltpu.VMEM((rows, features), F32),
            pltpu.VMEM((rows, features), BF16),
            pltpu.VMEM((features, rows), BF16),
            pltpu.VMEM((features, rows), BF16),
            pltpu.VMEM((rows, features), BF16),
            pltpu.VMEM((rows, features), F32),
            pltpu.VMEM((rows, features), F32),
            DMA((n_t,)), DMA, DMA((n_t,)),
        ],
        compiler_params=params(),
        cost_estimate=cost(2 * rows * features * features * (6 * n_t + 4), 30e6),
    )(mix, x, g, vecs, w)


def attend_back_kernel(
    heads, proj_ref, dmix_ref, mix_ref, lse_ref, cos_ref, sin_ref, out_ref,
    key_ref, keyt_ref, val_ref, dkey_ref, dval_ref,
):
    i = pl.program_id(0)
    blocks, total, rows = proj_ref.shape
    width = total // 3
    half = HEAD_DIM // 2

    @pl.when(i == 0)
    def _():
        dkey_ref[...] = jnp.zeros_like(dkey_ref)
        dval_ref[...] = jnp.zeros_like(dval_ref)
        for b in range(blocks):
            part = slice(b * rows, (b + 1) * rows)
            keyt_ref[:, part] = proj_ref[b, width : 2 * width]
            for h in range(heads):
                at = h * HEAD_DIM
                key_ref[h, part] = proj_ref[b, width + at : width + at + HEAD_DIM].T
                val_ref[h, part] = proj_ref[b, 2 * width + at : 2 * width + at + HEAD_DIM].T

    def unrotate(block, at, rows_at, factor, a, b):
        cos, sin = cos_ref[:, rows_at], sin_ref[:, rows_at]
        out_ref[block, at : at + half] = ((a * cos + b * sin) * factor).astype(BF16)
        out_ref[block, at + half : at + HEAD_DIM] = ((b * cos - a * sin) * factor).astype(BF16)

    for h in range(heads):
        at = h * HEAD_DIM
        query_t = proj_ref[i, at : at + HEAD_DIM]
        dmix_t = dmix_ref[i, at : at + HEAD_DIM]
        mix_t = mix_ref[i, at : at + HEAD_DIM]
        inner = jnp.sum(dmix_t.astype(F32) * mix_t.astype(F32), axis=0, keepdims=True)
        probs = jnp.exp(dot(key_ref[h], query_t, 1, 0) - lse_ref[i, h : h + 1])
        d_probs = dot(val_ref[h], dmix_t, 1, 0)
        d_scores = (probs * (d_probs - inner)).astype(BF16)
        dval_ref[h] += dot(probs.astype(BF16), dmix_t.T, 1, 0)
        dkey_ref[h] += dot(d_scores, query_t.T, 1, 0)
        d_query = dot(keyt_ref[at : at + HEAD_DIM], d_scores, 1, 0)
        unrotate(
            i, at, pl.ds(pl.multiple_of(i * rows, rows), rows), HEAD_DIM**-0.5,
            d_query[:half], d_query[half:],
        )

    @pl.when(i == blocks - 1)
    def _():
        for b in range(blocks):
            part = slice(b * rows, (b + 1) * rows)
            for h in range(heads):
                at = h * HEAD_DIM
                d_key = dkey_ref[h, part].T
                unrotate(b, width + at, part, 1.0, d_key[:half], d_key[half:])
                out_ref[b, 2 * width + at : 2 * width + at + HEAD_DIM] = (
                    dval_ref[h, part].T.astype(BF16)
                )


def attend_back_call(proj, dmix, mix, lse, cos, sin):
    blocks, total, rows = proj.shape
    width = total // 3
    heads = width // HEAD_DIM
    length = blocks * rows
    whole = lambda a: pl.BlockSpec(a.shape, lambda i: (0,) * a.ndim)
    return pl.pallas_call(
        partial(attend_back_kernel, heads),
        name="attend_back",
        grid=(blocks,),
        in_specs=[whole(a) for a in (proj, dmix, mix, lse, cos, sin)],
        out_specs=whole(proj),
        out_shape=struct(proj.shape, BF16),
        scratch_shapes=[
            pltpu.VMEM((heads, length, HEAD_DIM), BF16),
            pltpu.VMEM((width, length), BF16),
            pltpu.VMEM((heads, length, HEAD_DIM), BF16),
            pltpu.VMEM((heads, length, HEAD_DIM), F32),
            pltpu.VMEM((heads, length, HEAD_DIM), F32),
        ],
        compiler_params=params(),
        cost_estimate=cost(40 * heads * length * length * HEAD_DIM, 6e6, heads * length * length),
    )(proj, dmix, mix, lse, cos, sin)


def project_back_kernel(n_d, dproj_ref, in_ref, w_ref, part_ref, grad_ref, acc_ref):
    i = pl.program_id(0)

    @pl.when(i == 0)
    def _():
        acc_ref[...] = jnp.zeros_like(acc_ref)

    d_proj = dproj_ref[0]
    part_ref[0] = dot(d_proj.T, w_ref[...], 1, 1).astype(BF16)
    acc_ref[...] += dot(d_proj, in_ref[0], 1, 0)

    @pl.when(i == pl.num_programs(0) - 1)
    def _():
        grad_ref[...] = acc_ref[...].T.astype(BF16).reshape(grad_ref.shape)


def project_back_call(dproj, attn_in, w, n_d):
    n_t, rows, features = attn_in.shape
    width = w.shape[1]
    return pl.pallas_call(
        partial(project_back_kernel, n_d),
        name="project_back",
        grid=(n_t,),
        in_specs=[
            pl.BlockSpec((1, width, rows), lambda i: (i, 0, 0)),
            pl.BlockSpec((1, rows, features), lambda i: (i, 0, 0)),
            pl.BlockSpec(w.shape, lambda i: (0, 0)),
        ],
        out_specs=[
            pl.BlockSpec((1, rows, features), lambda i: (i, 0, 0)),
            pl.BlockSpec((n_d, features // n_d, width), lambda i: (0, 0, 0)),
        ],
        out_shape=[
            struct((n_t, rows, features), BF16),
            struct((n_d, features // n_d, width), BF16),
        ],
        scratch_shapes=[pltpu.VMEM((width, features), F32)],
        compiler_params=params(),
        cost_estimate=cost(4 * n_t * rows * features * width, 12e6),
    )(dproj, attn_in, w)


def reduce_kernel(
    n_d, n_t, parts,
    part_ref, grad_ref, sum_ref, gsum_ref,
    rc, sx, rx, ry, sz, rz,
    s_c, r_c, s_x, r_x, s_y, r_y, s_z, r_z,
):
    d, t = lax.axis_index("dp"), lax.axis_index("tensor")
    nx, no = n_t // CORES, n_d // INNER
    xi, ci = t // CORES, lax.rem(t, CORES)
    oi, ii = d // INNER, lax.rem(d, INNER)
    other = xi * CORES + (1 - ci)
    rows = sum_ref.shape[0] // parts
    greet(n_d, n_t)
    y_copies = []
    for q in range(1, INNER):
        to = lax.rem(ii + q, INNER)
        copy = remote(
            grad_ref.at[:, to], ry.at[q - 1], s_y.at[q - 1], r_y.at[q - 1], oi * INNER + to, t
        )
        copy.start()
        y_copies.append(copy)
    c_copies = []
    for r in list(range(1, nx)) + [0]:
        block = lax.rem(xi + r, nx) * CORES + (1 - ci)
        for p in range(parts):
            at = pl.ds(p * rows, rows)
            copy = remote(
                part_ref.at[block, at], rc.at[r, at], s_c.at[r, p], r_c.at[r, p], d, other
            )
            copy.start()
            c_copies.append((r, p, copy))
    x_copies = []
    for r, p, copy in c_copies:
        copy.wait()
        if r > 0:
            to = lax.rem(xi + r, nx) * CORES + ci
            at = pl.ds(p * rows, rows)
            sx[r - 1, at] = (part_ref[to, at].astype(F32) + rc[r, at].astype(F32)).astype(BF16)
            copy = remote(
                sx.at[r - 1, at], rx.at[r - 1, at], s_x.at[r - 1, p], r_x.at[r - 1, p], d, to
            )
            copy.start()
            x_copies.append((r, p, copy))
    for copy in y_copies:
        copy.wait()
    z_copies = []
    for r in range(1, no):
        to = lax.rem(oi + r, no)
        total = grad_ref[to, ii].astype(F32)
        for q in range(1, INNER):
            total += ry[q - 1, to].astype(F32)
        sz[r - 1] = total.astype(BF16)
        copy = remote(sz.at[r - 1], rz.at[r - 1], s_z.at[r - 1], r_z.at[r - 1], to * INNER + ii, t)
        copy.start()
        z_copies.append(copy)
    total = grad_ref[oi, ii].astype(F32)
    for q in range(1, INNER):
        total += ry[q - 1, oi].astype(F32)
    for copy in z_copies:
        copy.wait()
    for r in range(1, no):
        total += rz[r - 1].astype(F32)
    gsum_ref[...] = total
    for r, p, copy in x_copies:
        copy.wait()
    for p in range(parts):
        at = pl.ds(p * rows, rows)
        total = part_ref[t, at].astype(F32) + rc[0, at].astype(F32)
        for r in range(1, nx):
            total += rx[r - 1, at].astype(F32)
        sum_ref[at] = total


def reduce_call(part, grad, n_d, n_t):
    parts = 4
    nx, no = n_t // CORES, n_d // INNER
    block = part.shape[1:]
    piece = grad.shape[1:]
    grad = grad.reshape((no, INNER) + piece)
    return pl.pallas_call(
        partial(reduce_kernel, n_d, n_t, parts),
        name="reduce_parts",
        out_shape=[struct(block, F32), struct(piece, F32)],
        in_specs=[VMEM, VMEM],
        out_specs=[VMEM, VMEM],
        scratch_shapes=[
            pltpu.VMEM((nx,) + block, BF16),
            pltpu.VMEM((nx - 1,) + block, BF16),
            pltpu.VMEM((nx - 1,) + block, BF16),
            pltpu.VMEM((INNER - 1, no) + piece, BF16),
            pltpu.VMEM((no - 1,) + piece, BF16),
            pltpu.VMEM((no - 1,) + piece, BF16),
            DMA((nx, parts)), DMA((nx, parts)),
            DMA((nx - 1, parts)), DMA((nx - 1, parts)),
            DMA((INNER - 1,)), DMA((INNER - 1,)),
            DMA((no - 1,)), DMA((no - 1,)),
        ],
        compiler_params=params(3),
        cost_estimate=cost(1e6, 60e6),
    )(part, grad)


def norm_back_kernel(x_ref, e_ref, dmid_ref, vec_ref, stat_in_ref, out_ref, stat_ref):
    x = x_ref[...].astype(F32)
    e = e_ref[...]
    gain, scale = vec_ref[GAIN1 : GAIN1 + 1], 1.0 + vec_ref[SCALE_A : SCALE_A + 1]
    centred = x - mean_rows(x)
    inv = lax.rsqrt(mean_rows(centred * centred) + EPSILON)
    nhat = centred * inv
    dn = e * (scale * gain)
    out_ref[...] = dmid_ref[...] + inv * (dn - mean_rows(dn) - nhat * mean_rows(dn * nhat))
    by_nhat = sum_tokens(e * nhat)
    stat_ref[...] = stat_in_ref[...]
    stat_ref[S_SHIFT_A : S_SHIFT_A + 1] = sum_tokens(e)
    stat_ref[S_SCALE_A : S_SCALE_A + 1] = by_nhat * gain
    stat_ref[S_GAIN1 : S_GAIN1 + 1] = by_nhat * scale


def norm_back_call(x, e, dmid, vecs, stat):
    return pl.pallas_call(
        norm_back_kernel,
        name="norm_back",
        out_shape=[struct(x.shape, F32), struct(stat.shape, F32)],
        in_specs=[VMEM] * 5,
        out_specs=[VMEM] * 2,
        compiler_params=params(),
        cost_estimate=cost(20 * x.size, 8e6),
    )(x, e, dmid, vecs, stat)


def stat_kernel(
    n_d, n_t, stat_ref, ada_ref, table_ref, cond_ref,
    got, mine, rows_out, rows_in, s_t, r_t, s_d, r_d, s_p, r_p, s_l,
):
    d, t = lax.axis_index("dp"), lax.axis_index("tensor")
    greet(n_d, n_t)
    copies = []
    for r in range(1, n_t):
        copy = remote(
            stat_ref, got.at[r - 1], s_t.at[r - 1], r_t.at[r - 1], d, lax.rem(t + r, n_t)
        )
        copy.start()
        copies.append(copy)
    total = stat_ref[...]
    for copy in copies:
        copy.wait()
    for r in range(1, n_t):
        total += got[r - 1]
    mine[...] = total
    own = pltpu.make_async_copy(mine, table_ref.at[d], s_l.at[0])
    own.start()
    copies = []
    for r in range(1, n_d):
        copy = remote(mine, table_ref.at[d], s_d.at[r - 1], r_d.at[r - 1], lax.rem(d + r, n_d), t)
        copy.start()
        copies.append(copy)
    own.wait()
    for copy in copies:
        copy.wait()
    columns = ada_ref.shape[1]
    features = table_ref.shape[2]
    flat = jnp.concatenate([table_ref[:, row, :] for row in range(6)], axis=1)
    moved = pltpu.roll(flat, lax.rem(n_d - d, n_d) * columns, 1)[:, :columns]
    product = lax.dot_general(
        moved, ada_ref[...].astype(F32), (((1,), (1,)), ((), ())),
        precision=lax.Precision.HIGHEST, preferred_element_type=F32,
    )
    rows_out[:, 0, :] = product
    own = pltpu.make_async_copy(rows_out.at[d], rows_in.at[d], s_l.at[1])
    own.start()
    copies = []
    for r in range(1, n_d):
        peer = lax.rem(d + r, n_d)
        copy = remote(rows_out.at[peer], rows_in.at[d], s_p.at[r - 1], r_p.at[r - 1], peer, t)
        copy.start()
        copies.append(copy)
    own.wait()
    for copy in copies:
        copy.wait()
    cond_ref[...] = jnp.sum(rows_in[:, 0, :], axis=0, keepdims=True)


def stat_call(stat, ada, n_d, n_t):
    width = ada.shape[0]
    return pl.pallas_call(
        partial(stat_kernel, n_d, n_t),
        name="gather_statistics",
        out_shape=[struct((n_d,) + stat.shape, F32), struct((1, width), F32)],
        in_specs=[VMEM, VMEM],
        out_specs=[VMEM, VMEM],
        scratch_shapes=[
            pltpu.VMEM((n_t - 1,) + stat.shape, F32),
            pltpu.VMEM(stat.shape, F32),
            pltpu.VMEM((n_d, 1, width), F32),
            pltpu.VMEM((n_d, 1, width), F32),
            DMA((n_t - 1,)), DMA((n_t - 1,)),
            DMA((n_d - 1,)), DMA((n_d - 1,)),
            DMA((n_d - 1,)), DMA((n_d - 1,)),
            DMA((2,)),
        ],
        compiler_params=params(4),
        cost_estimate=cost(1e6, 20e6),
    )(stat, ada)


def finish_kernel(n_units, count, table_ref, cond_ref, ada_ref, bias_ref, sum_ref, root_ref):
    n_d = table_ref.shape[0]
    features = table_ref.shape[2]
    for row in range(6):
        at = slice(row * features, (row + 1) * features)
        total = jnp.zeros((cond_ref.shape[0], features), F32)
        for s in range(n_d):
            total += cond_ref[:, s : s + 1] * table_ref[s, row : row + 1, :]
        ada_ref[:, at] = total
        bias_ref[:, at] = jnp.sum(table_ref[:, row, :], axis=0, keepdims=True)
    total = table_ref[0]
    for s in range(1, n_d):
        total += table_ref[s]
    sum_ref[...] = total
    for k, row in enumerate((S_SQ_A, S_SQ_M, S_SQ_R)):
        root_ref[k : k + 1] = jnp.broadcast_to(
            jnp.sqrt(jnp.sum(total[row : row + 1], axis=1, keepdims=True) / count),
            (1, root_ref.shape[1]),
        )


def finish_call(table, cond_t, count):
    features = table.shape[2]
    width = cond_t.shape[0]
    return pl.pallas_call(
        partial(finish_kernel, 0, count),
        name="finish",
        out_shape=[
            struct((width, 6 * features), F32),
            struct((1, 6 * features), F32),
            struct(table.shape[1:], F32),
            struct((3, 128), F32),
        ],
        in_specs=[VMEM] * 2,
        out_specs=[VMEM] * 4,
        compiler_params=params(),
        cost_estimate=cost(1e7, 4e6),
    )(table, cond_t)


def shards(
    block_input, condition, modulation_weight, modulation_bias, first_gain, qkv_weight, out_weight,
    second_gain, up_weight, up_bias, down_weight, down_bias, grad_output,
):
    n_t, n_d = lax.axis_size("tensor"), lax.axis_size("dp")
    rows, sequences, features = block_input.shape
    assert sequences == 1
    length = rows * n_t
    part, width = qkv_weight.shape[1:]
    units = up_weight.shape[1]
    assert units == features and n_t % CORES == 0 and n_d % INNER == 0
    cond_width = condition.shape[1]
    extra = -width % 128
    x = block_input.reshape(rows, features)
    g = grad_output.reshape(rows, features)

    pack = jnp.concatenate(
        [up_weight, down_weight.T, out_weight.T, jnp.zeros((part, extra), BF16)], axis=1
    )
    w_rest = lax.all_gather(pack, ("dp", "tensor"), axis=0, tiled=False)
    w_rest = w_rest.reshape(n_d, n_t, part, pack.shape[1])

    small = jnp.concatenate(
        [first_gain, second_gain, down_bias, up_bias]
    ).astype(F32)
    cond_at = -(-small.shape[0] // 128) * 128
    small = jnp.concatenate(
        [small, jnp.zeros((cond_at - small.shape[0],), F32), condition[0].astype(F32)]
    )[None]
    qkv = qkv_weight.transpose(1, 0, 2).reshape(part, 3 * width)
    x_all, w_qkv, small_all, mod_all = gather_call(
        x, qkv, small, modulation_weight, modulation_bias[None], cond_at, n_d, n_t
    )
    w_qkv = w_qkv.reshape(features, 3 * width)
    mod = mod_all.reshape(6, features)
    pick = lambda at, count: small_all[:, 0, at : at + count].reshape(-1, features)
    own = first_gain.shape[0]
    vecs = jnp.concatenate(
        [
            pick(0, own), mod[0:3], pick(own, own), mod[3:6], pick(2 * own, own),
            pick(3 * own, up_bias.shape[0]),
        ]
    )
    inverse = 10000.0 ** (-np.arange(HEAD_DIM // 2) * 2.0 / HEAD_DIM)
    angles = inverse[:, None] * np.arange(length)[None, :]
    cos, sin = jnp.asarray(np.cos(angles), F32), jnp.asarray(np.sin(angles), F32)

    attn_in, proj = project_call(x_all, w_qkv, vecs[:3], cos, sin)
    mix, lse = attend_call(proj)
    mix_own = swap_call(mix, n_t, 1)
    stat_rows = -(-(S_B_UP + n_t) // 8) * 8
    out, d_middle, d_mix, stat, grads = middle_call(
        mix_own, x, g, vecs, w_rest, n_d, n_t, stat_rows
    )
    g_rest = lax.psum_scatter(
        grads.reshape(n_d * n_t, part, pack.shape[1]), ("dp", "tensor"),
        scatter_dimension=0, tiled=False,
    ).astype(F32)
    d_mix_all = swap_call(d_mix, n_t, 2)
    d_proj = attend_back_call(proj, d_mix_all, mix, lse, cos, sin)
    shares, g_qkv = project_back_call(d_proj, attn_in, w_qkv, n_d)
    d_attn_in, g_qkv = reduce_call(shares, g_qkv, n_d, n_t)
    grad_input, stat = norm_back_call(x, d_attn_in, d_middle, vecs, stat)
    table, grad_cond = stat_call(stat, modulation_weight, n_d, n_t)
    cond_t = small_all[:, 0, cond_at:].T
    grad_ada, grad_ada_b, sums, roots = finish_call(table, cond_t, float(length * n_d * features))
    return (
        out.reshape(block_input.shape),
        grad_input.reshape(block_input.shape),
        grad_cond,
        grad_ada,
        grad_ada_b[0],
        sums[S_GAIN1],
        g_qkv.reshape(part, 3, width).transpose(1, 0, 2),
        g_rest[:, 2 * units : 2 * units + width].T,
        sums[S_GAIN2],
        g_rest[:, :units],
        sums[S_B_UP : S_B_UP + n_t].reshape(-1),
        g_rest[:, units : 2 * units].T,
        sums[S_B_DOWN],
        roots[:, 0],
    )


def solution(mesh):
    in_specs = (
        P("tensor", "dp", None),
        P("dp", None),
        P(None, "dp"),
        P("dp"),
        P("dp"),
        P(None, "dp", "tensor"),
        P("tensor", "dp"),
        P("dp"),
        P("dp", "tensor"),
        P("dp"),
        P("tensor", "dp"),
        P("dp"),
        P("tensor", "dp", None),
    )
    out_specs = (
        P("tensor", "dp", None),
        P("tensor", "dp", None),
        P("dp", None),
        P(),
        P(),
        P(),
        P(None, "dp", "tensor"),
        P("tensor", "dp"),
        P(),
        P("dp", "tensor"),
        P(),
        P("tensor", "dp"),
        P(),
        P(),
    )
    return jax.shard_map(shards, mesh=mesh, in_specs=in_specs, out_specs=out_specs, check_vma=False)
```

```python
from functools import partial

import jax
import jax.numpy as jnp
import numpy as np
from jax import lax
from jax.experimental import pallas as pl
from jax.experimental.pallas import tpu as pltpu
from jax.sharding import PartitionSpec as P

HEAD_DIM = 64
EPSILON = 1e-05
CORES = 2
INNER = 2
MESH = pl.DeviceIdType.MESH
VMEM_LIMIT = 58 << 20
GELU_C = float(np.sqrt(2.0 / np.pi))
GELU_A = 0.044715
F32 = jnp.float32
BF16 = jnp.bfloat16
ANY = pl.BlockSpec(memory_space=pl.ANY)
VMEM = pl.BlockSpec(memory_space=pltpu.VMEM)
DMA = pltpu.SemaphoreType.DMA


def dot(lhs, rhs, lhs_dim, rhs_dim):
    return lax.dot_general(
        lhs, rhs, (((lhs_dim,), (rhs_dim,)), ((), ())), preferred_element_type=F32
    )


def params(collective_id=None, **more):
    if collective_id is not None:
        more.update(collective_id=collective_id, has_side_effects=True)
    return pltpu.CompilerParams(vmem_limit_bytes=VMEM_LIMIT, **more)


def cost(flops, moved, special=0):
    return pl.CostEstimate(flops=int(flops), bytes_accessed=int(moved), transcendentals=int(special))


def struct(shape, dtype):
    return jax.ShapeDtypeStruct(shape, dtype)


def mean_rows(values):
    return jnp.mean(values, axis=-1, keepdims=True)


def sum_tokens(values):
    return jnp.sum(values, axis=0, keepdims=True)


GAIN1, SHIFT_A, SCALE_A, GATE_A, GAIN2, SHIFT_M, SCALE_M, GATE_M, B_DOWN, B_UP = range(10)
MOD_ROWS = (SHIFT_A, SCALE_A, GATE_A, SHIFT_M, SCALE_M, GATE_M)
S_GATE_A, S_SHIFT_M, S_SCALE_M, S_GATE_M, S_GAIN2, S_B_DOWN, S_SQ_A, S_SQ_M, S_SQ_R, S_B_UP = range(10)
L_SHIFT_A, L_SCALE_A, L_GAIN1 = range(3)


def order(k, xi, ci, nx):
    return lax.rem(xi + k // CORES, nx) * CORES + lax.rem(ci + k % CORES, CORES)


def mirror(k, nx):
    return (nx - k // CORES) % nx * CORES + (CORES - k % CORES) % CORES


def place(n_d, n_t):
    d, t = lax.axis_index("dp"), lax.axis_index("tensor")
    return d, t, d // INNER, lax.rem(d, INNER), t // CORES, lax.rem(t, CORES)


def greet(n_d, n_t):
    d, t = lax.axis_index("dp"), lax.axis_index("tensor")
    barrier = pltpu.get_barrier_semaphore()
    for r in range(1, n_t):
        pl.semaphore_signal(
            barrier, 1, device_id=(d, lax.rem(t + r, n_t)), device_id_type=MESH
        )
    for r in range(1, n_d):
        pl.semaphore_signal(
            barrier, 1, device_id=(lax.rem(d + r, n_d), t), device_id_type=MESH
        )
    pl.semaphore_wait(barrier, n_t - 1 + n_d - 1)


def remote(src, dst, send, recv, d, t):
    return pltpu.make_async_remote_copy(
        src_ref=src, dst_ref=dst, send_sem=send, recv_sem=recv, device_id=(d, t), device_id_type=MESH
    )

def front_kernel(
    n_d, n_t, parts, heads, cond_at, bias_at, sizes, chunks, plan, hand,
    x_ref, qkv_ref, small_ref, ada_ref, up_ref, down_ref, outw_ref, cos_ref, sin_ref,
    in_all, proj_ref, mix_ref, lse_ref, mix_own, vec_ref, cond_ref, w_all, w_up, w_down, w_out,
    x_all, w_pack, wt_ref, out_pack, small_all, mod_all, mod_rows, key_ref,
    s_x, r_x, s_c, r_c, s_f, r_f, s_z, r_z, s_y, r_y, s_s, r_s, s_m, r_m, s_l,
    s_w, r_w, s_k, r_k, s_o, r_o,
):
    d, t, oi, ii, xi, ci = place(n_d, n_t)
    nx, no = n_t // CORES, n_d // INNER
    other = xi * CORES + (1 - ci)
    piece = x_ref.shape[0] // parts
    rows, features = x_ref.shape
    width = qkv_ref.shape[2]
    half = HEAD_DIM // 2
    for j in range(3):
        w_pack[:, j * width : (j + 1) * width] = qkv_ref[j]
    out_pack[:, :width] = outw_ref[...].T
    if out_pack.shape[1] > width:
        out_pack[:, width:] = jnp.zeros((out_pack.shape[0], out_pack.shape[1] - width), BF16)
    greet(n_d, n_t)
    s_copies = []
    for r in range(1, n_d):
        copy = remote(
            small_ref, small_all.at[d], s_s.at[r - 1], r_s.at[r - 1], lax.rem(d + r, n_d), t
        )
        copy.start()
        s_copies.append(copy)
    x_copies = []
    for r in range(1, nx):
        peer = lax.rem(xi + r, nx) * CORES + ci
        for p in range(parts):
            at = pl.ds(p * piece, piece)
            copy = remote(
                x_ref.at[at], x_all.at[t, at], s_x.at[r - 1, p], r_x.at[r - 1, p], d, peer
            )
            copy.start()
            x_copies.append((r, p, copy))
    z_copies = []
    for r in range(1, no):
        copy = remote(
            w_pack, w_all.at[d], s_z.at[r - 1], r_z.at[r - 1], lax.rem(oi + r, no) * INNER + ii, t
        )
        copy.start()
        z_copies.append(copy)
    y_copies = []
    for q in range(1, INNER):
        copy = remote(
            w_pack, w_all.at[d], s_y.at[q - 1, 0], r_y.at[q - 1, 0],
            oi * INNER + lax.rem(ii + q, INNER), t,
        )
        copy.start()
        y_copies.append(copy)
    core_copy = remote(x_ref, x_all.at[t], s_c, r_c, d, other)
    core_copy.start()
    local = []
    for n, (src, dst) in enumerate(
        (
            (small_ref, small_all.at[d]),
            (x_ref, x_all.at[t]),
            (w_pack, w_all.at[d]),
            (up_ref, w_up.at[oi, ii, xi, ci]),
            (down_ref, w_down.at[oi, ii, xi, ci]),
            (out_pack, w_out.at[oi, ii, xi, ci]),
        )
    ):
        copy = pltpu.make_async_copy(src, dst, s_l.at[n])
        copy.start()
        local.append(copy)

    every = slice(None)
    axes = {"z": (0, no), "y": (1, INNER), "x": (2, nx)}
    me = (oi, ii, xi)
    arrays = (w_up, w_down, w_out)
    sources = (up_ref, down_ref, out_pack)
    flights = {}
    k_copies = []

    def launch(c, s):
        which, lanes, path = chunks[c]
        array = arrays[which]
        spot = [oi, ii, xi, ci, every, lanes]
        for axis in path[:s]:
            spot[axes[axis][0]] = every
        dim, count = axes[path[s]]
        flights[c, s] = []
        for r in range(1, count):
            peer = list(me)
            peer[dim] = lax.rem(me[dim] + r, count)
            src = sources[which].at[:, lanes] if s == 0 else array.at[tuple(spot)]
            flights[c, s].append(
                remote(
                    src, array.at[tuple(spot)], s_w.at[3 * c + s, r - 1], r_w.at[3 * c + s, r - 1],
                    peer[0] * INNER + peer[1], peer[2] * CORES + ci,
                )
            )
        return flights[c, s]

    def hand_over(c, s):
        which, lanes, path = chunks[c]
        array = arrays[which]
        spot = [oi, ii, xi, ci, every, lanes]
        for axis in path[: min(s, 2)]:
            spot[axes[axis][0]] = every
        dim, count = axes[path[2]]
        copies = []
        for r in range(1, count) if s == 3 else (0,):
            spot[dim] = lax.rem(me[dim] + r, count)
            n = c * hand + (r if s == 3 else 0)
            copies.append(
                remote(
                    array.at[tuple(spot)], array.at[tuple(spot)], s_k.at[n], r_k.at[n], d, other
                )
            )
        k_copies.extend(copies)
        return copies

    for s in range(3):
        for c in range(len(chunks)):
            launch(c, s)
    given = {(c, s): hand_over(c, s) for s in (2, 3) for c in range(len(chunks))}

    def advance(c, s):
        for copy in flights[c, s]:
            copy.wait()
        if s < 2:
            for copy in flights[c, s + 1]:
                copy.start()
        for copy in given.get((c, s + 1), ()):
            copy.start()

    for c in range(len(chunks)):
        for copy in flights[c, 0]:
            copy.start()

    local[0].wait()
    for copy in s_copies:
        copy.wait()
    cond = small_all[:, 0, cond_at : cond_at + ada_ref.shape[1]]
    for s in range(n_d):
        cond_ref[:, s : s + 1] = cond[s : s + 1].T
    bias = small_ref[:, bias_at : bias_at + ada_ref.shape[0]]
    mod_rows[:, 0, :] = dot(cond.astype(BF16), ada_ref[...], 1, 1) + bias
    own_mod = pltpu.make_async_copy(mod_rows.at[d], mod_all.at[d], s_l.at[6])
    own_mod.start()
    m_copies = []
    for r in range(1, n_d):
        peer = lax.rem(d + r, n_d)
        copy = remote(mod_rows.at[peer], mod_all.at[d], s_m.at[r - 1], r_m.at[r - 1], peer, t)
        copy.start()
        m_copies.append(copy)
    for r in range(1, no):
        z_copies[r - 1].wait()
        origin = lax.rem(oi + no - r, no) * INNER + ii
        for q in range(1, INNER):
            copy = remote(
                w_all.at[origin], w_all.at[origin], s_y.at[q - 1, r], r_y.at[q - 1, r],
                oi * INNER + lax.rem(ii + q, INNER), t,
            )
            copy.start()
            y_copies.append(copy)
    f_copies = []
    for r, p, copy in x_copies:
        copy.wait()
        origin = lax.rem(xi + nx - r, nx) * CORES + ci
        at = pl.ds(p * piece, piece)
        copy = remote(
            x_all.at[origin, at], x_all.at[origin, at],
            s_f.at[r - 1, p], r_f.at[r - 1, p], d, other,
        )
        copy.start()
        f_copies.append(copy)

    for copy in m_copies + [own_mod]:
        copy.wait()
    def put(first, piece_of, count):
        for s in range(n_d):
            value = piece_of(s)
            start = s * count
            done = 0
            while done < count:
                row, column = divmod(start + done, features)
                take = min(count - done, features - column)
                vec_ref[first + row : first + row + 1, column : column + take] = value[
                    :, done : done + take
                ]
                done += take

    vec_ref[...] = jnp.zeros_like(vec_ref)
    at = 0
    for first, count in sizes:
        put(first, lambda s: small_all[s, :, at : at + count], count)
        at += count
    columns = ada_ref.shape[0]
    for s in range(n_d):
        done = 0
        while done < columns:
            row, column = divmod(s * columns + done, features)
            take = min(columns - done, features - column)
            row = MOD_ROWS[row]
            vec_ref[row : row + 1, column : column + take] = mod_all[s, :, done : done + take]
            done += take

    for copy in y_copies + f_copies + local[1:3] + [core_copy]:
        copy.wait()
    wt_ref[...] = w_all[...].reshape(features, 3 * width).T

    for copy in local[3:]:
        copy.wait()
    for step in plan[0]:
        advance(*step)

    def project(b, carry):
        x = x_all[b].astype(F32)
        centred = x - mean_rows(x)
        normed = centred * lax.rsqrt(mean_rows(centred * centred) + EPSILON)
        normed = normed * vec_ref[GAIN1 : GAIN1 + 1]
        low = (normed * (1.0 + vec_ref[SCALE_A : SCALE_A + 1]) + vec_ref[SHIFT_A : SHIFT_A + 1])
        low = low.astype(BF16)
        in_all[b] = low
        proj = dot(wt_ref[...], low, 1, 1)
        lanes = pl.ds(pl.multiple_of(b * rows, rows), rows)
        cos, sin = cos_ref[:, lanes], sin_ref[:, lanes]
        for j in range(2):
            factor = HEAD_DIM**-0.5 if j == 0 else 1.0
            for h in range(heads):
                at = j * width + h * HEAD_DIM
                first, last = proj[at : at + half], proj[at + half : at + HEAD_DIM]
                top = ((first * cos - last * sin) * factor).astype(BF16)
                bottom = ((last * cos + first * sin) * factor).astype(BF16)
                proj_ref[b, at : at + half] = top
                proj_ref[b, at + half : at + HEAD_DIM] = bottom
                if j == 1:
                    key_ref[h, lanes, :] = jnp.concatenate([top, bottom], axis=0).T
        proj_ref[b, 2 * width :] = proj[2 * width :].astype(BF16)
        return carry

    lax.fori_loop(0, n_t, project, 0)

    def attend(k, carry):
        shift = n_t - 1 - k
        b = lax.rem(xi + shift // CORES, nx) * CORES + lax.rem(ci + lax.rem(shift, CORES), CORES)
        for h in range(heads):
            at = h * HEAD_DIM
            scores = dot(key_ref[h], proj_ref[b, at : at + HEAD_DIM], 1, 0)
            top = jnp.max(scores, axis=0, keepdims=True)
            grown = jnp.exp(scores - top)
            total = jnp.sum(grown, axis=0, keepdims=True)
            low = grown.astype(BF16)
            mixed = jnp.zeros((HEAD_DIM, rows), F32)
            for v in range(n_t):
                value = proj_ref[v, 2 * width + at : 2 * width + at + HEAD_DIM]
                mixed += dot(value, low[v * rows : (v + 1) * rows], 1, 0)
            mix_ref[b, at : at + HEAD_DIM] = (mixed / total).astype(BF16)
            lse_ref[b, h : h + 1] = top + jnp.log(total)
        for m in range(1, n_t):
            @pl.when(k == n_t - 1 - m)
            def _(m=m):
                o_copies[m].start()

        for n in range(1, n_t):
            if n < len(plan) - 1 and plan[n]:
                @pl.when(k == n - 1)
                def _(n=n):
                    for step in plan[n]:
                        advance(*step)

        return carry

    o_copies = {}
    for m in range(1, n_t):
        b = order(m, xi, ci, nx)
        o_copies[m] = remote(
            mix_ref.at[b], mix_own.at[t], s_o.at[m - 1], r_o.at[mirror(m, nx) - 1], d, b
        )
    lax.fori_loop(0, n_t, attend, 0)
    mine = pltpu.make_async_copy(mix_ref.at[t], mix_own.at[t], s_l.at[7])
    mine.start()
    for step in plan[-1]:
        advance(*step)
    mine.wait()
    for copy in list(o_copies.values()) + k_copies:
        copy.wait()


def front_call(x, qkv, small, ada_t, up, down_t, outw, cos, sin, cond_at, bias_at, sizes, n_d, n_t):
    parts = 4
    nx, no = n_t // CORES, n_d // INNER
    rows, features = x.shape
    part, width = qkv.shape[1:]
    heads = width // HEAD_DIM
    length = rows * n_t
    wide = -(-width // 128) * 128
    units = up.shape[1]
    steps = max(no, INNER, nx) - 1
    hand = max(no, INNER, nx)
    cut = units // 2
    low, high = slice(0, cut), slice(cut, units)
    chunks = (
        (0, low, "zyx"), (1, low, "xzy"), (0, high, "zyx"), (1, high, "xzy"),
        (2, slice(0, wide), "yzx"),
    )
    plan = (
        [(1, 0), (3, 0), (4, 0), (0, 0), (2, 0)],
        [(0, 1), (1, 1)],
        [(2, 1), (4, 1)],
        [(3, 1)],
        [(4, 2), (0, 2), (1, 2), (2, 2), (3, 2)],
    )
    grid_of = (no, INNER, nx, CORES, part)
    columns = ada_t.shape[0]
    return pl.pallas_call(
        partial(front_kernel, n_d, n_t, parts, heads, cond_at, bias_at, sizes, chunks, plan, hand),
        name="front",
        out_shape=[
            struct((n_t, rows, features), BF16),
            struct((n_t, 3 * width, rows), BF16),
            struct((n_t, width, rows), BF16),
            struct((n_t, heads, rows), F32),
            struct((n_t, width, rows), BF16),
            struct((16, features), F32),
            struct((ada_t.shape[1], n_d), F32),
            struct((n_d, part, 3 * width), BF16),
            struct(grid_of + (units,), BF16),
            struct(grid_of + (units,), BF16),
            struct(grid_of + (wide,), BF16),
        ],
        in_specs=[VMEM, VMEM, VMEM, VMEM, ANY, ANY, VMEM, VMEM, VMEM],
        out_specs=[VMEM] * 8 + [ANY] * 3,
        scratch_shapes=[
            pltpu.VMEM((n_t, rows, features), BF16),
            pltpu.VMEM((part, 3 * width), BF16),
            pltpu.VMEM((3 * width, features), BF16),
            pltpu.VMEM((part, wide), BF16),
            pltpu.VMEM((n_d,) + small.shape, F32),
            pltpu.VMEM((n_d, 1, columns), F32),
            pltpu.VMEM((n_d, 1, columns), F32),
            pltpu.VMEM((heads, length, HEAD_DIM), BF16),
            DMA((nx - 1, parts)), DMA((nx - 1, parts)), DMA, DMA,
            DMA((nx - 1, parts)), DMA((nx - 1, parts)),
            DMA((no - 1,)), DMA((no - 1,)),
            DMA((INNER - 1, no)), DMA((INNER - 1, no)),
            DMA((n_d - 1,)), DMA((n_d - 1,)), DMA((n_d - 1,)), DMA((n_d - 1,)),
            DMA((8,)),
            DMA((3 * len(chunks), steps)), DMA((3 * len(chunks), steps)),
            DMA((len(chunks) * hand,)), DMA((len(chunks) * hand,)),
            DMA((n_t - 1,)), DMA((n_t - 1,)),
        ],
        compiler_params=params(0),
        cost_estimate=cost(20 * heads * length * length * HEAD_DIM, 40e6, heads * length * length),
    )(x, qkv, small, ada_t, up, down_t, outw, cos, sin)


def middle_kernel(
    mix_ref, x_ref, g_ref, vec_ref, up_ref, down_ref, wout_ref,
    out_ref, dmid_ref, dmix_ref, stat_ref, gup_ref, gdown_ref, gout_ref,
    up_buf, down_buf, o_buf, gu_buf, gd_buf, go_buf,
    mid_ref, attn_ref, low_ref, lowt_ref, dl_ref, dlt_ref, acc_out, acc_in, s_u, s_d, s_o, s_gu, s_gd,
):
    rows, features = x_ref.shape
    n_d, n_t = up_ref.shape[:2]
    width = mix_ref.shape[1]
    units = up_ref.shape[3]
    wide = wout_ref.shape[3]
    load_out = pltpu.make_async_copy(wout_ref, o_buf, s_o)
    load_up = lambda b: pltpu.make_async_copy(up_ref.at[:, b], up_buf.at[b], s_u.at[b])
    load_down = lambda b: pltpu.make_async_copy(down_ref.at[:, b], down_buf.at[b], s_d.at[b])
    keep_up = lambda b: pltpu.make_async_copy(gu_buf.at[b], gup_ref.at[:, b], s_gu.at[b])
    keep_down = lambda b: pltpu.make_async_copy(gd_buf.at[b], gdown_ref.at[:, b], s_gd.at[b])
    load_out.start()
    for b in range(n_t):
        load_up(b).start()
        load_down(b).start()
    vec = lambda row: vec_ref[row : row + 1]
    cot = g_ref[...].astype(F32)
    d_mlp = (vec(GATE_M) * cot).astype(BF16)
    dl_ref[...] = d_mlp
    dlt_ref[...] = d_mlp.T
    stat_ref[...] = jnp.zeros_like(stat_ref)
    stat_ref[S_B_DOWN : S_B_DOWN + 1] = sum_tokens(d_mlp.astype(F32))
    go_buf[...] = jnp.zeros_like(go_buf)
    load_out.wait()
    w_out = lambda b: o_buf[:, b].reshape(features, wide)[:, :width]
    attn_out = jnp.zeros((rows, features), F32)
    for b in range(n_t):
        attn_out += dot(mix_ref[b].T, w_out(b), 1, 1)
    attn_ref[...] = attn_out
    branch = vec(GATE_A) * attn_out
    stat_ref[S_SQ_A : S_SQ_A + 1] = sum_tokens(branch * branch)
    middle = x_ref[...].astype(F32) + branch
    mid_ref[...] = middle
    centred = middle - mean_rows(middle)
    inv = lax.rsqrt(mean_rows(centred * centred) + EPSILON)
    low = (centred * inv * vec(GAIN2) * (1.0 + vec(SCALE_M)) + vec(SHIFT_M)).astype(BF16)
    low_ref[...] = low
    lowt_ref[...] = low.T
    acc_out[...] = jnp.zeros_like(acc_out)
    acc_in[...] = jnp.zeros_like(acc_in)

    def block(b, carry):
        load_up(b).wait()
        load_down(b).wait()
        up = up_buf[b].reshape(features, units)
        down = down_buf[b].reshape(features, units)
        hidden = dot(low_ref[...], up, 1, 0) + vec_ref[pl.ds(B_UP + b, 1)]
        square = hidden * hidden
        bent = jnp.tanh(GELU_C * hidden * (1.0 + GELU_A * square))
        half = 0.5 * (1.0 + bent)
        active = (hidden * half).astype(BF16)
        slope = half + (0.5 * GELU_C) * hidden * (1.0 - bent * bent) * (
            1.0 + (3.0 * GELU_A) * square
        )
        acc_out[...] += dot(active, down, 1, 1)
        gd_buf[b] = dot(dlt_ref[...], active, 1, 0).astype(BF16).reshape(n_d, -1, units)
        keep_down(b).start()
        d_hidden = (dot(dl_ref[...], down, 1, 0) * slope).astype(BF16)
        stat_ref[pl.ds(S_B_UP + b, 1)] = sum_tokens(d_hidden.astype(F32))
        gu_buf[b] = dot(lowt_ref[...], d_hidden, 1, 0).astype(BF16).reshape(n_d, -1, units)
        keep_up(b).start()
        acc_in[...] += dot(d_hidden, up, 1, 1)
        return carry

    lax.fori_loop(0, n_t, block, 0)
    middle = mid_ref[...]
    mlp_out = acc_out[...] + vec(B_DOWN)
    mlp_branch = vec(GATE_M) * mlp_out
    result = middle + mlp_branch
    out_ref[...] = result.astype(BF16)
    cot = g_ref[...].astype(F32)
    stat_ref[S_SQ_M : S_SQ_M + 1] = sum_tokens(mlp_branch * mlp_branch)
    stat_ref[S_SQ_R : S_SQ_R + 1] = sum_tokens(result * result)
    stat_ref[S_GATE_M : S_GATE_M + 1] = sum_tokens(cot * mlp_out)
    e = acc_in[...]
    centred = middle - mean_rows(middle)
    inv = lax.rsqrt(mean_rows(centred * centred) + EPSILON)
    nhat = centred * inv
    gain, scale = vec(GAIN2), 1.0 + vec(SCALE_M)
    by_nhat = sum_tokens(e * nhat)
    stat_ref[S_SHIFT_M : S_SHIFT_M + 1] = sum_tokens(e)
    stat_ref[S_SCALE_M : S_SCALE_M + 1] = by_nhat * gain
    stat_ref[S_GAIN2 : S_GAIN2 + 1] = by_nhat * scale
    dn = e * (scale * gain)
    d_middle = cot + inv * (dn - mean_rows(dn) - nhat * mean_rows(dn * nhat))
    dmid_ref[...] = d_middle
    stat_ref[S_GATE_A : S_GATE_A + 1] = sum_tokens(d_middle * attn_ref[...])
    d_attn = (vec(GATE_A) * d_middle).astype(BF16)
    d_attn_t = d_attn.T
    for b in range(n_t):
        dmix_ref[b] = dot(d_attn, w_out(b), 1, 0).astype(BF16).T
        go_buf[:, b, :, :width] = (
            dot(d_attn_t, mix_ref[b], 1, 1).astype(BF16).reshape(n_d, -1, width)
        )
    copy = pltpu.make_async_copy(go_buf, gout_ref, s_o)
    copy.start()
    for b in range(n_t):
        keep_up(b).wait()
        keep_down(b).wait()
    copy.wait()


def middle_call(mix, x, g, vecs, w_up, w_down, w_out, stat_rows):
    rows, features = x.shape
    n_d, n_t, part, units = w_up.shape
    wide = w_out.shape[3]
    width = mix.shape[1]
    per = (n_t, n_d, part, units)
    return pl.pallas_call(
        middle_kernel,
        name="middle",
        out_shape=[
            struct((rows, features), BF16),
            struct((rows, features), F32),
            struct((n_t, width, rows), BF16),
            struct((stat_rows, features), F32),
            struct(w_up.shape, BF16),
            struct(w_down.shape, BF16),
            struct(w_out.shape, BF16),
        ],
        in_specs=[VMEM] * 4 + [ANY] * 3,
        out_specs=[VMEM] * 4 + [ANY] * 3,
        scratch_shapes=[
            pltpu.VMEM(per, BF16), pltpu.VMEM(per, BF16), pltpu.VMEM(w_out.shape, BF16),
            pltpu.VMEM(per, BF16), pltpu.VMEM(per, BF16), pltpu.VMEM(w_out.shape, BF16),
            pltpu.VMEM((rows, features), F32),
            pltpu.VMEM((rows, features), F32),
            pltpu.VMEM((rows, features), BF16),
            pltpu.VMEM((features, rows), BF16),
            pltpu.VMEM((rows, features), BF16),
            pltpu.VMEM((features, rows), BF16),
            pltpu.VMEM((rows, features), F32),
            pltpu.VMEM((rows, features), F32),
            DMA((n_t,)), DMA((n_t,)), DMA, DMA((n_t,)), DMA((n_t,)),
        ],
        compiler_params=params(),
        cost_estimate=cost(2 * rows * features * features * (6 * n_t + 4), 30e6),
    )(mix, x, g, vecs, w_up, w_down, w_out)


def back_kernel(
    n_d, n_t, parts, heads, chunks, plan,
    dmix_ref, proj_ref, mix_ref, lse_ref, cos_ref, sin_ref, in_hbm, wq_hbm, stat_ref,
    gup_ref, gdown_ref, gout_ref,
    sum_ref, gq_ref, up_ref, down_ref, out_ref, table_ref,
    dmix_all, key_ref, keyt_ref, val_ref, dkey_ref, dval_ref, dproj_ref, in_ref, wq_ref,
    acc_ref, grad_ref, rc, rx, ry, sz, rz, got_ref, mine_ref, *more,
):
    n_chunks = len(chunks)
    held = more[:n_chunks]
    met = more[n_chunks : 2 * n_chunks]
    arrived = more[2 * n_chunks : 5 * n_chunks]
    (
        s_a, r_a, s_l, s_h, s_e, r_e, s_g, r_g, s_t, r_t, s_d, r_d,
        s_c, r_c, s_x, r_x, s_y, r_y, s_z, r_z,
    ) = more[5 * n_chunks :]
    d, t, oi, ii, xi, ci = place(n_d, n_t)
    nx, no = n_t // CORES, n_d // INNER
    other = xi * CORES + (1 - ci)
    blocks, total, rows = proj_ref.shape
    width = total // 3
    half = HEAD_DIM // 2
    length = blocks * rows
    every = slice(None)
    axes = {"z": (0, no), "y": (1, INNER), "x": (2, nx)}
    me = (oi, ii, xi)
    sources = (gup_ref, gdown_ref, gout_ref)
    results = (up_ref, down_ref, out_ref)

    firsts = []
    for c, (which, lanes, path) in enumerate(chunks):
        array = sources[which]
        firsts.append(
            (
                pltpu.make_async_copy(
                    array.at[:, :, :, ci, :, lanes], held[c], s_h.at[c]
                ),
                remote(
                    array.at[:, :, :, 1 - ci, :, lanes], met[c], s_e.at[c], r_e.at[c], d, other
                ),
            )
        )
    flights = {}
    for c, (which, lanes, path) in enumerate(chunks):
        for s in range(3):
            dim, count = axes[path[s]]
            flights[c, s] = []
            for r in range(1, count):
                to = lax.rem(me[dim] + r, count)
                spot = [every, every, every]
                for axis in path[:s]:
                    spot[axes[axis][0]] = me[axes[axis][0]]
                spot[dim] = to
                peer = list(me)
                peer[dim] = to
                flights[c, s].append(
                    remote(
                        held[c].at[tuple(spot)], arrived[3 * c + s].at[r - 1],
                        s_g.at[3 * c + s, r - 1], r_g.at[3 * c + s, r - 1],
                        peer[0] * INNER + peer[1], peer[2] * CORES + ci,
                    )
                )

    def begin(c):
        for copy in firsts[c]:
            copy.wait()
        block = held[c].shape[1:3]

        def add(n, carry):
            at = (n // (block[0] * block[1]), lax.rem(n // block[1], block[0]), lax.rem(n, block[1]))
            held[c][at] = (held[c][at].astype(F32) + met[c][at].astype(F32)).astype(BF16)
            return carry

        lax.fori_loop(0, held[c].shape[0] * block[0] * block[1], add, 0)
        for copy in flights[c, 0]:
            copy.start()

    def advance(c, s):
        if s < 0:
            return begin(c)
        which, lanes, path = chunks[c]
        for copy in flights[c, s]:
            copy.wait()
        got = arrived[3 * c + s]
        left = [axes[a][0] for a in "zyx" if a in path[s + 1 :]]
        sizes = [axes[a][1] for a in "zyx" if a in path[s + 1 :]]

        def fold(n, carry):
            spot = list(me)
            slot = []
            for dim, size in reversed(list(zip(left, sizes))):
                spot[dim] = lax.rem(n, size)
                slot.insert(0, spot[dim])
                n = n // size
            value = held[c][tuple(spot)].astype(F32)
            for r in range(axes[path[s]][1] - 1):
                value += got[(r,) + tuple(slot)].astype(F32)
            if s == 2:
                results[which][:, lanes] = value
            else:
                held[c][tuple(spot)] = value.astype(BF16)
            return carry

        if sizes:
            lax.fori_loop(0, int(np.prod(sizes)), fold, 0)
        else:
            fold(0, 0)
        if s < 2:
            for copy in flights[c, s + 1]:
                copy.start()

    greet(n_d, n_t)
    a_copies = {}
    for m in range(1, n_t):
        b = order(m, xi, ci, nx)
        a_copies[mirror(m, nx)] = remote(
            dmix_ref.at[b], dmix_all.at[t], s_a.at[m - 1], r_a.at[mirror(m, nx) - 1], d, b
        )
    for m in range(n_t - 1, 0, -1):
        a_copies[mirror(m, nx)].start()
    loads = [
        pltpu.make_async_copy(dmix_ref.at[t], dmix_all.at[t], s_l.at[0]),
        pltpu.make_async_copy(in_hbm, in_ref, s_l.at[1]),
        pltpu.make_async_copy(wq_hbm, wq_ref, s_l.at[2]),
    ]
    for copy in loads:
        copy.start()
    t_copies = []
    for r in range(1, n_t):
        copy = remote(
            stat_ref, got_ref.at[r - 1], s_t.at[r - 1], r_t.at[r - 1], d, lax.rem(t + r, n_t)
        )
        copy.start()
        t_copies.append(copy)
    for pair in firsts:
        for copy in pair:
            copy.start()
    d_copies = [pltpu.make_async_copy(mine_ref, table_ref.at[d], s_l.at[3])]
    for r in range(1, n_d):
        d_copies.append(
            remote(mine_ref, table_ref.at[d], s_d.at[r - 1], r_d.at[r - 1], lax.rem(d + r, n_d), t)
        )

    def share_statistics():
        for copy in t_copies:
            copy.wait()
        value = stat_ref[...]
        for r in range(1, n_t):
            value += got_ref[r - 1]
        mine_ref[...] = value
        for copy in d_copies:
            copy.start()

    dkey_ref[...] = jnp.zeros_like(dkey_ref)
    dval_ref[...] = jnp.zeros_like(dval_ref)

    def turn(b, carry):
        lanes = pl.ds(pl.multiple_of(b * rows, rows), rows)
        keyt_ref[:, lanes] = proj_ref[b, width : 2 * width]
        for h in range(heads):
            at = h * HEAD_DIM
            key_ref[h, lanes] = proj_ref[b, width + at : width + at + HEAD_DIM].T
            val_ref[h, lanes] = proj_ref[b, 2 * width + at : 2 * width + at + HEAD_DIM].T
        return carry

    lax.fori_loop(0, blocks, turn, 0)
    loads[0].wait()

    def unrotate(block, at, factor, first, last):
        lanes = pl.ds(pl.multiple_of(block * rows, rows), rows)
        cos, sin = cos_ref[:, lanes], sin_ref[:, lanes]
        dproj_ref[block, at : at + half] = ((first * cos + last * sin) * factor).astype(BF16)
        dproj_ref[block, at + half : at + HEAD_DIM] = ((last * cos - first * sin) * factor).astype(
            BF16
        )

    def attend(k, carry):
        for m in range(1, n_t):
            @pl.when(k == m)
            def _(m=m):
                a_copies[m].wait()
        i = lax.rem(xi + k // CORES, nx) * CORES + lax.rem(ci + lax.rem(k, CORES), CORES)
        for h in range(heads):
            at = h * HEAD_DIM
            query_t = proj_ref[i, at : at + HEAD_DIM]
            dmix_t = dmix_all[i, at : at + HEAD_DIM]
            mix_t = mix_ref[i, at : at + HEAD_DIM]
            inner = jnp.sum(dmix_t.astype(F32) * mix_t.astype(F32), axis=0, keepdims=True)
            d_query = jnp.zeros((HEAD_DIM, rows), F32)
            for v in range(2):
                keys = slice(v * length // 2, (v + 1) * length // 2)
                probs = jnp.exp(dot(key_ref[h, keys], query_t, 1, 0) - lse_ref[i, h : h + 1])
                d_probs = dot(val_ref[h, keys], dmix_t, 1, 0)
                d_scores = (probs * (d_probs - inner)).astype(BF16)
                dval_ref[h, keys] += dot(probs.astype(BF16), dmix_t.T, 1, 0)
                dkey_ref[h, keys] += dot(d_scores, query_t.T, 1, 0)
                d_query += dot(keyt_ref[at : at + HEAD_DIM, keys], d_scores, 1, 0)
            unrotate(i, at, HEAD_DIM**-0.5, d_query[:half], d_query[half:])
        for n in range(n_t):
            @pl.when(k == n)
            def _(n=n):
                for step in plan[n]:
                    advance(*step)
                if n == 1:
                    share_statistics()
        return carry

    lax.fori_loop(0, n_t, attend, 0)
    loads[1].wait()
    loads[2].wait()
    acc_ref[...] = jnp.zeros_like(acc_ref)

    def project(b, carry):
        lanes = pl.ds(pl.multiple_of(b * rows, rows), rows)
        for h in range(heads):
            at = h * HEAD_DIM
            d_key = dkey_ref[h, lanes].T
            unrotate(b, width + at, 1.0, d_key[:half], d_key[half:])
            dproj_ref[b, 2 * width + at : 2 * width + at + HEAD_DIM] = (
                dval_ref[h, lanes].T.astype(BF16)
            )
        acc_ref[...] += dot(dproj_ref[b], in_ref[b], 1, 0)
        return carry

    lax.fori_loop(0, blocks, project, 0)
    grad_ref[...] = acc_ref[...].T.astype(BF16).reshape(grad_ref.shape)
    y_copies = []
    for q in range(1, INNER):
        to = lax.rem(ii + q, INNER)
        copy = remote(
            grad_ref.at[:, to], ry.at[q - 1], s_y.at[q - 1], r_y.at[q - 1], oi * INNER + to, t
        )
        copy.start()
        y_copies.append(copy)
    for step in plan[n_t]:
        advance(*step)

    part_ref = in_ref
    c_copies = {}
    for r in range(nx):
        for p in range(parts):
            c_copies[r, p] = remote(
                part_ref.at[lax.rem(xi + r, nx) * CORES + 1 - ci, pl.ds(p * (rows // parts), rows // parts)],
                rc.at[r, pl.ds(p * (rows // parts), rows // parts)],
                s_c.at[r, p], r_c.at[r, p], d, other,
            )

    def share(k, carry):
        shift = n_t - 1 - k
        b = lax.rem(xi + shift // CORES, nx) * CORES + lax.rem(ci + lax.rem(shift, CORES), CORES)
        part_ref[b] = dot(dproj_ref[b].T, wq_ref[...], 1, 1).astype(BF16)
        for r in range(nx):
            @pl.when(k == n_t - 1 - (r * CORES + 1))
            def _(r=r):
                for p in range(parts):
                    c_copies[r, p].start()
        return carry

    lax.fori_loop(0, n_t, share, 0)
    x_copies = []
    for r in range(1, nx):
        for p in range(parts):
            at = pl.ds(p * (rows // parts), rows // parts)
            c_copies[r, p].wait()
            to = lax.rem(xi + r, nx) * CORES + ci
            part_ref[to, at] = (part_ref[to, at].astype(F32) + rc[r, at].astype(F32)).astype(BF16)
            copy = remote(
                part_ref.at[to, at], rx.at[r - 1, at], s_x.at[r - 1, p], r_x.at[r - 1, p], d, to
            )
            copy.start()
            x_copies.append(copy)
    for copy in y_copies:
        copy.wait()
    z_copies = []
    for r in range(1, no):
        to = lax.rem(oi + r, no)
        value = grad_ref[to, ii].astype(F32)
        for q in range(1, INNER):
            value += ry[q - 1, to].astype(F32)
        sz[r - 1] = value.astype(BF16)
        copy = remote(sz.at[r - 1], rz.at[r - 1], s_z.at[r - 1], r_z.at[r - 1], to * INNER + ii, t)
        copy.start()
        z_copies.append(copy)
    for step in plan[n_t + 1]:
        advance(*step)
    value = grad_ref[oi, ii].astype(F32)
    for q in range(1, INNER):
        value += ry[q - 1, oi].astype(F32)
    for copy in z_copies:
        copy.wait()
    for r in range(1, no):
        value += rz[r - 1].astype(F32)
    for j in range(3):
        gq_ref[j] = value[:, j * width : (j + 1) * width]
    for copy in d_copies:
        copy.wait()
    for p in range(parts):
        c_copies[0, p].wait()
    for copy in x_copies:
        copy.wait()
    for p in range(parts):
        at = pl.ds(p * (rows // parts), rows // parts)
        value = part_ref[t, at].astype(F32) + rc[0, at].astype(F32)
        for r in range(1, nx):
            value += rx[r - 1, at].astype(F32)
        sum_ref[at] = value


def back_call(dmix, proj, mix, lse, cos, sin, attn_in, w_qkv, stat, g_up, g_down, g_out, n_d, n_t):
    parts = 4
    nx, no = n_t // CORES, n_d // INNER
    blocks, total, rows = proj.shape
    width = total // 3
    heads = width // HEAD_DIM
    length = blocks * rows
    features = attn_in.shape[2]
    part = features // n_d
    units, wide = g_up.shape[-1], g_out.shape[-1]
    grid_of = (no, INNER, nx, CORES, part)
    g_up, g_down = g_up.reshape(grid_of + (units,)), g_down.reshape(grid_of + (units,))
    g_out = g_out.reshape(grid_of + (wide,))
    cut = units // 2
    low, high = slice(0, cut), slice(cut, units)
    chunks = (
        (0, low, "xyz"), (1, low, "yzx"), (2, slice(0, wide), "xzy"),
        (0, high, "xyz"), (1, high, "yzx"),
    )
    plan = (
        [(0, -1), (1, -1), (2, -1), (3, -1), (4, -1)],
        [(0, 0), (1, 0)],
        [(2, 0), (4, 0)],
        [(3, 0), (0, 1), (1, 1)],
        [(2, 1), (4, 1)],
        [(3, 1), (0, 2), (1, 2), (2, 2), (4, 2), (3, 2)],
    )
    sizes = {"z": no, "y": INNER, "x": nx}
    held, arrived = [], []
    for which, lanes, path in chunks:
        tail = (part, lanes.stop - lanes.start)
        held.append(pltpu.VMEM((no, INNER, nx) + tail, BF16))
        for s in range(3):
            rest = tuple(sizes[a] for a in "zyx" if a in path[s + 1 :])
            arrived.append(pltpu.VMEM((sizes[path[s]] - 1,) + rest + tail, BF16))
    n_chunks = len(chunks)
    steps = max(no, INNER, nx) - 1
    return pl.pallas_call(
        partial(back_kernel, n_d, n_t, parts, heads, chunks, plan),
        name="back",
        out_shape=[
            struct((rows, features), F32),
            struct((3, part, width), F32),
            struct((part, units), F32),
            struct((part, units), F32),
            struct((part, wide), F32),
            struct((n_d,) + stat.shape, F32),
        ],
        in_specs=[VMEM] * 6 + [ANY] * 2 + [VMEM] + [ANY] * 3,
        out_specs=[VMEM] * 5 + [ANY],
        scratch_shapes=[
            pltpu.VMEM(dmix.shape, BF16),
            pltpu.VMEM((heads, length, HEAD_DIM), BF16),
            pltpu.VMEM((width, length), BF16),
            pltpu.VMEM((heads, length, HEAD_DIM), BF16),
            pltpu.VMEM((heads, length, HEAD_DIM), F32),
            pltpu.VMEM((heads, length, HEAD_DIM), F32),
            pltpu.VMEM(proj.shape, BF16),
            pltpu.VMEM(attn_in.shape, BF16),
            pltpu.VMEM(w_qkv.shape, BF16),
            pltpu.VMEM((total, features), F32),
            pltpu.VMEM((no, INNER, part, total), BF16),
            pltpu.VMEM((nx, rows, features), BF16),
            pltpu.VMEM((nx - 1, rows, features), BF16),
            pltpu.VMEM((INNER - 1, no, part, total), BF16),
            pltpu.VMEM((no - 1, part, total), BF16),
            pltpu.VMEM((no - 1, part, total), BF16),
            pltpu.VMEM((n_t - 1,) + stat.shape, F32),
            pltpu.VMEM(stat.shape, F32),
        ]
        + held + held + arrived
        + [
            DMA((n_t - 1,)), DMA((n_t - 1,)), DMA((4,)), DMA((n_chunks,)),
            DMA((n_chunks,)), DMA((n_chunks,)),
            DMA((3 * n_chunks, steps)), DMA((3 * n_chunks, steps)),
            DMA((n_t - 1,)), DMA((n_t - 1,)), DMA((n_d - 1,)), DMA((n_d - 1,)),
            DMA((nx, parts)), DMA((nx, parts)), DMA((nx - 1, parts)), DMA((nx - 1, parts)),
            DMA((INNER - 1,)), DMA((INNER - 1,)), DMA((no - 1,)), DMA((no - 1,)),
        ],
        compiler_params=params(1),
        cost_estimate=cost(45 * heads * length * length * HEAD_DIM, 40e6, heads * length * length),
    )(dmix, proj, mix, lse, cos, sin, attn_in, w_qkv, stat, g_up, g_down, g_out)


def tail_kernel(
    n_d, n_t, count,
    x_ref, e_ref, dmid_ref, vec_ref, ada_ref, table_ref, cond_ref,
    grad_ref, gada_ref, bias_ref, gcond_ref, sum_ref, gain_ref, root_ref,
    late_ref, got_ref, mine_ref, late_all, flat_ref, rows_out, rows_in, s_t, r_t, s_d, r_d, s_p, r_p, s_l,
):
    d, t = lax.axis_index("dp"), lax.axis_index("tensor")
    features = x_ref.shape[1]
    x = x_ref[...].astype(F32)
    e = e_ref[...]
    gain, scale = vec_ref[GAIN1 : GAIN1 + 1], 1.0 + vec_ref[SCALE_A : SCALE_A + 1]
    centred = x - mean_rows(x)
    inv = lax.rsqrt(mean_rows(centred * centred) + EPSILON)
    nhat = centred * inv
    by_nhat = sum_tokens(e * nhat)
    late_ref[:, :features] = sum_tokens(e)
    late_ref[:, features : 2 * features] = by_nhat * gain
    late_ref[:, 2 * features :] = by_nhat * scale
    greet(n_d, n_t)
    copies = []
    for r in range(1, n_t):
        copy = remote(
            late_ref, got_ref.at[r - 1], s_t.at[r - 1], r_t.at[r - 1], d, lax.rem(t + r, n_t)
        )
        copy.start()
        copies.append(copy)
    dn = e * (scale * gain)
    grad_ref[...] = dmid_ref[...] + inv * (dn - mean_rows(dn) - nhat * mean_rows(dn * nhat))
    value = late_ref[...]
    for r in range(1, n_t):
        copies[r - 1].wait()
        value += got_ref[r - 1]
    mine_ref[...] = value
    copies = [pltpu.make_async_copy(mine_ref, late_all.at[d], s_l.at[0])]
    for r in range(1, n_d):
        copies.append(
            remote(mine_ref, late_all.at[d], s_d.at[r - 1], r_d.at[r - 1], lax.rem(d + r, n_d), t)
        )
    for copy in copies:
        copy.start()
    total = table_ref[0]
    for s in range(1, n_d):
        total += table_ref[s]
    sum_ref[...] = total
    for k, row in enumerate((S_SQ_A, S_SQ_M, S_SQ_R)):
        root_ref[k : k + 1] = jnp.broadcast_to(
            jnp.sqrt(jnp.sum(total[row : row + 1], axis=1, keepdims=True) / count),
            (1, root_ref.shape[1]),
        )

    def outer(block, row_of):
        at = slice(block * features, (block + 1) * features)
        value = jnp.zeros((cond_ref.shape[0], features), F32)
        for s in range(n_d):
            value += cond_ref[:, s : s + 1] * row_of(s)
        gada_ref[:, at] = value

    early = ((2, S_GATE_A), (3, S_SHIFT_M), (4, S_SCALE_M), (5, S_GATE_M))
    for block, row in early:
        outer(block, lambda s: table_ref[s, row : row + 1, :])
    for copy in copies:
        copy.wait()
    for s in range(n_d):
        flat_ref[s : s + 1, : 2 * features] = late_all[s, :, : 2 * features]
        for block, row in early:
            flat_ref[s : s + 1, block * features : (block + 1) * features] = table_ref[
                s, row : row + 1
            ]
    flat = flat_ref[...]
    columns = ada_ref.shape[0]
    moved = pltpu.roll(flat, lax.rem(n_d - d, n_d) * columns, 1)[:, :columns]
    rows_out[:, 0, :] = lax.dot_general(
        moved, ada_ref[...].astype(F32), (((1,), (0,)), ((), ())),
        precision=lax.Precision.HIGHEST, preferred_element_type=F32,
    )
    copies = [pltpu.make_async_copy(rows_out.at[d], rows_in.at[d], s_l.at[1])]
    for r in range(1, n_d):
        peer = lax.rem(d + r, n_d)
        copies.append(remote(rows_out.at[peer], rows_in.at[d], s_p.at[r - 1], r_p.at[r - 1], peer, t))
    for copy in copies:
        copy.start()
    for block in (0, 1):
        outer(block, lambda s: late_all[s, :, block * features : (block + 1) * features])
    bias_ref[...] = jnp.sum(flat, axis=0, keepdims=True)
    value = late_all[0, :, 2 * features :]
    for s in range(1, n_d):
        value += late_all[s, :, 2 * features :]
    gain_ref[...] = value
    for copy in copies:
        copy.wait()
    gcond_ref[...] = jnp.sum(rows_in[:, 0, :], axis=0, keepdims=True)


def tail_call(x, e, dmid, vecs, ada_t, table, cond_t, count, n_d, n_t):
    features = x.shape[1]
    width = ada_t.shape[1]
    return pl.pallas_call(
        partial(tail_kernel, n_d, n_t, count),
        name="tail",
        out_shape=[
            struct(x.shape, F32),
            struct((width, 6 * features), F32),
            struct((1, 6 * features), F32),
            struct((1, width), F32),
            struct(table.shape[1:], F32),
            struct((1, features), F32),
            struct((3, 128), F32),
        ],
        in_specs=[VMEM] * 7,
        out_specs=[VMEM] * 7,
        scratch_shapes=[
            pltpu.VMEM((1, 3 * features), F32),
            pltpu.VMEM((n_t - 1, 1, 3 * features), F32),
            pltpu.VMEM((1, 3 * features), F32),
            pltpu.VMEM((n_d, 1, 3 * features), F32),
            pltpu.VMEM((n_d, 6 * features), F32),
            pltpu.VMEM((n_d, 1, width), F32),
            pltpu.VMEM((n_d, 1, width), F32),
            DMA((n_t - 1,)), DMA((n_t - 1,)),
            DMA((n_d - 1,)), DMA((n_d - 1,)),
            DMA((n_d - 1,)), DMA((n_d - 1,)),
            DMA((2,)),
        ],
        compiler_params=params(2),
        cost_estimate=cost(20 * x.size, 10e6),
    )(x, e, dmid, vecs, ada_t, table, cond_t)


def shards(
    block_input, condition, modulation_weight, modulation_bias, first_gain, qkv_weight, out_weight,
    second_gain, up_weight, up_bias, down_weight, down_bias, grad_output,
):
    n_t, n_d = lax.axis_size("tensor"), lax.axis_size("dp")
    rows, sequences, features = block_input.shape
    assert sequences == 1
    length = rows * n_t
    part, width = qkv_weight.shape[1:]
    units = up_weight.shape[1]
    assert units == features and n_t % CORES == 0 and n_d % INNER == 0
    x = block_input.reshape(rows, features)
    g = grad_output.reshape(rows, features)
    ada_t = modulation_weight.T

    small = jnp.concatenate([first_gain, second_gain, down_bias, up_bias]).astype(F32)
    cond_at = -(-small.shape[0] // 128) * 128
    bias_at = cond_at + condition.shape[1]
    small = jnp.concatenate(
        [
            small, jnp.zeros((cond_at - small.shape[0],), F32),
            condition[0].astype(F32), modulation_bias.astype(F32),
        ]
    )[None]
    own = first_gain.shape[0]
    sizes = ((GAIN1, own), (GAIN2, own), (B_DOWN, own), (B_UP, up_bias.shape[0]))
    inverse = 10000.0 ** (-np.arange(HEAD_DIM // 2) * 2.0 / HEAD_DIM)
    angles = inverse[:, None] * np.arange(length)[None, :]
    cos, sin = jnp.asarray(np.cos(angles), F32), jnp.asarray(np.sin(angles), F32)

    attn_in, proj, mix, lse, mix_own, vecs, cond_t, w_qkv, w_up, w_down, w_out = front_call(
        x, qkv_weight, small, ada_t, up_weight, down_weight.T, out_weight, cos, sin,
        cond_at, bias_at, sizes, n_d, n_t,
    )
    merge = lambda a: a.reshape((n_d, n_t) + a.shape[4:])
    stat_rows = -(-(S_B_UP + n_t) // 8) * 8
    out, d_middle, d_mix, stat, g_up, g_down, g_out = middle_call(
        mix_own, x, g, vecs, merge(w_up), merge(w_down), merge(w_out), stat_rows
    )
    d_attn_in, g_qkv, g_up, g_down, g_out, table = back_call(
        d_mix, proj, mix, lse, cos, sin, attn_in, w_qkv.reshape(features, 3 * width), stat,
        g_up, g_down, g_out, n_d, n_t,
    )
    grad_input, grad_ada, grad_ada_b, grad_cond, sums, gain1, roots = tail_call(
        x, d_attn_in, d_middle, vecs, ada_t, table, cond_t, float(length * n_d * features), n_d, n_t
    )
    return (
        out.reshape(block_input.shape),
        grad_input.reshape(block_input.shape),
        grad_cond,
        grad_ada,
        grad_ada_b[0],
        gain1[0],
        g_qkv,
        g_out[:, :width].T,
        sums[S_GAIN2],
        g_up,
        sums[S_B_UP : S_B_UP + n_t].reshape(-1),
        g_down.T,
        sums[S_B_DOWN],
        roots[:, 0],
    )


def solution(mesh):
    in_specs = (
        P("tensor", "dp", None),
        P("dp", None),
        P(None, "dp"),
        P("dp"),
        P("dp"),
        P(None, "dp", "tensor"),
        P("tensor", "dp"),
        P("dp"),
        P("dp", "tensor"),
        P("dp"),
        P("tensor", "dp"),
        P("dp"),
        P("tensor", "dp", None),
    )
    out_specs = (
        P("tensor", "dp", None),
        P("tensor", "dp", None),
        P("dp", None),
        P(),
        P(),
        P(),
        P(None, "dp", "tensor"),
        P("tensor", "dp"),
        P(),
        P("dp", "tensor"),
        P(),
        P("tensor", "dp"),
        P(),
        P(),
    )
    return jax.shard_map(shards, mesh=mesh, in_specs=in_specs, out_specs=out_specs, check_vma=False)
```

```python
from functools import partial

import jax
import jax.numpy as jnp
import numpy as np
from jax import lax
from jax.experimental import pallas as pl
from jax.experimental.pallas import tpu as pltpu
from jax.sharding import PartitionSpec as P

HEAD_DIM = 64
EPSILON = 1e-05
CORES = 2
INNER = 2
MESH = pl.DeviceIdType.MESH
VMEM_LIMIT = 58 << 20
GELU_C = float(np.sqrt(2.0 / np.pi))
GELU_A = 0.044715
F32 = jnp.float32
BF16 = jnp.bfloat16
ANY = pl.BlockSpec(memory_space=pl.ANY)
VMEM = pl.BlockSpec(memory_space=pltpu.VMEM)
DMA = pltpu.SemaphoreType.DMA


def dot(lhs, rhs, lhs_dim, rhs_dim):
    return lax.dot_general(
        lhs, rhs, (((lhs_dim,), (rhs_dim,)), ((), ())), preferred_element_type=F32
    )


def params(collective_id=None, **more):
    if collective_id is not None:
        more.update(collective_id=collective_id, has_side_effects=True)
    return pltpu.CompilerParams(vmem_limit_bytes=VMEM_LIMIT, **more)


def cost(flops, moved, special=0):
    return pl.CostEstimate(flops=int(flops), bytes_accessed=int(moved), transcendentals=int(special))


def struct(shape, dtype):
    return jax.ShapeDtypeStruct(shape, dtype)


def mean_rows(values):
    return jnp.mean(values, axis=-1, keepdims=True)


def sum_tokens(values):
    return jnp.sum(values, axis=0, keepdims=True)


GAIN1, SHIFT_A, SCALE_A, GATE_A, GAIN2, SHIFT_M, SCALE_M, GATE_M, B_DOWN, B_UP = range(10)
MOD_ROWS = (SHIFT_A, SCALE_A, GATE_A, SHIFT_M, SCALE_M, GATE_M)
S_GATE_A, S_SHIFT_M, S_SCALE_M, S_GATE_M, S_GAIN2, S_B_DOWN, S_SQ_A, S_SQ_M, S_SQ_R, S_B_UP = range(10)
L_SHIFT_A, L_SCALE_A, L_GAIN1 = range(3)


def order(k, xi, ci, nx):
    return lax.rem(xi + k // CORES, nx) * CORES + lax.rem(ci + k % CORES, CORES)


def mirror(k, nx):
    return (nx - k // CORES) % nx * CORES + (CORES - k % CORES) % CORES


def place(n_d, n_t):
    d, t = lax.axis_index("dp"), lax.axis_index("tensor")
    return d, t, d // INNER, lax.rem(d, INNER), t // CORES, lax.rem(t, CORES)


def greet(n_d, n_t):
    d, t = lax.axis_index("dp"), lax.axis_index("tensor")
    barrier = pltpu.get_barrier_semaphore()
    for r in range(1, n_t):
        pl.semaphore_signal(
            barrier, 1, device_id=(d, lax.rem(t + r, n_t)), device_id_type=MESH
        )
    for r in range(1, n_d):
        pl.semaphore_signal(
            barrier, 1, device_id=(lax.rem(d + r, n_d), t), device_id_type=MESH
        )
    pl.semaphore_wait(barrier, n_t - 1 + n_d - 1)


def remote(src, dst, send, recv, d, t):
    return pltpu.make_async_remote_copy(
        src_ref=src, dst_ref=dst, send_sem=send, recv_sem=recv, device_id=(d, t), device_id_type=MESH
    )


class Places:
    def __init__(self, n_d, n_t):
        d, t = lax.axis_index("dp"), lax.axis_index("tensor")
        self.d, self.t = d, t
        self.me = {"z": d // INNER, "y": lax.rem(d, INNER), "x": t // CORES, "c": lax.rem(t, CORES)}
        self.count = counts(n_d, n_t)

    def peer(self, axis, r):
        at = dict(self.me)
        at[axis] = lax.rem(at[axis] + r, self.count[axis])
        return at[axis], (at["z"] * INNER + at["y"], at["x"] * CORES + at["c"])


def counts(n_d, n_t):
    return {"z": n_d // INNER, "y": INNER, "x": n_t // CORES, "c": CORES}


class Spread:
    def __init__(self, places, dims, known, path, array, source, send, recv, row, lanes=slice(None)):
        self.path, self.flights = path, []
        for s, axis in enumerate(path):
            region = tuple(
                slice(None) if a in known or a in path[:s] else places.me[a] for a in dims
            ) + (slice(None), lanes)
            src = source if s == 0 else array.at[region]
            self.flights.append([])
            for r in range(1, places.count[axis]):
                _, (d, t) = places.peer(axis, r)
                self.flights[s].append(
                    remote(
                        src, array.at[region], send.at[row + s, r - 1], recv.at[row + s, r - 1], d, t
                    )
                )

    def start(self, s):
        for copy in self.flights[s]:
            copy.start()

    def wait(self, s):
        for copy in self.flights[s]:
            copy.wait()

    def advance(self, s, last=None):
        self.wait(s)
        if s + 1 < len(self.path) and s != last:
            self.start(s + 1)


class Reduce:
    def __init__(self, places, dims, path, source, own, met, results, send, recv, local, row):
        self.places, self.path, self.own, self.met = places, path, own, met
        self.results, self.flights, self.dims = results, [], []
        current = source
        for s, axis in enumerate(path):
            at = dims.index(axis)
            self.dims.append((current, dims, at))
            self.flights.append([])
            for r in range(1, places.count[axis]):
                to, (d, t) = places.peer(axis, r)
                self.flights[s].append(
                    remote(
                        current.at[(slice(None),) * at + (to,)], met[s].at[r - 1],
                        send.at[row + s, r - 1], recv.at[row + s, r - 1], d, t,
                    )
                )
            if s == 0:
                self.load = None
                if own is not None:
                    self.load = pltpu.make_async_copy(
                        current.at[(slice(None),) * at + (places.me[axis],)], own, local
                    )
            dims = dims.replace(axis, "")
            current = results[s]

    def start(self, s):
        for copy in self.flights[s]:
            copy.start()
        if s == 0 and self.load is not None:
            self.load.start()

    def advance(self, s):
        places, path = self.places, self.path
        for copy in self.flights[s]:
            copy.wait()
        current, dims, at = self.dims[s]
        rest = dims.replace(path[s], "")
        if s == 0 and self.load is not None:
            self.load.wait()
            current, at = self.own, None
        sizes = [places.count[a] for a in rest]

        def fold(n, carry):
            spot = []
            for size in reversed(sizes):
                spot.insert(0, lax.rem(n, size))
                n = n // size
            own = list(spot)
            if at is not None:
                own.insert(at, places.me[path[s]])
            value = current[tuple(own)].astype(F32)
            for r in range(places.count[path[s]] - 1):
                value += self.met[s][(r,) + tuple(spot)].astype(F32)
            if callable(self.results[s]):
                self.results[s](value)
            else:
                self.results[s][tuple(spot)] = value.astype(BF16)
            return carry

        if sizes:
            lax.fori_loop(0, int(np.prod(sizes)), fold, 0)
        else:
            fold(0, 0)
        if s + 1 < len(path):
            self.start(s + 1)


def reduce_scratch(count, dims, path, tail, own=True, last=True):
    shapes = []
    rest = dims.replace(path[0], "")
    if own:
        shapes.append(tuple(count[a] for a in rest) + tail)
    left = dims
    for axis in path:
        left = left.replace(axis, "")
        shapes.append((count[axis] - 1,) + tuple(count[a] for a in left) + tail)
    left = dims
    for axis in path if not last else path[:-1]:
        left = left.replace(axis, "")
        shapes.append(tuple(count[a] for a in left) + tail)
    return [pltpu.VMEM(shape, BF16) for shape in shapes]


BACK_SUMS = (("zy", "zy"), ("zx", "xz"), ("zyx", "xyz"), ("zyx", "yxz"), ("czyx", "czxy"))
CODE = {"z": 2, "y": 2, "x": 2, "c": 2}
EARLY = ((2, S_GATE_A), (3, S_SHIFT_M), (4, S_SCALE_M), (5, S_GATE_M))


def front_kernel(
    n_d, n_t, parts, heads, cond_at, bias_at, sizes,
    x_ref, qkv_ref, small_ref, ada_ref, up_ref, down_ref, outw_ref, cos_ref, sin_ref,
    in_all, proj_ref, mix_ref, lse_ref, mix_own, vec_ref, cond_ref, w_all, w_ul, w_dl, w_uh, w_dh, w_out,
    x_all, w_pack, wt_ref, out_pack, small_all, mod_all, mod_rows, key_ref,
    s_x, r_x, s_c, r_c, s_f, r_f, s_z, r_z, s_y, r_y, s_s, r_s, s_m, r_m, s_l,
    s_w, r_w, s_o, r_o,
):
    d, t, oi, ii, xi, ci = place(n_d, n_t)
    nx, no = n_t // CORES, n_d // INNER
    other = xi * CORES + (1 - ci)
    piece = x_ref.shape[0] // parts
    rows, features = x_ref.shape
    width = qkv_ref.shape[2]
    half = HEAD_DIM // 2
    cut = w_ul.shape[5]
    low_half, high_half = slice(0, cut), slice(cut, 2 * cut)
    for j in range(3):
        w_pack[:, j * width : (j + 1) * width] = qkv_ref[j]
    out_pack[:, :width] = outw_ref[...].T
    if out_pack.shape[1] > width:
        out_pack[:, width:] = jnp.zeros((out_pack.shape[0], out_pack.shape[1] - width), BF16)
    greet(n_d, n_t)
    places = Places(n_d, n_t)
    spread = lambda row, dims, path, array, source: Spread(
        places, dims, "", path, array, source, s_w, r_w, row
    )
    up_low = spread(0, "zyxc", "zyxc", w_ul, up_ref.at[:, low_half])
    down_low = spread(4, "zyxc", "xzyc", w_dl, down_ref.at[:, low_half])
    out_all = spread(8, "zyxc", "zxyc", w_out, out_pack)
    up_high = spread(12, "zy", "zy", w_uh, up_ref.at[:, high_half])
    down_high = spread(16, "zx", "zx", w_dh, down_ref.at[:, high_half])
    s_copies = []
    for r in range(1, n_d):
        copy = remote(
            small_ref, small_all.at[d], s_s.at[r - 1], r_s.at[r - 1], lax.rem(d + r, n_d), t
        )
        copy.start()
        s_copies.append(copy)
    down_low.start(0)
    x_copies = []
    for r in range(1, nx):
        peer = lax.rem(xi + r, nx) * CORES + ci
        for p in range(parts):
            at = pl.ds(p * piece, piece)
            copy = remote(
                x_ref.at[at], x_all.at[t, at], s_x.at[r - 1, p], r_x.at[r - 1, p], d, peer
            )
            copy.start()
            x_copies.append((r, p, copy))
    z_copies = []
    for r in range(1, no):
        copy = remote(
            w_pack, w_all.at[d], s_z.at[r - 1], r_z.at[r - 1], lax.rem(oi + r, no) * INNER + ii, t
        )
        copy.start()
        z_copies.append(copy)
    y_copies = []
    for q in range(1, INNER):
        copy = remote(
            w_pack, w_all.at[d], s_y.at[q - 1, 0], r_y.at[q - 1, 0],
            oi * INNER + lax.rem(ii + q, INNER), t,
        )
        copy.start()
        y_copies.append(copy)
    core_copy = remote(x_ref, x_all.at[t], s_c, r_c, d, other)
    core_copy.start()
    local = []
    for n, (src, dst) in enumerate(
        (
            (small_ref, small_all.at[d]),
            (x_ref, x_all.at[t]),
            (w_pack, w_all.at[d]),
            (up_ref.at[:, low_half], w_ul.at[oi, ii, xi, ci]),
            (down_ref.at[:, low_half], w_dl.at[oi, ii, xi, ci]),
            (up_ref.at[:, high_half], w_uh.at[oi, ii]),
            (down_ref.at[:, high_half], w_dh.at[oi, xi]),
            (out_pack, w_out.at[oi, ii, xi, ci]),
        )
    ):
        copy = pltpu.make_async_copy(src, dst, s_l.at[n])
        copy.start()
        local.append(copy)

    up_low.start(0)

    local[0].wait()
    for copy in s_copies:
        copy.wait()
    cond = small_all[:, 0, cond_at : cond_at + ada_ref.shape[1]]
    for s in range(n_d):
        cond_ref[:, s : s + 1] = cond[s : s + 1].T
    bias = small_ref[:, bias_at : bias_at + ada_ref.shape[0]]
    mod_rows[:, 0, :] = dot(cond.astype(BF16), ada_ref[...], 1, 1) + bias
    own_mod = pltpu.make_async_copy(mod_rows.at[d], mod_all.at[d], s_l.at[8])
    own_mod.start()
    m_copies = []
    for r in range(1, n_d):
        peer = lax.rem(d + r, n_d)
        copy = remote(mod_rows.at[peer], mod_all.at[d], s_m.at[r - 1], r_m.at[r - 1], peer, t)
        copy.start()
        m_copies.append(copy)
    for r in range(1, no):
        z_copies[r - 1].wait()
        origin = lax.rem(oi + no - r, no) * INNER + ii
        for q in range(1, INNER):
            copy = remote(
                w_all.at[origin], w_all.at[origin], s_y.at[q - 1, r], r_y.at[q - 1, r],
                oi * INNER + lax.rem(ii + q, INNER), t,
            )
            copy.start()
            y_copies.append(copy)
    for n in (3, 4, 7):
        local[n].wait()
    down_low.advance(0)
    up_low.advance(0)
    out_all.start(0)
    f_copies = []
    for r, p, copy in x_copies:
        copy.wait()
        origin = lax.rem(xi + nx - r, nx) * CORES + ci
        at = pl.ds(p * piece, piece)
        copy = remote(
            x_all.at[origin, at], x_all.at[origin, at],
            s_f.at[r - 1, p], r_f.at[r - 1, p], d, other,
        )
        copy.start()
        f_copies.append(copy)

    for copy in m_copies + [own_mod]:
        copy.wait()
    def put(first, piece_of, count):
        for s in range(n_d):
            value = piece_of(s)
            start = s * count
            done = 0
            while done < count:
                row, column = divmod(start + done, features)
                take = min(count - done, features - column)
                vec_ref[first + row : first + row + 1, column : column + take] = value[
                    :, done : done + take
                ]
                done += take

    vec_ref[...] = jnp.zeros_like(vec_ref)
    at = 0
    for first, count in sizes:
        put(first, lambda s: small_all[s, :, at : at + count], count)
        at += count
    columns = ada_ref.shape[0]
    for s in range(n_d):
        done = 0
        while done < columns:
            row, column = divmod(s * columns + done, features)
            take = min(columns - done, features - column)
            row = MOD_ROWS[row]
            vec_ref[row : row + 1, column : column + take] = mod_all[s, :, done : done + take]
            done += take

    for copy in f_copies + [local[1], core_copy]:
        copy.wait()

    def norm(b, carry):
        x = x_all[b].astype(F32)
        centred = x - mean_rows(x)
        normed = centred * lax.rsqrt(mean_rows(centred * centred) + EPSILON)
        normed = normed * vec_ref[GAIN1 : GAIN1 + 1]
        low = (normed * (1.0 + vec_ref[SCALE_A : SCALE_A + 1]) + vec_ref[SHIFT_A : SHIFT_A + 1])
        in_all[b] = low.astype(BF16)
        return carry

    lax.fori_loop(0, n_t, norm, 0)
    for copy in y_copies + [local[2]]:
        copy.wait()
    wt_ref[...] = w_all[...].reshape(features, 3 * width).T

    for n in (5, 6):
        local[n].wait()
    out_all.advance(0)
    down_high.start(0)
    up_high.start(0)

    def project(b, carry):
        proj = dot(wt_ref[...], in_all[b], 1, 1)
        lanes = pl.ds(pl.multiple_of(b * rows, rows), rows)
        cos, sin = cos_ref[:, lanes], sin_ref[:, lanes]
        for j in range(2):
            factor = HEAD_DIM**-0.5 if j == 0 else 1.0
            for h in range(heads):
                at = j * width + h * HEAD_DIM
                first, last = proj[at : at + half], proj[at + half : at + HEAD_DIM]
                top = ((first * cos - last * sin) * factor).astype(BF16)
                bottom = ((last * cos + first * sin) * factor).astype(BF16)
                proj_ref[b, at : at + half] = top
                proj_ref[b, at + half : at + HEAD_DIM] = bottom
                if j == 1:
                    key_ref[h, lanes, :] = jnp.concatenate([top, bottom], axis=0).T
        proj_ref[b, 2 * width :] = proj[2 * width :].astype(BF16)

        @pl.when(b == n_t - 2)
        def _():
            up_low.advance(1)

        return carry

    lax.fori_loop(0, n_t, project, 0)

    def attend(u, carry):
        plane = lax.rem(xi + nx - 1 - u // heads, nx)
        h = lax.rem(u, heads)
        at = pl.ds(pl.multiple_of(h * HEAD_DIM, HEAD_DIM), HEAD_DIM)
        value_at = pl.ds(pl.multiple_of(2 * width + h * HEAD_DIM, HEAD_DIM), HEAD_DIM)
        first = plane * CORES
        query = jnp.concatenate([proj_ref[first + c, at] for c in range(CORES)], axis=1)
        scores = dot(key_ref[h], query, 1, 0)
        top = jnp.max(scores, axis=0, keepdims=True)
        grown = jnp.exp(scores - top)
        total = jnp.sum(grown, axis=0, keepdims=True)
        value = jnp.concatenate([proj_ref[v, value_at] for v in range(n_t)], axis=1)
        mixed = (dot(value, grown.astype(BF16), 1, 0) / total).astype(BF16)
        log_total = top + jnp.log(total)
        for c in range(CORES):
            part = slice(c * rows, (c + 1) * rows)
            mix_ref[first + c, at] = mixed[:, part]
            lse_ref[first + c, pl.ds(h, 1)] = log_total[:, part]
        for r in range(nx):
            @pl.when(u == (nx - r) * heads - 1)
            def _(r=r):
                for c in range(CORES):
                    if r * CORES + c > 0:
                        o_copies[r * CORES + c].start()

        @pl.when(u == 0)
        def _():
            down_low.advance(1)
            out_all.advance(1)

        @pl.when(u == 4)
        def _():
            up_low.advance(2)

        @pl.when(u == 5)
        def _():
            down_high.advance(0)
            up_high.advance(0)
            out_all.advance(2)

        return carry

    o_copies = {}
    for m in range(1, n_t):
        b = order(m, xi, ci, nx)
        o_copies[m] = remote(
            mix_ref.at[b], mix_own.at[t], s_o.at[m - 1], r_o.at[mirror(m, nx) - 1], d, b
        )
    lax.fori_loop(0, nx * heads, attend, 0)
    mine = pltpu.make_async_copy(mix_ref.at[t], mix_own.at[t], s_l.at[9])
    mine.start()
    down_low.advance(2)
    down_high.wait(1)
    up_high.wait(1)
    for one in (out_all, up_low, down_low):
        one.wait(3)
    mine.wait()
    for copy in list(o_copies.values()):
        copy.wait()


def front_call(x, qkv, small, ada_t, up, down_t, outw, cos, sin, cond_at, bias_at, sizes, n_d, n_t):
    parts = 4
    nx, no = n_t // CORES, n_d // INNER
    rows, features = x.shape
    part, width = qkv.shape[1:]
    heads = width // HEAD_DIM
    length = rows * n_t
    wide = -(-width // 128) * 128
    units = up.shape[1]
    steps = max(no, INNER, nx) - 1
    cut = units // 2
    grid_of = (no, INNER, nx, CORES, part)
    columns = ada_t.shape[0]
    return pl.pallas_call(
        partial(front_kernel, n_d, n_t, parts, heads, cond_at, bias_at, sizes),
        name="front",
        out_shape=[
            struct((n_t, rows, features), BF16),
            struct((n_t, 3 * width, rows), BF16),
            struct((n_t, width, rows), BF16),
            struct((n_t, heads, rows), F32),
            struct((n_t, width, rows), BF16),
            struct((16, features), F32),
            struct((ada_t.shape[1], n_d), F32),
            struct((n_d, part, 3 * width), BF16),
            struct(grid_of + (cut,), BF16),
            struct(grid_of + (cut,), BF16),
            struct((no, INNER, part, cut), BF16),
            struct((no, nx, part, cut), BF16),
            struct(grid_of + (wide,), BF16),
        ],
        in_specs=[VMEM, VMEM, VMEM, VMEM, ANY, ANY, VMEM, VMEM, VMEM],
        out_specs=[VMEM] * 8 + [ANY] * 5,
        scratch_shapes=[
            pltpu.VMEM((n_t, rows, features), BF16),
            pltpu.VMEM((part, 3 * width), BF16),
            pltpu.VMEM((3 * width, features), BF16),
            pltpu.VMEM((part, wide), BF16),
            pltpu.VMEM((n_d,) + small.shape, F32),
            pltpu.VMEM((n_d, 1, columns), F32),
            pltpu.VMEM((n_d, 1, columns), F32),
            pltpu.VMEM((heads, length, HEAD_DIM), BF16),
            DMA((nx - 1, parts)), DMA((nx - 1, parts)), DMA, DMA,
            DMA((nx - 1, parts)), DMA((nx - 1, parts)),
            DMA((no - 1,)), DMA((no - 1,)),
            DMA((INNER - 1, no)), DMA((INNER - 1, no)),
            DMA((n_d - 1,)), DMA((n_d - 1,)), DMA((n_d - 1,)), DMA((n_d - 1,)),
            DMA((10,)),
            DMA((20, steps)), DMA((20, steps)),
            DMA((n_t - 1,)), DMA((n_t - 1,)),
        ],
        compiler_params=params(0),
        cost_estimate=cost(20 * heads * length * length * HEAD_DIM, 40e6, heads * length * length),
    )(x, qkv, small, ada_t, up, down_t, outw, cos, sin)


def middle_kernel(
    n_d, n_t,
    mix_ref, x_ref, g_ref, vec_ref, ul_ref, dl_ref, uh_ref, dh_ref, wout_ref,
    out_ref, dmid_ref, dmix_ref, stat_ref, hul_ref, hdl_ref, huh_ref, hdh_ref, gout_ref,
    up_buf, down_buf, o_buf, go_buf,
    attn_ref, low_ref, lowt_ref, dl_t_ref, dlt_ref, acc_out, acc_in,
    mul_c, rul, mul_x, mdl_c, mdl_y, rdl, muh, mdh,
    s_u, s_d, s_o, s_w, r_w, s_r, r_r,
):
    places = Places(n_d, n_t)
    count, me = places.count, places.me
    rows, features = x_ref.shape
    width = mix_ref.shape[1]
    cut = up_buf.shape[-1]
    wide = wout_ref.shape[-1]
    loads = [
        pltpu.make_async_copy(wout_ref, o_buf, s_o.at[0]),
        pltpu.make_async_copy(ul_ref, up_buf.at[0], s_u.at[0]),
        pltpu.make_async_copy(dl_ref, down_buf.at[0], s_d.at[0]),
        pltpu.make_async_copy(uh_ref, up_buf.at[1, :, :, me["x"], me["c"]], s_u.at[1]),
        pltpu.make_async_copy(dh_ref, down_buf.at[1, :, me["y"], :, me["c"]], s_d.at[1]),
    ]
    for copy in loads:
        copy.start()
    greet(n_d, n_t)
    up_high = Spread(places, "zyxc", "zy", "xc", up_buf.at[1], uh_ref, s_w, r_w, 0)
    down_high = Spread(places, "zyxc", "zx", "yc", down_buf.at[1], dh_ref, s_w, r_w, 2)
    up_high.start(0)
    down_high.start(0)
    nx = count["x"]
    planes = [lax.rem(me["x"] + nx - 1 - n, nx) for n in range(nx)]
    ul = [
        Reduce(
            places, "zyc", "c", up_buf.at[2, :, :, planes[n]], None, [mul_c.at[n]], [rul.at[n]],
            s_r, r_r, None, n,
        )
        for n in range(nx)
    ]
    ul_x = [
        remote(
            rul.at[nx - 1 - r], mul_x.at[r - 1], s_r.at[4 * nx + 2, r - 1], r_r.at[4 * nx + 2, r - 1],
            *places.peer("x", r)[1],
        )
        for r in range(1, nx)
    ]
    dl = [
        Reduce(
            places, "zyc", "c", down_buf.at[2, :, :, planes[n]], None, [mdl_c.at[n]],
            [rdl.at[:, :, planes[n]]], s_r, r_r, None, nx + n,
        )
        for n in range(nx)
    ]
    dl_y = Reduce(
        places, "zyx", "y", rdl, None, [mdl_y], [rdl.at[:, me["y"]]], s_r, r_r, None, 2 * nx
    )
    high_up, high_down = up_buf.at[0, :, :, :, me["c"]], down_buf.at[0, :, :, :, me["c"]]
    uh = Reduce(places, "zyxc", "c", up_buf.at[0], None, [muh], [high_up], s_r, r_r, None, 2 * nx + 1)
    dh = Reduce(
        places, "zyxc", "c", down_buf.at[0], None, [mdh], [high_down], s_r, r_r, None, 2 * nx + 2
    )
    keeps = [
        pltpu.make_async_copy(go_buf, gout_ref, s_o.at[1]),
        pltpu.make_async_copy(high_up, huh_ref, s_o.at[2]),
        pltpu.make_async_copy(high_down, hdh_ref, s_o.at[3]),
        pltpu.make_async_copy(rul.at[nx - 1], hul_ref, s_o.at[4]),
        pltpu.make_async_copy(rdl.at[:, me["y"]], hdl_ref, s_o.at[5]),
    ]
    vec = lambda row: vec_ref[row : row + 1]
    cot = g_ref[...].astype(F32)
    d_mlp = (vec(GATE_M) * cot).astype(BF16)
    dl_t_ref[...] = d_mlp
    dlt_ref[...] = d_mlp.T
    stat_ref[...] = jnp.zeros_like(stat_ref)
    stat_ref[S_B_DOWN : S_B_DOWN + 1] = sum_tokens(d_mlp.astype(F32))
    if wide > width:
        go_buf[...] = jnp.zeros_like(go_buf)
    loads[0].wait()
    w_out = lambda b: o_buf[:, :, b // CORES, b % CORES].reshape(features, wide)[:, :width]
    attn_out = jnp.zeros((rows, features), F32)
    for b in range(n_t):
        attn_out += dot(mix_ref[b].T, w_out(b), 1, 1)
    attn_ref[...] = attn_out
    branch = vec(GATE_A) * attn_out
    stat_ref[S_SQ_A : S_SQ_A + 1] = sum_tokens(branch * branch)
    middle = x_ref[...].astype(F32) + branch
    dmid_ref[...] = middle
    centred = middle - mean_rows(middle)
    inv = lax.rsqrt(mean_rows(centred * centred) + EPSILON)
    low = (centred * inv * vec(GAIN2) * (1.0 + vec(SCALE_M)) + vec(SHIFT_M)).astype(BF16)
    low_ref[...] = low
    lowt_ref[...] = low.T
    acc_out[...] = jnp.zeros_like(acc_out)
    acc_in[...] = jnp.zeros_like(acc_in)
    loads[1].wait()
    loads[2].wait()

    def block(n, carry):
        j, p = n // nx, lax.rem(me["x"] + nx - 1 - lax.rem(n, nx), nx)
        slot = 2 - 2 * j
        lanes = pl.ds(pl.multiple_of(j * cut, cut), cut)

        @pl.when(n == nx)
        def _():
            for one in (up_high, down_high):
                one.wait(1)

        both = lambda buf: jnp.concatenate(
            [buf[j, :, :, p, c].reshape(features, cut) for c in range(CORES)], axis=1
        )
        up, down = both(up_buf), both(down_buf)
        bias = jnp.concatenate(
            [vec_ref[pl.ds(B_UP + p * CORES + c, 1), lanes] for c in range(CORES)], axis=1
        )
        hidden = dot(low_ref[...], up, 1, 0) + bias
        square = hidden * hidden
        bent = jnp.tanh(GELU_C * hidden * (1.0 + GELU_A * square))
        half = 0.5 * (1.0 + bent)
        active = (hidden * half).astype(BF16)
        slope = half + (0.5 * GELU_C) * hidden * (1.0 - bent * bent) * (
            1.0 + (3.0 * GELU_A) * square
        )
        acc_out[...] += dot(active, down, 1, 1)
        grad_down = dot(dlt_ref[...], active, 1, 0).astype(BF16)
        d_hidden = (dot(dl_t_ref[...], down, 1, 0) * slope).astype(BF16)
        sums = sum_tokens(d_hidden.astype(F32))
        for c in range(CORES):
            stat_ref[pl.ds(S_B_UP + p * CORES + c, 1), lanes] = sums[:, c * cut : (c + 1) * cut]
        grad_up = dot(lowt_ref[...], d_hidden, 1, 0).astype(BF16)
        acc_in[...] += dot(d_hidden, up, 1, 1)
        for c in range(CORES):
            lanes_of = slice(c * cut, (c + 1) * cut)
            shape = up_buf.shape[1:3] + (-1, cut)
            down_buf[slot, :, :, p, c] = grad_down[:, lanes_of].reshape(shape)
            up_buf[slot, :, :, p, c] = grad_up[:, lanes_of].reshape(shape)

        for m in range(nx):
            @pl.when(n == m)
            def _(m=m):
                if m == nx - 1:
                    for copy in loads[3:]:
                        copy.wait()
                    for one in (up_high, down_high):
                        one.advance(0)
                ul[m].start(0)
                dl[m].start(0)
                if m > 0:
                    ul[m - 1].advance(0)
                    ul_x[nx - 1 - m].start()
                    dl[m - 1].advance(0)

        @pl.when(n == nx)
        def _():
            dl[nx - 1].advance(0)
            dl_y.start(0)
            ul[nx - 1].advance(0)

        return carry

    lax.fori_loop(0, 2 * nx, block, 0)
    uh.start(0)
    dh.start(0)
    middle = dmid_ref[...]
    mlp_out = acc_out[...] + vec(B_DOWN)
    mlp_branch = vec(GATE_M) * mlp_out
    result = middle + mlp_branch
    out_ref[...] = result.astype(BF16)
    cot = g_ref[...].astype(F32)
    stat_ref[S_SQ_M : S_SQ_M + 1] = sum_tokens(mlp_branch * mlp_branch)
    stat_ref[S_SQ_R : S_SQ_R + 1] = sum_tokens(result * result)
    stat_ref[S_GATE_M : S_GATE_M + 1] = sum_tokens(cot * mlp_out)
    e = acc_in[...]
    centred = middle - mean_rows(middle)
    inv = lax.rsqrt(mean_rows(centred * centred) + EPSILON)
    nhat = centred * inv
    gain, scale = vec(GAIN2), 1.0 + vec(SCALE_M)
    by_nhat = sum_tokens(e * nhat)
    stat_ref[S_SHIFT_M : S_SHIFT_M + 1] = sum_tokens(e)
    stat_ref[S_SCALE_M : S_SCALE_M + 1] = by_nhat * gain
    stat_ref[S_GAIN2 : S_GAIN2 + 1] = by_nhat * scale
    dn = e * (scale * gain)
    d_middle = cot + inv * (dn - mean_rows(dn) - nhat * mean_rows(dn * nhat))
    dmid_ref[...] = d_middle
    stat_ref[S_GATE_A : S_GATE_A + 1] = sum_tokens(d_middle * attn_ref[...])
    d_attn = (vec(GATE_A) * d_middle).astype(BF16)
    d_attn_t = d_attn.T
    for b in range(n_t):
        dmix_ref[b] = dot(d_attn, w_out(b), 1, 0).astype(BF16).T
        go_buf[b % CORES, :, :, b // CORES, :, :width] = (
            dot(d_attn_t, mix_ref[b], 1, 1).astype(BF16).reshape(go_buf.shape[1:3] + (-1, width))
        )
    keeps[0].start()
    uh.advance(0)
    keeps[1].start()
    dh.advance(0)
    keeps[2].start()
    for one in ul_x:
        one.wait()
    no = count["z"]

    def fold(n, carry):
        at = (n // INNER, lax.rem(n, INNER))
        value = rul[(nx - 1,) + at].astype(F32)
        for r in range(nx - 1):
            value += mul_x[(r,) + at].astype(F32)
        rul[(nx - 1,) + at] = value.astype(BF16)
        return carry

    lax.fori_loop(0, no * INNER, fold, 0)
    keeps[3].start()
    dl_y.advance(0)
    keeps[4].start()
    for copy in keeps:
        copy.wait()


def middle_call(mix, x, g, vecs, w_ul, w_dl, w_uh, w_dh, w_out, stat_rows, n_d, n_t):
    rows, features = x.shape
    cut = w_ul.shape[-1]
    part, wide = w_out.shape[-2:]
    width = mix.shape[1]
    count = counts(n_d, n_t)
    no, nx = count["z"], count["x"]
    per = (3,) + w_ul.shape
    plane = (no, INNER, part, cut)
    tail = (part, cut)
    g_out = (CORES, no, INNER, nx, part, wide)
    return pl.pallas_call(
        partial(middle_kernel, n_d, n_t),
        name="middle",
        out_shape=[
            struct((rows, features), BF16),
            struct((rows, features), F32),
            struct((n_t, width, rows), BF16),
            struct((stat_rows, features), F32),
            struct((no, INNER) + tail, BF16),
            struct((no, nx) + tail, BF16),
            struct((no, INNER, nx) + tail, BF16),
            struct((no, INNER, nx) + tail, BF16),
            struct(g_out, BF16),
        ],
        in_specs=[VMEM] * 4 + [ANY] * 5,
        out_specs=[VMEM] * 4 + [ANY] * 5,
        scratch_shapes=[
            pltpu.VMEM(per, BF16), pltpu.VMEM(per, BF16), pltpu.VMEM(w_out.shape, BF16),
            pltpu.VMEM(g_out, BF16),
            pltpu.VMEM((rows, features), F32),
            pltpu.VMEM((rows, features), BF16),
            pltpu.VMEM((features, rows), BF16),
            pltpu.VMEM((rows, features), BF16),
            pltpu.VMEM((features, rows), BF16),
            pltpu.VMEM((rows, features), F32),
            pltpu.VMEM((rows, features), F32),
        ]
        + [
            pltpu.VMEM((nx, 1) + plane, BF16), pltpu.VMEM((nx,) + plane, BF16),
            pltpu.VMEM((nx - 1,) + plane, BF16),
            pltpu.VMEM((nx, 1) + plane, BF16), pltpu.VMEM((INNER - 1, no, nx) + tail, BF16),
            pltpu.VMEM((no, INNER, nx) + tail, BF16),
            pltpu.VMEM((1, no, INNER, nx) + tail, BF16),
            pltpu.VMEM((1, no, INNER, nx) + tail, BF16),
        ]
        + [
            DMA((2,)), DMA((2,)), DMA((6,)),
            DMA((4, max(nx, INNER, CORES) - 1)), DMA((4, max(nx, INNER, CORES) - 1)),
            DMA((4 * nx + 3, max(nx, INNER, CORES) - 1)), DMA((4 * nx + 3, max(nx, INNER, CORES) - 1)),
        ],
        compiler_params=params(1),
        cost_estimate=cost(2 * rows * features * features * (6 * n_t + 4), 30e6),
    )(mix, x, g, vecs, w_ul, w_dl, w_uh, w_dh, w_out)


def back_kernel(
    n_d, n_t, parts, heads,
    dmix_ref, proj_ref, mix_ref, lse_ref, cos_ref, sin_ref, in_hbm, wq_hbm, stat_ref,
    x_hbm, dmid_hbm, vec_ref, ada_ref,
    hul_ref, hdl_ref, huh_ref, hdh_ref, gout_ref,
    grad_in_ref, gq_ref, up_ref, down_ref, out_ref, table_ref, flat_ref, gain_ref, gcond_ref,
    dmix_all, key_ref, keyt_ref, val_ref, dkey_ref, dval_ref, dquery_ref, dproj_ref, in_ref, wq_ref,
    acc_ref, grad_ref, rc, rx, ry, sz, rz, got_ref, mine_ref,
    x_ref, dmid_ref, late_ref, late_got, late_mine, late_all, rows_out, rows_in, *more,
):
    buffers, at = [], 0
    for size in (len(reduce_scratch(CODE, dims, path, (1, 1))) for dims, path in BACK_SUMS):
        buffers.append(more[at : at + size])
        at += size
    (
        s_a, r_a, s_l, s_g, r_g, s_t, r_t, s_d, r_d, s_c, r_c, s_x, r_x, s_y, r_y, s_z, r_z,
        s_v, r_v, s_e, r_e, s_p, r_p,
    ) = more[at:]
    places = Places(n_d, n_t)
    d, t, oi, ii, xi, ci = place(n_d, n_t)
    nx, no = n_t // CORES, n_d // INNER
    other = xi * CORES + (1 - ci)
    blocks, total, rows = proj_ref.shape
    width = total // 3
    half = HEAD_DIM // 2
    features = x_ref.shape[1]
    assert nx == 2 and CORES == 2

    cut = hul_ref.shape[-1]

    def put(target, lanes):
        def store(value):
            target[:, lanes] = value
        return store

    def put_out(value):
        out_ref[...] = value.T[:width]

    sinks = (
        put(up_ref, slice(0, cut)), put(down_ref, slice(0, cut)),
        put(up_ref, slice(cut, 2 * cut)), put(down_ref, slice(cut, 2 * cut)), put_out,
    )
    sums = []
    row = 0
    for n, ((dims, path), source) in enumerate(
        zip(BACK_SUMS, (hul_ref, hdl_ref, huh_ref, hdh_ref, gout_ref))
    ):
        steps = len(path)
        sums.append(
            Reduce(
                places, dims, path, source, buffers[n][0], buffers[n][1 : 1 + steps],
                list(buffers[n][1 + steps :]) + [sinks[n]], s_g, r_g, s_l.at[6 + n], row,
            )
        )
        row += steps
    ul, dl, uh, dh, go = sums

    greet(n_d, n_t)
    a_copies = {}
    for m in range(1, n_t):
        b = order(m, xi, ci, nx)
        a_copies[mirror(m, nx)] = remote(
            dmix_ref.at[b], dmix_all.at[t], s_a.at[m - 1], r_a.at[mirror(m, nx) - 1], d, b
        )
    for m in range(n_t - 1, 0, -1):
        a_copies[mirror(m, nx)].start()
    for one in (dh, go):
        one.start(0)
    loads = [
        pltpu.make_async_copy(dmix_ref.at[t], dmix_all.at[t], s_l.at[0]),
        pltpu.make_async_copy(in_hbm, in_ref, s_l.at[1]),
        pltpu.make_async_copy(wq_hbm, wq_ref, s_l.at[2]),
        pltpu.make_async_copy(x_hbm, x_ref, s_l.at[3]),
        pltpu.make_async_copy(dmid_hbm, dmid_ref, s_l.at[4]),
    ]
    for copy in loads:
        copy.start()
    t_copies = []
    for r in range(1, n_t):
        copy = remote(
            stat_ref, got_ref.at[r - 1], s_t.at[r - 1], r_t.at[r - 1], d, lax.rem(t + r, n_t)
        )
        copy.start()
        t_copies.append(copy)
    d_copies = [pltpu.make_async_copy(mine_ref, table_ref.at[d], s_l.at[5])]
    for r in range(1, n_d):
        d_copies.append(
            remote(mine_ref, table_ref.at[d], s_d.at[r - 1], r_d.at[r - 1], lax.rem(d + r, n_d), t)
        )

    def share_statistics():
        for copy in t_copies:
            copy.wait()
        value = stat_ref[...]
        for r in range(1, n_t):
            value += got_ref[r - 1]
        mine_ref[...] = value
        for copy in d_copies:
            copy.start()

    dkey_ref[...] = jnp.zeros_like(dkey_ref)
    dval_ref[...] = jnp.zeros_like(dval_ref)

    def turn(b, carry):
        lanes = pl.ds(pl.multiple_of(b * rows, rows), rows)
        keyt_ref[:, lanes] = proj_ref[b, width : 2 * width]
        for h in range(heads):
            at = h * HEAD_DIM
            key_ref[h, lanes] = proj_ref[b, width + at : width + at + HEAD_DIM].T
            val_ref[h, lanes] = proj_ref[b, 2 * width + at : 2 * width + at + HEAD_DIM].T
        return carry

    lax.fori_loop(0, blocks, turn, 0)
    loads[0].wait()

    loads[1].wait()
    loads[2].wait()
    dquery_ref[...] = jnp.zeros_like(dquery_ref)
    acc_ref[...] = jnp.zeros_like(acc_ref)
    part_ref = in_ref
    piece = rows // parts
    c_copies = {}
    for r in range(nx):
        block = lax.rem(xi + r, nx) * CORES + 1 - ci
        for p in range(parts):
            at = pl.ds(p * piece, piece)
            c_copies[r, p] = remote(
                part_ref.at[block, at], rc.at[r, at], s_c.at[r, p], r_c.at[r, p], d, other
            )
    x_copies = {}
    for p in range(parts):
        at = pl.ds(p * piece, piece)
        x_copies[p] = remote(
            part_ref.at[lax.rem(xi + 1, nx) * CORES + ci, at], rx.at[0, at],
            s_x.at[0, p], r_x.at[0, p], d, lax.rem(xi + 1, nx) * CORES + ci,
        )

    def unrotate(b, at, factor, first, last):
        lanes = pl.ds(pl.multiple_of(b * rows, rows), rows)
        cos, sin = cos_ref[:, lanes], sin_ref[:, lanes]
        dproj_ref[b, at : at + half] = ((first * cos + last * sin) * factor).astype(BF16)
        dproj_ref[b, at + half : at + HEAD_DIM] = ((last * cos - first * sin) * factor).astype(BF16)

    def close(b):
        lanes = pl.ds(pl.multiple_of(b * rows, rows), rows)
        for h in range(heads):
            at = h * HEAD_DIM
            d_query = dquery_ref[b, at : at + HEAD_DIM]
            unrotate(b, at, HEAD_DIM**-0.5, d_query[:half], d_query[half:])
            d_key = dkey_ref[h, lanes].T
            unrotate(b, width + at, 1.0, d_key[:half], d_key[half:])
            dproj_ref[b, 2 * width + at : 2 * width + at + HEAD_DIM] = (
                dval_ref[h, lanes].T.astype(BF16)
            )
        d_proj = dproj_ref[b]
        acc_ref[...] += dot(d_proj, in_ref[b], 1, 0)
        part_ref[b] = dot(d_proj.T, wq_ref[...], 1, 1).astype(BF16)

    def attend(n, carry):
        for m, at_step in ((1, 1), (2, 2), (3, 4)):
            @pl.when(n == at_step)
            def _(m=m):
                a_copies[m].wait()
        late_part, last_part = (n + 6) // 8, (n + 2) // 8
        q_other = late_part - last_part
        k_other = (1 - late_part) + q_other * lax.rem(n + 1, 2)
        offset = (1 - late_part) * n + q_other * (n // 2 - 1) + last_part * (n - 6)
        i = lax.rem(xi + q_other, nx) * CORES + lax.rem(ci + offset, CORES)
        span = CORES * rows
        keys = pl.ds(pl.multiple_of(lax.rem(xi + k_other, nx) * span, span), span)
        for h in range(heads):
            at = h * HEAD_DIM
            query_t = proj_ref[i, at : at + HEAD_DIM]
            dmix_t = dmix_all[i, at : at + HEAD_DIM]
            mix_t = mix_ref[i, at : at + HEAD_DIM]
            inner = jnp.sum(dmix_t.astype(F32) * mix_t.astype(F32), axis=0, keepdims=True)
            probs = jnp.exp(dot(key_ref[h, keys], query_t, 1, 0) - lse_ref[i, h : h + 1])
            d_probs = dot(val_ref[h, keys], dmix_t, 1, 0)
            d_scores = (probs * (d_probs - inner)).astype(BF16)
            dval_ref[h, keys] += dot(probs.astype(BF16), dmix_t.T, 1, 0)
            dkey_ref[h, keys] += dot(d_scores, query_t.T, 1, 0)
            dquery_ref[i, at : at + HEAD_DIM] += dot(keyt_ref[at : at + HEAD_DIM, keys], d_scores, 1, 0)

        @pl.when(n == 0)
        def _():
            go.advance(0)

        @pl.when(n == 1)
        def _():
            for one in (uh, dl, ul):
                one.start(0)
            share_statistics()

        @pl.when(n == 2)
        def _():
            dh.advance(0)

        @pl.when(n == 5)
        def _():
            dl.advance(0)

        @pl.when((n == 5) | (n == 7))
        def _():
            plane = lax.rem(xi + 1 - last_part, nx)

            def one(c, carry):
                close(plane * CORES + c)
                return carry

            lax.fori_loop(0, CORES, one, 0)

        @pl.when(n == 5)
        def _():
            for p in range(parts):
                c_copies[1, p].start()

        @pl.when(n == 6)
        def _():
            to = lax.rem(xi + 1, nx) * CORES + ci
            for p in range(parts):
                at = pl.ds(p * piece, piece)
                c_copies[1, p].wait()
                part_ref[to, at] = (part_ref[to, at].astype(F32) + rc[1, at].astype(F32)).astype(BF16)
                x_copies[p].start()
            dh.advance(1)
            go.advance(1)
            ul.advance(0)
            uh.advance(0)

        return carry

    lax.fori_loop(0, 2 * n_t, attend, 0)
    for p in range(parts):
        c_copies[0, p].start()
    grad_ref[...] = acc_ref[...].T.astype(BF16).reshape(grad_ref.shape)
    y_copies = []
    for q in range(1, INNER):
        to = lax.rem(ii + q, INNER)
        copy = remote(
            grad_ref.at[:, to], ry.at[q - 1], s_y.at[q - 1], r_y.at[q - 1], oi * INNER + to, t
        )
        copy.start()
        y_copies.append(copy)
    ul.advance(1)
    dl.advance(1)
    dh.advance(2)
    uh.advance(1)
    for copy in d_copies:
        copy.wait()
    loads[3].wait()
    loads[4].wait()
    for copy in y_copies:
        copy.wait()
    z_copies = []
    for r in range(1, no):
        to = lax.rem(oi + r, no)
        value = grad_ref[to, ii].astype(F32)
        for q in range(1, INNER):
            value += ry[q - 1, to].astype(F32)
        sz[r - 1] = value.astype(BF16)
        copy = remote(sz.at[r - 1], rz.at[r - 1], s_z.at[r - 1], r_z.at[r - 1], to * INNER + ii, t)
        copy.start()
        z_copies.append(copy)
    go.advance(2)

    gain, scale = vec_ref[GAIN1 : GAIN1 + 1], 1.0 + vec_ref[SCALE_A : SCALE_A + 1]
    shift_sum = jnp.zeros((1, features), F32)
    nhat_sum = jnp.zeros((1, features), F32)
    for p in range(parts):
        c_copies[0, p].wait()
        x_copies[p].wait()
        at = pl.ds(p * (rows // parts), rows // parts)
        e = part_ref[t, at].astype(F32) + rc[0, at].astype(F32)
        for r in range(1, nx):
            e += rx[r - 1, at].astype(F32)
        x = x_ref[at].astype(F32)
        centred = x - mean_rows(x)
        inv = lax.rsqrt(mean_rows(centred * centred) + EPSILON)
        nhat = centred * inv
        shift_sum += sum_tokens(e)
        nhat_sum += sum_tokens(e * nhat)
        dn = e * (scale * gain)
        grad_in_ref[at, 0, :] = dmid_ref[at] + inv * (
            dn - mean_rows(dn) - nhat * mean_rows(dn * nhat)
        )
    late_ref[:, :features] = shift_sum
    late_ref[:, features : 2 * features] = nhat_sum * gain
    late_ref[:, 2 * features :] = nhat_sum * scale

    copies = []
    for r in range(1, n_t):
        copy = remote(
            late_ref, late_got.at[r - 1], s_v.at[r - 1], r_v.at[r - 1], d, lax.rem(t + r, n_t)
        )
        copy.start()
        copies.append(copy)
    value = late_ref[...]
    for r in range(1, n_t):
        copies[r - 1].wait()
        value += late_got[r - 1]
    late_mine[...] = value
    copies = [pltpu.make_async_copy(late_mine, late_all.at[d], s_l.at[0])]
    for r in range(1, n_d):
        copies.append(
            remote(
                late_mine, late_all.at[d], s_e.at[r - 1], r_e.at[r - 1], lax.rem(d + r, n_d), t
            )
        )
    for copy in copies:
        copy.start()
    go.advance(3)
    for s in range(n_d):
        for block, row in EARLY:
            flat_ref[s : s + 1, block * features : (block + 1) * features] = table_ref[
                s, row : row + 1
            ]
    for copy in copies:
        copy.wait()
    value = late_all[0, :, 2 * features :]
    for s in range(1, n_d):
        value += late_all[s, :, 2 * features :]
    gain_ref[...] = value
    for s in range(n_d):
        flat_ref[s : s + 1, : 2 * features] = late_all[s, :, : 2 * features]
    columns = ada_ref.shape[0]
    moved = pltpu.roll(flat_ref[...], lax.rem(n_d - d, n_d) * columns, 1)[:, :columns]
    rows_out[:, 0, :] = lax.dot_general(
        moved, ada_ref[...].astype(F32), (((1,), (0,)), ((), ())),
        precision=lax.Precision.HIGHEST, preferred_element_type=F32,
    )
    copies = [pltpu.make_async_copy(rows_out.at[d], rows_in.at[d], s_l.at[1])]
    for r in range(1, n_d):
        peer = lax.rem(d + r, n_d)
        copies.append(remote(rows_out.at[peer], rows_in.at[d], s_p.at[r - 1], r_p.at[r - 1], peer, t))
    for copy in copies:
        copy.start()
    uh.advance(2)
    value = grad_ref[oi, ii].astype(F32)
    for q in range(1, INNER):
        value += ry[q - 1, oi].astype(F32)
    for copy in z_copies:
        copy.wait()
    for r in range(1, no):
        value += rz[r - 1].astype(F32)
    for j in range(3):
        gq_ref[j] = value[:, j * width : (j + 1) * width]
    for copy in copies:
        copy.wait()
    gcond_ref[...] = jnp.sum(rows_in[:, 0, :], axis=0, keepdims=True)


def back_call(
    dmix, proj, mix, lse, cos, sin, attn_in, w_qkv, stat, x, dmid, vecs, ada_t, partial_sums, n_d, n_t
):
    parts = 4
    count = counts(n_d, n_t)
    nx, no = count["x"], count["z"]
    blocks, total, rows = proj.shape
    width = total // 3
    heads = width // HEAD_DIM
    length = blocks * rows
    features = attn_in.shape[2]
    part = features // n_d
    cond_width = ada_t.shape[1]
    cut = partial_sums[0].shape[-1]
    buffers = []
    for (dims, path), source in zip(BACK_SUMS, partial_sums):
        buffers += reduce_scratch(count, dims, path, source.shape[-2:])
    stages = sum(len(path) for _, path in BACK_SUMS)
    widest = max(count.values()) - 1
    late = (1, 3 * features)
    return pl.pallas_call(
        partial(back_kernel, n_d, n_t, parts, heads),
        name="back",
        out_shape=[
            struct((rows, 1, features), F32),
            struct((3, part, width), F32),
            struct((part, 2 * cut), F32),
            struct((part, 2 * cut), F32),
            struct((width, part), F32),
            struct((n_d,) + stat.shape, F32),
            struct((n_d, 6 * features), F32),
            struct((1, features), F32),
            struct((1, cond_width), F32),
        ],
        in_specs=[VMEM] * 6 + [ANY] * 2 + [VMEM] + [ANY] * 2 + [VMEM] * 2 + [ANY] * 5,
        out_specs=[VMEM] * 9,
        scratch_shapes=[
            pltpu.VMEM(dmix.shape, BF16),
            pltpu.VMEM((heads, length, HEAD_DIM), BF16),
            pltpu.VMEM((width, length), BF16),
            pltpu.VMEM((heads, length, HEAD_DIM), BF16),
            pltpu.VMEM((heads, length, HEAD_DIM), F32),
            pltpu.VMEM((heads, length, HEAD_DIM), F32),
            pltpu.VMEM((n_t, width, rows), F32),
            pltpu.VMEM(proj.shape, BF16),
            pltpu.VMEM(attn_in.shape, BF16),
            pltpu.VMEM(w_qkv.shape, BF16),
            pltpu.VMEM((total, features), F32),
            pltpu.VMEM((no, INNER, part, total), BF16),
            pltpu.VMEM((nx, rows, features), BF16),
            pltpu.VMEM((nx - 1, rows, features), BF16),
            pltpu.VMEM((INNER - 1, no, part, total), BF16),
            pltpu.VMEM((no - 1, part, total), BF16),
            pltpu.VMEM((no - 1, part, total), BF16),
            pltpu.VMEM((n_t - 1,) + stat.shape, F32),
            pltpu.VMEM(stat.shape, F32),
            pltpu.VMEM(x.shape, BF16),
            pltpu.VMEM(x.shape, F32),
            pltpu.VMEM(late, F32),
            pltpu.VMEM((n_t - 1,) + late, F32),
            pltpu.VMEM(late, F32),
            pltpu.VMEM((n_d,) + late, F32),
            pltpu.VMEM((n_d, 1, cond_width), F32),
            pltpu.VMEM((n_d, 1, cond_width), F32),
        ]
        + buffers
        + [
            DMA((n_t - 1,)), DMA((n_t - 1,)), DMA((6 + len(BACK_SUMS),)),
            DMA((stages, widest)), DMA((stages, widest)),
            DMA((n_t - 1,)), DMA((n_t - 1,)), DMA((n_d - 1,)), DMA((n_d - 1,)),
            DMA((nx, parts)), DMA((nx, parts)), DMA((nx - 1, parts)), DMA((nx - 1, parts)),
            DMA((INNER - 1,)), DMA((INNER - 1,)), DMA((no - 1,)), DMA((no - 1,)),
            DMA((n_t - 1,)), DMA((n_t - 1,)), DMA((n_d - 1,)), DMA((n_d - 1,)),
            DMA((n_d - 1,)), DMA((n_d - 1,)),
        ],
        compiler_params=params(2),
        cost_estimate=cost(45 * heads * length * length * HEAD_DIM, 40e6, heads * length * length),
    )(dmix, proj, mix, lse, cos, sin, attn_in, w_qkv, stat, x, dmid, vecs, ada_t, *partial_sums)


def finish_kernel(
    count, n_units, table_ref, flat_ref, cond_ref, gain_in, gcond_in,
    ada_ref, bias_ref, gain1_ref, gain2_ref, bdown_ref, bup_ref, root_ref, gcond_ref,
):
    n_d = table_ref.shape[0]
    features = table_ref.shape[2]
    total = table_ref[0]
    for s in range(1, n_d):
        total += table_ref[s]
    for k, row in enumerate((S_SQ_A, S_SQ_M, S_SQ_R)):
        root_ref[k : k + 1] = jnp.broadcast_to(
            jnp.sqrt(jnp.sum(total[row : row + 1], axis=1, keepdims=True) / count),
            (1, root_ref.shape[1]),
        )
    gain2_ref[...] = total[S_GAIN2]
    bdown_ref[...] = total[S_B_DOWN]
    for u in range(n_units):
        bup_ref[u * features : (u + 1) * features] = total[S_B_UP + u]
    gain1_ref[...] = gain_in[0]
    gcond_ref[...] = gcond_in[...]
    for block in range(6):
        at = slice(block * features, (block + 1) * features)
        value = jnp.zeros((cond_ref.shape[0], features), F32)
        for s in range(n_d):
            value += cond_ref[:, s : s + 1] * flat_ref[s : s + 1, at]
        ada_ref[:, at] = value
        bias_ref[at] = jnp.sum(flat_ref[:, at], axis=0)


def finish_call(table, flat, cond_t, gain, gcond, count, n_units):
    features = table.shape[2]
    width = cond_t.shape[0]
    return pl.pallas_call(
        partial(finish_kernel, count, n_units),
        name="finish",
        out_shape=[
            struct((width, 6 * features), F32),
            struct((6 * features,), F32),
            struct((features,), F32),
            struct((features,), F32),
            struct((features,), F32),
            struct((n_units * features,), F32),
            struct((3, 128), F32),
            struct((1, width), F32),
        ],
        in_specs=[VMEM] * 5,
        out_specs=[VMEM] * 8,
        compiler_params=params(),
        cost_estimate=cost(1e7, 4e6),
    )(table, flat, cond_t, gain, gcond)


def shards(
    block_input, condition, modulation_weight, modulation_bias, first_gain, qkv_weight, out_weight,
    second_gain, up_weight, up_bias, down_weight, down_bias, grad_output,
):
    n_t, n_d = lax.axis_size("tensor"), lax.axis_size("dp")
    rows, sequences, features = block_input.shape
    assert sequences == 1
    length = rows * n_t
    part, width = qkv_weight.shape[1:]
    units = up_weight.shape[1]
    assert units == features and n_t % CORES == 0 and n_d % INNER == 0
    x = block_input.reshape(rows, features)
    g = grad_output.reshape(rows, features)
    ada_t = modulation_weight.T

    small = jnp.concatenate([first_gain, second_gain, down_bias, up_bias]).astype(F32)
    cond_at = -(-small.shape[0] // 128) * 128
    bias_at = cond_at + condition.shape[1]
    small = jnp.concatenate(
        [
            small, jnp.zeros((cond_at - small.shape[0],), F32),
            condition[0].astype(F32), modulation_bias.astype(F32),
        ]
    )[None]
    own = first_gain.shape[0]
    sizes = ((GAIN1, own), (GAIN2, own), (B_DOWN, own), (B_UP, up_bias.shape[0]))
    inverse = 10000.0 ** (-np.arange(HEAD_DIM // 2) * 2.0 / HEAD_DIM)
    angles = inverse[:, None] * np.arange(length)[None, :]
    cos, sin = jnp.asarray(np.cos(angles), F32), jnp.asarray(np.sin(angles), F32)

    attn_in, proj, mix, lse, mix_own, vecs, cond_t, w_qkv, w_ul, w_dl, w_uh, w_dh, w_out = front_call(
        x, qkv_weight, small, ada_t, up_weight, down_weight.T, out_weight, cos, sin,
        cond_at, bias_at, sizes, n_d, n_t,
    )
    stat_rows = -(-(S_B_UP + n_t) // 8) * 8
    out, d_middle, d_mix, stat, *partial_sums = middle_call(
        mix_own, x, g, vecs, w_ul, w_dl, w_uh, w_dh, w_out, stat_rows, n_d, n_t
    )
    grad_input, g_qkv, g_up, g_down, g_out, table, flat, gain1, grad_cond = back_call(
        d_mix, proj, mix, lse, cos, sin, attn_in, w_qkv.reshape(features, 3 * width), stat,
        x, d_middle, vecs, ada_t, partial_sums, n_d, n_t,
    )
    grad_ada, grad_ada_b, gain1, gain2, b_down, b_up, roots, grad_cond = finish_call(
        table, flat, cond_t, gain1, grad_cond, float(length * n_d * features), n_t
    )
    return (
        out.reshape(block_input.shape), grad_input, grad_cond, grad_ada, grad_ada_b, gain1, g_qkv,
        g_out, gain2, g_up, b_up, g_down.T, b_down, roots[:, 0],
    )


def solution(mesh):
    in_specs = (
        P("tensor", "dp", None),
        P("dp", None),
        P(None, "dp"),
        P("dp"),
        P("dp"),
        P(None, "dp", "tensor"),
        P("tensor", "dp"),
        P("dp"),
        P("dp", "tensor"),
        P("dp"),
        P("tensor", "dp"),
        P("dp"),
        P("tensor", "dp", None),
    )
    out_specs = (
        P("tensor", "dp", None),
        P("tensor", "dp", None),
        P("dp", None),
        P(),
        P(),
        P(),
        P(None, "dp", "tensor"),
        P("tensor", "dp"),
        P(),
        P("dp", "tensor"),
        P(),
        P("tensor", "dp"),
        P(),
        P(),
    )
    return jax.shard_map(shards, mesh=mesh, in_specs=in_specs, out_specs=out_specs, check_vma=False)
```

```python
from functools import partial

import jax
import jax.numpy as jnp
import numpy as np
from jax import lax
from jax.experimental import pallas as pl
from jax.experimental.pallas import tpu as pltpu
from jax.sharding import PartitionSpec as P

HEAD_DIM = 64
EPSILON = 1e-05
CORES = 2
INNER = 2
MESH = pl.DeviceIdType.MESH
VMEM_LIMIT = 58 << 20
GELU_C = float(np.sqrt(2.0 / np.pi))
GELU_A = 0.044715
F32 = jnp.float32
BF16 = jnp.bfloat16
ANY = pl.BlockSpec(memory_space=pl.ANY)
VMEM = pl.BlockSpec(memory_space=pltpu.VMEM)
DMA = pltpu.SemaphoreType.DMA


def dot(lhs, rhs, lhs_dim, rhs_dim):
    return lax.dot_general(
        lhs, rhs, (((lhs_dim,), (rhs_dim,)), ((), ())), preferred_element_type=F32
    )


def params(collective_id=None, **more):
    if collective_id is not None:
        more.update(collective_id=collective_id, has_side_effects=True)
    return pltpu.CompilerParams(vmem_limit_bytes=VMEM_LIMIT, **more)


def cost(flops, moved, special=0):
    return pl.CostEstimate(flops=int(flops), bytes_accessed=int(moved), transcendentals=int(special))


def struct(shape, dtype):
    return jax.ShapeDtypeStruct(shape, dtype)


def mean_rows(values):
    return jnp.mean(values, axis=-1, keepdims=True)


def sum_tokens(values):
    return jnp.sum(values, axis=0, keepdims=True)


GAIN1, SHIFT_A, SCALE_A, GATE_A, GAIN2, SHIFT_M, SCALE_M, GATE_M, B_DOWN, B_UP = range(10)
MOD_ROWS = (SHIFT_A, SCALE_A, GATE_A, SHIFT_M, SCALE_M, GATE_M)
S_GATE_A, S_SHIFT_M, S_SCALE_M, S_GATE_M, S_GAIN2, S_B_DOWN, S_SQ_A, S_SQ_M, S_SQ_R, S_B_UP = range(10)
L_SHIFT_A, L_SCALE_A, L_GAIN1 = range(3)


def order(k, xi, ci, nx):
    return lax.rem(xi + k // CORES, nx) * CORES + lax.rem(ci + k % CORES, CORES)


def mirror(k, nx):
    return (nx - k // CORES) % nx * CORES + (CORES - k % CORES) % CORES


def place(n_d, n_t):
    d, t = lax.axis_index("dp"), lax.axis_index("tensor")
    return d, t, d // INNER, lax.rem(d, INNER), t // CORES, lax.rem(t, CORES)


def greet(n_d, n_t):
    d, t = lax.axis_index("dp"), lax.axis_index("tensor")
    barrier = pltpu.get_barrier_semaphore()
    for r in range(1, n_t):
        pl.semaphore_signal(
            barrier, 1, device_id=(d, lax.rem(t + r, n_t)), device_id_type=MESH
        )
    for r in range(1, n_d):
        pl.semaphore_signal(
            barrier, 1, device_id=(lax.rem(d + r, n_d), t), device_id_type=MESH
        )
    pl.semaphore_wait(barrier, n_t - 1 + n_d - 1)


def remote(src, dst, send, recv, d, t):
    return pltpu.make_async_remote_copy(
        src_ref=src, dst_ref=dst, send_sem=send, recv_sem=recv, device_id=(d, t), device_id_type=MESH
    )


class Places:
    def __init__(self, n_d, n_t):
        d, t = lax.axis_index("dp"), lax.axis_index("tensor")
        self.d, self.t = d, t
        self.me = {"z": d // INNER, "y": lax.rem(d, INNER), "x": t // CORES, "c": lax.rem(t, CORES)}
        self.count = counts(n_d, n_t)

    def peer(self, axis, r):
        at = dict(self.me)
        at[axis] = lax.rem(at[axis] + r, self.count[axis])
        return at[axis], (at["z"] * INNER + at["y"], at["x"] * CORES + at["c"])


def counts(n_d, n_t):
    return {"z": n_d // INNER, "y": INNER, "x": n_t // CORES, "c": CORES}


class Spread:
    def __init__(self, places, dims, known, path, array, source, send, recv, row, lanes=slice(None)):
        self.path, self.flights = path, []
        for s, axis in enumerate(path):
            region = tuple(
                slice(None) if a in known or a in path[:s] else places.me[a] for a in dims
            ) + (slice(None), lanes)
            src = source if s == 0 else array.at[region]
            self.flights.append([])
            for r in range(1, places.count[axis]):
                _, (d, t) = places.peer(axis, r)
                self.flights[s].append(
                    remote(
                        src, array.at[region], send.at[row + s, r - 1], recv.at[row + s, r - 1], d, t
                    )
                )

    def start(self, s):
        for copy in self.flights[s]:
            copy.start()

    def wait(self, s):
        for copy in self.flights[s]:
            copy.wait()

    def advance(self, s, last=None):
        self.wait(s)
        if s + 1 < len(self.path) and s != last:
            self.start(s + 1)


class Reduce:
    def __init__(self, places, dims, path, source, own, met, results, send, recv, local, row):
        self.places, self.path, self.own, self.met = places, path, own, met
        self.results, self.flights, self.dims = results, [], []
        current = source
        for s, axis in enumerate(path):
            at = dims.index(axis)
            self.dims.append((current, dims, at))
            self.flights.append([])
            for r in range(1, places.count[axis]):
                to, (d, t) = places.peer(axis, r)
                self.flights[s].append(
                    remote(
                        current.at[(slice(None),) * at + (to,)], met[s].at[r - 1],
                        send.at[row + s, r - 1], recv.at[row + s, r - 1], d, t,
                    )
                )
            if s == 0:
                self.load = None
                if own is not None:
                    self.load = pltpu.make_async_copy(
                        current.at[(slice(None),) * at + (places.me[axis],)], own, local
                    )
            dims = dims.replace(axis, "")
            current = results[s]

    def start(self, s):
        for copy in self.flights[s]:
            copy.start()
        if s == 0 and self.load is not None:
            self.load.start()

    def advance(self, s):
        places, path = self.places, self.path
        for copy in self.flights[s]:
            copy.wait()
        current, dims, at = self.dims[s]
        rest = dims.replace(path[s], "")
        if s == 0 and self.load is not None:
            self.load.wait()
            current, at = self.own, None
        sizes = [places.count[a] for a in rest]

        def fold(n, carry):
            spot = []
            for size in reversed(sizes):
                spot.insert(0, lax.rem(n, size))
                n = n // size
            own = list(spot)
            if at is not None:
                own.insert(at, places.me[path[s]])
            value = current[tuple(own)].astype(F32)
            for r in range(places.count[path[s]] - 1):
                value += self.met[s][(r,) + tuple(spot)].astype(F32)
            if callable(self.results[s]):
                self.results[s](value)
            else:
                self.results[s][tuple(spot)] = value.astype(BF16)
            return carry

        if sizes:
            lax.fori_loop(0, int(np.prod(sizes)), fold, 0)
        else:
            fold(0, 0)
        if s + 1 < len(path):
            self.start(s + 1)


def reduce_scratch(count, dims, path, tail, own=True, last=True):
    shapes = []
    rest = dims.replace(path[0], "")
    if own:
        shapes.append(tuple(count[a] for a in rest) + tail)
    left = dims
    for axis in path:
        left = left.replace(axis, "")
        shapes.append((count[axis] - 1,) + tuple(count[a] for a in left) + tail)
    left = dims
    for axis in path if not last else path[:-1]:
        left = left.replace(axis, "")
        shapes.append(tuple(count[a] for a in left) + tail)
    return [pltpu.VMEM(shape, BF16) for shape in shapes]


FRONT_PATHS = {"ul": "zyxc", "dl": "xzyc", "o": "xzyc", "uh": "zy", "dh": "zx"}
FRONT_PLAN = {
    "pre": ("s dl",),
    "0": ("s ul",),
    "qz": ("a dl", "a ul",),
    "n": ("s o",),
    "g": ("a o",),
    "p3": ("a dl", "a ul",),
    "a0": ("s uh", "s dh",),
    "a2": ("a o",),
    "a5": ("a dl", "a ul", "a uh", "a dh",),
    "end": ("a o", "a dl", "a ul", "a o", "a uh", "a dh",),
}
BACK_SUMS = (("zy", "zy"), ("zx", "xz"), ("zyx", "xyz"), ("zyx", "yxz"), ("czyx", "czxy"))
CODE = {"z": 2, "y": 2, "x": 2, "c": 2}
EARLY = ((2, S_GATE_A), (3, S_SHIFT_M), (4, S_SCALE_M), (5, S_GATE_M))


def front_kernel(
    n_d, n_t, parts, heads, cond_at, bias_at, sizes,
    x_ref, qkv_ref, gain1_ref, gain2_ref, bdown_ref, bup_ref, cond_in, ada_b_ref,
    ada_ref, up_ref, down_ref, outw_ref, cos_ref, sin_ref,
    in_all, proj_ref, mix_ref, lse_ref, mix_own, vec_ref, cond_ref, w_all, w_ul, w_dl, w_uh, w_dh, w_out,
    x_all, w_pack, wt_ref, out_pack, small_ref, small_all, mod_all, mod_rows, key_ref,
    s_x, r_x, s_c, r_c, s_f, r_f, s_z, r_z, s_y, r_y, s_s, r_s, s_m, r_m, s_l,
    s_w, r_w, s_o, r_o,
):
    d, t, oi, ii, xi, ci = place(n_d, n_t)
    nx, no = n_t // CORES, n_d // INNER
    other = xi * CORES + (1 - ci)
    piece = x_ref.shape[0] // parts
    rows, features = x_ref.shape
    width = qkv_ref.shape[2]
    half = HEAD_DIM // 2
    cut = w_ul.shape[5]
    low_half, high_half = slice(0, cut), slice(cut, 2 * cut)
    for j in range(3):
        w_pack[:, j * width : (j + 1) * width] = qkv_ref[j]
    out_pack[:, :width] = outw_ref[...].T
    small_ref[...] = jnp.zeros_like(small_ref)
    at = 0
    for ref in (gain1_ref, gain2_ref, bdown_ref, bup_ref):
        small_ref[:, at : at + ref.shape[0]] = ref[...].astype(F32).reshape(1, -1)
        at += ref.shape[0]
    small_ref[:, cond_at : cond_at + cond_in.shape[1]] = cond_in[...].astype(F32)
    small_ref[:, bias_at : bias_at + ada_b_ref.shape[0]] = ada_b_ref[...].astype(F32).reshape(1, -1)
    if out_pack.shape[1] > width:
        out_pack[:, width:] = jnp.zeros((out_pack.shape[0], out_pack.shape[1] - width), BF16)
    greet(n_d, n_t)
    places = Places(n_d, n_t)
    flows = {}
    for row, (name, dims, array, source) in enumerate(
        (
            ("ul", "zyxc", w_ul, up_ref.at[:, low_half]),
            ("dl", "zyxc", w_dl, down_ref.at[:, low_half]),
            ("o", "zyxc", w_out, out_pack),
            ("uh", "zy", w_uh, up_ref.at[:, high_half]),
            ("dh", "zx", w_dh, down_ref.at[:, high_half]),
        )
    ):
        flows[name] = Spread(
            places, dims, "", FRONT_PATHS[name], array, source, s_w, r_w, 4 * row
        )
    stage = dict.fromkeys(flows, 0)

    def at_point(point):
        for step in FRONT_PLAN.get(point, ()):
            what, name = step.split()
            if what == "s":
                flows[name].start(0)
            else:
                flows[name].advance(stage[name])
                stage[name] += 1

    s_copies = []
    for r in range(1, n_d):
        copy = remote(
            small_ref, small_all.at[d], s_s.at[r - 1], r_s.at[r - 1], lax.rem(d + r, n_d), t
        )
        copy.start()
        s_copies.append(copy)
    at_point("pre")
    x_copies = []
    for r in range(1, nx):
        peer = lax.rem(xi + r, nx) * CORES + ci
        for p in range(parts):
            at = pl.ds(p * piece, piece)
            copy = remote(
                x_ref.at[at], x_all.at[t, at], s_x.at[r - 1, p], r_x.at[r - 1, p], d, peer
            )
            copy.start()
            x_copies.append((r, p, copy))
    z_copies = []
    for r in range(1, no):
        copy = remote(
            w_pack, w_all.at[d], s_z.at[r - 1], r_z.at[r - 1], lax.rem(oi + r, no) * INNER + ii, t
        )
        copy.start()
        z_copies.append(copy)
    y_copies = []
    for q in range(1, INNER):
        copy = remote(
            w_pack, w_all.at[d], s_y.at[q - 1, 0], r_y.at[q - 1, 0],
            oi * INNER + lax.rem(ii + q, INNER), t,
        )
        copy.start()
        y_copies.append(copy)
    core_copy = remote(x_ref, x_all.at[t], s_c, r_c, d, other)
    core_copy.start()
    local = []
    for n, (src, dst) in enumerate(
        (
            (small_ref, small_all.at[d]),
            (x_ref, x_all.at[t]),
            (w_pack, w_all.at[d]),
            (up_ref.at[:, low_half], w_ul.at[oi, ii, xi, ci]),
            (down_ref.at[:, low_half], w_dl.at[oi, ii, xi, ci]),
            (up_ref.at[:, high_half], w_uh.at[oi, ii]),
            (down_ref.at[:, high_half], w_dh.at[oi, xi]),
            (out_pack, w_out.at[oi, ii, xi, ci]),
        )
    ):
        copy = pltpu.make_async_copy(src, dst, s_l.at[n])
        copy.start()
        local.append(copy)

    at_point("0")

    local[0].wait()
    for copy in s_copies:
        copy.wait()
    cond = small_all[:, 0, cond_at : cond_at + ada_ref.shape[1]]
    for s in range(n_d):
        cond_ref[:, s : s + 1] = cond[s : s + 1].T
    bias = small_ref[:, bias_at : bias_at + ada_ref.shape[0]]
    mod_rows[:, 0, :] = dot(cond.astype(BF16), ada_ref[...], 1, 1) + bias
    own_mod = pltpu.make_async_copy(mod_rows.at[d], mod_all.at[d], s_l.at[8])
    own_mod.start()
    m_copies = []
    for r in range(1, n_d):
        peer = lax.rem(d + r, n_d)
        copy = remote(mod_rows.at[peer], mod_all.at[d], s_m.at[r - 1], r_m.at[r - 1], peer, t)
        copy.start()
        m_copies.append(copy)
    for r in range(1, no):
        z_copies[r - 1].wait()
        origin = lax.rem(oi + no - r, no) * INNER + ii
        for q in range(1, INNER):
            copy = remote(
                w_all.at[origin], w_all.at[origin], s_y.at[q - 1, r], r_y.at[q - 1, r],
                oi * INNER + lax.rem(ii + q, INNER), t,
            )
            copy.start()
            y_copies.append(copy)
    for n in range(3, 8):
        local[n].wait()
    at_point("qz")
    f_copies = []
    for r, p, copy in x_copies:
        copy.wait()
        origin = lax.rem(xi + nx - r, nx) * CORES + ci
        at = pl.ds(p * piece, piece)
        copy = remote(
            x_all.at[origin, at], x_all.at[origin, at],
            s_f.at[r - 1, p], r_f.at[r - 1, p], d, other,
        )
        copy.start()
        f_copies.append(copy)

    at_point("X")
    for copy in m_copies + [own_mod]:
        copy.wait()
    def put(first, piece_of, count):
        for s in range(n_d):
            value = piece_of(s)
            start = s * count
            done = 0
            while done < count:
                row, column = divmod(start + done, features)
                take = min(count - done, features - column)
                vec_ref[first + row : first + row + 1, column : column + take] = value[
                    :, done : done + take
                ]
                done += take

    vec_ref[...] = jnp.zeros_like(vec_ref)
    at = 0
    for first, count in sizes:
        put(first, lambda s: small_all[s, :, at : at + count], count)
        at += count
    columns = ada_ref.shape[0]
    for s in range(n_d):
        done = 0
        while done < columns:
            row, column = divmod(s * columns + done, features)
            take = min(columns - done, features - column)
            row = MOD_ROWS[row]
            vec_ref[row : row + 1, column : column + take] = mod_all[s, :, done : done + take]
            done += take

    for copy in f_copies + [local[1], core_copy]:
        copy.wait()

    def norm(b, carry):
        x = x_all[b].astype(F32)
        centred = x - mean_rows(x)
        normed = centred * lax.rsqrt(mean_rows(centred * centred) + EPSILON)
        normed = normed * vec_ref[GAIN1 : GAIN1 + 1]
        low = (normed * (1.0 + vec_ref[SCALE_A : SCALE_A + 1]) + vec_ref[SHIFT_A : SHIFT_A + 1])
        in_all[b] = low.astype(BF16)
        return carry

    lax.fori_loop(0, n_t, norm, 0)
    at_point("n")
    for copy in y_copies + [local[2]]:
        copy.wait()
    wt_ref[...] = w_all[...].reshape(features, 3 * width).T

    at_point("g")

    def project(b, carry):
        proj = dot(wt_ref[...], in_all[b], 1, 1)
        lanes = pl.ds(pl.multiple_of(b * rows, rows), rows)
        cos, sin = cos_ref[:, lanes], sin_ref[:, lanes]
        for j in range(2):
            factor = HEAD_DIM**-0.5 if j == 0 else 1.0
            for h in range(heads):
                at = j * width + h * HEAD_DIM
                first, last = proj[at : at + half], proj[at + half : at + HEAD_DIM]
                top = ((first * cos - last * sin) * factor).astype(BF16)
                bottom = ((last * cos + first * sin) * factor).astype(BF16)
                proj_ref[b, at : at + half] = top
                proj_ref[b, at + half : at + HEAD_DIM] = bottom
                if j == 1:
                    key_ref[h, lanes, :] = jnp.concatenate([top, bottom], axis=0).T
        proj_ref[b, 2 * width :] = proj[2 * width :].astype(BF16)

        for m in range(n_t):
            if f"p{m}" in FRONT_PLAN:
                @pl.when(b == m)
                def _(m=m):
                    at_point(f"p{m}")

        return carry

    lax.fori_loop(0, n_t, project, 0)

    def attend(u, carry):
        plane = lax.rem(xi + nx - 1 - u // heads, nx)
        h = lax.rem(u, heads)
        at = pl.ds(pl.multiple_of(h * HEAD_DIM, HEAD_DIM), HEAD_DIM)
        value_at = pl.ds(pl.multiple_of(2 * width + h * HEAD_DIM, HEAD_DIM), HEAD_DIM)
        first = plane * CORES
        query = jnp.concatenate([proj_ref[first + c, at] for c in range(CORES)], axis=1)
        scores = dot(key_ref[h], query, 1, 0)
        top = jnp.max(scores, axis=0, keepdims=True)
        grown = jnp.exp(scores - top)
        total = jnp.sum(grown, axis=0, keepdims=True)
        value = jnp.concatenate([proj_ref[v, value_at] for v in range(n_t)], axis=1)
        mixed = (dot(value, grown.astype(BF16), 1, 0) / total).astype(BF16)
        log_total = top + jnp.log(total)
        for c in range(CORES):
            part = slice(c * rows, (c + 1) * rows)
            mix_ref[first + c, at] = mixed[:, part]
            lse_ref[first + c, pl.ds(h, 1)] = log_total[:, part]
        for r in range(nx):
            @pl.when(u == (nx - r) * heads - 1)
            def _(r=r):
                for c in range(CORES):
                    if r * CORES + c > 0:
                        o_copies[r * CORES + c].start()

        for m in range(nx * heads):
            if f"a{m}" in FRONT_PLAN:
                @pl.when(u == m)
                def _(m=m):
                    at_point(f"a{m}")

        return carry

    o_copies = {}
    for m in range(1, n_t):
        b = order(m, xi, ci, nx)
        o_copies[m] = remote(
            mix_ref.at[b], mix_own.at[t], s_o.at[m - 1], r_o.at[mirror(m, nx) - 1], d, b
        )
    lax.fori_loop(0, nx * heads, attend, 0)
    mine = pltpu.make_async_copy(mix_ref.at[t], mix_own.at[t], s_l.at[9])
    mine.start()
    at_point("end")
    for name, flow in flows.items():
        assert stage[name] == len(flow.path), name
    mine.wait()
    for copy in list(o_copies.values()):
        copy.wait()


def front_call(x, qkv, smalls, ada_t, up, down_t, outw, cos, sin, n_d, n_t):
    cond, ada_b = smalls[4:]
    sizes = tuple(zip((GAIN1, GAIN2, B_DOWN, B_UP), (a.shape[0] for a in smalls[:4])))
    cond_at = -(-sum(size for _, size in sizes) // 128) * 128
    bias_at = cond_at + cond.shape[1]
    small = bias_at + ada_b.shape[0]
    parts = 4
    nx, no = n_t // CORES, n_d // INNER
    rows, features = x.shape
    part, width = qkv.shape[1:]
    heads = width // HEAD_DIM
    length = rows * n_t
    wide = -(-width // 128) * 128
    units = up.shape[1]
    steps = max(no, INNER, nx) - 1
    cut = units // 2
    grid_of = (no, INNER, nx, CORES, part)
    columns = ada_t.shape[0]
    return pl.pallas_call(
        partial(front_kernel, n_d, n_t, parts, heads, cond_at, bias_at, sizes),
        name="front",
        out_shape=[
            struct((n_t, rows, features), BF16),
            struct((n_t, 3 * width, rows), BF16),
            struct((n_t, width, rows), BF16),
            struct((n_t, heads, rows), F32),
            struct((n_t, width, rows), BF16),
            struct((16, features), F32),
            struct((ada_t.shape[1], n_d), F32),
            struct((n_d, part, 3 * width), BF16),
            struct(grid_of + (cut,), BF16),
            struct(grid_of + (cut,), BF16),
            struct((no, INNER, part, cut), BF16),
            struct((no, nx, part, cut), BF16),
            struct(grid_of + (wide,), BF16),
        ],
        in_specs=[VMEM] * 9 + [ANY] * 2 + [VMEM] * 3,
        out_specs=[VMEM] * 8 + [ANY] * 5,
        scratch_shapes=[
            pltpu.VMEM((n_t, rows, features), BF16),
            pltpu.VMEM((part, 3 * width), BF16),
            pltpu.VMEM((3 * width, features), BF16),
            pltpu.VMEM((part, wide), BF16),
            pltpu.VMEM((1, small), F32),
            pltpu.VMEM((n_d, 1, small), F32),
            pltpu.VMEM((n_d, 1, columns), F32),
            pltpu.VMEM((n_d, 1, columns), F32),
            pltpu.VMEM((heads, length, HEAD_DIM), BF16),
            DMA((nx - 1, parts)), DMA((nx - 1, parts)), DMA, DMA,
            DMA((nx - 1, parts)), DMA((nx - 1, parts)),
            DMA((no - 1,)), DMA((no - 1,)),
            DMA((INNER - 1, no)), DMA((INNER - 1, no)),
            DMA((n_d - 1,)), DMA((n_d - 1,)), DMA((n_d - 1,)), DMA((n_d - 1,)),
            DMA((10,)),
            DMA((20, steps)), DMA((20, steps)),
            DMA((n_t - 1,)), DMA((n_t - 1,)),
        ],
        compiler_params=params(0),
        cost_estimate=cost(20 * heads * length * length * HEAD_DIM, 40e6, heads * length * length),
    )(x, qkv, *smalls, ada_t, up, down_t, outw, cos, sin)


def middle_kernel(
    n_d, n_t,
    mix_ref, x_ref, g_ref, vec_ref, ul_ref, dl_ref, uh_ref, dh_ref, wout_ref,
    out_ref, dmid_ref, dmix_ref, stat_ref, hul_ref, hdl_ref, huh_ref, hdh_ref, gout_ref,
    up_buf, down_buf, o_buf, go_buf,
    attn_ref, low_ref, lowt_ref, dl_t_ref, dlt_ref, acc_out, acc_in,
    mul_c, rul, mul_x, mdl_c, mdl_y, rdl, muh, mdh,
    s_u, s_d, s_o, s_w, r_w, s_r, r_r,
):
    places = Places(n_d, n_t)
    count, me = places.count, places.me
    rows, features = x_ref.shape
    width = mix_ref.shape[1]
    cut = up_buf.shape[-1]
    wide = wout_ref.shape[-1]
    loads = [
        pltpu.make_async_copy(wout_ref, o_buf, s_o.at[0]),
        pltpu.make_async_copy(ul_ref, up_buf.at[0], s_u.at[0]),
        pltpu.make_async_copy(dl_ref, down_buf.at[0], s_d.at[0]),
        pltpu.make_async_copy(uh_ref, up_buf.at[1, :, :, me["x"], me["c"]], s_u.at[1]),
        pltpu.make_async_copy(dh_ref, down_buf.at[1, :, me["y"], :, me["c"]], s_d.at[1]),
    ]
    for copy in loads:
        copy.start()
    greet(n_d, n_t)
    nx = count["x"]
    every, mx, my, mc = slice(None), me["x"], me["y"], me["c"]
    taken = [0]

    def send(target, region, axis, r, source=None):
        at = target.at[(1,) + region]
        n = taken[0]
        taken[0] += 1
        return remote(
            at if source is None else source, at, s_w.at[n], r_w.at[n], *places.peer(axis, r)[1]
        )

    own_up = [send(up_buf, (every, every, mx, mc), "c", 1, uh_ref)]
    own_down = [send(down_buf, (every, my, every, mc), "c", 1, dh_ref)]
    near_down, far_down, near_on, far_on, far_up = [], [], [], [], []
    for r in range(1, INNER):
        near_down.append(send(down_buf, (every, my, mx, mc), "y", r, dh_ref.at[:, mx]))
        near_on.append(send(down_buf, (every, places.peer("y", r)[0], mx, mc), "c", 1))
    for r in range(1, nx):
        far_up.append(send(up_buf, (every, every, mx, mc), "x", r, uh_ref))
        far_on.append(send(up_buf, (every, every, places.peer("x", r)[0], mc), "c", 1))
    for r in range(1, INNER):
        for q in range(1, nx):
            x_at = places.peer("x", q)[0]
            far_down.append(send(down_buf, (every, my, x_at, mc), "y", r, dh_ref.at[:, x_at]))
            far_on.append(
                send(down_buf, (every, places.peer("y", r)[0], x_at, mc), "c", 1)
            )
    for copy in near_down + far_up + own_up + own_down + far_down:
        copy.start()
    planes = [lax.rem(me["x"] + nx - 1 - n, nx) for n in range(nx)]
    ul = [
        Reduce(
            places, "zyc", "c", up_buf.at[2, :, :, planes[n]], None, [mul_c.at[n]], [rul.at[n]],
            s_r, r_r, None, n,
        )
        for n in range(nx)
    ]
    ul_x = [
        remote(
            rul.at[nx - 1 - r], mul_x.at[r - 1], s_r.at[4 * nx + 3, r - 1], r_r.at[4 * nx + 3, r - 1],
            *places.peer("x", r)[1],
        )
        for r in range(1, nx)
    ]
    dl = [
        Reduce(
            places, "zyc", "c", down_buf.at[2, :, :, planes[n]], None, [mdl_c.at[n]],
            [rdl.at[:, :, planes[n]]], s_r, r_r, None, nx + n,
        )
        for n in range(nx)
    ]
    dl_y = [
        Reduce(
            places, "zy", "y", rdl.at[:, :, planes[n]], None, [mdl_y.at[n]],
            [rdl.at[:, my, planes[n]]], s_r, r_r, None, 3 * nx + 3 + n,
        )
        for n in range(nx)
    ]
    high_up, high_down = up_buf.at[0, :, :, :, me["c"]], down_buf.at[0, :, :, :, me["c"]]
    uh = Reduce(places, "zyxc", "c", up_buf.at[0], None, [muh], [high_up], s_r, r_r, None, 2 * nx + 1)
    dh = Reduce(
        places, "zyxc", "c", down_buf.at[0], None, [mdh], [high_down], s_r, r_r, None, 2 * nx + 2
    )
    keeps = [
        pltpu.make_async_copy(go_buf, gout_ref, s_o.at[1]),
        pltpu.make_async_copy(high_up, huh_ref, s_o.at[2]),
        pltpu.make_async_copy(high_down, hdh_ref, s_o.at[3]),
        pltpu.make_async_copy(rul.at[nx - 1], hul_ref, s_o.at[4]),
        pltpu.make_async_copy(rdl.at[:, me["y"]], hdl_ref, s_o.at[5]),
    ]
    vec = lambda row: vec_ref[row : row + 1]
    cot = g_ref[...].astype(F32)
    d_mlp = (vec(GATE_M) * cot).astype(BF16)
    dl_t_ref[...] = d_mlp
    dlt_ref[...] = d_mlp.T
    stat_ref[...] = jnp.zeros_like(stat_ref)
    stat_ref[S_B_DOWN : S_B_DOWN + 1] = sum_tokens(d_mlp.astype(F32))
    if wide > width:
        go_buf[...] = jnp.zeros_like(go_buf)
    loads[0].wait()
    w_out = lambda b: o_buf[:, :, b // CORES, b % CORES].reshape(features, wide)[:, :width]
    attn_out = jnp.zeros((rows, features), F32)
    for b in range(n_t):
        attn_out += dot(mix_ref[b].T, w_out(b), 1, 1)
    attn_ref[...] = attn_out
    branch = vec(GATE_A) * attn_out
    stat_ref[S_SQ_A : S_SQ_A + 1] = sum_tokens(branch * branch)
    middle = x_ref[...].astype(F32) + branch
    dmid_ref[...] = middle
    centred = middle - mean_rows(middle)
    inv = lax.rsqrt(mean_rows(centred * centred) + EPSILON)
    low = (centred * inv * vec(GAIN2) * (1.0 + vec(SCALE_M)) + vec(SHIFT_M)).astype(BF16)
    low_ref[...] = low
    lowt_ref[...] = low.T
    acc_out[...] = jnp.zeros_like(acc_out)
    acc_in[...] = jnp.zeros_like(acc_in)
    loads[1].wait()
    loads[2].wait()

    def block(n, carry):
        j = n // nx
        step = lax.rem(n, nx)
        p = lax.rem(mx + (1 - j) * (nx - 1 - step) + j * step, nx)
        slot = 2 - 2 * j
        lanes = pl.ds(pl.multiple_of(j * cut, cut), cut)

        @pl.when(n == nx)
        def _():
            for copy in loads[3:] + own_up + own_down + near_on:
                copy.wait()

        @pl.when(n == nx + 1)
        def _():
            for copy in far_on:
                copy.wait()

        both = lambda buf: jnp.concatenate(
            [buf[j, :, :, p, c].reshape(features, cut) for c in range(CORES)], axis=1
        )
        up, down = both(up_buf), both(down_buf)
        bias = jnp.concatenate(
            [vec_ref[pl.ds(B_UP + p * CORES + c, 1), lanes] for c in range(CORES)], axis=1
        )
        hidden = dot(low_ref[...], up, 1, 0) + bias
        square = hidden * hidden
        bent = jnp.tanh(GELU_C * hidden * (1.0 + GELU_A * square))
        half = 0.5 * (1.0 + bent)
        active = (hidden * half).astype(BF16)
        slope = half + (0.5 * GELU_C) * hidden * (1.0 - bent * bent) * (
            1.0 + (3.0 * GELU_A) * square
        )
        acc_out[...] += dot(active, down, 1, 1)
        for m in range(1, nx):
            @pl.when(n == m)
            def _(m=m):
                ul[m - 1].advance(0)
                ul_x[nx - 1 - m].start()
                dl[m - 1].advance(0)
                dl_y[m - 1].start(0)

        @pl.when(n == nx)
        def _():
            ul[nx - 1].advance(0)
            dl[nx - 1].advance(0)
            dl_y[nx - 1].start(0)
            for copy in far_up + far_down:
                copy.wait()
            for copy in far_on:
                copy.start()

        grad_down = dot(dlt_ref[...], active, 1, 0).astype(BF16)
        d_hidden = (dot(dl_t_ref[...], down, 1, 0) * slope).astype(BF16)
        sums = sum_tokens(d_hidden.astype(F32))
        for c in range(CORES):
            stat_ref[pl.ds(S_B_UP + p * CORES + c, 1), lanes] = sums[:, c * cut : (c + 1) * cut]
        grad_up = dot(lowt_ref[...], d_hidden, 1, 0).astype(BF16)
        acc_in[...] += dot(d_hidden, up, 1, 1)
        for c in range(CORES):
            lanes_of = slice(c * cut, (c + 1) * cut)
            shape = up_buf.shape[1:3] + (-1, cut)
            down_buf[slot, :, :, p, c] = grad_down[:, lanes_of].reshape(shape)
            up_buf[slot, :, :, p, c] = grad_up[:, lanes_of].reshape(shape)

        for m in range(nx):
            @pl.when(n == m)
            def _(m=m):
                ul[m].start(0)
                dl[m].start(0)
                if m == 0:
                    for copy in near_down:
                        copy.wait()
                    for copy in near_on:
                        copy.start()

        return carry

    lax.fori_loop(0, 2 * nx, block, 0)
    uh.start(0)
    dh.start(0)
    middle = dmid_ref[...]
    mlp_out = acc_out[...] + vec(B_DOWN)
    mlp_branch = vec(GATE_M) * mlp_out
    result = middle + mlp_branch
    out_ref[...] = result.astype(BF16)
    cot = g_ref[...].astype(F32)
    stat_ref[S_SQ_M : S_SQ_M + 1] = sum_tokens(mlp_branch * mlp_branch)
    stat_ref[S_SQ_R : S_SQ_R + 1] = sum_tokens(result * result)
    stat_ref[S_GATE_M : S_GATE_M + 1] = sum_tokens(cot * mlp_out)
    e = acc_in[...]
    centred = middle - mean_rows(middle)
    inv = lax.rsqrt(mean_rows(centred * centred) + EPSILON)
    nhat = centred * inv
    gain, scale = vec(GAIN2), 1.0 + vec(SCALE_M)
    by_nhat = sum_tokens(e * nhat)
    stat_ref[S_SHIFT_M : S_SHIFT_M + 1] = sum_tokens(e)
    stat_ref[S_SCALE_M : S_SCALE_M + 1] = by_nhat * gain
    stat_ref[S_GAIN2 : S_GAIN2 + 1] = by_nhat * scale
    dn = e * (scale * gain)
    d_middle = cot + inv * (dn - mean_rows(dn) - nhat * mean_rows(dn * nhat))
    dmid_ref[...] = d_middle
    stat_ref[S_GATE_A : S_GATE_A + 1] = sum_tokens(d_middle * attn_ref[...])
    d_attn = (vec(GATE_A) * d_middle).astype(BF16)
    d_attn_t = d_attn.T
    for b in range(n_t):
        dmix_ref[b] = dot(d_attn, w_out(b), 1, 0).astype(BF16).T
        go_buf[b % CORES, :, :, b // CORES, :, :width] = (
            dot(d_attn_t, mix_ref[b], 1, 1).astype(BF16).reshape(go_buf.shape[1:3] + (-1, width))
        )
    keeps[0].start()
    uh.advance(0)
    keeps[1].start()
    dh.advance(0)
    keeps[2].start()
    for one in ul_x:
        one.wait()
    no = count["z"]

    def fold(n, carry):
        at = (n // INNER, lax.rem(n, INNER))
        value = rul[(nx - 1,) + at].astype(F32)
        for r in range(nx - 1):
            value += mul_x[(r,) + at].astype(F32)
        rul[(nx - 1,) + at] = value.astype(BF16)
        return carry

    lax.fori_loop(0, no * INNER, fold, 0)
    keeps[3].start()
    for one in dl_y:
        one.advance(0)
    keeps[4].start()
    for copy in keeps:
        copy.wait()


def middle_call(mix, x, g, vecs, w_ul, w_dl, w_uh, w_dh, w_out, stat_rows, n_d, n_t):
    rows, features = x.shape
    cut = w_ul.shape[-1]
    part, wide = w_out.shape[-2:]
    width = mix.shape[1]
    count = counts(n_d, n_t)
    no, nx = count["z"], count["x"]
    per = (3,) + w_ul.shape
    plane = (no, INNER, part, cut)
    tail = (part, cut)
    g_out = (CORES, no, INNER, nx, part, wide)
    return pl.pallas_call(
        partial(middle_kernel, n_d, n_t),
        name="middle",
        out_shape=[
            struct((rows, features), BF16),
            struct((rows, features), F32),
            struct((n_t, width, rows), BF16),
            struct((stat_rows, features), F32),
            struct((no, INNER) + tail, BF16),
            struct((no, nx) + tail, BF16),
            struct((no, INNER, nx) + tail, BF16),
            struct((no, INNER, nx) + tail, BF16),
            struct(g_out, BF16),
        ],
        in_specs=[VMEM] * 4 + [ANY] * 5,
        out_specs=[VMEM] * 4 + [ANY] * 5,
        scratch_shapes=[
            pltpu.VMEM(per, BF16), pltpu.VMEM(per, BF16), pltpu.VMEM(w_out.shape, BF16),
            pltpu.VMEM(g_out, BF16),
            pltpu.VMEM((rows, features), F32),
            pltpu.VMEM((rows, features), BF16),
            pltpu.VMEM((features, rows), BF16),
            pltpu.VMEM((rows, features), BF16),
            pltpu.VMEM((features, rows), BF16),
            pltpu.VMEM((rows, features), F32),
            pltpu.VMEM((rows, features), F32),
        ]
        + [
            pltpu.VMEM((nx, 1) + plane, BF16), pltpu.VMEM((nx,) + plane, BF16),
            pltpu.VMEM((nx - 1,) + plane, BF16),
            pltpu.VMEM((nx, 1) + plane, BF16), pltpu.VMEM((nx, INNER - 1, no) + tail, BF16),
            pltpu.VMEM((no, INNER, nx) + tail, BF16),
            pltpu.VMEM((1, no, INNER, nx) + tail, BF16),
            pltpu.VMEM((1, no, INNER, nx) + tail, BF16),
        ]
        + [
            DMA((2,)), DMA((2,)), DMA((6,)),
            DMA((2 + 2 * (INNER - 1 + nx - 1 + (INNER - 1) * (nx - 1)),)),
            DMA((2 + 2 * (INNER - 1 + nx - 1 + (INNER - 1) * (nx - 1)),)),
            DMA((4 * nx + 4, max(nx, INNER, CORES) - 1)), DMA((4 * nx + 4, max(nx, INNER, CORES) - 1)),
        ],
        compiler_params=params(1),
        cost_estimate=cost(2 * rows * features * features * (6 * n_t + 4), 30e6),
    )(mix, x, g, vecs, w_ul, w_dl, w_uh, w_dh, w_out)


def back_kernel(
    n_d, n_t, parts, heads,
    dmix_ref, proj_ref, mix_ref, lse_ref, cos_ref, sin_ref, in_hbm, wq_hbm, stat_ref,
    x_hbm, dmid_hbm, vec_ref, ada_ref,
    hul_ref, hdl_ref, huh_ref, hdh_ref, gout_ref,
    grad_in_ref, gq_ref, up_ref, down_ref, out_ref, table_ref, flat_ref, gain_ref, gcond_ref,
    dmix_all, key_ref, keyt_ref, val_ref, dkey_ref, dval_ref, dquery_ref, dproj_ref, in_ref, wq_ref,
    acc_ref, grad_ref, rc, rx, ry, sz, rz, got_ref, mine_ref,
    x_ref, dmid_ref, late_ref, late_got, late_mine, late_all, rows_out, rows_in, *more,
):
    buffers, at = [], 0
    for size in (len(reduce_scratch(CODE, dims, path, (1, 1))) for dims, path in BACK_SUMS):
        buffers.append(more[at : at + size])
        at += size
    (
        s_a, r_a, s_l, s_g, r_g, s_t, r_t, s_d, r_d, s_c, r_c, s_x, r_x, s_y, r_y, s_z, r_z,
        s_v, r_v, s_e, r_e, s_p, r_p,
    ) = more[at:]
    places = Places(n_d, n_t)
    d, t, oi, ii, xi, ci = place(n_d, n_t)
    nx, no = n_t // CORES, n_d // INNER
    other = xi * CORES + (1 - ci)
    blocks, total, rows = proj_ref.shape
    width = total // 3
    half = HEAD_DIM // 2
    features = x_ref.shape[1]
    assert nx == 2 and CORES == 2

    cut = hul_ref.shape[-1]

    def put(target, lanes):
        def store(value):
            target[:, lanes] = value
        return store

    def put_out(value):
        out_ref[...] = value.T[:width]

    sinks = (
        put(up_ref, slice(0, cut)), put(down_ref, slice(0, cut)),
        put(up_ref, slice(cut, 2 * cut)), put(down_ref, slice(cut, 2 * cut)), put_out,
    )
    sums = []
    row = 0
    for n, ((dims, path), source) in enumerate(
        zip(BACK_SUMS, (hul_ref, hdl_ref, huh_ref, hdh_ref, gout_ref))
    ):
        steps = len(path)
        sums.append(
            Reduce(
                places, dims, path, source, buffers[n][0], buffers[n][1 : 1 + steps],
                list(buffers[n][1 + steps :]) + [sinks[n]], s_g, r_g, s_l.at[6 + n], row,
            )
        )
        row += steps
    ul, dl, uh, dh, go = sums

    greet(n_d, n_t)
    a_copies = {}
    for m in range(1, n_t):
        b = order(m, xi, ci, nx)
        a_copies[mirror(m, nx)] = remote(
            dmix_ref.at[b], dmix_all.at[t], s_a.at[m - 1], r_a.at[mirror(m, nx) - 1], d, b
        )
    for m in range(n_t - 1, 0, -1):
        a_copies[mirror(m, nx)].start()
    for one in (dh, go):
        one.start(0)
    loads = [
        pltpu.make_async_copy(dmix_ref.at[t], dmix_all.at[t], s_l.at[0]),
        pltpu.make_async_copy(in_hbm, in_ref, s_l.at[1]),
        pltpu.make_async_copy(wq_hbm, wq_ref, s_l.at[2]),
        pltpu.make_async_copy(x_hbm, x_ref, s_l.at[3]),
        pltpu.make_async_copy(dmid_hbm, dmid_ref, s_l.at[4]),
    ]
    for copy in loads:
        copy.start()
    t_copies = []
    for r in range(1, n_t):
        copy = remote(
            stat_ref, got_ref.at[r - 1], s_t.at[r - 1], r_t.at[r - 1], d, lax.rem(t + r, n_t)
        )
        copy.start()
        t_copies.append(copy)
    d_copies = [pltpu.make_async_copy(mine_ref, table_ref.at[d], s_l.at[5])]
    for r in range(1, n_d):
        d_copies.append(
            remote(mine_ref, table_ref.at[d], s_d.at[r - 1], r_d.at[r - 1], lax.rem(d + r, n_d), t)
        )

    def share_statistics():
        for copy in t_copies:
            copy.wait()
        value = stat_ref[...]
        for r in range(1, n_t):
            value += got_ref[r - 1]
        mine_ref[...] = value
        for copy in d_copies:
            copy.start()

    dkey_ref[...] = jnp.zeros_like(dkey_ref)
    dval_ref[...] = jnp.zeros_like(dval_ref)

    def turn(b, carry):
        lanes = pl.ds(pl.multiple_of(b * rows, rows), rows)
        keyt_ref[:, lanes] = proj_ref[b, width : 2 * width]
        for h in range(heads):
            at = h * HEAD_DIM
            key_ref[h, lanes] = proj_ref[b, width + at : width + at + HEAD_DIM].T
            val_ref[h, lanes] = proj_ref[b, 2 * width + at : 2 * width + at + HEAD_DIM].T
        return carry

    lax.fori_loop(0, blocks, turn, 0)
    loads[0].wait()

    loads[1].wait()
    loads[2].wait()
    dquery_ref[...] = jnp.zeros_like(dquery_ref)
    acc_ref[...] = jnp.zeros_like(acc_ref)
    part_ref = in_ref
    piece = rows // parts
    c_copies = {}
    for r in range(nx):
        block = lax.rem(xi + r, nx) * CORES + 1 - ci
        for p in range(parts):
            at = pl.ds(p * piece, piece)
            c_copies[r, p] = remote(
                part_ref.at[block, at], rc.at[r, at], s_c.at[r, p], r_c.at[r, p], d, other
            )
    x_copies = {}
    for p in range(parts):
        at = pl.ds(p * piece, piece)
        x_copies[p] = remote(
            part_ref.at[lax.rem(xi + 1, nx) * CORES + ci, at], rx.at[0, at],
            s_x.at[0, p], r_x.at[0, p], d, lax.rem(xi + 1, nx) * CORES + ci,
        )

    def unrotate(b, at, factor, first, last):
        lanes = pl.ds(pl.multiple_of(b * rows, rows), rows)
        cos, sin = cos_ref[:, lanes], sin_ref[:, lanes]
        dproj_ref[b, at : at + half] = ((first * cos + last * sin) * factor).astype(BF16)
        dproj_ref[b, at + half : at + HEAD_DIM] = ((last * cos - first * sin) * factor).astype(BF16)

    def close(b):
        lanes = pl.ds(pl.multiple_of(b * rows, rows), rows)
        for h in range(heads):
            at = h * HEAD_DIM
            d_query = dquery_ref[b, at : at + HEAD_DIM]
            unrotate(b, at, HEAD_DIM**-0.5, d_query[:half], d_query[half:])
            d_key = dkey_ref[h, lanes].T
            unrotate(b, width + at, 1.0, d_key[:half], d_key[half:])
            dproj_ref[b, 2 * width + at : 2 * width + at + HEAD_DIM] = (
                dval_ref[h, lanes].T.astype(BF16)
            )
        d_proj = dproj_ref[b]
        acc_ref[...] += dot(d_proj, in_ref[b], 1, 0)
        part_ref[b] = dot(d_proj.T, wq_ref[...], 1, 1).astype(BF16)

    def attend(n, carry):
        for m, at_step in ((1, 1), (2, 2), (3, 4)):
            @pl.when(n == at_step)
            def _(m=m):
                a_copies[m].wait()
        late_part, last_part = (n + 6) // 8, (n + 2) // 8
        q_other = late_part - last_part
        k_other = (1 - late_part) + q_other * lax.rem(n + 1, 2)
        offset = (1 - late_part) * n + q_other * (n // 2 - 1) + last_part * (n - 6)
        i = lax.rem(xi + q_other, nx) * CORES + lax.rem(ci + offset, CORES)
        span = CORES * rows
        keys = pl.ds(pl.multiple_of(lax.rem(xi + k_other, nx) * span, span), span)
        for h in range(heads):
            at = h * HEAD_DIM
            query_t = proj_ref[i, at : at + HEAD_DIM]
            dmix_t = dmix_all[i, at : at + HEAD_DIM]
            mix_t = mix_ref[i, at : at + HEAD_DIM]
            inner = jnp.sum(dmix_t.astype(F32) * mix_t.astype(F32), axis=0, keepdims=True)
            probs = jnp.exp(dot(key_ref[h, keys], query_t, 1, 0) - lse_ref[i, h : h + 1])
            d_probs = dot(val_ref[h, keys], dmix_t, 1, 0)
            d_scores = (probs * (d_probs - inner)).astype(BF16)
            dval_ref[h, keys] += dot(probs.astype(BF16), dmix_t.T, 1, 0)
            dkey_ref[h, keys] += dot(d_scores, query_t.T, 1, 0)
            dquery_ref[i, at : at + HEAD_DIM] += dot(keyt_ref[at : at + HEAD_DIM, keys], d_scores, 1, 0)

        @pl.when(n == 0)
        def _():
            go.advance(0)

        @pl.when(n == 1)
        def _():
            for one in (uh, dl, ul):
                one.start(0)
            share_statistics()

        @pl.when(n == 2)
        def _():
            dh.advance(0)

        @pl.when(n == 5)
        def _():
            dl.advance(0)

        @pl.when((n == 5) | (n == 7))
        def _():
            plane = lax.rem(xi + 1 - last_part, nx)

            def one(c, carry):
                close(plane * CORES + c)
                return carry

            lax.fori_loop(0, CORES, one, 0)

        @pl.when(n == 5)
        def _():
            for p in range(parts):
                c_copies[1, p].start()

        @pl.when(n == 6)
        def _():
            to = lax.rem(xi + 1, nx) * CORES + ci
            for p in range(parts):
                at = pl.ds(p * piece, piece)
                c_copies[1, p].wait()
                part_ref[to, at] = (part_ref[to, at].astype(F32) + rc[1, at].astype(F32)).astype(BF16)
                x_copies[p].start()
            dh.advance(1)
            go.advance(1)
            ul.advance(0)
            uh.advance(0)

        return carry

    lax.fori_loop(0, 2 * n_t, attend, 0)
    for p in range(parts):
        c_copies[0, p].start()
    grad_ref[...] = acc_ref[...].T.astype(BF16).reshape(grad_ref.shape)
    y_copies = []
    for q in range(1, INNER):
        to = lax.rem(ii + q, INNER)
        copy = remote(
            grad_ref.at[:, to], ry.at[q - 1], s_y.at[q - 1], r_y.at[q - 1], oi * INNER + to, t
        )
        copy.start()
        y_copies.append(copy)
    ul.advance(1)
    dl.advance(1)
    dh.advance(2)
    uh.advance(1)
    for copy in d_copies:
        copy.wait()
    loads[3].wait()
    loads[4].wait()
    for copy in y_copies:
        copy.wait()
    z_copies = []
    for r in range(1, no):
        to = lax.rem(oi + r, no)
        value = grad_ref[to, ii].astype(F32)
        for q in range(1, INNER):
            value += ry[q - 1, to].astype(F32)
        sz[r - 1] = value.astype(BF16)
        copy = remote(sz.at[r - 1], rz.at[r - 1], s_z.at[r - 1], r_z.at[r - 1], to * INNER + ii, t)
        copy.start()
        z_copies.append(copy)
    go.advance(2)

    gain, scale = vec_ref[GAIN1 : GAIN1 + 1], 1.0 + vec_ref[SCALE_A : SCALE_A + 1]
    shift_sum = jnp.zeros((1, features), F32)
    nhat_sum = jnp.zeros((1, features), F32)
    for p in range(parts):
        c_copies[0, p].wait()
        x_copies[p].wait()
        at = pl.ds(p * (rows // parts), rows // parts)
        e = part_ref[t, at].astype(F32) + rc[0, at].astype(F32)
        for r in range(1, nx):
            e += rx[r - 1, at].astype(F32)
        x = x_ref[at].astype(F32)
        centred = x - mean_rows(x)
        inv = lax.rsqrt(mean_rows(centred * centred) + EPSILON)
        nhat = centred * inv
        shift_sum += sum_tokens(e)
        nhat_sum += sum_tokens(e * nhat)
        dn = e * (scale * gain)
        grad_in_ref[at] = dmid_ref[at] + inv * (
            dn - mean_rows(dn) - nhat * mean_rows(dn * nhat)
        )
    late_ref[:, :features] = shift_sum
    late_ref[:, features : 2 * features] = nhat_sum * gain
    late_ref[:, 2 * features :] = nhat_sum * scale

    copies = []
    for r in range(1, n_t):
        copy = remote(
            late_ref, late_got.at[r - 1], s_v.at[r - 1], r_v.at[r - 1], d, lax.rem(t + r, n_t)
        )
        copy.start()
        copies.append(copy)
    value = late_ref[...]
    for r in range(1, n_t):
        copies[r - 1].wait()
        value += late_got[r - 1]
    late_mine[...] = value
    copies = [pltpu.make_async_copy(late_mine, late_all.at[d], s_l.at[0])]
    for r in range(1, n_d):
        copies.append(
            remote(
                late_mine, late_all.at[d], s_e.at[r - 1], r_e.at[r - 1], lax.rem(d + r, n_d), t
            )
        )
    for copy in copies:
        copy.start()
    go.advance(3)
    for s in range(n_d):
        for block, row in EARLY:
            flat_ref[s : s + 1, block * features : (block + 1) * features] = table_ref[
                s, row : row + 1
            ]
    for copy in copies:
        copy.wait()
    value = late_all[0, :, 2 * features :]
    for s in range(1, n_d):
        value += late_all[s, :, 2 * features :]
    gain_ref[...] = value
    for s in range(n_d):
        flat_ref[s : s + 1, : 2 * features] = late_all[s, :, : 2 * features]
    columns = ada_ref.shape[0]
    moved = pltpu.roll(flat_ref[...], lax.rem(n_d - d, n_d) * columns, 1)[:, :columns]
    rows_out[:, 0, :] = lax.dot_general(
        moved, ada_ref[...].astype(F32), (((1,), (0,)), ((), ())),
        precision=lax.Precision.HIGHEST, preferred_element_type=F32,
    )
    copies = [pltpu.make_async_copy(rows_out.at[d], rows_in.at[d], s_l.at[1])]
    for r in range(1, n_d):
        peer = lax.rem(d + r, n_d)
        copies.append(remote(rows_out.at[peer], rows_in.at[d], s_p.at[r - 1], r_p.at[r - 1], peer, t))
    for copy in copies:
        copy.start()
    uh.advance(2)
    value = grad_ref[oi, ii].astype(F32)
    for q in range(1, INNER):
        value += ry[q - 1, oi].astype(F32)
    for copy in z_copies:
        copy.wait()
    for r in range(1, no):
        value += rz[r - 1].astype(F32)
    for j in range(3):
        gq_ref[j] = value[:, j * width : (j + 1) * width]
    for copy in copies:
        copy.wait()
    gcond_ref[...] = jnp.sum(rows_in[:, 0, :], axis=0, keepdims=True)


def back_call(
    dmix, proj, mix, lse, cos, sin, attn_in, w_qkv, stat, x, dmid, vecs, ada_t, partial_sums, n_d, n_t
):
    parts = 4
    count = counts(n_d, n_t)
    nx, no = count["x"], count["z"]
    blocks, total, rows = proj.shape
    width = total // 3
    heads = width // HEAD_DIM
    length = blocks * rows
    features = attn_in.shape[2]
    part = features // n_d
    cond_width = ada_t.shape[1]
    cut = partial_sums[0].shape[-1]
    buffers = []
    for (dims, path), source in zip(BACK_SUMS, partial_sums):
        buffers += reduce_scratch(count, dims, path, source.shape[-2:])
    stages = sum(len(path) for _, path in BACK_SUMS)
    widest = max(count.values()) - 1
    late = (1, 3 * features)
    return pl.pallas_call(
        partial(back_kernel, n_d, n_t, parts, heads),
        name="back",
        out_shape=[
            struct((rows, features), F32),
            struct((3, part, width), F32),
            struct((part, 2 * cut), F32),
            struct((part, 2 * cut), F32),
            struct((width, part), F32),
            struct((n_d,) + stat.shape, F32),
            struct((n_d, 6 * features), F32),
            struct((1, features), F32),
            struct((1, cond_width), F32),
        ],
        in_specs=[VMEM] * 6 + [ANY] * 2 + [VMEM] + [ANY] * 2 + [VMEM] * 2 + [ANY] * 5,
        out_specs=[VMEM] * 9,
        scratch_shapes=[
            pltpu.VMEM(dmix.shape, BF16),
            pltpu.VMEM((heads, length, HEAD_DIM), BF16),
            pltpu.VMEM((width, length), BF16),
            pltpu.VMEM((heads, length, HEAD_DIM), BF16),
            pltpu.VMEM((heads, length, HEAD_DIM), F32),
            pltpu.VMEM((heads, length, HEAD_DIM), F32),
            pltpu.VMEM((n_t, width, rows), F32),
            pltpu.VMEM(proj.shape, BF16),
            pltpu.VMEM(attn_in.shape, BF16),
            pltpu.VMEM(w_qkv.shape, BF16),
            pltpu.VMEM((total, features), F32),
            pltpu.VMEM((no, INNER, part, total), BF16),
            pltpu.VMEM((nx, rows, features), BF16),
            pltpu.VMEM((nx - 1, rows, features), BF16),
            pltpu.VMEM((INNER - 1, no, part, total), BF16),
            pltpu.VMEM((no - 1, part, total), BF16),
            pltpu.VMEM((no - 1, part, total), BF16),
            pltpu.VMEM((n_t - 1,) + stat.shape, F32),
            pltpu.VMEM(stat.shape, F32),
            pltpu.VMEM(x.shape, BF16),
            pltpu.VMEM(x.shape, F32),
            pltpu.VMEM(late, F32),
            pltpu.VMEM((n_t - 1,) + late, F32),
            pltpu.VMEM(late, F32),
            pltpu.VMEM((n_d,) + late, F32),
            pltpu.VMEM((n_d, 1, cond_width), F32),
            pltpu.VMEM((n_d, 1, cond_width), F32),
        ]
        + buffers
        + [
            DMA((n_t - 1,)), DMA((n_t - 1,)), DMA((6 + len(BACK_SUMS),)),
            DMA((stages, widest)), DMA((stages, widest)),
            DMA((n_t - 1,)), DMA((n_t - 1,)), DMA((n_d - 1,)), DMA((n_d - 1,)),
            DMA((nx, parts)), DMA((nx, parts)), DMA((nx - 1, parts)), DMA((nx - 1, parts)),
            DMA((INNER - 1,)), DMA((INNER - 1,)), DMA((no - 1,)), DMA((no - 1,)),
            DMA((n_t - 1,)), DMA((n_t - 1,)), DMA((n_d - 1,)), DMA((n_d - 1,)),
            DMA((n_d - 1,)), DMA((n_d - 1,)),
        ],
        compiler_params=params(2),
        cost_estimate=cost(45 * heads * length * length * HEAD_DIM, 40e6, heads * length * length),
    )(dmix, proj, mix, lse, cos, sin, attn_in, w_qkv, stat, x, dmid, vecs, ada_t, *partial_sums)


def finish_kernel(
    count, n_units, n_moved, table_ref, flat_ref, cond_ref, gain_in, gcond_in, *more
):
    sources, more = more[:n_moved], more[n_moved:]
    ada_ref, bias_ref, gain1_ref, gain2_ref, bdown_ref, bup_ref, root_ref, gcond_ref = more[:8]
    for src, dst in zip(sources, more[8:]):
        if len(dst.shape) > len(src.shape):
            dst[:, 0, :] = src[...]
        else:
            dst[...] = src[...]
    n_d = table_ref.shape[0]
    features = table_ref.shape[2]
    total = table_ref[0]
    for s in range(1, n_d):
        total += table_ref[s]
    root_ref[...] = jnp.sqrt(jnp.sum(total[S_SQ_A : S_SQ_R + 1], axis=1) / count)
    gain2_ref[...] = total[S_GAIN2]
    bdown_ref[...] = total[S_B_DOWN]
    for u in range(n_units):
        bup_ref[u * features : (u + 1) * features] = total[S_B_UP + u]
    gain1_ref[...] = gain_in[0]
    gcond_ref[...] = gcond_in[...]
    for block in range(6):
        at = slice(block * features, (block + 1) * features)
        value = jnp.zeros((cond_ref.shape[0], features), F32)
        for s in range(n_d):
            value += cond_ref[:, s : s + 1] * flat_ref[s : s + 1, at]
        ada_ref[:, at] = value
        bias_ref[at] = jnp.sum(flat_ref[:, at], axis=0)


def finish_call(table, flat, cond_t, gain, gcond, moved, count, n_units):
    rows, wide = moved[1].shape
    shapes = [a.shape for a in moved]
    shapes[1] = (rows, 1, wide)
    features = table.shape[2]
    width = cond_t.shape[0]
    return pl.pallas_call(
        partial(finish_kernel, count, n_units, len(moved)),
        name="finish",
        out_shape=[
            struct((width, 6 * features), F32),
            struct((6 * features,), F32),
            struct((features,), F32),
            struct((features,), F32),
            struct((features,), F32),
            struct((n_units * features,), F32),
            struct((3,), F32),
            struct((1, width), F32),
        ]
        + [struct(shape, a.dtype) for a, shape in zip(moved, shapes)],
        in_specs=[VMEM] * (5 + len(moved)),
        out_specs=[VMEM] * (8 + len(moved)),
        compiler_params=params(),
        cost_estimate=cost(1e7, 4e6),
    )(table, flat, cond_t, gain, gcond, *moved)


def shards(
    block_input, condition, modulation_weight, modulation_bias, first_gain, qkv_weight, out_weight,
    second_gain, up_weight, up_bias, down_weight, down_bias, grad_output,
):
    n_t, n_d = lax.axis_size("tensor"), lax.axis_size("dp")
    rows, sequences, features = block_input.shape
    assert sequences == 1
    length = rows * n_t
    part, width = qkv_weight.shape[1:]
    units = up_weight.shape[1]
    assert units == features and n_t % CORES == 0 and n_d % INNER == 0
    x = block_input.reshape(rows, features)
    g = grad_output.reshape(rows, features)
    ada_t = modulation_weight.T

    smalls = (first_gain, second_gain, down_bias, up_bias, condition, modulation_bias)
    inverse = 10000.0 ** (-np.arange(HEAD_DIM // 2) * 2.0 / HEAD_DIM)
    angles = inverse[:, None] * np.arange(length)[None, :]
    cos, sin = jnp.asarray(np.cos(angles), F32), jnp.asarray(np.sin(angles), F32)

    attn_in, proj, mix, lse, mix_own, vecs, cond_t, w_qkv, w_ul, w_dl, w_uh, w_dh, w_out = front_call(
        x, qkv_weight, smalls, ada_t, up_weight, down_weight.T, out_weight, cos, sin, n_d, n_t
    )
    stat_rows = -(-(S_B_UP + n_t) // 8) * 8
    out, d_middle, d_mix, stat, *partial_sums = middle_call(
        mix_own, x, g, vecs, w_ul, w_dl, w_uh, w_dh, w_out, stat_rows, n_d, n_t
    )
    grad_input, g_qkv, g_up, g_down, g_out, table, flat, gain1, grad_cond = back_call(
        d_mix, proj, mix, lse, cos, sin, attn_in, w_qkv.reshape(features, 3 * width), stat,
        x, d_middle, vecs, ada_t, partial_sums, n_d, n_t,
    )
    moved = (out, grad_input, g_qkv, g_up, g_down, g_out)
    grad_ada, grad_ada_b, gain1, gain2, b_down, b_up, roots, grad_cond, *moved = finish_call(
        table, flat, cond_t, gain1, grad_cond, moved, float(length * n_d * features), n_t
    )
    out, grad_input, g_qkv, g_up, g_down, g_out = moved
    return (
        out.reshape(block_input.shape), grad_input, grad_cond, grad_ada, grad_ada_b, gain1, g_qkv,
        g_out, gain2, g_up, b_up, g_down.T, b_down, roots,
    )


def solution(mesh):
    in_specs = (
        P("tensor", "dp", None),
        P("dp", None),
        P(None, "dp"),
        P("dp"),
        P("dp"),
        P(None, "dp", "tensor"),
        P("tensor", "dp"),
        P("dp"),
        P("dp", "tensor"),
        P("dp"),
        P("tensor", "dp"),
        P("dp"),
        P("tensor", "dp", None),
    )
    out_specs = (
        P("tensor", "dp", None),
        P("tensor", "dp", None),
        P("dp", None),
        P(),
        P(),
        P(),
        P(None, "dp", "tensor"),
        P("tensor", "dp"),
        P(),
        P("dp", "tensor"),
        P(),
        P("tensor", "dp"),
        P(),
        P(),
    )
    return jax.shard_map(shards, mesh=mesh, in_specs=in_specs, out_specs=out_specs, check_vma=False)
```

```python
from functools import partial

import jax
import jax.numpy as jnp
import numpy as np
from jax import lax
from jax.experimental import pallas as pl
from jax.experimental.pallas import tpu as pltpu
from jax.sharding import PartitionSpec as P

HEAD_DIM = 64
EPSILON = 1e-05
CORES = 2
INNER = 2
MESH = pl.DeviceIdType.MESH
VMEM_LIMIT = 58 << 20
GELU_C = float(np.sqrt(2.0 / np.pi))
GELU_A = 0.044715
F32 = jnp.float32
BF16 = jnp.bfloat16
ANY = pl.BlockSpec(memory_space=pl.ANY)
VMEM = pl.BlockSpec(memory_space=pltpu.VMEM)
DMA = pltpu.SemaphoreType.DMA


def dot(lhs, rhs, lhs_dim, rhs_dim):
    return lax.dot_general(
        lhs, rhs, (((lhs_dim,), (rhs_dim,)), ((), ())), preferred_element_type=F32
    )


def params(collective_id=None, **more):
    if collective_id is not None:
        more.update(collective_id=collective_id, has_side_effects=True)
    return pltpu.CompilerParams(vmem_limit_bytes=VMEM_LIMIT, **more)


def cost(flops, moved, special=0):
    return pl.CostEstimate(flops=int(flops), bytes_accessed=int(moved), transcendentals=int(special))


def struct(shape, dtype):
    return jax.ShapeDtypeStruct(shape, dtype)


def mean_rows(values):
    return jnp.mean(values, axis=-1, keepdims=True)


def sum_tokens(values):
    return jnp.sum(values, axis=0, keepdims=True)


GAIN1, SHIFT_A, SCALE_A, GATE_A, GAIN2, SHIFT_M, SCALE_M, GATE_M, B_DOWN, B_UP = range(10)
MOD_ROWS = (SHIFT_A, SCALE_A, GATE_A, SHIFT_M, SCALE_M, GATE_M)
S_GATE_A, S_SHIFT_M, S_SCALE_M, S_GATE_M, S_GAIN2, S_B_DOWN, S_SQ_A, S_SQ_M, S_SQ_R, S_B_UP = range(10)
L_SHIFT_A, L_SCALE_A, L_GAIN1 = range(3)


def order(k, xi, ci, nx):
    return lax.rem(xi + k // CORES, nx) * CORES + lax.rem(ci + k % CORES, CORES)


def mirror(k, nx):
    return (nx - k // CORES) % nx * CORES + (CORES - k % CORES) % CORES


def place(n_d, n_t):
    d, t = lax.axis_index("dp"), lax.axis_index("tensor")
    return d, t, d // INNER, lax.rem(d, INNER), t // CORES, lax.rem(t, CORES)


def greet(n_d, n_t):
    d, t = lax.axis_index("dp"), lax.axis_index("tensor")
    barrier = pltpu.get_barrier_semaphore()
    for r in range(1, n_t):
        pl.semaphore_signal(
            barrier, 1, device_id=(d, lax.rem(t + r, n_t)), device_id_type=MESH
        )
    for r in range(1, n_d):
        pl.semaphore_signal(
            barrier, 1, device_id=(lax.rem(d + r, n_d), t), device_id_type=MESH
        )
    pl.semaphore_wait(barrier, n_t - 1 + n_d - 1)


def remote(src, dst, send, recv, d, t):
    return pltpu.make_async_remote_copy(
        src_ref=src, dst_ref=dst, send_sem=send, recv_sem=recv, device_id=(d, t), device_id_type=MESH
    )


class Places:
    def __init__(self, n_d, n_t):
        d, t = lax.axis_index("dp"), lax.axis_index("tensor")
        self.d, self.t = d, t
        self.me = {"z": d // INNER, "y": lax.rem(d, INNER), "x": t // CORES, "c": lax.rem(t, CORES)}
        self.count = counts(n_d, n_t)

    def peer(self, axis, r):
        at = dict(self.me)
        at[axis] = lax.rem(at[axis] + r, self.count[axis])
        return at[axis], (at["z"] * INNER + at["y"], at["x"] * CORES + at["c"])


def counts(n_d, n_t):
    return {"z": n_d // INNER, "y": INNER, "x": n_t // CORES, "c": CORES}


class Spread:
    def __init__(self, places, dims, known, path, array, source, send, recv, row, lanes=slice(None)):
        self.path, self.flights = path, []
        for s, axis in enumerate(path):
            region = tuple(
                slice(None) if a in known or a in path[:s] else places.me[a] for a in dims
            ) + (slice(None), lanes)
            src = source if s == 0 else array.at[region]
            self.flights.append([])
            for r in range(1, places.count[axis]):
                _, (d, t) = places.peer(axis, r)
                self.flights[s].append(
                    remote(
                        src, array.at[region], send.at[row + s, r - 1], recv.at[row + s, r - 1], d, t
                    )
                )

    def start(self, s):
        for copy in self.flights[s]:
            copy.start()

    def wait(self, s):
        for copy in self.flights[s]:
            copy.wait()

    def advance(self, s, last=None):
        self.wait(s)
        if s + 1 < len(self.path) and s != last:
            self.start(s + 1)


class Reduce:
    def __init__(self, places, dims, path, source, own, met, results, send, recv, local, row):
        self.places, self.path, self.own, self.met = places, path, own, met
        self.results, self.flights, self.dims = results, [], []
        current = source
        for s, axis in enumerate(path):
            at = dims.index(axis)
            self.dims.append((current, dims, at))
            self.flights.append([])
            for r in range(1, places.count[axis]):
                to, (d, t) = places.peer(axis, r)
                self.flights[s].append(
                    remote(
                        current.at[(slice(None),) * at + (to,)], met[s].at[r - 1],
                        send.at[row + s, r - 1], recv.at[row + s, r - 1], d, t,
                    )
                )
            if s == 0:
                self.load = None
                if own is not None:
                    self.load = pltpu.make_async_copy(
                        current.at[(slice(None),) * at + (places.me[axis],)], own, local
                    )
            dims = dims.replace(axis, "")
            current = results[s]

    def start(self, s):
        for copy in self.flights[s]:
            copy.start()
        if s == 0 and self.load is not None:
            self.load.start()

    def advance(self, s):
        places, path = self.places, self.path
        for copy in self.flights[s]:
            copy.wait()
        current, dims, at = self.dims[s]
        rest = dims.replace(path[s], "")
        if s == 0 and self.load is not None:
            self.load.wait()
            current, at = self.own, None
        sizes = [places.count[a] for a in rest]

        def fold(n, carry):
            spot = []
            for size in reversed(sizes):
                spot.insert(0, lax.rem(n, size))
                n = n // size
            own = list(spot)
            if at is not None:
                own.insert(at, places.me[path[s]])
            value = current[tuple(own)].astype(F32)
            for r in range(places.count[path[s]] - 1):
                value += self.met[s][(r,) + tuple(spot)].astype(F32)
            if callable(self.results[s]):
                self.results[s](value)
            else:
                self.results[s][tuple(spot)] = value.astype(BF16)
            return carry

        if sizes:
            lax.fori_loop(0, int(np.prod(sizes)), fold, 0)
        else:
            fold(0, 0)
        if s + 1 < len(path):
            self.start(s + 1)


def reduce_scratch(count, dims, path, tail, own=True, last=True):
    shapes = []
    rest = dims.replace(path[0], "")
    if own:
        shapes.append(tuple(count[a] for a in rest) + tail)
    left = dims
    for axis in path:
        left = left.replace(axis, "")
        shapes.append((count[axis] - 1,) + tuple(count[a] for a in left) + tail)
    left = dims
    for axis in path if not last else path[:-1]:
        left = left.replace(axis, "")
        shapes.append(tuple(count[a] for a in left) + tail)
    return [pltpu.VMEM(shape, BF16) for shape in shapes]


FRONT_PATHS = {"ul": "zyxc", "dl": "xzyc", "o": "xzyc", "uh": "zy", "dh": "zx"}
FRONT_PLAN = {
    "pre": ("s dl",),
    "0": ("s ul",),
    "qz": ("a dl", "a ul",),
    "n": ("s o",),
    "g": ("a o",),
    "p3": ("a dl", "a ul",),
    "a0": ("s uh", "s dh",),
    "a2": ("a o",),
    "a5": ("a dl", "a ul", "a uh", "a dh",),
    "end": ("a o", "a dl", "a ul", "a o", "a uh", "a dh",),
}
BACK_DIMS = {"ul": "zy", "dl": "zx", "uh": "zyx", "dh": "zyx", "o": "czyx"}
BACK_PATHS = {"ul": "yz", "dl": "xz", "uh": "xyz", "dh": "yxz", "o": "czxy"}
BACK_PLAN = {
    "0": ("s dh", "s o",),
    "n0": ("a o",),
    "n1": ("s uh", "s dl", "s ul",),
    "n2": ("a dh",),
    "n5": ("a dl", "a ul",),
    "n6": ("a dh", "a o", "a uh",),
    "n7": ("a ul", "a dl",),
    "t4": ("a dh",),
    "t5": ("a uh", "a o",),
    "t0": ("a uh",),
    "t2": ("a o",),
}
BACK_SUMS = tuple((BACK_DIMS[name], BACK_PATHS[name]) for name in BACK_DIMS)
CODE = {"z": 2, "y": 2, "x": 2, "c": 2}
EARLY = ((2, S_GATE_A), (3, S_SHIFT_M), (4, S_SCALE_M), (5, S_GATE_M))


def front_kernel(
    n_d, n_t, parts, heads, cond_at, bias_at, sizes,
    x_ref, qkv_ref, gain1_ref, gain2_ref, bdown_ref, bup_ref, cond_in, ada_b_ref,
    ada_ref, up_ref, down_ref, outw_ref, cos_ref, sin_ref,
    in_all, proj_ref, mix_ref, lse_ref, mix_own, vec_ref, cond_ref, w_all, w_ul, w_dl, w_uh, w_dh, w_out,
    x_all, w_pack, wt_ref, out_pack, small_ref, small_all, mod_all, mod_rows, key_ref,
    s_x, r_x, s_c, r_c, s_f, r_f, s_z, r_z, s_y, r_y, s_s, r_s, s_m, r_m, s_l,
    s_w, r_w, s_o, r_o,
):
    d, t, oi, ii, xi, ci = place(n_d, n_t)
    nx, no = n_t // CORES, n_d // INNER
    other = xi * CORES + (1 - ci)
    piece = x_ref.shape[0] // parts
    rows, features = x_ref.shape
    width = qkv_ref.shape[2]
    half = HEAD_DIM // 2
    cut = w_ul.shape[5]
    low_half, high_half = slice(0, cut), slice(cut, 2 * cut)
    for j in range(3):
        w_pack[:, j * width : (j + 1) * width] = qkv_ref[j]
    out_pack[:, :width] = outw_ref[...].T
    small_ref[...] = jnp.zeros_like(small_ref)
    at = 0
    for ref in (gain1_ref, gain2_ref, bdown_ref, bup_ref):
        small_ref[:, at : at + ref.shape[0]] = ref[...].astype(F32).reshape(1, -1)
        at += ref.shape[0]
    small_ref[:, cond_at : cond_at + cond_in.shape[1]] = cond_in[...].astype(F32)
    small_ref[:, bias_at : bias_at + ada_b_ref.shape[0]] = ada_b_ref[...].astype(F32).reshape(1, -1)
    if out_pack.shape[1] > width:
        out_pack[:, width:] = jnp.zeros((out_pack.shape[0], out_pack.shape[1] - width), BF16)
    greet(n_d, n_t)
    places = Places(n_d, n_t)
    flows = {}
    for row, (name, dims, array, source) in enumerate(
        (
            ("ul", "zyxc", w_ul, up_ref.at[:, low_half]),
            ("dl", "zyxc", w_dl, down_ref.at[:, low_half]),
            ("o", "zyxc", w_out, out_pack),
            ("uh", "zy", w_uh, up_ref.at[:, high_half]),
            ("dh", "zx", w_dh, down_ref.at[:, high_half]),
        )
    ):
        flows[name] = Spread(
            places, dims, "", FRONT_PATHS[name], array, source, s_w, r_w, 4 * row
        )
    stage = dict.fromkeys(flows, 0)

    def at_point(point):
        for step in FRONT_PLAN.get(point, ()):
            what, name = step.split()
            if what == "s":
                flows[name].start(0)
            else:
                flows[name].advance(stage[name])
                stage[name] += 1

    s_copies = []
    for r in range(1, n_d):
        copy = remote(
            small_ref, small_all.at[d], s_s.at[r - 1], r_s.at[r - 1], lax.rem(d + r, n_d), t
        )
        copy.start()
        s_copies.append(copy)
    at_point("pre")
    x_copies = []
    for r in range(1, nx):
        peer = lax.rem(xi + r, nx) * CORES + ci
        for p in range(parts):
            at = pl.ds(p * piece, piece)
            copy = remote(
                x_ref.at[at], x_all.at[t, at], s_x.at[r - 1, p], r_x.at[r - 1, p], d, peer
            )
            copy.start()
            x_copies.append((r, p, copy))
    z_copies = []
    for r in range(1, no):
        copy = remote(
            w_pack, w_all.at[d], s_z.at[r - 1], r_z.at[r - 1], lax.rem(oi + r, no) * INNER + ii, t
        )
        copy.start()
        z_copies.append(copy)
    y_copies = []
    for q in range(1, INNER):
        copy = remote(
            w_pack, w_all.at[d], s_y.at[q - 1, 0], r_y.at[q - 1, 0],
            oi * INNER + lax.rem(ii + q, INNER), t,
        )
        copy.start()
        y_copies.append(copy)
    core_copy = remote(x_ref, x_all.at[t], s_c, r_c, d, other)
    core_copy.start()
    local = []
    for n, (src, dst) in enumerate(
        (
            (small_ref, small_all.at[d]),
            (x_ref, x_all.at[t]),
            (w_pack, w_all.at[d]),
            (up_ref.at[:, low_half], w_ul.at[oi, ii, xi, ci]),
            (down_ref.at[:, low_half], w_dl.at[oi, ii, xi, ci]),
            (up_ref.at[:, high_half], w_uh.at[oi, ii]),
            (down_ref.at[:, high_half], w_dh.at[oi, xi]),
            (out_pack, w_out.at[oi, ii, xi, ci]),
        )
    ):
        copy = pltpu.make_async_copy(src, dst, s_l.at[n])
        copy.start()
        local.append(copy)

    at_point("0")

    local[0].wait()
    for copy in s_copies:
        copy.wait()
    cond = small_all[:, 0, cond_at : cond_at + ada_ref.shape[1]]
    for s in range(n_d):
        cond_ref[:, s : s + 1] = cond[s : s + 1].T
    bias = small_ref[:, bias_at : bias_at + ada_ref.shape[0]]
    mod_rows[:, 0, :] = dot(cond.astype(BF16), ada_ref[...], 1, 1) + bias
    own_mod = pltpu.make_async_copy(mod_rows.at[d], mod_all.at[d], s_l.at[8])
    own_mod.start()
    m_copies = []
    for r in range(1, n_d):
        peer = lax.rem(d + r, n_d)
        copy = remote(mod_rows.at[peer], mod_all.at[d], s_m.at[r - 1], r_m.at[r - 1], peer, t)
        copy.start()
        m_copies.append(copy)
    for r in range(1, no):
        z_copies[r - 1].wait()
        origin = lax.rem(oi + no - r, no) * INNER + ii
        for q in range(1, INNER):
            copy = remote(
                w_all.at[origin], w_all.at[origin], s_y.at[q - 1, r], r_y.at[q - 1, r],
                oi * INNER + lax.rem(ii + q, INNER), t,
            )
            copy.start()
            y_copies.append(copy)
    for n in range(3, 8):
        local[n].wait()
    at_point("qz")
    f_copies = []
    for r, p, copy in x_copies:
        copy.wait()
        origin = lax.rem(xi + nx - r, nx) * CORES + ci
        at = pl.ds(p * piece, piece)
        copy = remote(
            x_all.at[origin, at], x_all.at[origin, at],
            s_f.at[r - 1, p], r_f.at[r - 1, p], d, other,
        )
        copy.start()
        f_copies.append(copy)

    at_point("X")
    for copy in m_copies + [own_mod]:
        copy.wait()
    def put(first, piece_of, count):
        for s in range(n_d):
            value = piece_of(s)
            start = s * count
            done = 0
            while done < count:
                row, column = divmod(start + done, features)
                take = min(count - done, features - column)
                vec_ref[first + row : first + row + 1, column : column + take] = value[
                    :, done : done + take
                ]
                done += take

    vec_ref[...] = jnp.zeros_like(vec_ref)
    at = 0
    for first, count in sizes:
        put(first, lambda s: small_all[s, :, at : at + count], count)
        at += count
    columns = ada_ref.shape[0]
    for s in range(n_d):
        done = 0
        while done < columns:
            row, column = divmod(s * columns + done, features)
            take = min(columns - done, features - column)
            row = MOD_ROWS[row]
            vec_ref[row : row + 1, column : column + take] = mod_all[s, :, done : done + take]
            done += take

    for copy in f_copies + [local[1], core_copy]:
        copy.wait()

    def norm(b, carry):
        x = x_all[b].astype(F32)
        centred = x - mean_rows(x)
        normed = centred * lax.rsqrt(mean_rows(centred * centred) + EPSILON)
        normed = normed * vec_ref[GAIN1 : GAIN1 + 1]
        low = (normed * (1.0 + vec_ref[SCALE_A : SCALE_A + 1]) + vec_ref[SHIFT_A : SHIFT_A + 1])
        in_all[b] = low.astype(BF16)
        return carry

    lax.fori_loop(0, n_t, norm, 0)
    at_point("n")
    for copy in y_copies + [local[2]]:
        copy.wait()
    wt_ref[...] = w_all[...].reshape(features, 3 * width).T

    at_point("g")

    def project(b, carry):
        proj = dot(wt_ref[...], in_all[b], 1, 1)
        lanes = pl.ds(pl.multiple_of(b * rows, rows), rows)
        cos, sin = cos_ref[:, lanes], sin_ref[:, lanes]
        for j in range(2):
            factor = HEAD_DIM**-0.5 if j == 0 else 1.0
            for h in range(heads):
                at = j * width + h * HEAD_DIM
                first, last = proj[at : at + half], proj[at + half : at + HEAD_DIM]
                top = ((first * cos - last * sin) * factor).astype(BF16)
                bottom = ((last * cos + first * sin) * factor).astype(BF16)
                proj_ref[b, at : at + half] = top
                proj_ref[b, at + half : at + HEAD_DIM] = bottom
                if j == 1:
                    key_ref[h, lanes, :] = jnp.concatenate([top, bottom], axis=0).T
        proj_ref[b, 2 * width :] = proj[2 * width :].astype(BF16)

        for m in range(n_t):
            if f"p{m}" in FRONT_PLAN:
                @pl.when(b == m)
                def _(m=m):
                    at_point(f"p{m}")

        return carry

    lax.fori_loop(0, n_t, project, 0)

    def attend(u, carry):
        plane = lax.rem(xi + nx - 1 - u // heads, nx)
        h = lax.rem(u, heads)
        at = pl.ds(pl.multiple_of(h * HEAD_DIM, HEAD_DIM), HEAD_DIM)
        value_at = pl.ds(pl.multiple_of(2 * width + h * HEAD_DIM, HEAD_DIM), HEAD_DIM)
        first = plane * CORES
        query = jnp.concatenate([proj_ref[first + c, at] for c in range(CORES)], axis=1)
        scores = dot(key_ref[h], query, 1, 0)
        top = jnp.max(scores, axis=0, keepdims=True)
        grown = jnp.exp(scores - top)
        total = jnp.sum(grown, axis=0, keepdims=True)
        value = jnp.concatenate([proj_ref[v, value_at] for v in range(n_t)], axis=1)
        mixed = (dot(value, grown.astype(BF16), 1, 0) / total).astype(BF16)
        log_total = top + jnp.log(total)
        for c in range(CORES):
            part = slice(c * rows, (c + 1) * rows)
            mix_ref[first + c, at] = mixed[:, part]
            lse_ref[first + c, pl.ds(h, 1)] = log_total[:, part]
        for r in range(nx):
            @pl.when(u == (nx - r) * heads - 1)
            def _(r=r):
                for c in range(CORES):
                    if r * CORES + c > 0:
                        o_copies[r * CORES + c].start()

        for m in range(nx * heads):
            if f"a{m}" in FRONT_PLAN:
                @pl.when(u == m)
                def _(m=m):
                    at_point(f"a{m}")

        return carry

    o_copies = {}
    for m in range(1, n_t):
        b = order(m, xi, ci, nx)
        o_copies[m] = remote(
            mix_ref.at[b], mix_own.at[t], s_o.at[m - 1], r_o.at[mirror(m, nx) - 1], d, b
        )
    lax.fori_loop(0, nx * heads, attend, 0)
    mine = pltpu.make_async_copy(mix_ref.at[t], mix_own.at[t], s_l.at[9])
    mine.start()
    at_point("end")
    for name, flow in flows.items():
        assert stage[name] == len(flow.path), name
    mine.wait()
    for copy in list(o_copies.values()):
        copy.wait()


def front_call(x, qkv, smalls, ada_t, up, down_t, outw, cos, sin, n_d, n_t):
    cond, ada_b = smalls[4:]
    sizes = tuple(zip((GAIN1, GAIN2, B_DOWN, B_UP), (a.shape[0] for a in smalls[:4])))
    cond_at = -(-sum(size for _, size in sizes) // 128) * 128
    bias_at = cond_at + cond.shape[1]
    small = bias_at + ada_b.shape[0]
    parts = 4
    nx, no = n_t // CORES, n_d // INNER
    rows, features = x.shape
    part, width = qkv.shape[1:]
    heads = width // HEAD_DIM
    length = rows * n_t
    wide = -(-width // 128) * 128
    units = up.shape[1]
    steps = max(no, INNER, nx) - 1
    cut = units // 2
    grid_of = (no, INNER, nx, CORES, part)
    columns = ada_t.shape[0]
    return pl.pallas_call(
        partial(front_kernel, n_d, n_t, parts, heads, cond_at, bias_at, sizes),
        name="front",
        out_shape=[
            struct((n_t, rows, features), BF16),
            struct((n_t, 3 * width, rows), BF16),
            struct((n_t, width, rows), BF16),
            struct((n_t, heads, rows), F32),
            struct((n_t, width, rows), BF16),
            struct((16, features), F32),
            struct((ada_t.shape[1], n_d), F32),
            struct((n_d, part, 3 * width), BF16),
            struct(grid_of + (cut,), BF16),
            struct(grid_of + (cut,), BF16),
            struct((no, INNER, part, cut), BF16),
            struct((no, nx, part, cut), BF16),
            struct(grid_of + (wide,), BF16),
        ],
        in_specs=[VMEM] * 9 + [ANY] * 2 + [VMEM] * 3,
        out_specs=[VMEM] * 8 + [ANY] * 5,
        scratch_shapes=[
            pltpu.VMEM((n_t, rows, features), BF16),
            pltpu.VMEM((part, 3 * width), BF16),
            pltpu.VMEM((3 * width, features), BF16),
            pltpu.VMEM((part, wide), BF16),
            pltpu.VMEM((1, small), F32),
            pltpu.VMEM((n_d, 1, small), F32),
            pltpu.VMEM((n_d, 1, columns), F32),
            pltpu.VMEM((n_d, 1, columns), F32),
            pltpu.VMEM((heads, length, HEAD_DIM), BF16),
            DMA((nx - 1, parts)), DMA((nx - 1, parts)), DMA, DMA,
            DMA((nx - 1, parts)), DMA((nx - 1, parts)),
            DMA((no - 1,)), DMA((no - 1,)),
            DMA((INNER - 1, no)), DMA((INNER - 1, no)),
            DMA((n_d - 1,)), DMA((n_d - 1,)), DMA((n_d - 1,)), DMA((n_d - 1,)),
            DMA((10,)),
            DMA((20, steps)), DMA((20, steps)),
            DMA((n_t - 1,)), DMA((n_t - 1,)),
        ],
        compiler_params=params(0),
        cost_estimate=cost(20 * heads * length * length * HEAD_DIM, 40e6, heads * length * length),
    )(x, qkv, *smalls, ada_t, up, down_t, outw, cos, sin)


def middle_kernel(
    n_d, n_t,
    mix_ref, x_ref, g_ref, vec_ref, ul_ref, dl_ref, uh_ref, dh_ref, wout_ref,
    out_ref, dmid_ref, dmix_ref, stat_ref, hul_ref, hdl_ref, huh_ref, hdh_ref, gout_ref,
    up_buf, down_buf, o_buf, go_buf,
    attn_ref, low_ref, lowt_ref, dl_t_ref, dlt_ref, acc_out, acc_in,
    mul_c, rul, mul_x, mdl_c, mdl_y, rdl, muh, mdh,
    s_u, s_d, s_o, s_w, r_w, s_r, r_r,
):
    places = Places(n_d, n_t)
    count, me = places.count, places.me
    rows, features = x_ref.shape
    width = mix_ref.shape[1]
    cut = up_buf.shape[-1]
    wide = wout_ref.shape[-1]
    loads = [
        pltpu.make_async_copy(wout_ref, o_buf, s_o.at[0]),
        pltpu.make_async_copy(ul_ref, up_buf.at[0], s_u.at[0]),
        pltpu.make_async_copy(dl_ref, down_buf.at[0], s_d.at[0]),
        pltpu.make_async_copy(uh_ref, up_buf.at[1, :, :, me["x"], me["c"]], s_u.at[1]),
        pltpu.make_async_copy(dh_ref, down_buf.at[1, :, me["y"], :, me["c"]], s_d.at[1]),
    ]
    for copy in loads:
        copy.start()
    greet(n_d, n_t)
    nx = count["x"]
    every, mx, my, mc = slice(None), me["x"], me["y"], me["c"]
    taken = [0]

    def send(target, region, axis, r, source=None):
        at = target.at[(1,) + region]
        n = taken[0]
        taken[0] += 1
        return remote(
            at if source is None else source, at, s_w.at[n], r_w.at[n], *places.peer(axis, r)[1]
        )

    own_up = [send(up_buf, (every, every, mx, mc), "c", 1, uh_ref)]
    own_down = [send(down_buf, (every, my, every, mc), "c", 1, dh_ref)]
    near_down, far_down, near_on, far_on, far_up = [], [], [], [], []
    for r in range(1, INNER):
        near_down.append(send(down_buf, (every, my, mx, mc), "y", r, dh_ref.at[:, mx]))
        near_on.append(send(down_buf, (every, places.peer("y", r)[0], mx, mc), "c", 1))
    for r in range(1, nx):
        far_up.append(send(up_buf, (every, every, mx, mc), "x", r, uh_ref))
        far_on.append(send(up_buf, (every, every, places.peer("x", r)[0], mc), "c", 1))
    for r in range(1, INNER):
        for q in range(1, nx):
            x_at = places.peer("x", q)[0]
            far_down.append(send(down_buf, (every, my, x_at, mc), "y", r, dh_ref.at[:, x_at]))
            far_on.append(
                send(down_buf, (every, places.peer("y", r)[0], x_at, mc), "c", 1)
            )
    for copy in near_down + far_up + own_up + own_down + far_down:
        copy.start()
    planes = [lax.rem(me["x"] + nx - 1 - n, nx) for n in range(nx)]
    ul = [
        Reduce(
            places, "zyc", "c", up_buf.at[2, :, :, planes[n]], None, [mul_c.at[n]], [rul.at[n]],
            s_r, r_r, None, n,
        )
        for n in range(nx)
    ]
    ul_x = [
        remote(
            rul.at[nx - 1 - r], mul_x.at[r - 1], s_r.at[4 * nx + 3, r - 1], r_r.at[4 * nx + 3, r - 1],
            *places.peer("x", r)[1],
        )
        for r in range(1, nx)
    ]
    dl = [
        Reduce(
            places, "zyc", "c", down_buf.at[2, :, :, planes[n]], None, [mdl_c.at[n]],
            [rdl.at[:, :, planes[n]]], s_r, r_r, None, nx + n,
        )
        for n in range(nx)
    ]
    dl_y = [
        Reduce(
            places, "zy", "y", rdl.at[:, :, planes[n]], None, [mdl_y.at[n]],
            [rdl.at[:, my, planes[n]]], s_r, r_r, None, 3 * nx + 3 + n,
        )
        for n in range(nx)
    ]
    high_up, high_down = up_buf.at[0, :, :, :, me["c"]], down_buf.at[0, :, :, :, me["c"]]
    uh = Reduce(places, "zyxc", "c", up_buf.at[0], None, [muh], [high_up], s_r, r_r, None, 2 * nx + 1)
    dh = Reduce(
        places, "zyxc", "c", down_buf.at[0], None, [mdh], [high_down], s_r, r_r, None, 2 * nx + 2
    )
    keeps = [
        pltpu.make_async_copy(go_buf, gout_ref, s_o.at[1]),
        pltpu.make_async_copy(high_up, huh_ref, s_o.at[2]),
        pltpu.make_async_copy(high_down, hdh_ref, s_o.at[3]),
        pltpu.make_async_copy(rul.at[nx - 1], hul_ref, s_o.at[4]),
        pltpu.make_async_copy(rdl.at[:, me["y"]], hdl_ref, s_o.at[5]),
    ]
    vec = lambda row: vec_ref[row : row + 1]
    cot = g_ref[...].astype(F32)
    d_mlp = (vec(GATE_M) * cot).astype(BF16)
    dl_t_ref[...] = d_mlp
    dlt_ref[...] = d_mlp.T
    stat_ref[...] = jnp.zeros_like(stat_ref)
    stat_ref[S_B_DOWN : S_B_DOWN + 1] = sum_tokens(d_mlp.astype(F32))
    if wide > width:
        go_buf[...] = jnp.zeros_like(go_buf)
    loads[0].wait()
    w_out = lambda b: o_buf[:, :, b // CORES, b % CORES].reshape(features, wide)[:, :width]
    attn_out = jnp.zeros((rows, features), F32)
    for b in range(n_t):
        attn_out += dot(mix_ref[b].T, w_out(b), 1, 1)
    attn_ref[...] = attn_out
    branch = vec(GATE_A) * attn_out
    stat_ref[S_SQ_A : S_SQ_A + 1] = sum_tokens(branch * branch)
    middle = x_ref[...].astype(F32) + branch
    dmid_ref[...] = middle
    centred = middle - mean_rows(middle)
    inv = lax.rsqrt(mean_rows(centred * centred) + EPSILON)
    low = (centred * inv * vec(GAIN2) * (1.0 + vec(SCALE_M)) + vec(SHIFT_M)).astype(BF16)
    low_ref[...] = low
    lowt_ref[...] = low.T
    acc_out[...] = jnp.zeros_like(acc_out)
    acc_in[...] = jnp.zeros_like(acc_in)
    loads[1].wait()
    loads[2].wait()

    def block(n, carry):
        j = n // nx
        step = lax.rem(n, nx)
        p = lax.rem(mx + (1 - j) * (nx - 1 - step) + j * step, nx)
        slot = 2 - 2 * j
        lanes = pl.ds(pl.multiple_of(j * cut, cut), cut)

        @pl.when(n == nx)
        def _():
            for copy in loads[3:] + own_up + own_down + near_on:
                copy.wait()

        @pl.when(n == nx + 1)
        def _():
            for copy in far_on:
                copy.wait()

        both = lambda buf: jnp.concatenate(
            [buf[j, :, :, p, c].reshape(features, cut) for c in range(CORES)], axis=1
        )
        up, down = both(up_buf), both(down_buf)
        bias = jnp.concatenate(
            [vec_ref[pl.ds(B_UP + p * CORES + c, 1), lanes] for c in range(CORES)], axis=1
        )
        hidden = dot(low_ref[...], up, 1, 0) + bias
        square = hidden * hidden
        bent = jnp.tanh(GELU_C * hidden * (1.0 + GELU_A * square))
        half = 0.5 * (1.0 + bent)
        active = (hidden * half).astype(BF16)
        slope = half + (0.5 * GELU_C) * hidden * (1.0 - bent * bent) * (
            1.0 + (3.0 * GELU_A) * square
        )
        acc_out[...] += dot(active, down, 1, 1)
        for m in range(1, nx):
            @pl.when(n == m)
            def _(m=m):
                ul[m - 1].advance(0)
                ul_x[nx - 1 - m].start()
                dl[m - 1].advance(0)
                dl_y[m - 1].start(0)

        @pl.when(n == nx)
        def _():
            ul[nx - 1].advance(0)
            dl[nx - 1].advance(0)
            dl_y[nx - 1].start(0)
            for copy in far_up + far_down:
                copy.wait()
            for copy in far_on:
                copy.start()

        grad_down = dot(dlt_ref[...], active, 1, 0).astype(BF16)
        d_hidden = (dot(dl_t_ref[...], down, 1, 0) * slope).astype(BF16)
        sums = sum_tokens(d_hidden.astype(F32))
        for c in range(CORES):
            stat_ref[pl.ds(S_B_UP + p * CORES + c, 1), lanes] = sums[:, c * cut : (c + 1) * cut]
        grad_up = dot(lowt_ref[...], d_hidden, 1, 0).astype(BF16)
        acc_in[...] += dot(d_hidden, up, 1, 1)
        for c in range(CORES):
            lanes_of = slice(c * cut, (c + 1) * cut)
            shape = up_buf.shape[1:3] + (-1, cut)
            down_buf[slot, :, :, p, c] = grad_down[:, lanes_of].reshape(shape)
            up_buf[slot, :, :, p, c] = grad_up[:, lanes_of].reshape(shape)

        for m in range(nx):
            @pl.when(n == m)
            def _(m=m):
                ul[m].start(0)
                dl[m].start(0)
                if m == 0:
                    for copy in near_down:
                        copy.wait()
                    for copy in near_on:
                        copy.start()

        return carry

    lax.fori_loop(0, 2 * nx, block, 0)
    uh.start(0)
    dh.start(0)
    middle = dmid_ref[...]
    mlp_out = acc_out[...] + vec(B_DOWN)
    mlp_branch = vec(GATE_M) * mlp_out
    result = middle + mlp_branch
    out_ref[...] = result.astype(BF16)
    cot = g_ref[...].astype(F32)
    stat_ref[S_SQ_M : S_SQ_M + 1] = sum_tokens(mlp_branch * mlp_branch)
    stat_ref[S_SQ_R : S_SQ_R + 1] = sum_tokens(result * result)
    stat_ref[S_GATE_M : S_GATE_M + 1] = sum_tokens(cot * mlp_out)
    e = acc_in[...]
    centred = middle - mean_rows(middle)
    inv = lax.rsqrt(mean_rows(centred * centred) + EPSILON)
    nhat = centred * inv
    gain, scale = vec(GAIN2), 1.0 + vec(SCALE_M)
    by_nhat = sum_tokens(e * nhat)
    stat_ref[S_SHIFT_M : S_SHIFT_M + 1] = sum_tokens(e)
    stat_ref[S_SCALE_M : S_SCALE_M + 1] = by_nhat * gain
    stat_ref[S_GAIN2 : S_GAIN2 + 1] = by_nhat * scale
    dn = e * (scale * gain)
    d_middle = cot + inv * (dn - mean_rows(dn) - nhat * mean_rows(dn * nhat))
    dmid_ref[...] = d_middle
    stat_ref[S_GATE_A : S_GATE_A + 1] = sum_tokens(d_middle * attn_ref[...])
    d_attn = (vec(GATE_A) * d_middle).astype(BF16)
    d_attn_t = d_attn.T
    for b in range(n_t):
        dmix_ref[b] = dot(d_attn, w_out(b), 1, 0).astype(BF16).T
        go_buf[b % CORES, :, :, b // CORES, :, :width] = (
            dot(d_attn_t, mix_ref[b], 1, 1).astype(BF16).reshape(go_buf.shape[1:3] + (-1, width))
        )
    keeps[0].start()
    uh.advance(0)
    keeps[1].start()
    dh.advance(0)
    keeps[2].start()
    for one in ul_x:
        one.wait()
    no = count["z"]

    def fold(n, carry):
        at = (n // INNER, lax.rem(n, INNER))
        value = rul[(nx - 1,) + at].astype(F32)
        for r in range(nx - 1):
            value += mul_x[(r,) + at].astype(F32)
        rul[(nx - 1,) + at] = value.astype(BF16)
        return carry

    lax.fori_loop(0, no * INNER, fold, 0)
    keeps[3].start()
    for one in dl_y:
        one.advance(0)
    keeps[4].start()
    for copy in keeps:
        copy.wait()


def middle_call(mix, x, g, vecs, w_ul, w_dl, w_uh, w_dh, w_out, stat_rows, n_d, n_t):
    rows, features = x.shape
    cut = w_ul.shape[-1]
    part, wide = w_out.shape[-2:]
    width = mix.shape[1]
    count = counts(n_d, n_t)
    no, nx = count["z"], count["x"]
    per = (3,) + w_ul.shape
    plane = (no, INNER, part, cut)
    tail = (part, cut)
    g_out = (CORES, no, INNER, nx, part, wide)
    return pl.pallas_call(
        partial(middle_kernel, n_d, n_t),
        name="middle",
        out_shape=[
            struct((rows, features), BF16),
            struct((rows, features), F32),
            struct((n_t, width, rows), BF16),
            struct((stat_rows, features), F32),
            struct((no, INNER) + tail, BF16),
            struct((no, nx) + tail, BF16),
            struct((no, INNER, nx) + tail, BF16),
            struct((no, INNER, nx) + tail, BF16),
            struct(g_out, BF16),
        ],
        in_specs=[VMEM] * 4 + [ANY] * 5,
        out_specs=[VMEM] * 4 + [ANY] * 5,
        scratch_shapes=[
            pltpu.VMEM(per, BF16), pltpu.VMEM(per, BF16), pltpu.VMEM(w_out.shape, BF16),
            pltpu.VMEM(g_out, BF16),
            pltpu.VMEM((rows, features), F32),
            pltpu.VMEM((rows, features), BF16),
            pltpu.VMEM((features, rows), BF16),
            pltpu.VMEM((rows, features), BF16),
            pltpu.VMEM((features, rows), BF16),
            pltpu.VMEM((rows, features), F32),
            pltpu.VMEM((rows, features), F32),
        ]
        + [
            pltpu.VMEM((nx, 1) + plane, BF16), pltpu.VMEM((nx,) + plane, BF16),
            pltpu.VMEM((nx - 1,) + plane, BF16),
            pltpu.VMEM((nx, 1) + plane, BF16), pltpu.VMEM((nx, INNER - 1, no) + tail, BF16),
            pltpu.VMEM((no, INNER, nx) + tail, BF16),
            pltpu.VMEM((1, no, INNER, nx) + tail, BF16),
            pltpu.VMEM((1, no, INNER, nx) + tail, BF16),
        ]
        + [
            DMA((2,)), DMA((2,)), DMA((6,)),
            DMA((2 + 2 * (INNER - 1 + nx - 1 + (INNER - 1) * (nx - 1)),)),
            DMA((2 + 2 * (INNER - 1 + nx - 1 + (INNER - 1) * (nx - 1)),)),
            DMA((4 * nx + 4, max(nx, INNER, CORES) - 1)), DMA((4 * nx + 4, max(nx, INNER, CORES) - 1)),
        ],
        compiler_params=params(1),
        cost_estimate=cost(2 * rows * features * features * (6 * n_t + 4), 30e6),
    )(mix, x, g, vecs, w_ul, w_dl, w_uh, w_dh, w_out)


def back_kernel(
    n_d, n_t, parts, heads,
    dmix_ref, proj_ref, mix_ref, lse_ref, cos_ref, sin_ref, in_hbm, wq_hbm, stat_ref,
    x_hbm, dmid_hbm, vec_ref, ada_ref,
    hul_ref, hdl_ref, huh_ref, hdh_ref, gout_ref,
    grad_in_ref, gq_ref, up_ref, down_ref, out_ref, table_ref, flat_ref, gain_ref, gcond_ref,
    dmix_all, key_ref, keyt_ref, val_ref, dkey_ref, dval_ref, dquery_ref, dproj_ref, in_ref, wq_ref,
    acc_ref, pair_ref, value_ref, rc, rx, pair_y, pair_z, pair_sum, value_z, value_y, value_mid,
    got_ref, mine_ref,
    x_ref, dmid_ref, late_ref, late_got, late_mine, late_all, rows_out, rows_in, *more,
):
    buffers, at = [], 0
    for size in (len(reduce_scratch(CODE, dims, path, (1, 1))) for dims, path in BACK_SUMS):
        buffers.append(more[at : at + size])
        at += size
    (
        s_a, r_a, s_l, s_g, r_g, s_t, r_t, s_d, r_d, s_c, r_c, s_x, r_x,
        s_v, r_v, s_e, r_e, s_p, r_p,
    ) = more[at:]
    places = Places(n_d, n_t)
    d, t, oi, ii, xi, ci = place(n_d, n_t)
    nx, no = n_t // CORES, n_d // INNER
    other = xi * CORES + (1 - ci)
    blocks, total, rows = proj_ref.shape
    width = total // 3
    half = HEAD_DIM // 2
    features = x_ref.shape[1]
    assert nx == 2 and CORES == 2

    cut = hul_ref.shape[-1]

    def put(target, lanes):
        def store(value):
            target[:, lanes] = value
        return store

    def put_out(value):
        out_ref[...] = value.T[:width]

    sinks = (
        put(up_ref, slice(0, cut)), put(down_ref, slice(0, cut)),
        put(up_ref, slice(cut, 2 * cut)), put(down_ref, slice(cut, 2 * cut)), put_out,
    )
    sums = []
    row = 0
    for n, ((dims, path), source) in enumerate(
        zip(BACK_SUMS, (hul_ref, hdl_ref, huh_ref, hdh_ref, gout_ref))
    ):
        steps = len(path)
        sums.append(
            Reduce(
                places, dims, path, source, buffers[n][0], buffers[n][1 : 1 + steps],
                list(buffers[n][1 + steps :]) + [sinks[n]], s_g, r_g, s_l.at[6 + n], row,
            )
        )
        row += steps
    flows = dict(zip(BACK_DIMS, sums))
    stage = dict.fromkeys(flows, 0)

    def at_point(point):
        for step in BACK_PLAN.get(point, ()):
            what, name = step.split()
            if what == "s":
                flows[name].start(0)
            else:
                flows[name].advance(stage[name])
                stage[name] += 1

    def put_low(value):
        gq_ref[0] = value[:, :width]
        gq_ref[1] = value[:, width:]

    def put_high(value):
        gq_ref[2] = value

    pair = Reduce(
        places, "zy", "yz", pair_ref, None, [pair_y, pair_z], [pair_sum, put_low], s_g, r_g, None, row
    )
    value_sum = Reduce(
        places, "zy", "zy", value_ref, None, [value_z, value_y], [value_mid, put_high],
        s_g, r_g, None, row + 2,
    )

    greet(n_d, n_t)
    a_copies = {}
    for m in range(1, n_t):
        b = order(m, xi, ci, nx)
        a_copies[mirror(m, nx)] = remote(
            dmix_ref.at[b], dmix_all.at[t], s_a.at[m - 1], r_a.at[mirror(m, nx) - 1], d, b
        )
    for m in range(n_t - 1, 0, -1):
        a_copies[mirror(m, nx)].start()
    at_point("0")
    loads = [
        pltpu.make_async_copy(dmix_ref.at[t], dmix_all.at[t], s_l.at[0]),
        pltpu.make_async_copy(in_hbm, in_ref, s_l.at[1]),
        pltpu.make_async_copy(wq_hbm, wq_ref, s_l.at[2]),
        pltpu.make_async_copy(x_hbm, x_ref, s_l.at[3]),
        pltpu.make_async_copy(dmid_hbm, dmid_ref, s_l.at[4]),
    ]
    for copy in loads:
        copy.start()
    t_copies = []
    for r in range(1, n_t):
        copy = remote(
            stat_ref, got_ref.at[r - 1], s_t.at[r - 1], r_t.at[r - 1], d, lax.rem(t + r, n_t)
        )
        copy.start()
        t_copies.append(copy)
    d_copies = [pltpu.make_async_copy(mine_ref, table_ref.at[d], s_l.at[5])]
    for r in range(1, n_d):
        d_copies.append(
            remote(mine_ref, table_ref.at[d], s_d.at[r - 1], r_d.at[r - 1], lax.rem(d + r, n_d), t)
        )

    def share_statistics():
        for copy in t_copies:
            copy.wait()
        value = stat_ref[...]
        for r in range(1, n_t):
            value += got_ref[r - 1]
        mine_ref[...] = value
        for copy in d_copies:
            copy.start()

    dkey_ref[...] = jnp.zeros_like(dkey_ref)
    dval_ref[...] = jnp.zeros_like(dval_ref)

    def turn(b, carry):
        lanes = pl.ds(pl.multiple_of(b * rows, rows), rows)
        keyt_ref[:, lanes] = proj_ref[b, width : 2 * width]
        for h in range(heads):
            at = h * HEAD_DIM
            key_ref[h, lanes] = proj_ref[b, width + at : width + at + HEAD_DIM].T
            val_ref[h, lanes] = proj_ref[b, 2 * width + at : 2 * width + at + HEAD_DIM].T
        return carry

    lax.fori_loop(0, blocks, turn, 0)
    loads[0].wait()

    loads[1].wait()
    loads[2].wait()
    dquery_ref[...] = jnp.zeros_like(dquery_ref)
    acc_ref[...] = jnp.zeros_like(acc_ref)
    part_ref = in_ref
    piece = rows // parts
    c_copies = {}
    for r in range(nx):
        block = lax.rem(xi + r, nx) * CORES + 1 - ci
        for p in range(parts):
            at = pl.ds(p * piece, piece)
            c_copies[r, p] = remote(
                part_ref.at[block, at], rc.at[r, at], s_c.at[r, p], r_c.at[r, p], d, other
            )
    x_copies = {}
    for p in range(parts):
        at = pl.ds(p * piece, piece)
        x_copies[p] = remote(
            part_ref.at[lax.rem(xi + 1, nx) * CORES + ci, at], rx.at[0, at],
            s_x.at[0, p], r_x.at[0, p], d, lax.rem(xi + 1, nx) * CORES + ci,
        )

    def unrotate(b, at, factor, first, last):
        lanes = pl.ds(pl.multiple_of(b * rows, rows), rows)
        cos, sin = cos_ref[:, lanes], sin_ref[:, lanes]
        dproj_ref[b, at : at + half] = ((first * cos + last * sin) * factor).astype(BF16)
        dproj_ref[b, at + half : at + HEAD_DIM] = ((last * cos - first * sin) * factor).astype(BF16)

    def close(b):
        lanes = pl.ds(pl.multiple_of(b * rows, rows), rows)
        for h in range(heads):
            at = h * HEAD_DIM
            d_query = dquery_ref[b, at : at + HEAD_DIM]
            unrotate(b, at, HEAD_DIM**-0.5, d_query[:half], d_query[half:])
            d_key = dkey_ref[h, lanes].T
            unrotate(b, width + at, 1.0, d_key[:half], d_key[half:])
            dproj_ref[b, 2 * width + at : 2 * width + at + HEAD_DIM] = (
                dval_ref[h, lanes].T.astype(BF16)
            )
        d_proj = dproj_ref[b]
        acc_ref[...] += dot(d_proj, in_ref[b], 1, 0)
        part_ref[b] = dot(d_proj.T, wq_ref[...], 1, 1).astype(BF16)

    def attend(n, carry):
        for m, at_step in ((1, 1), (2, 2), (3, 4)):
            @pl.when(n == at_step)
            def _(m=m):
                a_copies[m].wait()
        late_part, last_part = (n + 6) // 8, (n + 2) // 8
        q_other = late_part - last_part
        k_other = (1 - late_part) + q_other * lax.rem(n + 1, 2)
        offset = (1 - late_part) * n + q_other * (n // 2 - 1) + last_part * (n - 6)
        i = lax.rem(xi + q_other, nx) * CORES + lax.rem(ci + offset, CORES)
        span = CORES * rows
        keys = pl.ds(pl.multiple_of(lax.rem(xi + k_other, nx) * span, span), span)
        for h in range(heads):
            at = h * HEAD_DIM
            query_t = proj_ref[i, at : at + HEAD_DIM]
            dmix_t = dmix_all[i, at : at + HEAD_DIM]
            mix_t = mix_ref[i, at : at + HEAD_DIM]
            inner = jnp.sum(dmix_t.astype(F32) * mix_t.astype(F32), axis=0, keepdims=True)
            probs = jnp.exp(dot(key_ref[h, keys], query_t, 1, 0) - lse_ref[i, h : h + 1])
            d_probs = dot(val_ref[h, keys], dmix_t, 1, 0)
            d_scores = (probs * (d_probs - inner)).astype(BF16)
            dval_ref[h, keys] += dot(probs.astype(BF16), dmix_t.T, 1, 0)
            dkey_ref[h, keys] += dot(d_scores, query_t.T, 1, 0)
            dquery_ref[i, at : at + HEAD_DIM] += dot(keyt_ref[at : at + HEAD_DIM, keys], d_scores, 1, 0)

        @pl.when(n == 1)
        def _():
            share_statistics()

        @pl.when((n == 5) | (n == 7))
        def _():
            plane = lax.rem(xi + 1 - last_part, nx)

            def one(c, carry):
                close(plane * CORES + c)
                return carry

            lax.fori_loop(0, CORES, one, 0)

        @pl.when(n == 5)
        def _():
            for p in range(parts):
                c_copies[1, p].start()

        @pl.when(n == 6)
        def _():
            to = lax.rem(xi + 1, nx) * CORES + ci
            for p in range(parts):
                at = pl.ds(p * piece, piece)
                c_copies[1, p].wait()
                part_ref[to, at] = (part_ref[to, at].astype(F32) + rc[1, at].astype(F32)).astype(BF16)
                x_copies[p].start()

        for m in range(2 * n_t):
            if f"n{m}" in BACK_PLAN:
                @pl.when(n == m)
                def _(m=m):
                    at_point(f"n{m}")

        return carry

    lax.fori_loop(0, 2 * n_t, attend, 0)
    for p in range(parts):
        c_copies[0, p].start()
    grads = acc_ref[...].T.astype(BF16)
    pair_ref[...] = grads[:, : 2 * width].reshape(pair_ref.shape)
    value_ref[...] = grads[:, 2 * width :].reshape(value_ref.shape)
    pair.start(0)
    value_sum.start(0)
    at_point("t0")
    for copy in d_copies:
        copy.wait()
    loads[3].wait()
    loads[4].wait()
    pair.advance(0)
    at_point("t1")
    value_sum.advance(0)
    at_point("t2")

    gain, scale = vec_ref[GAIN1 : GAIN1 + 1], 1.0 + vec_ref[SCALE_A : SCALE_A + 1]
    shift_sum = jnp.zeros((1, features), F32)
    nhat_sum = jnp.zeros((1, features), F32)
    for p in range(parts):
        c_copies[0, p].wait()
        x_copies[p].wait()
        at = pl.ds(p * (rows // parts), rows // parts)
        e = part_ref[t, at].astype(F32) + rc[0, at].astype(F32)
        for r in range(1, nx):
            e += rx[r - 1, at].astype(F32)
        x = x_ref[at].astype(F32)
        centred = x - mean_rows(x)
        inv = lax.rsqrt(mean_rows(centred * centred) + EPSILON)
        nhat = centred * inv
        shift_sum += sum_tokens(e)
        nhat_sum += sum_tokens(e * nhat)
        dn = e * (scale * gain)
        grad_in_ref[at] = dmid_ref[at] + inv * (
            dn - mean_rows(dn) - nhat * mean_rows(dn * nhat)
        )
    at_point("t3")
    late_ref[:, :features] = shift_sum
    late_ref[:, features : 2 * features] = nhat_sum * gain
    late_ref[:, 2 * features :] = nhat_sum * scale

    copies = []
    for r in range(1, n_t):
        copy = remote(
            late_ref, late_got.at[r - 1], s_v.at[r - 1], r_v.at[r - 1], d, lax.rem(t + r, n_t)
        )
        copy.start()
        copies.append(copy)
    value = late_ref[...]
    for r in range(1, n_t):
        copies[r - 1].wait()
        value += late_got[r - 1]
    late_mine[...] = value
    copies = [pltpu.make_async_copy(late_mine, late_all.at[d], s_l.at[0])]
    for r in range(1, n_d):
        copies.append(
            remote(
                late_mine, late_all.at[d], s_e.at[r - 1], r_e.at[r - 1], lax.rem(d + r, n_d), t
            )
        )
    for copy in copies:
        copy.start()
    at_point("t4")
    for s in range(n_d):
        for block, row in EARLY:
            flat_ref[s : s + 1, block * features : (block + 1) * features] = table_ref[
                s, row : row + 1
            ]
    for copy in copies:
        copy.wait()
    value = late_all[0, :, 2 * features :]
    for s in range(1, n_d):
        value += late_all[s, :, 2 * features :]
    gain_ref[...] = value
    for s in range(n_d):
        flat_ref[s : s + 1, : 2 * features] = late_all[s, :, : 2 * features]
    columns = ada_ref.shape[0]
    moved = pltpu.roll(flat_ref[...], lax.rem(n_d - d, n_d) * columns, 1)[:, :columns]
    rows_out[:, 0, :] = lax.dot_general(
        moved, ada_ref[...].astype(F32), (((1,), (0,)), ((), ())),
        precision=lax.Precision.HIGHEST, preferred_element_type=F32,
    )
    copies = [pltpu.make_async_copy(rows_out.at[d], rows_in.at[d], s_l.at[1])]
    for r in range(1, n_d):
        peer = lax.rem(d + r, n_d)
        copies.append(remote(rows_out.at[peer], rows_in.at[d], s_p.at[r - 1], r_p.at[r - 1], peer, t))
    for copy in copies:
        copy.start()
    at_point("t5")
    pair.advance(1)
    value_sum.advance(1)
    at_point("t6")
    at_point("end")
    for name, flow in flows.items():
        assert stage[name] == len(flow.path), name
    for copy in copies:
        copy.wait()
    gcond_ref[...] = jnp.sum(rows_in[:, 0, :], axis=0, keepdims=True)


def back_call(
    dmix, proj, mix, lse, cos, sin, attn_in, w_qkv, stat, x, dmid, vecs, ada_t, partial_sums, n_d, n_t
):
    parts = 4
    count = counts(n_d, n_t)
    nx, no = count["x"], count["z"]
    blocks, total, rows = proj.shape
    width = total // 3
    heads = width // HEAD_DIM
    length = blocks * rows
    features = attn_in.shape[2]
    part = features // n_d
    cond_width = ada_t.shape[1]
    cut = partial_sums[0].shape[-1]
    buffers = []
    for (dims, path), source in zip(BACK_SUMS, partial_sums):
        buffers += reduce_scratch(count, dims, path, source.shape[-2:])
    stages = sum(len(path) for _, path in BACK_SUMS)
    widest = max(count.values()) - 1
    late = (1, 3 * features)
    return pl.pallas_call(
        partial(back_kernel, n_d, n_t, parts, heads),
        name="back",
        out_shape=[
            struct((rows, features), F32),
            struct((3, part, width), F32),
            struct((part, 2 * cut), F32),
            struct((part, 2 * cut), F32),
            struct((width, part), F32),
            struct((n_d,) + stat.shape, F32),
            struct((n_d, 6 * features), F32),
            struct((1, features), F32),
            struct((1, cond_width), F32),
        ],
        in_specs=[VMEM] * 6 + [ANY] * 2 + [VMEM] + [ANY] * 2 + [VMEM] * 2 + [ANY] * 5,
        out_specs=[VMEM] * 9,
        scratch_shapes=[
            pltpu.VMEM(dmix.shape, BF16),
            pltpu.VMEM((heads, length, HEAD_DIM), BF16),
            pltpu.VMEM((width, length), BF16),
            pltpu.VMEM((heads, length, HEAD_DIM), BF16),
            pltpu.VMEM((heads, length, HEAD_DIM), F32),
            pltpu.VMEM((heads, length, HEAD_DIM), F32),
            pltpu.VMEM((n_t, width, rows), F32),
            pltpu.VMEM(proj.shape, BF16),
            pltpu.VMEM(attn_in.shape, BF16),
            pltpu.VMEM(w_qkv.shape, BF16),
            pltpu.VMEM((total, features), F32),
            pltpu.VMEM((no, INNER, part, 2 * width), BF16),
            pltpu.VMEM((no, INNER, part, width), BF16),
            pltpu.VMEM((nx, rows, features), BF16),
            pltpu.VMEM((nx - 1, rows, features), BF16),
            *reduce_scratch(count, "zy", "yz", (part, 2 * width), own=False),
            *reduce_scratch(count, "zy", "zy", (part, width), own=False),
            pltpu.VMEM((n_t - 1,) + stat.shape, F32),
            pltpu.VMEM(stat.shape, F32),
            pltpu.VMEM(x.shape, BF16),
            pltpu.VMEM(x.shape, F32),
            pltpu.VMEM(late, F32),
            pltpu.VMEM((n_t - 1,) + late, F32),
            pltpu.VMEM(late, F32),
            pltpu.VMEM((n_d,) + late, F32),
            pltpu.VMEM((n_d, 1, cond_width), F32),
            pltpu.VMEM((n_d, 1, cond_width), F32),
        ]
        + buffers
        + [
            DMA((n_t - 1,)), DMA((n_t - 1,)), DMA((6 + len(BACK_SUMS),)),
            DMA((stages + 4, widest)), DMA((stages + 4, widest)),
            DMA((n_t - 1,)), DMA((n_t - 1,)), DMA((n_d - 1,)), DMA((n_d - 1,)),
            DMA((nx, parts)), DMA((nx, parts)), DMA((nx - 1, parts)), DMA((nx - 1, parts)),
            DMA((n_t - 1,)), DMA((n_t - 1,)), DMA((n_d - 1,)), DMA((n_d - 1,)),
            DMA((n_d - 1,)), DMA((n_d - 1,)),
        ],
        compiler_params=params(2),
        cost_estimate=cost(45 * heads * length * length * HEAD_DIM, 40e6, heads * length * length),
    )(dmix, proj, mix, lse, cos, sin, attn_in, w_qkv, stat, x, dmid, vecs, ada_t, *partial_sums)


def finish_kernel(
    count, n_units, n_moved, table_ref, flat_ref, cond_ref, gain_in, gcond_in, *more
):
    sources, more = more[:n_moved], more[n_moved:]
    ada_ref, bias_ref, gain1_ref, gain2_ref, bdown_ref, bup_ref, root_ref, gcond_ref = more[:8]
    for src, dst in zip(sources, more[8:]):
        if len(dst.shape) > len(src.shape):
            dst[:, 0, :] = src[...]
        else:
            dst[...] = src[...]
    n_d = table_ref.shape[0]
    features = table_ref.shape[2]
    total = table_ref[0]
    for s in range(1, n_d):
        total += table_ref[s]
    root_ref[...] = jnp.sqrt(jnp.sum(total[S_SQ_A : S_SQ_R + 1], axis=1) / count)
    gain2_ref[...] = total[S_GAIN2]
    bdown_ref[...] = total[S_B_DOWN]
    for u in range(n_units):
        bup_ref[u * features : (u + 1) * features] = total[S_B_UP + u]
    gain1_ref[...] = gain_in[0]
    gcond_ref[...] = gcond_in[...]
    for block in range(6):
        at = slice(block * features, (block + 1) * features)
        value = jnp.zeros((cond_ref.shape[0], features), F32)
        for s in range(n_d):
            value += cond_ref[:, s : s + 1] * flat_ref[s : s + 1, at]
        ada_ref[:, at] = value
        bias_ref[at] = jnp.sum(flat_ref[:, at], axis=0)


def finish_call(table, flat, cond_t, gain, gcond, moved, count, n_units):
    rows, wide = moved[1].shape
    shapes = [a.shape for a in moved]
    shapes[1] = (rows, 1, wide)
    features = table.shape[2]
    width = cond_t.shape[0]
    return pl.pallas_call(
        partial(finish_kernel, count, n_units, len(moved)),
        name="finish",
        out_shape=[
            struct((width, 6 * features), F32),
            struct((6 * features,), F32),
            struct((features,), F32),
            struct((features,), F32),
            struct((features,), F32),
            struct((n_units * features,), F32),
            struct((3,), F32),
            struct((1, width), F32),
        ]
        + [struct(shape, a.dtype) for a, shape in zip(moved, shapes)],
        in_specs=[VMEM] * (5 + len(moved)),
        out_specs=[VMEM] * (8 + len(moved)),
        compiler_params=params(),
        cost_estimate=cost(1e7, 4e6),
    )(table, flat, cond_t, gain, gcond, *moved)


def shards(
    block_input, condition, modulation_weight, modulation_bias, first_gain, qkv_weight, out_weight,
    second_gain, up_weight, up_bias, down_weight, down_bias, grad_output,
):
    n_t, n_d = lax.axis_size("tensor"), lax.axis_size("dp")
    rows, sequences, features = block_input.shape
    assert sequences == 1
    length = rows * n_t
    part, width = qkv_weight.shape[1:]
    units = up_weight.shape[1]
    assert units == features and n_t % CORES == 0 and n_d % INNER == 0
    x = block_input.reshape(rows, features)
    g = grad_output.reshape(rows, features)
    ada_t = modulation_weight.T

    smalls = (first_gain, second_gain, down_bias, up_bias, condition, modulation_bias)
    inverse = 10000.0 ** (-np.arange(HEAD_DIM // 2) * 2.0 / HEAD_DIM)
    angles = inverse[:, None] * np.arange(length)[None, :]
    cos, sin = jnp.asarray(np.cos(angles), F32), jnp.asarray(np.sin(angles), F32)

    attn_in, proj, mix, lse, mix_own, vecs, cond_t, w_qkv, w_ul, w_dl, w_uh, w_dh, w_out = front_call(
        x, qkv_weight, smalls, ada_t, up_weight, down_weight.T, out_weight, cos, sin, n_d, n_t
    )
    stat_rows = -(-(S_B_UP + n_t) // 8) * 8
    out, d_middle, d_mix, stat, *partial_sums = middle_call(
        mix_own, x, g, vecs, w_ul, w_dl, w_uh, w_dh, w_out, stat_rows, n_d, n_t
    )
    grad_input, g_qkv, g_up, g_down, g_out, table, flat, gain1, grad_cond = back_call(
        d_mix, proj, mix, lse, cos, sin, attn_in, w_qkv.reshape(features, 3 * width), stat,
        x, d_middle, vecs, ada_t, partial_sums, n_d, n_t,
    )
    moved = (out, grad_input, g_qkv, g_up, g_down, g_out)
    grad_ada, grad_ada_b, gain1, gain2, b_down, b_up, roots, grad_cond, *moved = finish_call(
        table, flat, cond_t, gain1, grad_cond, moved, float(length * n_d * features), n_t
    )
    out, grad_input, g_qkv, g_up, g_down, g_out = moved
    return (
        out.reshape(block_input.shape), grad_input, grad_cond, grad_ada, grad_ada_b, gain1, g_qkv,
        g_out, gain2, g_up, b_up, g_down.T, b_down, roots,
    )


def solution(mesh):
    in_specs = (
        P("tensor", "dp", None),
        P("dp", None),
        P(None, "dp"),
        P("dp"),
        P("dp"),
        P(None, "dp", "tensor"),
        P("tensor", "dp"),
        P("dp"),
        P("dp", "tensor"),
        P("dp"),
        P("tensor", "dp"),
        P("dp"),
        P("tensor", "dp", None),
    )
    out_specs = (
        P("tensor", "dp", None),
        P("tensor", "dp", None),
        P("dp", None),
        P(),
        P(),
        P(),
        P(None, "dp", "tensor"),
        P("tensor", "dp"),
        P(),
        P("dp", "tensor"),
        P(),
        P("tensor", "dp"),
        P(),
        P(),
    )
    return jax.shard_map(shards, mesh=mesh, in_specs=in_specs, out_specs=out_specs, check_vma=False)
```

```python
from functools import partial

import jax
import jax.numpy as jnp
import numpy as np
from jax import lax
from jax.experimental import pallas as pl
from jax.experimental.pallas import tpu as pltpu
from jax.sharding import PartitionSpec as P

HEAD_DIM = 64
EPSILON = 1e-05
CORES = 2
INNER = 2
MESH = pl.DeviceIdType.MESH
VMEM_LIMIT = 58 << 20
GELU_C = float(np.sqrt(2.0 / np.pi))
GELU_A = 0.044715
F32 = jnp.float32
BF16 = jnp.bfloat16
ANY = pl.BlockSpec(memory_space=pl.ANY)
VMEM = pl.BlockSpec(memory_space=pltpu.VMEM)
DMA = pltpu.SemaphoreType.DMA


def dot(lhs, rhs, lhs_dim, rhs_dim):
    return lax.dot_general(
        lhs, rhs, (((lhs_dim,), (rhs_dim,)), ((), ())), preferred_element_type=F32
    )


def params(collective_id=None, **more):
    if collective_id is not None:
        more.update(collective_id=collective_id, has_side_effects=True)
    return pltpu.CompilerParams(vmem_limit_bytes=VMEM_LIMIT, **more)


def cost(flops, moved, special=0):
    return pl.CostEstimate(flops=int(flops), bytes_accessed=int(moved), transcendentals=int(special))


def struct(shape, dtype):
    return jax.ShapeDtypeStruct(shape, dtype)


def mean_rows(values):
    return jnp.mean(values, axis=-1, keepdims=True)


def sum_tokens(values):
    return jnp.sum(values, axis=0, keepdims=True)


GAIN1, SHIFT_A, SCALE_A, GATE_A, GAIN2, SHIFT_M, SCALE_M, GATE_M, B_DOWN, B_UP = range(10)
MOD_ROWS = (SHIFT_A, SCALE_A, GATE_A, SHIFT_M, SCALE_M, GATE_M)
S_GATE_A, S_SHIFT_M, S_SCALE_M, S_GATE_M, S_GAIN2, S_B_DOWN, S_SQ_A, S_SQ_M, S_SQ_R, S_B_UP = range(10)
L_SHIFT_A, L_SCALE_A, L_GAIN1 = range(3)


def order(k, xi, ci, nx):
    return lax.rem(xi + k // CORES, nx) * CORES + lax.rem(ci + k % CORES, CORES)


def mirror(k, nx):
    return (nx - k // CORES) % nx * CORES + (CORES - k % CORES) % CORES


def place(n_d, n_t):
    d, t = lax.axis_index("dp"), lax.axis_index("tensor")
    return d, t, d // INNER, lax.rem(d, INNER), t // CORES, lax.rem(t, CORES)


def greet(n_d, n_t):
    d, t = lax.axis_index("dp"), lax.axis_index("tensor")
    barrier = pltpu.get_barrier_semaphore()
    for r in range(1, n_t):
        pl.semaphore_signal(
            barrier, 1, device_id=(d, lax.rem(t + r, n_t)), device_id_type=MESH
        )
    for r in range(1, n_d):
        pl.semaphore_signal(
            barrier, 1, device_id=(lax.rem(d + r, n_d), t), device_id_type=MESH
        )
    pl.semaphore_wait(barrier, n_t - 1 + n_d - 1)


def remote(src, dst, send, recv, d, t):
    return pltpu.make_async_remote_copy(
        src_ref=src, dst_ref=dst, send_sem=send, recv_sem=recv, device_id=(d, t), device_id_type=MESH
    )


class Places:
    def __init__(self, n_d, n_t):
        d, t = lax.axis_index("dp"), lax.axis_index("tensor")
        self.d, self.t = d, t
        self.me = {"z": d // INNER, "y": lax.rem(d, INNER), "x": t // CORES, "c": lax.rem(t, CORES)}
        self.count = counts(n_d, n_t)

    def peer(self, axis, r):
        at = dict(self.me)
        at[axis] = lax.rem(at[axis] + r, self.count[axis])
        return at[axis], (at["z"] * INNER + at["y"], at["x"] * CORES + at["c"])


def counts(n_d, n_t):
    return {"z": n_d // INNER, "y": INNER, "x": n_t // CORES, "c": CORES}


class Spread:
    def __init__(self, places, dims, known, path, array, source, send, recv, row, lanes=slice(None)):
        self.path, self.flights = path, []
        for s, axis in enumerate(path):
            region = tuple(
                slice(None) if a in known or a in path[:s] else places.me[a] for a in dims
            ) + (slice(None), lanes)
            src = source if s == 0 else array.at[region]
            self.flights.append([])
            for r in range(1, places.count[axis]):
                _, (d, t) = places.peer(axis, r)
                self.flights[s].append(
                    remote(
                        src, array.at[region], send.at[row + s, r - 1], recv.at[row + s, r - 1], d, t
                    )
                )

    def start(self, s):
        for copy in self.flights[s]:
            copy.start()

    def wait(self, s):
        for copy in self.flights[s]:
            copy.wait()

    def advance(self, s, last=None):
        self.wait(s)
        if s + 1 < len(self.path) and s != last:
            self.start(s + 1)


class Reduce:
    def __init__(self, places, dims, path, source, own, met, results, send, recv, local, row):
        self.places, self.path, self.own, self.met = places, path, own, met
        self.results, self.flights, self.dims = results, [], []
        current = source
        for s, axis in enumerate(path):
            at = dims.index(axis)
            self.dims.append((current, dims, at))
            self.flights.append([])
            for r in range(1, places.count[axis]):
                to, (d, t) = places.peer(axis, r)
                self.flights[s].append(
                    remote(
                        current.at[(slice(None),) * at + (to,)], met[s].at[r - 1],
                        send.at[row + s, r - 1], recv.at[row + s, r - 1], d, t,
                    )
                )
            if s == 0:
                self.load = None
                if own is not None:
                    self.load = pltpu.make_async_copy(
                        current.at[(slice(None),) * at + (places.me[axis],)], own, local
                    )
            dims = dims.replace(axis, "")
            current = results[s]

    def start(self, s):
        for copy in self.flights[s]:
            copy.start()
        if s == 0 and self.load is not None:
            self.load.start()

    def advance(self, s):
        places, path = self.places, self.path
        for copy in self.flights[s]:
            copy.wait()
        current, dims, at = self.dims[s]
        rest = dims.replace(path[s], "")
        if s == 0 and self.load is not None:
            self.load.wait()
            current, at = self.own, None
        sizes = [places.count[a] for a in rest]

        def fold(n, carry):
            spot = []
            for size in reversed(sizes):
                spot.insert(0, lax.rem(n, size))
                n = n // size
            own = list(spot)
            if at is not None:
                own.insert(at, places.me[path[s]])
            value = current[tuple(own)].astype(F32)
            for r in range(places.count[path[s]] - 1):
                value += self.met[s][(r,) + tuple(spot)].astype(F32)
            if callable(self.results[s]):
                self.results[s](value)
            else:
                self.results[s][tuple(spot)] = value.astype(BF16)
            return carry

        if sizes:
            lax.fori_loop(0, int(np.prod(sizes)), fold, 0)
        else:
            fold(0, 0)
        if s + 1 < len(path):
            self.start(s + 1)


def reduce_scratch(count, dims, path, tail, own=True, last=True):
    shapes = []
    rest = dims.replace(path[0], "")
    if own:
        shapes.append(tuple(count[a] for a in rest) + tail)
    left = dims
    for axis in path:
        left = left.replace(axis, "")
        shapes.append((count[axis] - 1,) + tuple(count[a] for a in left) + tail)
    left = dims
    for axis in path if not last else path[:-1]:
        left = left.replace(axis, "")
        shapes.append(tuple(count[a] for a in left) + tail)
    return [pltpu.VMEM(shape, BF16) for shape in shapes]


FRONT_PATHS = {"ula": "zyxc", "ulb": "zxyc", "dla": "zxyc", "dlb": "zxyc", "o": "xyzc", "uh": "zy", "dh": "zx"}
FRONT_PLAN = {
    "pre": ("s ula",),
    "qz": ("a ula", "s ulb", "s dlb", "s o",),
    "X": ("s dla",),
    "n": ("a ulb", "a dlb", "a o", "s uh",),
    "g": ("a dla",),
    "p1": ("s dh",),
    "p3": ("a ula", "a ulb", "a dlb", "a o",),
    "a0": ("a uh",),
    "a1": ("a dla",),
    "a3": ("a ula", "a dh",),
    "a4": ("a ula", "a ulb", "a dlb",),
    "a5": ("a ulb", "a dlb",),
    "end": ("a uh", "a o", "a dla", "a o", "a dh", "a dla",),
}
BACK_DIMS = {"ul": "zy", "dl": "zx", "uh": "zyx", "dh": "zyx", "o": "czyx"}
BACK_PATHS = {"ul": "yz", "dl": "xz", "uh": "xyz", "dh": "yxz", "o": "czxy"}
BACK_PLAN = {
    "0": ("s dh", "s o",),
    "n0": ("a o",),
    "n1": ("s uh", "s dl", "s ul",),
    "n2": ("a dh",),
    "n5": ("a dl", "a ul",),
    "n6": ("a dh", "a o", "a uh",),
    "n7": ("a ul", "a dl",),
    "t4": ("a dh",),
    "t5": ("a uh", "a o",),
    "t0": ("a uh",),
    "t2": ("a o",),
}
BACK_SUMS = tuple((BACK_DIMS[name], BACK_PATHS[name]) for name in BACK_DIMS)
CODE = {"z": 2, "y": 2, "x": 2, "c": 2}
EARLY = ((2, S_GATE_A), (3, S_SHIFT_M), (4, S_SCALE_M), (5, S_GATE_M))


def front_kernel(
    n_d, n_t, parts, heads, cond_at, bias_at, sizes,
    x_ref, qkv_ref, gain1_ref, gain2_ref, bdown_ref, bup_ref, cond_in, ada_b_ref,
    ada_ref, up_ref, down_ref, outw_ref, cos_ref, sin_ref,
    in_all, proj_ref, mix_ref, lse_ref, mix_own, vec_ref, cond_ref, w_all, w_ul, w_dl, w_uh, w_dh, w_out,
    x_all, w_pack, wt_ref, out_pack, small_ref, small_all, mod_all, mod_rows, key_ref,
    s_x, r_x, s_c, r_c, s_f, r_f, s_z, r_z, s_y, r_y, s_s, r_s, s_m, r_m, s_l,
    s_w, r_w, s_o, r_o,
):
    d, t, oi, ii, xi, ci = place(n_d, n_t)
    nx, no = n_t // CORES, n_d // INNER
    other = xi * CORES + (1 - ci)
    piece = x_ref.shape[0] // parts
    rows, features = x_ref.shape
    width = qkv_ref.shape[2]
    half = HEAD_DIM // 2
    cut = w_ul.shape[5]
    low_half, high_half = slice(0, cut), slice(cut, 2 * cut)
    for j in range(3):
        w_pack[:, j * width : (j + 1) * width] = qkv_ref[j]
    out_pack[:, :width] = outw_ref[...].T
    small_ref[...] = jnp.zeros_like(small_ref)
    at = 0
    for ref in (gain1_ref, gain2_ref, bdown_ref, bup_ref):
        small_ref[:, at : at + ref.shape[0]] = ref[...].astype(F32).reshape(1, -1)
        at += ref.shape[0]
    small_ref[:, cond_at : cond_at + cond_in.shape[1]] = cond_in[...].astype(F32)
    small_ref[:, bias_at : bias_at + ada_b_ref.shape[0]] = ada_b_ref[...].astype(F32).reshape(1, -1)
    if out_pack.shape[1] > width:
        out_pack[:, width:] = jnp.zeros((out_pack.shape[0], out_pack.shape[1] - width), BF16)
    greet(n_d, n_t)
    places = Places(n_d, n_t)
    flows = {}
    split = 2 * cut // 3 // 128 * 128
    whole, first_lanes, last_lanes = slice(None), slice(0, split), slice(split, cut)
    for row, (name, dims, array, source, lanes) in enumerate(
        (
            ("ula", "zyxc", w_ul, up_ref.at[:, first_lanes], first_lanes),
            ("ulb", "zyxc", w_ul, up_ref.at[:, last_lanes], last_lanes),
            ("dla", "zyxc", w_dl, down_ref.at[:, first_lanes], first_lanes),
            ("dlb", "zyxc", w_dl, down_ref.at[:, last_lanes], last_lanes),
            ("o", "zyxc", w_out, out_pack, whole),
            ("uh", "zy", w_uh, up_ref.at[:, high_half], whole),
            ("dh", "zx", w_dh, down_ref.at[:, high_half], whole),
        )
    ):
        flows[name] = Spread(
            places, dims, "", FRONT_PATHS[name], array, source, s_w, r_w, 4 * row, lanes
        )
    stage = dict.fromkeys(flows, 0)

    def at_point(point):
        for step in FRONT_PLAN.get(point, ()):
            what, name = step.split()
            if what == "s":
                flows[name].start(0)
            else:
                flows[name].advance(stage[name])
                stage[name] += 1

    s_copies = []
    for r in range(1, n_d):
        copy = remote(
            small_ref, small_all.at[d], s_s.at[r - 1], r_s.at[r - 1], lax.rem(d + r, n_d), t
        )
        copy.start()
        s_copies.append(copy)
    at_point("pre")
    x_copies = []
    for r in range(1, nx):
        peer = lax.rem(xi + r, nx) * CORES + ci
        for p in range(parts):
            at = pl.ds(p * piece, piece)
            copy = remote(
                x_ref.at[at], x_all.at[t, at], s_x.at[r - 1, p], r_x.at[r - 1, p], d, peer
            )
            copy.start()
            x_copies.append((r, p, copy))
    z_copies = []
    for r in range(1, no):
        copy = remote(
            w_pack, w_all.at[d], s_z.at[r - 1], r_z.at[r - 1], lax.rem(oi + r, no) * INNER + ii, t
        )
        copy.start()
        z_copies.append(copy)
    y_copies = []
    for q in range(1, INNER):
        copy = remote(
            w_pack, w_all.at[d], s_y.at[q - 1, 0], r_y.at[q - 1, 0],
            oi * INNER + lax.rem(ii + q, INNER), t,
        )
        copy.start()
        y_copies.append(copy)
    core_copy = remote(x_ref, x_all.at[t], s_c, r_c, d, other)
    core_copy.start()
    local = []
    for n, (src, dst) in enumerate(
        (
            (small_ref, small_all.at[d]),
            (x_ref, x_all.at[t]),
            (w_pack, w_all.at[d]),
            (up_ref.at[:, low_half], w_ul.at[oi, ii, xi, ci]),
            (down_ref.at[:, low_half], w_dl.at[oi, ii, xi, ci]),
            (up_ref.at[:, high_half], w_uh.at[oi, ii]),
            (down_ref.at[:, high_half], w_dh.at[oi, xi]),
            (out_pack, w_out.at[oi, ii, xi, ci]),
        )
    ):
        copy = pltpu.make_async_copy(src, dst, s_l.at[n])
        copy.start()
        local.append(copy)

    at_point("0")

    local[0].wait()
    for copy in s_copies:
        copy.wait()
    cond = small_all[:, 0, cond_at : cond_at + ada_ref.shape[1]]
    for s in range(n_d):
        cond_ref[:, s : s + 1] = cond[s : s + 1].T
    bias = small_ref[:, bias_at : bias_at + ada_ref.shape[0]]
    mod_rows[:, 0, :] = dot(cond.astype(BF16), ada_ref[...], 1, 1) + bias
    own_mod = pltpu.make_async_copy(mod_rows.at[d], mod_all.at[d], s_l.at[8])
    own_mod.start()
    m_copies = []
    for r in range(1, n_d):
        peer = lax.rem(d + r, n_d)
        copy = remote(mod_rows.at[peer], mod_all.at[d], s_m.at[r - 1], r_m.at[r - 1], peer, t)
        copy.start()
        m_copies.append(copy)
    for r in range(1, no):
        z_copies[r - 1].wait()
        origin = lax.rem(oi + no - r, no) * INNER + ii
        for q in range(1, INNER):
            copy = remote(
                w_all.at[origin], w_all.at[origin], s_y.at[q - 1, r], r_y.at[q - 1, r],
                oi * INNER + lax.rem(ii + q, INNER), t,
            )
            copy.start()
            y_copies.append(copy)
    for n in range(3, 8):
        local[n].wait()
    at_point("qz")
    f_copies = []
    for r, p, copy in x_copies:
        copy.wait()
        origin = lax.rem(xi + nx - r, nx) * CORES + ci
        at = pl.ds(p * piece, piece)
        copy = remote(
            x_all.at[origin, at], x_all.at[origin, at],
            s_f.at[r - 1, p], r_f.at[r - 1, p], d, other,
        )
        copy.start()
        f_copies.append(copy)

    at_point("X")
    for copy in m_copies + [own_mod]:
        copy.wait()
    def put(first, piece_of, count):
        for s in range(n_d):
            value = piece_of(s)
            start = s * count
            done = 0
            while done < count:
                row, column = divmod(start + done, features)
                take = min(count - done, features - column)
                vec_ref[first + row : first + row + 1, column : column + take] = value[
                    :, done : done + take
                ]
                done += take

    vec_ref[...] = jnp.zeros_like(vec_ref)
    at = 0
    for first, count in sizes:
        put(first, lambda s: small_all[s, :, at : at + count], count)
        at += count
    columns = ada_ref.shape[0]
    for s in range(n_d):
        done = 0
        while done < columns:
            row, column = divmod(s * columns + done, features)
            take = min(columns - done, features - column)
            row = MOD_ROWS[row]
            vec_ref[row : row + 1, column : column + take] = mod_all[s, :, done : done + take]
            done += take

    for copy in f_copies + [local[1], core_copy]:
        copy.wait()

    def norm(b, carry):
        x = x_all[b].astype(F32)
        centred = x - mean_rows(x)
        normed = centred * lax.rsqrt(mean_rows(centred * centred) + EPSILON)
        normed = normed * vec_ref[GAIN1 : GAIN1 + 1]
        low = (normed * (1.0 + vec_ref[SCALE_A : SCALE_A + 1]) + vec_ref[SHIFT_A : SHIFT_A + 1])
        in_all[b] = low.astype(BF16)
        return carry

    lax.fori_loop(0, n_t, norm, 0)
    at_point("n")
    for copy in y_copies + [local[2]]:
        copy.wait()
    wt_ref[...] = w_all[...].reshape(features, 3 * width).T

    at_point("g")

    def project(b, carry):
        proj = dot(wt_ref[...], in_all[b], 1, 1)
        lanes = pl.ds(pl.multiple_of(b * rows, rows), rows)
        cos, sin = cos_ref[:, lanes], sin_ref[:, lanes]
        for j in range(2):
            factor = HEAD_DIM**-0.5 if j == 0 else 1.0
            for h in range(heads):
                at = j * width + h * HEAD_DIM
                first, last = proj[at : at + half], proj[at + half : at + HEAD_DIM]
                top = ((first * cos - last * sin) * factor).astype(BF16)
                bottom = ((last * cos + first * sin) * factor).astype(BF16)
                proj_ref[b, at : at + half] = top
                proj_ref[b, at + half : at + HEAD_DIM] = bottom
                if j == 1:
                    key_ref[h, lanes, :] = jnp.concatenate([top, bottom], axis=0).T
        proj_ref[b, 2 * width :] = proj[2 * width :].astype(BF16)

        for m in range(n_t):
            if f"p{m}" in FRONT_PLAN:
                @pl.when(b == m)
                def _(m=m):
                    at_point(f"p{m}")

        return carry

    lax.fori_loop(0, n_t, project, 0)

    def attend(u, carry):
        plane = lax.rem(xi + nx - 1 - u // heads, nx)
        h = lax.rem(u, heads)
        at = pl.ds(pl.multiple_of(h * HEAD_DIM, HEAD_DIM), HEAD_DIM)
        value_at = pl.ds(pl.multiple_of(2 * width + h * HEAD_DIM, HEAD_DIM), HEAD_DIM)
        first = plane * CORES
        query = jnp.concatenate([proj_ref[first + c, at] for c in range(CORES)], axis=1)
        scores = dot(key_ref[h], query, 1, 0)
        top = jnp.max(scores, axis=0, keepdims=True)
        grown = jnp.exp(scores - top)
        total = jnp.sum(grown, axis=0, keepdims=True)
        value = jnp.concatenate([proj_ref[v, value_at] for v in range(n_t)], axis=1)
        mixed = (dot(value, grown.astype(BF16), 1, 0) / total).astype(BF16)
        log_total = top + jnp.log(total)
        for c in range(CORES):
            part = slice(c * rows, (c + 1) * rows)
            mix_ref[first + c, at] = mixed[:, part]
            lse_ref[first + c, pl.ds(h, 1)] = log_total[:, part]
        for r in range(nx):
            @pl.when(u == (nx - r) * heads - 1)
            def _(r=r):
                for c in range(CORES):
                    if r * CORES + c > 0:
                        o_copies[r * CORES + c].start()

        for m in range(nx * heads):
            if f"a{m}" in FRONT_PLAN:
                @pl.when(u == m)
                def _(m=m):
                    at_point(f"a{m}")

        return carry

    o_copies = {}
    for m in range(1, n_t):
        b = order(m, xi, ci, nx)
        o_copies[m] = remote(
            mix_ref.at[b], mix_own.at[t], s_o.at[m - 1], r_o.at[mirror(m, nx) - 1], d, b
        )
    lax.fori_loop(0, nx * heads, attend, 0)
    mine = pltpu.make_async_copy(mix_ref.at[t], mix_own.at[t], s_l.at[9])
    mine.start()
    at_point("end")
    for name, flow in flows.items():
        assert stage[name] == len(flow.path), name
    mine.wait()
    for copy in list(o_copies.values()):
        copy.wait()


def front_call(x, qkv, smalls, ada_t, up, down_t, outw, cos, sin, n_d, n_t):
    cond, ada_b = smalls[4:]
    sizes = tuple(zip((GAIN1, GAIN2, B_DOWN, B_UP), (a.shape[0] for a in smalls[:4])))
    cond_at = -(-sum(size for _, size in sizes) // 128) * 128
    bias_at = cond_at + cond.shape[1]
    small = bias_at + ada_b.shape[0]
    parts = 4
    nx, no = n_t // CORES, n_d // INNER
    rows, features = x.shape
    part, width = qkv.shape[1:]
    heads = width // HEAD_DIM
    length = rows * n_t
    wide = -(-width // 128) * 128
    units = up.shape[1]
    steps = max(no, INNER, nx) - 1
    cut = units // 2
    grid_of = (no, INNER, nx, CORES, part)
    columns = ada_t.shape[0]
    return pl.pallas_call(
        partial(front_kernel, n_d, n_t, parts, heads, cond_at, bias_at, sizes),
        name="front",
        out_shape=[
            struct((n_t, rows, features), BF16),
            struct((n_t, 3 * width, rows), BF16),
            struct((n_t, width, rows), BF16),
            struct((n_t, heads, rows), F32),
            struct((n_t, width, rows), BF16),
            struct((16, features), F32),
            struct((ada_t.shape[1], n_d), F32),
            struct((n_d, part, 3 * width), BF16),
            struct(grid_of + (cut,), BF16),
            struct(grid_of + (cut,), BF16),
            struct((no, INNER, part, cut), BF16),
            struct((no, nx, part, cut), BF16),
            struct(grid_of + (wide,), BF16),
        ],
        in_specs=[VMEM] * 9 + [ANY] * 2 + [VMEM] * 3,
        out_specs=[VMEM] * 8 + [ANY] * 5,
        scratch_shapes=[
            pltpu.VMEM((n_t, rows, features), BF16),
            pltpu.VMEM((part, 3 * width), BF16),
            pltpu.VMEM((3 * width, features), BF16),
            pltpu.VMEM((part, wide), BF16),
            pltpu.VMEM((1, small), F32),
            pltpu.VMEM((n_d, 1, small), F32),
            pltpu.VMEM((n_d, 1, columns), F32),
            pltpu.VMEM((n_d, 1, columns), F32),
            pltpu.VMEM((heads, length, HEAD_DIM), BF16),
            DMA((nx - 1, parts)), DMA((nx - 1, parts)), DMA, DMA,
            DMA((nx - 1, parts)), DMA((nx - 1, parts)),
            DMA((no - 1,)), DMA((no - 1,)),
            DMA((INNER - 1, no)), DMA((INNER - 1, no)),
            DMA((n_d - 1,)), DMA((n_d - 1,)), DMA((n_d - 1,)), DMA((n_d - 1,)),
            DMA((10,)),
            DMA((28, steps)), DMA((28, steps)),
            DMA((n_t - 1,)), DMA((n_t - 1,)),
        ],
        compiler_params=params(0),
        cost_estimate=cost(20 * heads * length * length * HEAD_DIM, 40e6, heads * length * length),
    )(x, qkv, *smalls, ada_t, up, down_t, outw, cos, sin)


def middle_kernel(
    n_d, n_t,
    mix_ref, x_ref, g_ref, vec_ref, ul_ref, dl_ref, uh_ref, dh_ref, wout_ref,
    out_ref, dmid_ref, dmix_ref, stat_ref, hul_ref, hdl_ref, huh_ref, hdh_ref, gout_ref,
    up_buf, down_buf, o_buf, go_buf,
    attn_ref, low_ref, lowt_ref, dl_t_ref, dlt_ref, acc_out, acc_in,
    mul_c, rul, mul_x, mdl_c, mdl_y, rdl, muh, mdh,
    s_u, s_d, s_o, s_w, r_w, s_r, r_r,
):
    places = Places(n_d, n_t)
    count, me = places.count, places.me
    rows, features = x_ref.shape
    width = mix_ref.shape[1]
    cut = up_buf.shape[-1]
    wide = wout_ref.shape[-1]
    loads = [
        pltpu.make_async_copy(wout_ref, o_buf, s_o.at[0]),
        pltpu.make_async_copy(ul_ref, up_buf.at[0], s_u.at[0]),
        pltpu.make_async_copy(dl_ref, down_buf.at[0], s_d.at[0]),
        pltpu.make_async_copy(uh_ref, up_buf.at[1, :, :, me["x"], me["c"]], s_u.at[1]),
        pltpu.make_async_copy(dh_ref, down_buf.at[1, :, me["y"], :, me["c"]], s_d.at[1]),
    ]
    for copy in loads:
        copy.start()
    greet(n_d, n_t)
    nx = count["x"]
    every, mx, my, mc = slice(None), me["x"], me["y"], me["c"]
    taken = [0]

    def send(target, region, axis, r, source=None):
        at = target.at[(1,) + region]
        n = taken[0]
        taken[0] += 1
        return remote(
            at if source is None else source, at, s_w.at[n], r_w.at[n], *places.peer(axis, r)[1]
        )

    own_up = [send(up_buf, (every, every, mx, mc), "c", 1, uh_ref)]
    own_down = [send(down_buf, (every, my, every, mc), "c", 1, dh_ref)]
    near_down, far_down, near_on, far_on, far_up = [], [], [], [], []
    for r in range(1, INNER):
        near_down.append(send(down_buf, (every, my, mx, mc), "y", r, dh_ref.at[:, mx]))
        near_on.append(send(down_buf, (every, places.peer("y", r)[0], mx, mc), "c", 1))
    for r in range(1, nx):
        far_up.append(send(up_buf, (every, every, mx, mc), "x", r, uh_ref))
        far_on.append(send(up_buf, (every, every, places.peer("x", r)[0], mc), "c", 1))
    for r in range(1, INNER):
        for q in range(1, nx):
            x_at = places.peer("x", q)[0]
            far_down.append(send(down_buf, (every, my, x_at, mc), "y", r, dh_ref.at[:, x_at]))
            far_on.append(
                send(down_buf, (every, places.peer("y", r)[0], x_at, mc), "c", 1)
            )
    for copy in near_down + far_up + own_up + own_down + far_down:
        copy.start()
    planes = [lax.rem(me["x"] + nx - 1 - n, nx) for n in range(nx)]
    ul = [
        Reduce(
            places, "zyc", "c", up_buf.at[2, :, :, planes[n]], None, [mul_c.at[n]], [rul.at[n]],
            s_r, r_r, None, n,
        )
        for n in range(nx)
    ]
    ul_x = [
        remote(
            rul.at[nx - 1 - r], mul_x.at[r - 1], s_r.at[4 * nx + 3, r - 1], r_r.at[4 * nx + 3, r - 1],
            *places.peer("x", r)[1],
        )
        for r in range(1, nx)
    ]
    dl = [
        Reduce(
            places, "zyc", "c", down_buf.at[2, :, :, planes[n]], None, [mdl_c.at[n]],
            [rdl.at[:, :, planes[n]]], s_r, r_r, None, nx + n,
        )
        for n in range(nx)
    ]
    dl_y = [
        Reduce(
            places, "zy", "y", rdl.at[:, :, planes[n]], None, [mdl_y.at[n]],
            [rdl.at[:, my, planes[n]]], s_r, r_r, None, 3 * nx + 3 + n,
        )
        for n in range(nx)
    ]
    high_up, high_down = up_buf.at[0, :, :, :, me["c"]], down_buf.at[0, :, :, :, me["c"]]
    uh = Reduce(places, "zyxc", "c", up_buf.at[0], None, [muh], [high_up], s_r, r_r, None, 2 * nx + 1)
    dh = Reduce(
        places, "zyxc", "c", down_buf.at[0], None, [mdh], [high_down], s_r, r_r, None, 2 * nx + 2
    )
    keeps = [
        pltpu.make_async_copy(go_buf, gout_ref, s_o.at[1]),
        pltpu.make_async_copy(high_up, huh_ref, s_o.at[2]),
        pltpu.make_async_copy(high_down, hdh_ref, s_o.at[3]),
        pltpu.make_async_copy(rul.at[nx - 1], hul_ref, s_o.at[4]),
        pltpu.make_async_copy(rdl.at[:, me["y"]], hdl_ref, s_o.at[5]),
    ]
    vec = lambda row: vec_ref[row : row + 1]
    cot = g_ref[...].astype(F32)
    d_mlp = (vec(GATE_M) * cot).astype(BF16)
    dl_t_ref[...] = d_mlp
    dlt_ref[...] = d_mlp.T
    stat_ref[...] = jnp.zeros_like(stat_ref)
    stat_ref[S_B_DOWN : S_B_DOWN + 1] = sum_tokens(d_mlp.astype(F32))
    if wide > width:
        go_buf[...] = jnp.zeros_like(go_buf)
    loads[0].wait()
    w_out = lambda b: o_buf[:, :, b // CORES, b % CORES].reshape(features, wide)[:, :width]
    attn_out = jnp.zeros((rows, features), F32)
    for b in range(n_t):
        attn_out += dot(mix_ref[b].T, w_out(b), 1, 1)
    attn_ref[...] = attn_out
    branch = vec(GATE_A) * attn_out
    stat_ref[S_SQ_A : S_SQ_A + 1] = sum_tokens(branch * branch)
    middle = x_ref[...].astype(F32) + branch
    dmid_ref[...] = middle
    centred = middle - mean_rows(middle)
    inv = lax.rsqrt(mean_rows(centred * centred) + EPSILON)
    low = (centred * inv * vec(GAIN2) * (1.0 + vec(SCALE_M)) + vec(SHIFT_M)).astype(BF16)
    low_ref[...] = low
    lowt_ref[...] = low.T
    acc_out[...] = jnp.zeros_like(acc_out)
    acc_in[...] = jnp.zeros_like(acc_in)
    loads[1].wait()
    loads[2].wait()

    def block(n, carry):
        j = n // nx
        step = lax.rem(n, nx)
        p = lax.rem(mx + (1 - j) * (nx - 1 - step) + j * step, nx)
        slot = 2 - 2 * j
        lanes = pl.ds(pl.multiple_of(j * cut, cut), cut)

        @pl.when(n == nx)
        def _():
            for copy in loads[3:] + own_up + own_down + near_on:
                copy.wait()

        @pl.when(n == nx + 1)
        def _():
            for copy in far_on:
                copy.wait()

        both = lambda buf: jnp.concatenate(
            [buf[j, :, :, p, c].reshape(features, cut) for c in range(CORES)], axis=1
        )
        up, down = both(up_buf), both(down_buf)
        bias = jnp.concatenate(
            [vec_ref[pl.ds(B_UP + p * CORES + c, 1), lanes] for c in range(CORES)], axis=1
        )
        hidden = dot(low_ref[...], up, 1, 0) + bias
        square = hidden * hidden
        bent = jnp.tanh(GELU_C * hidden * (1.0 + GELU_A * square))
        half = 0.5 * (1.0 + bent)
        active = (hidden * half).astype(BF16)
        slope = half + (0.5 * GELU_C) * hidden * (1.0 - bent * bent) * (
            1.0 + (3.0 * GELU_A) * square
        )
        acc_out[...] += dot(active, down, 1, 1)
        for m in range(1, nx):
            @pl.when(n == m)
            def _(m=m):
                ul[m - 1].advance(0)
                ul_x[nx - 1 - m].start()
                dl[m - 1].advance(0)
                dl_y[m - 1].start(0)

        @pl.when(n == nx)
        def _():
            ul[nx - 1].advance(0)
            dl[nx - 1].advance(0)
            dl_y[nx - 1].start(0)
            for copy in far_up + far_down:
                copy.wait()
            for copy in far_on:
                copy.start()

        grad_down = dot(dlt_ref[...], active, 1, 0).astype(BF16)
        d_hidden = (dot(dl_t_ref[...], down, 1, 0) * slope).astype(BF16)
        sums = sum_tokens(d_hidden.astype(F32))
        for c in range(CORES):
            stat_ref[pl.ds(S_B_UP + p * CORES + c, 1), lanes] = sums[:, c * cut : (c + 1) * cut]
        grad_up = dot(lowt_ref[...], d_hidden, 1, 0).astype(BF16)
        acc_in[...] += dot(d_hidden, up, 1, 1)
        for c in range(CORES):
            lanes_of = slice(c * cut, (c + 1) * cut)
            shape = up_buf.shape[1:3] + (-1, cut)
            down_buf[slot, :, :, p, c] = grad_down[:, lanes_of].reshape(shape)
            up_buf[slot, :, :, p, c] = grad_up[:, lanes_of].reshape(shape)

        for m in range(nx):
            @pl.when(n == m)
            def _(m=m):
                ul[m].start(0)
                dl[m].start(0)
                if m == 0:
                    for copy in near_down:
                        copy.wait()
                    for copy in near_on:
                        copy.start()

        return carry

    lax.fori_loop(0, 2 * nx, block, 0)
    uh.start(0)
    dh.start(0)
    middle = dmid_ref[...]
    mlp_out = acc_out[...] + vec(B_DOWN)
    mlp_branch = vec(GATE_M) * mlp_out
    result = middle + mlp_branch
    out_ref[...] = result.astype(BF16)
    cot = g_ref[...].astype(F32)
    stat_ref[S_SQ_M : S_SQ_M + 1] = sum_tokens(mlp_branch * mlp_branch)
    stat_ref[S_SQ_R : S_SQ_R + 1] = sum_tokens(result * result)
    stat_ref[S_GATE_M : S_GATE_M + 1] = sum_tokens(cot * mlp_out)
    e = acc_in[...]
    centred = middle - mean_rows(middle)
    inv = lax.rsqrt(mean_rows(centred * centred) + EPSILON)
    nhat = centred * inv
    gain, scale = vec(GAIN2), 1.0 + vec(SCALE_M)
    by_nhat = sum_tokens(e * nhat)
    stat_ref[S_SHIFT_M : S_SHIFT_M + 1] = sum_tokens(e)
    stat_ref[S_SCALE_M : S_SCALE_M + 1] = by_nhat * gain
    stat_ref[S_GAIN2 : S_GAIN2 + 1] = by_nhat * scale
    dn = e * (scale * gain)
    d_middle = cot + inv * (dn - mean_rows(dn) - nhat * mean_rows(dn * nhat))
    dmid_ref[...] = d_middle
    stat_ref[S_GATE_A : S_GATE_A + 1] = sum_tokens(d_middle * attn_ref[...])
    d_attn = (vec(GATE_A) * d_middle).astype(BF16)
    d_attn_t = d_attn.T
    for b in range(n_t):
        dmix_ref[b] = dot(d_attn, w_out(b), 1, 0).astype(BF16).T
        go_buf[b % CORES, :, :, b // CORES, :, :width] = (
            dot(d_attn_t, mix_ref[b], 1, 1).astype(BF16).reshape(go_buf.shape[1:3] + (-1, width))
        )
    keeps[0].start()
    uh.advance(0)
    keeps[1].start()
    dh.advance(0)
    keeps[2].start()
    for one in ul_x:
        one.wait()
    no = count["z"]

    def fold(n, carry):
        at = (n // INNER, lax.rem(n, INNER))
        value = rul[(nx - 1,) + at].astype(F32)
        for r in range(nx - 1):
            value += mul_x[(r,) + at].astype(F32)
        rul[(nx - 1,) + at] = value.astype(BF16)
        return carry

    lax.fori_loop(0, no * INNER, fold, 0)
    keeps[3].start()
    for one in dl_y:
        one.advance(0)
    keeps[4].start()
    for copy in keeps:
        copy.wait()


def middle_call(mix, x, g, vecs, w_ul, w_dl, w_uh, w_dh, w_out, stat_rows, n_d, n_t):
    rows, features = x.shape
    cut = w_ul.shape[-1]
    part, wide = w_out.shape[-2:]
    width = mix.shape[1]
    count = counts(n_d, n_t)
    no, nx = count["z"], count["x"]
    per = (3,) + w_ul.shape
    plane = (no, INNER, part, cut)
    tail = (part, cut)
    g_out = (CORES, no, INNER, nx, part, wide)
    return pl.pallas_call(
        partial(middle_kernel, n_d, n_t),
        name="middle",
        out_shape=[
            struct((rows, features), BF16),
            struct((rows, features), F32),
            struct((n_t, width, rows), BF16),
            struct((stat_rows, features), F32),
            struct((no, INNER) + tail, BF16),
            struct((no, nx) + tail, BF16),
            struct((no, INNER, nx) + tail, BF16),
            struct((no, INNER, nx) + tail, BF16),
            struct(g_out, BF16),
        ],
        in_specs=[VMEM] * 4 + [ANY] * 5,
        out_specs=[VMEM] * 4 + [ANY] * 5,
        scratch_shapes=[
            pltpu.VMEM(per, BF16), pltpu.VMEM(per, BF16), pltpu.VMEM(w_out.shape, BF16),
            pltpu.VMEM(g_out, BF16),
            pltpu.VMEM((rows, features), F32),
            pltpu.VMEM((rows, features), BF16),
            pltpu.VMEM((features, rows), BF16),
            pltpu.VMEM((rows, features), BF16),
            pltpu.VMEM((features, rows), BF16),
            pltpu.VMEM((rows, features), F32),
            pltpu.VMEM((rows, features), F32),
        ]
        + [
            pltpu.VMEM((nx, 1) + plane, BF16), pltpu.VMEM((nx,) + plane, BF16),
            pltpu.VMEM((nx - 1,) + plane, BF16),
            pltpu.VMEM((nx, 1) + plane, BF16), pltpu.VMEM((nx, INNER - 1, no) + tail, BF16),
            pltpu.VMEM((no, INNER, nx) + tail, BF16),
            pltpu.VMEM((1, no, INNER, nx) + tail, BF16),
            pltpu.VMEM((1, no, INNER, nx) + tail, BF16),
        ]
        + [
            DMA((2,)), DMA((2,)), DMA((6,)),
            DMA((2 + 2 * (INNER - 1 + nx - 1 + (INNER - 1) * (nx - 1)),)),
            DMA((2 + 2 * (INNER - 1 + nx - 1 + (INNER - 1) * (nx - 1)),)),
            DMA((4 * nx + 4, max(nx, INNER, CORES) - 1)), DMA((4 * nx + 4, max(nx, INNER, CORES) - 1)),
        ],
        compiler_params=params(1),
        cost_estimate=cost(2 * rows * features * features * (6 * n_t + 4), 30e6),
    )(mix, x, g, vecs, w_ul, w_dl, w_uh, w_dh, w_out)


def back_kernel(
    n_d, n_t, parts, heads,
    dmix_ref, proj_ref, mix_ref, lse_ref, cos_ref, sin_ref, in_hbm, wq_hbm, stat_ref,
    x_hbm, dmid_hbm, vec_ref, ada_ref,
    hul_ref, hdl_ref, huh_ref, hdh_ref, gout_ref,
    grad_in_ref, gq_ref, up_ref, down_ref, out_ref, table_ref, flat_ref, gain_ref, gcond_ref,
    dmix_all, key_ref, keyt_ref, val_ref, dkey_ref, dval_ref, dquery_ref, dproj_ref, in_ref, wq_ref,
    acc_ref, pair_ref, value_ref, rc, rx, pair_y, pair_z, pair_sum, value_z, value_y, value_mid,
    got_ref, mine_ref,
    x_ref, dmid_ref, late_ref, late_got, late_mine, late_all, rows_out, rows_in, *more,
):
    buffers, at = [], 0
    for size in (len(reduce_scratch(CODE, dims, path, (1, 1))) for dims, path in BACK_SUMS):
        buffers.append(more[at : at + size])
        at += size
    (
        s_a, r_a, s_l, s_g, r_g, s_t, r_t, s_d, r_d, s_c, r_c, s_x, r_x,
        s_v, r_v, s_e, r_e, s_p, r_p,
    ) = more[at:]
    places = Places(n_d, n_t)
    d, t, oi, ii, xi, ci = place(n_d, n_t)
    nx, no = n_t // CORES, n_d // INNER
    other = xi * CORES + (1 - ci)
    blocks, total, rows = proj_ref.shape
    width = total // 3
    half = HEAD_DIM // 2
    features = x_ref.shape[1]
    assert nx == 2 and CORES == 2

    cut = hul_ref.shape[-1]

    def put(target, lanes):
        def store(value):
            target[:, lanes] = value
        return store

    def put_out(value):
        out_ref[...] = value.T[:width]

    sinks = (
        put(up_ref, slice(0, cut)), put(down_ref, slice(0, cut)),
        put(up_ref, slice(cut, 2 * cut)), put(down_ref, slice(cut, 2 * cut)), put_out,
    )
    sums = []
    row = 0
    for n, ((dims, path), source) in enumerate(
        zip(BACK_SUMS, (hul_ref, hdl_ref, huh_ref, hdh_ref, gout_ref))
    ):
        steps = len(path)
        sums.append(
            Reduce(
                places, dims, path, source, buffers[n][0], buffers[n][1 : 1 + steps],
                list(buffers[n][1 + steps :]) + [sinks[n]], s_g, r_g, s_l.at[6 + n], row,
            )
        )
        row += steps
    flows = dict(zip(BACK_DIMS, sums))
    stage = dict.fromkeys(flows, 0)

    def at_point(point):
        for step in BACK_PLAN.get(point, ()):
            what, name = step.split()
            if what == "s":
                flows[name].start(0)
            else:
                flows[name].advance(stage[name])
                stage[name] += 1

    def put_low(value):
        gq_ref[0] = value[:, :width]
        gq_ref[1] = value[:, width:]

    def put_high(value):
        gq_ref[2] = value

    pair = Reduce(
        places, "zy", "yz", pair_ref, None, [pair_y, pair_z], [pair_sum, put_low], s_g, r_g, None, row
    )
    value_sum = Reduce(
        places, "zy", "zy", value_ref, None, [value_z, value_y], [value_mid, put_high],
        s_g, r_g, None, row + 2,
    )

    greet(n_d, n_t)
    a_copies = {}
    for m in range(1, n_t):
        b = order(m, xi, ci, nx)
        a_copies[mirror(m, nx)] = remote(
            dmix_ref.at[b], dmix_all.at[t], s_a.at[m - 1], r_a.at[mirror(m, nx) - 1], d, b
        )
    for m in range(n_t - 1, 0, -1):
        a_copies[mirror(m, nx)].start()
    at_point("0")
    loads = [
        pltpu.make_async_copy(dmix_ref.at[t], dmix_all.at[t], s_l.at[0]),
        pltpu.make_async_copy(in_hbm, in_ref, s_l.at[1]),
        pltpu.make_async_copy(wq_hbm, wq_ref, s_l.at[2]),
        pltpu.make_async_copy(x_hbm, x_ref, s_l.at[3]),
        pltpu.make_async_copy(dmid_hbm, dmid_ref, s_l.at[4]),
    ]
    for copy in loads:
        copy.start()
    t_copies = []
    for r in range(1, n_t):
        copy = remote(
            stat_ref, got_ref.at[r - 1], s_t.at[r - 1], r_t.at[r - 1], d, lax.rem(t + r, n_t)
        )
        copy.start()
        t_copies.append(copy)
    d_copies = [pltpu.make_async_copy(mine_ref, table_ref.at[d], s_l.at[5])]
    for r in range(1, n_d):
        d_copies.append(
            remote(mine_ref, table_ref.at[d], s_d.at[r - 1], r_d.at[r - 1], lax.rem(d + r, n_d), t)
        )

    def share_statistics():
        for copy in t_copies:
            copy.wait()
        value = stat_ref[...]
        for r in range(1, n_t):
            value += got_ref[r - 1]
        mine_ref[...] = value
        for copy in d_copies:
            copy.start()

    dkey_ref[...] = jnp.zeros_like(dkey_ref)
    dval_ref[...] = jnp.zeros_like(dval_ref)

    def turn(b, carry):
        lanes = pl.ds(pl.multiple_of(b * rows, rows), rows)
        keyt_ref[:, lanes] = proj_ref[b, width : 2 * width]
        for h in range(heads):
            at = h * HEAD_DIM
            key_ref[h, lanes] = proj_ref[b, width + at : width + at + HEAD_DIM].T
            val_ref[h, lanes] = proj_ref[b, 2 * width + at : 2 * width + at + HEAD_DIM].T
        return carry

    lax.fori_loop(0, blocks, turn, 0)
    loads[0].wait()

    loads[1].wait()
    loads[2].wait()
    dquery_ref[...] = jnp.zeros_like(dquery_ref)
    acc_ref[...] = jnp.zeros_like(acc_ref)
    part_ref = in_ref
    piece = rows // parts
    c_copies = {}
    for r in range(nx):
        block = lax.rem(xi + r, nx) * CORES + 1 - ci
        for p in range(parts):
            at = pl.ds(p * piece, piece)
            c_copies[r, p] = remote(
                part_ref.at[block, at], rc.at[r, at], s_c.at[r, p], r_c.at[r, p], d, other
            )
    x_copies = {}
    for p in range(parts):
        at = pl.ds(p * piece, piece)
        x_copies[p] = remote(
            part_ref.at[lax.rem(xi + 1, nx) * CORES + ci, at], rx.at[0, at],
            s_x.at[0, p], r_x.at[0, p], d, lax.rem(xi + 1, nx) * CORES + ci,
        )

    def unrotate(b, at, factor, first, last):
        lanes = pl.ds(pl.multiple_of(b * rows, rows), rows)
        cos, sin = cos_ref[:, lanes], sin_ref[:, lanes]
        dproj_ref[b, at : at + half] = ((first * cos + last * sin) * factor).astype(BF16)
        dproj_ref[b, at + half : at + HEAD_DIM] = ((last * cos - first * sin) * factor).astype(BF16)

    def close(b):
        lanes = pl.ds(pl.multiple_of(b * rows, rows), rows)
        for h in range(heads):
            at = h * HEAD_DIM
            d_query = dquery_ref[b, at : at + HEAD_DIM]
            unrotate(b, at, HEAD_DIM**-0.5, d_query[:half], d_query[half:])
            d_key = dkey_ref[h, lanes].T
            unrotate(b, width + at, 1.0, d_key[:half], d_key[half:])
            dproj_ref[b, 2 * width + at : 2 * width + at + HEAD_DIM] = (
                dval_ref[h, lanes].T.astype(BF16)
            )
        d_proj = dproj_ref[b]
        acc_ref[...] += dot(d_proj, in_ref[b], 1, 0)
        part_ref[b] = dot(d_proj.T, wq_ref[...], 1, 1).astype(BF16)

    def attend(n, carry):
        for m, at_step in ((1, 1), (2, 2), (3, 4)):
            @pl.when(n == at_step)
            def _(m=m):
                a_copies[m].wait()
        late_part, last_part = (n + 6) // 8, (n + 2) // 8
        q_other = late_part - last_part
        k_other = (1 - late_part) + q_other * lax.rem(n + 1, 2)
        offset = (1 - late_part) * n + q_other * (n // 2 - 1) + last_part * (n - 6)
        i = lax.rem(xi + q_other, nx) * CORES + lax.rem(ci + offset, CORES)
        span = CORES * rows
        keys = pl.ds(pl.multiple_of(lax.rem(xi + k_other, nx) * span, span), span)
        for h in range(heads):
            at = h * HEAD_DIM
            query_t = proj_ref[i, at : at + HEAD_DIM]
            dmix_t = dmix_all[i, at : at + HEAD_DIM]
            mix_t = mix_ref[i, at : at + HEAD_DIM]
            inner = jnp.sum(dmix_t.astype(F32) * mix_t.astype(F32), axis=0, keepdims=True)
            probs = jnp.exp(dot(key_ref[h, keys], query_t, 1, 0) - lse_ref[i, h : h + 1])
            d_probs = dot(val_ref[h, keys], dmix_t, 1, 0)
            d_scores = (probs * (d_probs - inner)).astype(BF16)
            dval_ref[h, keys] += dot(probs.astype(BF16), dmix_t.T, 1, 0)
            dkey_ref[h, keys] += dot(d_scores, query_t.T, 1, 0)
            dquery_ref[i, at : at + HEAD_DIM] += dot(keyt_ref[at : at + HEAD_DIM, keys], d_scores, 1, 0)

        @pl.when(n == 1)
        def _():
            share_statistics()

        @pl.when((n == 5) | (n == 7))
        def _():
            plane = lax.rem(xi + 1 - last_part, nx)

            def one(c, carry):
                close(plane * CORES + c)
                return carry

            lax.fori_loop(0, CORES, one, 0)

        @pl.when(n == 5)
        def _():
            for p in range(parts):
                c_copies[1, p].start()

        @pl.when(n == 6)
        def _():
            to = lax.rem(xi + 1, nx) * CORES + ci
            for p in range(parts):
                at = pl.ds(p * piece, piece)
                c_copies[1, p].wait()
                part_ref[to, at] = (part_ref[to, at].astype(F32) + rc[1, at].astype(F32)).astype(BF16)
                x_copies[p].start()

        for m in range(2 * n_t):
            if f"n{m}" in BACK_PLAN:
                @pl.when(n == m)
                def _(m=m):
                    at_point(f"n{m}")

        return carry

    lax.fori_loop(0, 2 * n_t, attend, 0)
    for p in range(parts):
        c_copies[0, p].start()
    grads = acc_ref[...].T.astype(BF16)
    pair_ref[...] = grads[:, : 2 * width].reshape(pair_ref.shape)
    value_ref[...] = grads[:, 2 * width :].reshape(value_ref.shape)
    pair.start(0)
    value_sum.start(0)
    at_point("t0")
    for copy in d_copies:
        copy.wait()
    loads[3].wait()
    loads[4].wait()
    pair.advance(0)
    at_point("t1")
    value_sum.advance(0)
    at_point("t2")

    gain, scale = vec_ref[GAIN1 : GAIN1 + 1], 1.0 + vec_ref[SCALE_A : SCALE_A + 1]
    shift_sum = jnp.zeros((1, features), F32)
    nhat_sum = jnp.zeros((1, features), F32)
    for p in range(parts):
        c_copies[0, p].wait()
        x_copies[p].wait()
        at = pl.ds(p * (rows // parts), rows // parts)
        e = part_ref[t, at].astype(F32) + rc[0, at].astype(F32)
        for r in range(1, nx):
            e += rx[r - 1, at].astype(F32)
        x = x_ref[at].astype(F32)
        centred = x - mean_rows(x)
        inv = lax.rsqrt(mean_rows(centred * centred) + EPSILON)
        nhat = centred * inv
        shift_sum += sum_tokens(e)
        nhat_sum += sum_tokens(e * nhat)
        dn = e * (scale * gain)
        grad_in_ref[at] = dmid_ref[at] + inv * (
            dn - mean_rows(dn) - nhat * mean_rows(dn * nhat)
        )
    at_point("t3")
    late_ref[:, :features] = shift_sum
    late_ref[:, features : 2 * features] = nhat_sum * gain
    late_ref[:, 2 * features :] = nhat_sum * scale

    copies = []
    for r in range(1, n_t):
        copy = remote(
            late_ref, late_got.at[r - 1], s_v.at[r - 1], r_v.at[r - 1], d, lax.rem(t + r, n_t)
        )
        copy.start()
        copies.append(copy)
    value = late_ref[...]
    for r in range(1, n_t):
        copies[r - 1].wait()
        value += late_got[r - 1]
    late_mine[...] = value
    copies = [pltpu.make_async_copy(late_mine, late_all.at[d], s_l.at[0])]
    for r in range(1, n_d):
        copies.append(
            remote(
                late_mine, late_all.at[d], s_e.at[r - 1], r_e.at[r - 1], lax.rem(d + r, n_d), t
            )
        )
    for copy in copies:
        copy.start()
    at_point("t4")
    for s in range(n_d):
        for block, row in EARLY:
            flat_ref[s : s + 1, block * features : (block + 1) * features] = table_ref[
                s, row : row + 1
            ]
    for copy in copies:
        copy.wait()
    value = late_all[0, :, 2 * features :]
    for s in range(1, n_d):
        value += late_all[s, :, 2 * features :]
    gain_ref[...] = value
    for s in range(n_d):
        flat_ref[s : s + 1, : 2 * features] = late_all[s, :, : 2 * features]
    columns = ada_ref.shape[0]
    moved = pltpu.roll(flat_ref[...], lax.rem(n_d - d, n_d) * columns, 1)[:, :columns]
    rows_out[:, 0, :] = lax.dot_general(
        moved, ada_ref[...].astype(F32), (((1,), (0,)), ((), ())),
        precision=lax.Precision.HIGHEST, preferred_element_type=F32,
    )
    copies = [pltpu.make_async_copy(rows_out.at[d], rows_in.at[d], s_l.at[1])]
    for r in range(1, n_d):
        peer = lax.rem(d + r, n_d)
        copies.append(remote(rows_out.at[peer], rows_in.at[d], s_p.at[r - 1], r_p.at[r - 1], peer, t))
    for copy in copies:
        copy.start()
    at_point("t5")
    pair.advance(1)
    value_sum.advance(1)
    at_point("t6")
    at_point("end")
    for name, flow in flows.items():
        assert stage[name] == len(flow.path), name
    for copy in copies:
        copy.wait()
    gcond_ref[...] = jnp.sum(rows_in[:, 0, :], axis=0, keepdims=True)


def back_call(
    dmix, proj, mix, lse, cos, sin, attn_in, w_qkv, stat, x, dmid, vecs, ada_t, partial_sums, n_d, n_t
):
    parts = 4
    count = counts(n_d, n_t)
    nx, no = count["x"], count["z"]
    blocks, total, rows = proj.shape
    width = total // 3
    heads = width // HEAD_DIM
    length = blocks * rows
    features = attn_in.shape[2]
    part = features // n_d
    cond_width = ada_t.shape[1]
    cut = partial_sums[0].shape[-1]
    buffers = []
    for (dims, path), source in zip(BACK_SUMS, partial_sums):
        buffers += reduce_scratch(count, dims, path, source.shape[-2:])
    stages = sum(len(path) for _, path in BACK_SUMS)
    widest = max(count.values()) - 1
    late = (1, 3 * features)
    return pl.pallas_call(
        partial(back_kernel, n_d, n_t, parts, heads),
        name="back",
        out_shape=[
            struct((rows, features), F32),
            struct((3, part, width), F32),
            struct((part, 2 * cut), F32),
            struct((part, 2 * cut), F32),
            struct((width, part), F32),
            struct((n_d,) + stat.shape, F32),
            struct((n_d, 6 * features), F32),
            struct((1, features), F32),
            struct((1, cond_width), F32),
        ],
        in_specs=[VMEM] * 6 + [ANY] * 2 + [VMEM] + [ANY] * 2 + [VMEM] * 2 + [ANY] * 5,
        out_specs=[VMEM] * 9,
        scratch_shapes=[
            pltpu.VMEM(dmix.shape, BF16),
            pltpu.VMEM((heads, length, HEAD_DIM), BF16),
            pltpu.VMEM((width, length), BF16),
            pltpu.VMEM((heads, length, HEAD_DIM), BF16),
            pltpu.VMEM((heads, length, HEAD_DIM), F32),
            pltpu.VMEM((heads, length, HEAD_DIM), F32),
            pltpu.VMEM((n_t, width, rows), F32),
            pltpu.VMEM(proj.shape, BF16),
            pltpu.VMEM(attn_in.shape, BF16),
            pltpu.VMEM(w_qkv.shape, BF16),
            pltpu.VMEM((total, features), F32),
            pltpu.VMEM((no, INNER, part, 2 * width), BF16),
            pltpu.VMEM((no, INNER, part, width), BF16),
            pltpu.VMEM((nx, rows, features), BF16),
            pltpu.VMEM((nx - 1, rows, features), BF16),
            *reduce_scratch(count, "zy", "yz", (part, 2 * width), own=False),
            *reduce_scratch(count, "zy", "zy", (part, width), own=False),
            pltpu.VMEM((n_t - 1,) + stat.shape, F32),
            pltpu.VMEM(stat.shape, F32),
            pltpu.VMEM(x.shape, BF16),
            pltpu.VMEM(x.shape, F32),
            pltpu.VMEM(late, F32),
            pltpu.VMEM((n_t - 1,) + late, F32),
            pltpu.VMEM(late, F32),
            pltpu.VMEM((n_d,) + late, F32),
            pltpu.VMEM((n_d, 1, cond_width), F32),
            pltpu.VMEM((n_d, 1, cond_width), F32),
        ]
        + buffers
        + [
            DMA((n_t - 1,)), DMA((n_t - 1,)), DMA((6 + len(BACK_SUMS),)),
            DMA((stages + 4, widest)), DMA((stages + 4, widest)),
            DMA((n_t - 1,)), DMA((n_t - 1,)), DMA((n_d - 1,)), DMA((n_d - 1,)),
            DMA((nx, parts)), DMA((nx, parts)), DMA((nx - 1, parts)), DMA((nx - 1, parts)),
            DMA((n_t - 1,)), DMA((n_t - 1,)), DMA((n_d - 1,)), DMA((n_d - 1,)),
            DMA((n_d - 1,)), DMA((n_d - 1,)),
        ],
        compiler_params=params(2),
        cost_estimate=cost(45 * heads * length * length * HEAD_DIM, 40e6, heads * length * length),
    )(dmix, proj, mix, lse, cos, sin, attn_in, w_qkv, stat, x, dmid, vecs, ada_t, *partial_sums)


def finish_kernel(
    count, n_units, n_moved, table_ref, flat_ref, cond_ref, gain_in, gcond_in, *more
):
    sources, more = more[:n_moved], more[n_moved:]
    ada_ref, bias_ref, gain1_ref, gain2_ref, bdown_ref, bup_ref, root_ref, gcond_ref = more[:8]
    for src, dst in zip(sources, more[8:]):
        if len(dst.shape) > len(src.shape):
            dst[:, 0, :] = src[...]
        else:
            dst[...] = src[...]
    n_d = table_ref.shape[0]
    features = table_ref.shape[2]
    total = table_ref[0]
    for s in range(1, n_d):
        total += table_ref[s]
    root_ref[...] = jnp.sqrt(jnp.sum(total[S_SQ_A : S_SQ_R + 1], axis=1) / count)
    gain2_ref[...] = total[S_GAIN2]
    bdown_ref[...] = total[S_B_DOWN]
    for u in range(n_units):
        bup_ref[u * features : (u + 1) * features] = total[S_B_UP + u]
    gain1_ref[...] = gain_in[0]
    gcond_ref[...] = gcond_in[...]
    for block in range(6):
        at = slice(block * features, (block + 1) * features)
        value = jnp.zeros((cond_ref.shape[0], features), F32)
        for s in range(n_d):
            value += cond_ref[:, s : s + 1] * flat_ref[s : s + 1, at]
        ada_ref[:, at] = value
        bias_ref[at] = jnp.sum(flat_ref[:, at], axis=0)


def finish_call(table, flat, cond_t, gain, gcond, moved, count, n_units):
    rows, wide = moved[1].shape
    shapes = [a.shape for a in moved]
    shapes[1] = (rows, 1, wide)
    features = table.shape[2]
    width = cond_t.shape[0]
    return pl.pallas_call(
        partial(finish_kernel, count, n_units, len(moved)),
        name="finish",
        out_shape=[
            struct((width, 6 * features), F32),
            struct((6 * features,), F32),
            struct((features,), F32),
            struct((features,), F32),
            struct((features,), F32),
            struct((n_units * features,), F32),
            struct((3,), F32),
            struct((1, width), F32),
        ]
        + [struct(shape, a.dtype) for a, shape in zip(moved, shapes)],
        in_specs=[VMEM] * (5 + len(moved)),
        out_specs=[VMEM] * (8 + len(moved)),
        compiler_params=params(),
        cost_estimate=cost(1e7, 4e6),
    )(table, flat, cond_t, gain, gcond, *moved)


def shards(
    block_input, condition, modulation_weight, modulation_bias, first_gain, qkv_weight, out_weight,
    second_gain, up_weight, up_bias, down_weight, down_bias, grad_output,
):
    n_t, n_d = lax.axis_size("tensor"), lax.axis_size("dp")
    rows, sequences, features = block_input.shape
    assert sequences == 1
    length = rows * n_t
    part, width = qkv_weight.shape[1:]
    units = up_weight.shape[1]
    assert units == features and n_t % CORES == 0 and n_d % INNER == 0
    x = block_input.reshape(rows, features)
    g = grad_output.reshape(rows, features)
    ada_t = modulation_weight.T

    smalls = (first_gain, second_gain, down_bias, up_bias, condition, modulation_bias)
    inverse = 10000.0 ** (-np.arange(HEAD_DIM // 2) * 2.0 / HEAD_DIM)
    angles = inverse[:, None] * np.arange(length)[None, :]
    cos, sin = jnp.asarray(np.cos(angles), F32), jnp.asarray(np.sin(angles), F32)

    attn_in, proj, mix, lse, mix_own, vecs, cond_t, w_qkv, w_ul, w_dl, w_uh, w_dh, w_out = front_call(
        x, qkv_weight, smalls, ada_t, up_weight, down_weight.T, out_weight, cos, sin, n_d, n_t
    )
    stat_rows = -(-(S_B_UP + n_t) // 8) * 8
    out, d_middle, d_mix, stat, *partial_sums = middle_call(
        mix_own, x, g, vecs, w_ul, w_dl, w_uh, w_dh, w_out, stat_rows, n_d, n_t
    )
    grad_input, g_qkv, g_up, g_down, g_out, table, flat, gain1, grad_cond = back_call(
        d_mix, proj, mix, lse, cos, sin, attn_in, w_qkv.reshape(features, 3 * width), stat,
        x, d_middle, vecs, ada_t, partial_sums, n_d, n_t,
    )
    moved = (out, grad_input, g_qkv, g_up, g_down, g_out)
    grad_ada, grad_ada_b, gain1, gain2, b_down, b_up, roots, grad_cond, *moved = finish_call(
        table, flat, cond_t, gain1, grad_cond, moved, float(length * n_d * features), n_t
    )
    out, grad_input, g_qkv, g_up, g_down, g_out = moved
    return (
        out.reshape(block_input.shape), grad_input, grad_cond, grad_ada, grad_ada_b, gain1, g_qkv,
        g_out, gain2, g_up, b_up, g_down.T, b_down, roots,
    )


def solution(mesh):
    in_specs = (
        P("tensor", "dp", None),
        P("dp", None),
        P(None, "dp"),
        P("dp"),
        P("dp"),
        P(None, "dp", "tensor"),
        P("tensor", "dp"),
        P("dp"),
        P("dp", "tensor"),
        P("dp"),
        P("tensor", "dp"),
        P("dp"),
        P("tensor", "dp", None),
    )
    out_specs = (
        P("tensor", "dp", None),
        P("tensor", "dp", None),
        P("dp", None),
        P(),
        P(),
        P(),
        P(None, "dp", "tensor"),
        P("tensor", "dp"),
        P(),
        P("dp", "tensor"),
        P(),
        P("tensor", "dp"),
        P(),
        P(),
    )
    return jax.shard_map(shards, mesh=mesh, in_specs=in_specs, out_specs=out_specs, check_vma=False)
```

```python
from functools import partial

import jax
import jax.numpy as jnp
import numpy as np
from jax import lax
from jax.experimental import pallas as pl
from jax.experimental.pallas import tpu as pltpu
from jax.sharding import PartitionSpec as P

HEAD_DIM = 64
EPSILON = 1e-05
CORES = 2
INNER = 2
MESH = pl.DeviceIdType.MESH
VMEM_LIMIT = 58 << 20
GELU_C = float(np.sqrt(2.0 / np.pi))
GELU_A = 0.044715
F32 = jnp.float32
BF16 = jnp.bfloat16
ANY = pl.BlockSpec(memory_space=pl.ANY)
VMEM = pl.BlockSpec(memory_space=pltpu.VMEM)
DMA = pltpu.SemaphoreType.DMA


def dot(lhs, rhs, lhs_dim, rhs_dim):
    return lax.dot_general(
        lhs, rhs, (((lhs_dim,), (rhs_dim,)), ((), ())), preferred_element_type=F32
    )


def params(collective_id=None, **more):
    if collective_id is not None:
        more.update(collective_id=collective_id, has_side_effects=True)
    return pltpu.CompilerParams(vmem_limit_bytes=VMEM_LIMIT, **more)


def cost(flops, moved, special=0):
    return pl.CostEstimate(flops=int(flops), bytes_accessed=int(moved), transcendentals=int(special))


def struct(shape, dtype):
    return jax.ShapeDtypeStruct(shape, dtype)


def mean_rows(values):
    return jnp.mean(values, axis=-1, keepdims=True)


def sum_tokens(values):
    return jnp.sum(values, axis=0, keepdims=True)


GAIN1, SHIFT_A, SCALE_A, GATE_A, GAIN2, SHIFT_M, SCALE_M, GATE_M, B_DOWN, B_UP = range(10)
MOD_ROWS = (SHIFT_A, SCALE_A, GATE_A, SHIFT_M, SCALE_M, GATE_M)
S_GATE_A, S_SHIFT_M, S_SCALE_M, S_GATE_M, S_GAIN2, S_B_DOWN, S_SQ_A, S_SQ_M, S_SQ_R, S_B_UP = range(10)
L_SHIFT_A, L_SCALE_A, L_GAIN1 = range(3)


def order(k, xi, ci, nx):
    return lax.rem(xi + k // CORES, nx) * CORES + lax.rem(ci + k % CORES, CORES)


def mirror(k, nx):
    return (nx - k // CORES) % nx * CORES + (CORES - k % CORES) % CORES


def place(n_d, n_t):
    d, t = lax.axis_index("dp"), lax.axis_index("tensor")
    return d, t, d // INNER, lax.rem(d, INNER), t // CORES, lax.rem(t, CORES)


def greet(n_d, n_t, between=None):
    d, t = lax.axis_index("dp"), lax.axis_index("tensor")
    barrier = pltpu.get_barrier_semaphore()
    for r in range(1, n_t):
        pl.semaphore_signal(
            barrier, 1, device_id=(d, lax.rem(t + r, n_t)), device_id_type=MESH
        )
    for r in range(1, n_d):
        pl.semaphore_signal(
            barrier, 1, device_id=(lax.rem(d + r, n_d), t), device_id_type=MESH
        )
    if between is not None:
        between()
    pl.semaphore_wait(barrier, n_t - 1 + n_d - 1)


def remote(src, dst, send, recv, d, t):
    return pltpu.make_async_remote_copy(
        src_ref=src, dst_ref=dst, send_sem=send, recv_sem=recv, device_id=(d, t), device_id_type=MESH
    )


class Places:
    def __init__(self, n_d, n_t):
        d, t = lax.axis_index("dp"), lax.axis_index("tensor")
        self.d, self.t = d, t
        self.me = {"z": d // INNER, "y": lax.rem(d, INNER), "x": t // CORES, "c": lax.rem(t, CORES)}
        self.count = counts(n_d, n_t)

    def peer(self, axis, r):
        at = dict(self.me)
        at[axis] = lax.rem(at[axis] + r, self.count[axis])
        return at[axis], (at["z"] * INNER + at["y"], at["x"] * CORES + at["c"])


def counts(n_d, n_t):
    return {"z": n_d // INNER, "y": INNER, "x": n_t // CORES, "c": CORES}


class Spread:
    def __init__(self, places, dims, known, path, array, source, send, recv, row, lanes=slice(None)):
        self.path, self.flights = path, []
        for s, axis in enumerate(path):
            region = tuple(
                slice(None) if a in known or a in path[:s] else places.me[a] for a in dims
            ) + (slice(None), lanes)
            src = source if s == 0 else array.at[region]
            self.flights.append([])
            for r in range(1, places.count[axis]):
                _, (d, t) = places.peer(axis, r)
                self.flights[s].append(
                    remote(
                        src, array.at[region], send.at[row + s, r - 1], recv.at[row + s, r - 1], d, t
                    )
                )

    def start(self, s):
        for copy in self.flights[s]:
            copy.start()

    def wait(self, s):
        for copy in self.flights[s]:
            copy.wait()

    def advance(self, s, last=None):
        self.wait(s)
        if s + 1 < len(self.path) and s != last:
            self.start(s + 1)


class Reduce:
    def __init__(self, places, dims, path, source, own, met, results, send, recv, local, row):
        self.places, self.path, self.own, self.met = places, path, own, met
        self.results, self.flights, self.dims = results, [], []
        current = source
        for s, axis in enumerate(path):
            at = dims.index(axis)
            self.dims.append((current, dims, at))
            self.flights.append([])
            for r in range(1, places.count[axis]):
                to, (d, t) = places.peer(axis, r)
                self.flights[s].append(
                    remote(
                        current.at[(slice(None),) * at + (to,)], met[s].at[r - 1],
                        send.at[row + s, r - 1], recv.at[row + s, r - 1], d, t,
                    )
                )
            if s == 0:
                self.load = None
                if own is not None:
                    self.load = pltpu.make_async_copy(
                        current.at[(slice(None),) * at + (places.me[axis],)], own, local
                    )
            dims = dims.replace(axis, "")
            current = results[s]

    def start(self, s):
        for copy in self.flights[s]:
            copy.start()
        if s == 0 and self.load is not None:
            self.load.start()

    def advance(self, s):
        places, path = self.places, self.path
        for copy in self.flights[s]:
            copy.wait()
        current, dims, at = self.dims[s]
        rest = dims.replace(path[s], "")
        if s == 0 and self.load is not None:
            self.load.wait()
            current, at = self.own, None
        sizes = [places.count[a] for a in rest]

        def fold(n, carry):
            spot = []
            for size in reversed(sizes):
                spot.insert(0, lax.rem(n, size))
                n = n // size
            own = list(spot)
            if at is not None:
                own.insert(at, places.me[path[s]])
            value = current[tuple(own)].astype(F32)
            for r in range(places.count[path[s]] - 1):
                value += self.met[s][(r,) + tuple(spot)].astype(F32)
            if callable(self.results[s]):
                self.results[s](value)
            else:
                self.results[s][tuple(spot)] = value.astype(BF16)
            return carry

        if sizes:
            lax.fori_loop(0, int(np.prod(sizes)), fold, 0)
        else:
            fold(0, 0)
        if s + 1 < len(path):
            self.start(s + 1)


def reduce_scratch(count, dims, path, tail, own=True, last=True):
    shapes = []
    rest = dims.replace(path[0], "")
    if own:
        shapes.append(tuple(count[a] for a in rest) + tail)
    left = dims
    for axis in path:
        left = left.replace(axis, "")
        shapes.append((count[axis] - 1,) + tuple(count[a] for a in left) + tail)
    left = dims
    for axis in path if not last else path[:-1]:
        left = left.replace(axis, "")
        shapes.append(tuple(count[a] for a in left) + tail)
    return [pltpu.VMEM(shape, BF16) for shape in shapes]


FRONT_PATHS = {"ula": "zyxc", "ulb": "zxyc", "dla": "zxyc", "dlb": "zxyc", "o": "xyzc", "uh": "zy", "dh": "zx"}
FRONT_PLAN = {
    "pre": ("s ula",),
    "qz": ("a ula", "s ulb", "s dlb", "s o",),
    "X": ("s dla",),
    "n": ("a ulb", "a dlb", "a o", "s uh",),
    "g": ("a dla",),
    "p1": ("s dh",),
    "p3": ("a ula", "a ulb", "a dlb", "a o",),
    "a0": ("a uh",),
    "a1": ("a dla",),
    "a3": ("a ula", "a dh",),
    "a4": ("a ula", "a ulb", "a dlb",),
    "a5": ("a ulb", "a dlb",),
    "end": ("a uh", "a o", "a dla", "a o", "a dh", "a dla",),
}
BACK_DIMS = {"ul": "zy", "dl": "zx", "uh": "zyx", "dh": "zyx", "o": "czyx"}
BACK_PATHS = {"ul": "yz", "dl": "xz", "uh": "xyz", "dh": "yxz", "o": "czxy"}
BACK_PLAN = {
    "0": ("s dh", "s o",),
    "n0": ("a o",),
    "n1": ("s uh", "s dl", "s ul",),
    "n2": ("a dh",),
    "n5": ("a dl", "a ul",),
    "n6": ("a dh", "a o", "a uh",),
    "n7": ("a ul", "a dl",),
    "t4": ("a dh",),
    "t5": ("a uh", "a o",),
    "t0": ("a uh",),
    "t2": ("a o",),
}
BACK_SUMS = tuple((BACK_DIMS[name], BACK_PATHS[name]) for name in BACK_DIMS)
CODE = {"z": 2, "y": 2, "x": 2, "c": 2}
EARLY = ((2, S_GATE_A), (3, S_SHIFT_M), (4, S_SCALE_M), (5, S_GATE_M))


def front_kernel(
    n_d, n_t, parts, heads, cond_at, bias_at, sizes,
    x_ref, qkv_ref, gain1_ref, gain2_ref, bdown_ref, bup_ref, cond_in, ada_b_ref,
    ada_ref, up_ref, down_ref, outw_ref, cos_ref, sin_ref,
    in_all, proj_ref, mix_ref, lse_ref, mix_own, vec_ref, cond_ref, w_all, w_ul, w_dl, w_uh, w_dh, w_out,
    x_all, w_pack, wt_ref, out_pack, small_ref, small_all, mod_all, mod_rows, key_ref,
    s_x, r_x, s_c, r_c, s_f, r_f, s_z, r_z, s_y, r_y, s_s, r_s, s_m, r_m, s_l,
    s_w, r_w, s_o, r_o,
):
    d, t, oi, ii, xi, ci = place(n_d, n_t)
    nx, no = n_t // CORES, n_d // INNER
    other = xi * CORES + (1 - ci)
    piece = x_ref.shape[0] // parts
    rows, features = x_ref.shape
    width = qkv_ref.shape[2]
    half = HEAD_DIM // 2
    cut = w_ul.shape[5]
    low_half, high_half = slice(0, cut), slice(cut, 2 * cut)
    def pack():
        for j in range(3):
            w_pack[:, j * width : (j + 1) * width] = qkv_ref[j]
        out_pack[:, :width] = outw_ref[...].T
        small_ref[...] = jnp.zeros_like(small_ref)
        at = 0
        for ref in (gain1_ref, gain2_ref, bdown_ref, bup_ref):
            small_ref[:, at : at + ref.shape[0]] = ref[...].astype(F32).reshape(1, -1)
            at += ref.shape[0]
        small_ref[:, cond_at : cond_at + cond_in.shape[1]] = cond_in[...].astype(F32)
        small_ref[:, bias_at : bias_at + ada_b_ref.shape[0]] = ada_b_ref[...].astype(F32).reshape(1, -1)
        if out_pack.shape[1] > width:
            out_pack[:, width:] = jnp.zeros((out_pack.shape[0], out_pack.shape[1] - width), BF16)

    greet(n_d, n_t, pack)
    places = Places(n_d, n_t)
    flows = {}
    split = 2 * cut // 3 // 128 * 128
    whole, first_lanes, last_lanes = slice(None), slice(0, split), slice(split, cut)
    for row, (name, dims, array, source, lanes) in enumerate(
        (
            ("ula", "zyxc", w_ul, up_ref.at[:, first_lanes], first_lanes),
            ("ulb", "zyxc", w_ul, up_ref.at[:, last_lanes], last_lanes),
            ("dla", "zyxc", w_dl, down_ref.at[:, first_lanes], first_lanes),
            ("dlb", "zyxc", w_dl, down_ref.at[:, last_lanes], last_lanes),
            ("o", "zyxc", w_out, out_pack, whole),
            ("uh", "zy", w_uh, up_ref.at[:, high_half], whole),
            ("dh", "zx", w_dh, down_ref.at[:, high_half], whole),
        )
    ):
        flows[name] = Spread(
            places, dims, "", FRONT_PATHS[name], array, source, s_w, r_w, 4 * row, lanes
        )
    stage = dict.fromkeys(flows, 0)

    def at_point(point):
        for step in FRONT_PLAN.get(point, ()):
            what, name = step.split()
            if what == "s":
                flows[name].start(0)
            else:
                flows[name].advance(stage[name])
                stage[name] += 1

    s_copies = []
    for r in range(1, n_d):
        copy = remote(
            small_ref, small_all.at[d], s_s.at[r - 1], r_s.at[r - 1], lax.rem(d + r, n_d), t
        )
        copy.start()
        s_copies.append(copy)
    at_point("pre")
    x_copies = []
    for r in range(1, nx):
        peer = lax.rem(xi + r, nx) * CORES + ci
        for p in range(parts):
            at = pl.ds(p * piece, piece)
            copy = remote(
                x_ref.at[at], x_all.at[t, at], s_x.at[r - 1, p], r_x.at[r - 1, p], d, peer
            )
            copy.start()
            x_copies.append((r, p, copy))
    z_copies = []
    for r in range(1, no):
        copy = remote(
            w_pack, w_all.at[d], s_z.at[r - 1], r_z.at[r - 1], lax.rem(oi + r, no) * INNER + ii, t
        )
        copy.start()
        z_copies.append(copy)
    y_copies = []
    for q in range(1, INNER):
        copy = remote(
            w_pack, w_all.at[d], s_y.at[q - 1, 0], r_y.at[q - 1, 0],
            oi * INNER + lax.rem(ii + q, INNER), t,
        )
        copy.start()
        y_copies.append(copy)
    core_copy = remote(x_ref, x_all.at[t], s_c, r_c, d, other)
    core_copy.start()
    local = []
    for n, (src, dst) in enumerate(
        (
            (small_ref, small_all.at[d]),
            (x_ref, x_all.at[t]),
            (w_pack, w_all.at[d]),
            (up_ref.at[:, low_half], w_ul.at[oi, ii, xi, ci]),
            (down_ref.at[:, low_half], w_dl.at[oi, ii, xi, ci]),
            (up_ref.at[:, high_half], w_uh.at[oi, ii]),
            (down_ref.at[:, high_half], w_dh.at[oi, xi]),
            (out_pack, w_out.at[oi, ii, xi, ci]),
        )
    ):
        copy = pltpu.make_async_copy(src, dst, s_l.at[n])
        copy.start()
        local.append(copy)

    at_point("0")

    local[0].wait()
    for copy in s_copies:
        copy.wait()
    cond = small_all[:, 0, cond_at : cond_at + ada_ref.shape[1]]
    for s in range(n_d):
        cond_ref[:, s : s + 1] = cond[s : s + 1].T
    bias = small_ref[:, bias_at : bias_at + ada_ref.shape[0]]
    mod_rows[:, 0, :] = dot(cond.astype(BF16), ada_ref[...], 1, 1) + bias
    own_mod = pltpu.make_async_copy(mod_rows.at[d], mod_all.at[d], s_l.at[8])
    own_mod.start()
    m_copies = []
    for r in range(1, n_d):
        peer = lax.rem(d + r, n_d)
        copy = remote(mod_rows.at[peer], mod_all.at[d], s_m.at[r - 1], r_m.at[r - 1], peer, t)
        copy.start()
        m_copies.append(copy)
    for r in range(1, no):
        z_copies[r - 1].wait()
        origin = lax.rem(oi + no - r, no) * INNER + ii
        for q in range(1, INNER):
            copy = remote(
                w_all.at[origin], w_all.at[origin], s_y.at[q - 1, r], r_y.at[q - 1, r],
                oi * INNER + lax.rem(ii + q, INNER), t,
            )
            copy.start()
            y_copies.append(copy)
    for n in range(3, 8):
        local[n].wait()
    at_point("qz")
    f_copies = []
    for r, p, copy in x_copies:
        copy.wait()
        origin = lax.rem(xi + nx - r, nx) * CORES + ci
        at = pl.ds(p * piece, piece)
        copy = remote(
            x_all.at[origin, at], x_all.at[origin, at],
            s_f.at[r - 1, p], r_f.at[r - 1, p], d, other,
        )
        copy.start()
        f_copies.append(copy)

    at_point("X")
    for copy in m_copies + [own_mod]:
        copy.wait()
    def put(first, piece_of, count):
        for s in range(n_d):
            value = piece_of(s)
            start = s * count
            done = 0
            while done < count:
                row, column = divmod(start + done, features)
                take = min(count - done, features - column)
                vec_ref[first + row : first + row + 1, column : column + take] = value[
                    :, done : done + take
                ]
                done += take

    vec_ref[...] = jnp.zeros_like(vec_ref)
    at = 0
    for first, count in sizes:
        put(first, lambda s: small_all[s, :, at : at + count], count)
        at += count
    columns = ada_ref.shape[0]
    for s in range(n_d):
        done = 0
        while done < columns:
            row, column = divmod(s * columns + done, features)
            take = min(columns - done, features - column)
            row = MOD_ROWS[row]
            vec_ref[row : row + 1, column : column + take] = mod_all[s, :, done : done + take]
            done += take

    for copy in f_copies + [local[1], core_copy]:
        copy.wait()

    def norm(b, carry):
        x = x_all[b].astype(F32)
        centred = x - mean_rows(x)
        normed = centred * lax.rsqrt(mean_rows(centred * centred) + EPSILON)
        normed = normed * vec_ref[GAIN1 : GAIN1 + 1]
        low = (normed * (1.0 + vec_ref[SCALE_A : SCALE_A + 1]) + vec_ref[SHIFT_A : SHIFT_A + 1])
        in_all[b] = low.astype(BF16)
        return carry

    lax.fori_loop(0, n_t, norm, 0)
    at_point("n")
    for copy in y_copies + [local[2]]:
        copy.wait()
    wt_ref[...] = w_all[...].reshape(features, 3 * width).T

    at_point("g")

    def project(b, carry):
        proj = dot(wt_ref[...], in_all[b], 1, 1)
        lanes = pl.ds(pl.multiple_of(b * rows, rows), rows)
        cos, sin = cos_ref[:, lanes], sin_ref[:, lanes]
        for j in range(2):
            factor = HEAD_DIM**-0.5 if j == 0 else 1.0
            for h in range(heads):
                at = j * width + h * HEAD_DIM
                first, last = proj[at : at + half], proj[at + half : at + HEAD_DIM]
                top = ((first * cos - last * sin) * factor).astype(BF16)
                bottom = ((last * cos + first * sin) * factor).astype(BF16)
                proj_ref[b, at : at + half] = top
                proj_ref[b, at + half : at + HEAD_DIM] = bottom
                if j == 1:
                    key_ref[h, lanes, :] = jnp.concatenate([top, bottom], axis=0).T
        proj_ref[b, 2 * width :] = proj[2 * width :].astype(BF16)

        for m in range(n_t):
            if f"p{m}" in FRONT_PLAN:
                @pl.when(b == m)
                def _(m=m):
                    at_point(f"p{m}")

        return carry

    lax.fori_loop(0, n_t, project, 0)

    def attend(u, carry):
        plane = lax.rem(xi + nx - 1 - u // heads, nx)
        h = lax.rem(u, heads)
        at = pl.ds(pl.multiple_of(h * HEAD_DIM, HEAD_DIM), HEAD_DIM)
        value_at = pl.ds(pl.multiple_of(2 * width + h * HEAD_DIM, HEAD_DIM), HEAD_DIM)
        first = plane * CORES
        query = jnp.concatenate([proj_ref[first + c, at] for c in range(CORES)], axis=1)
        scores = dot(key_ref[h], query, 1, 0)
        top = jnp.max(scores, axis=0, keepdims=True)
        grown = jnp.exp(scores - top)
        total = jnp.sum(grown, axis=0, keepdims=True)
        value = jnp.concatenate([proj_ref[v, value_at] for v in range(n_t)], axis=1)
        mixed = (dot(value, grown.astype(BF16), 1, 0) / total).astype(BF16)
        log_total = top + jnp.log(total)
        for c in range(CORES):
            part = slice(c * rows, (c + 1) * rows)
            mix_ref[first + c, at] = mixed[:, part]
            lse_ref[first + c, pl.ds(h, 1)] = log_total[:, part]
        for r in range(nx):
            @pl.when(u == (nx - r) * heads - 1)
            def _(r=r):
                for c in range(CORES):
                    if r * CORES + c > 0:
                        o_copies[r * CORES + c].start()

        for m in range(nx * heads):
            if f"a{m}" in FRONT_PLAN:
                @pl.when(u == m)
                def _(m=m):
                    at_point(f"a{m}")

        return carry

    o_copies = {}
    for m in range(1, n_t):
        b = order(m, xi, ci, nx)
        o_copies[m] = remote(
            mix_ref.at[b], mix_own.at[t], s_o.at[m - 1], r_o.at[mirror(m, nx) - 1], d, b
        )
    lax.fori_loop(0, nx * heads, attend, 0)
    mine = pltpu.make_async_copy(mix_ref.at[t], mix_own.at[t], s_l.at[9])
    mine.start()
    at_point("end")
    for name, flow in flows.items():
        assert stage[name] == len(flow.path), name
    mine.wait()
    for copy in list(o_copies.values()):
        copy.wait()


def front_call(x, qkv, smalls, ada_t, up, down_t, outw, cos, sin, n_d, n_t):
    cond, ada_b = smalls[4:]
    sizes = tuple(zip((GAIN1, GAIN2, B_DOWN, B_UP), (a.shape[0] for a in smalls[:4])))
    cond_at = -(-sum(size for _, size in sizes) // 128) * 128
    bias_at = cond_at + cond.shape[1]
    small = bias_at + ada_b.shape[0]
    parts = 4
    nx, no = n_t // CORES, n_d // INNER
    rows, features = x.shape
    part, width = qkv.shape[1:]
    heads = width // HEAD_DIM
    length = rows * n_t
    wide = -(-width // 128) * 128
    units = up.shape[1]
    steps = max(no, INNER, nx) - 1
    cut = units // 2
    grid_of = (no, INNER, nx, CORES, part)
    columns = ada_t.shape[0]
    return pl.pallas_call(
        partial(front_kernel, n_d, n_t, parts, heads, cond_at, bias_at, sizes),
        name="front",
        out_shape=[
            struct((n_t, rows, features), BF16),
            struct((n_t, 3 * width, rows), BF16),
            struct((n_t, width, rows), BF16),
            struct((n_t, heads, rows), F32),
            struct((n_t, width, rows), BF16),
            struct((16, features), F32),
            struct((ada_t.shape[1], n_d), F32),
            struct((n_d, part, 3 * width), BF16),
            struct(grid_of + (cut,), BF16),
            struct(grid_of + (cut,), BF16),
            struct((no, INNER, part, cut), BF16),
            struct((no, nx, part, cut), BF16),
            struct(grid_of + (wide,), BF16),
        ],
        in_specs=[VMEM] * 9 + [ANY] * 2 + [VMEM] * 3,
        out_specs=[VMEM] * 8 + [ANY] * 5,
        scratch_shapes=[
            pltpu.VMEM((n_t, rows, features), BF16),
            pltpu.VMEM((part, 3 * width), BF16),
            pltpu.VMEM((3 * width, features), BF16),
            pltpu.VMEM((part, wide), BF16),
            pltpu.VMEM((1, small), F32),
            pltpu.VMEM((n_d, 1, small), F32),
            pltpu.VMEM((n_d, 1, columns), F32),
            pltpu.VMEM((n_d, 1, columns), F32),
            pltpu.VMEM((heads, length, HEAD_DIM), BF16),
            DMA((nx - 1, parts)), DMA((nx - 1, parts)), DMA, DMA,
            DMA((nx - 1, parts)), DMA((nx - 1, parts)),
            DMA((no - 1,)), DMA((no - 1,)),
            DMA((INNER - 1, no)), DMA((INNER - 1, no)),
            DMA((n_d - 1,)), DMA((n_d - 1,)), DMA((n_d - 1,)), DMA((n_d - 1,)),
            DMA((10,)),
            DMA((28, steps)), DMA((28, steps)),
            DMA((n_t - 1,)), DMA((n_t - 1,)),
        ],
        compiler_params=params(0),
        cost_estimate=cost(20 * heads * length * length * HEAD_DIM, 40e6, heads * length * length),
    )(x, qkv, *smalls, ada_t, up, down_t, outw, cos, sin)


def middle_kernel(
    n_d, n_t,
    mix_ref, x_ref, g_ref, vec_ref, ul_ref, dl_ref, uh_ref, dh_ref, wout_ref,
    out_ref, dmid_ref, dmix_ref, stat_ref, hul_ref, hdl_ref, huh_ref, hdh_ref, gout_ref,
    up_buf, down_buf, o_buf, go_buf,
    attn_ref, low_ref, lowt_ref, dl_t_ref, dlt_ref, acc_out, acc_in,
    mul_c, rul, mul_x, mdl_c, mdl_y, rdl, muh, mdh,
    s_u, s_d, s_o, s_w, r_w, s_r, r_r,
):
    places = Places(n_d, n_t)
    count, me = places.count, places.me
    rows, features = x_ref.shape
    width = mix_ref.shape[1]
    cut = up_buf.shape[-1]
    wide = wout_ref.shape[-1]
    loads = [
        pltpu.make_async_copy(wout_ref, o_buf, s_o.at[0]),
        pltpu.make_async_copy(ul_ref, up_buf.at[0], s_u.at[0]),
        pltpu.make_async_copy(dl_ref, down_buf.at[0], s_d.at[0]),
        pltpu.make_async_copy(uh_ref, up_buf.at[1, :, :, me["x"], me["c"]], s_u.at[1]),
        pltpu.make_async_copy(dh_ref, down_buf.at[1, :, me["y"], :, me["c"]], s_d.at[1]),
    ]
    for copy in loads:
        copy.start()
    greet(n_d, n_t)
    nx = count["x"]
    every, mx, my, mc = slice(None), me["x"], me["y"], me["c"]
    taken = [0]

    def send(target, region, axis, r, source=None):
        at = target.at[(1,) + region]
        n = taken[0]
        taken[0] += 1
        return remote(
            at if source is None else source, at, s_w.at[n], r_w.at[n], *places.peer(axis, r)[1]
        )

    own_up = [send(up_buf, (every, every, mx, mc), "c", 1, uh_ref)]
    own_down = [send(down_buf, (every, my, every, mc), "c", 1, dh_ref)]
    near_down, far_down, near_on, far_on, far_up = [], [], [], [], []
    for r in range(1, INNER):
        near_down.append(send(down_buf, (every, my, mx, mc), "y", r, dh_ref.at[:, mx]))
        near_on.append(send(down_buf, (every, places.peer("y", r)[0], mx, mc), "c", 1))
    for r in range(1, nx):
        far_up.append(send(up_buf, (every, every, mx, mc), "x", r, uh_ref))
        far_on.append(send(up_buf, (every, every, places.peer("x", r)[0], mc), "c", 1))
    for r in range(1, INNER):
        for q in range(1, nx):
            x_at = places.peer("x", q)[0]
            far_down.append(send(down_buf, (every, my, x_at, mc), "y", r, dh_ref.at[:, x_at]))
            far_on.append(
                send(down_buf, (every, places.peer("y", r)[0], x_at, mc), "c", 1)
            )
    for copy in near_down + far_up + own_up + own_down + far_down:
        copy.start()
    planes = [lax.rem(me["x"] + nx - 1 - n, nx) for n in range(nx)]
    ul = [
        Reduce(
            places, "zyc", "c", up_buf.at[2, :, :, planes[n]], None, [mul_c.at[n]], [rul.at[n]],
            s_r, r_r, None, n,
        )
        for n in range(nx)
    ]
    ul_x = [
        remote(
            rul.at[nx - 1 - r], mul_x.at[r - 1], s_r.at[4 * nx + 3, r - 1], r_r.at[4 * nx + 3, r - 1],
            *places.peer("x", r)[1],
        )
        for r in range(1, nx)
    ]
    dl = [
        Reduce(
            places, "zyc", "c", down_buf.at[2, :, :, planes[n]], None, [mdl_c.at[n]],
            [rdl.at[:, :, planes[n]]], s_r, r_r, None, nx + n,
        )
        for n in range(nx)
    ]
    dl_y = [
        Reduce(
            places, "zy", "y", rdl.at[:, :, planes[n]], None, [mdl_y.at[n]],
            [rdl.at[:, my, planes[n]]], s_r, r_r, None, 3 * nx + 3 + n,
        )
        for n in range(nx)
    ]
    high_up, high_down = up_buf.at[0, :, :, :, me["c"]], down_buf.at[0, :, :, :, me["c"]]
    uh = Reduce(places, "zyxc", "c", up_buf.at[0], None, [muh], [high_up], s_r, r_r, None, 2 * nx + 1)
    dh = Reduce(
        places, "zyxc", "c", down_buf.at[0], None, [mdh], [high_down], s_r, r_r, None, 2 * nx + 2
    )
    keeps = [
        pltpu.make_async_copy(go_buf, gout_ref, s_o.at[1]),
        pltpu.make_async_copy(high_up, huh_ref, s_o.at[2]),
        pltpu.make_async_copy(high_down, hdh_ref, s_o.at[3]),
        pltpu.make_async_copy(rul.at[nx - 1], hul_ref, s_o.at[4]),
        pltpu.make_async_copy(rdl.at[:, me["y"]], hdl_ref, s_o.at[5]),
    ]
    vec = lambda row: vec_ref[row : row + 1]
    cot = g_ref[...].astype(F32)
    d_mlp = (vec(GATE_M) * cot).astype(BF16)
    dl_t_ref[...] = d_mlp
    dlt_ref[...] = d_mlp.T
    stat_ref[...] = jnp.zeros_like(stat_ref)
    stat_ref[S_B_DOWN : S_B_DOWN + 1] = sum_tokens(d_mlp.astype(F32))
    if wide > width:
        go_buf[...] = jnp.zeros_like(go_buf)
    loads[0].wait()
    w_out = lambda b: o_buf[:, :, b // CORES, b % CORES].reshape(features, wide)[:, :width]
    attn_out = jnp.zeros((rows, features), F32)
    for b in range(n_t):
        attn_out += dot(mix_ref[b].T, w_out(b), 1, 1)
    attn_ref[...] = attn_out
    branch = vec(GATE_A) * attn_out
    stat_ref[S_SQ_A : S_SQ_A + 1] = sum_tokens(branch * branch)
    middle = x_ref[...].astype(F32) + branch
    dmid_ref[...] = middle
    centred = middle - mean_rows(middle)
    inv = lax.rsqrt(mean_rows(centred * centred) + EPSILON)
    low = (centred * inv * vec(GAIN2) * (1.0 + vec(SCALE_M)) + vec(SHIFT_M)).astype(BF16)
    low_ref[...] = low
    lowt_ref[...] = low.T
    acc_out[...] = jnp.zeros_like(acc_out)
    acc_in[...] = jnp.zeros_like(acc_in)
    loads[1].wait()
    loads[2].wait()

    def block(n, carry):
        j = n // nx
        step = lax.rem(n, nx)
        p = lax.rem(mx + (1 - j) * (nx - 1 - step) + j * step, nx)
        slot = 2 - 2 * j
        lanes = pl.ds(pl.multiple_of(j * cut, cut), cut)

        @pl.when(n == nx)
        def _():
            for copy in loads[3:] + own_up + own_down + near_on:
                copy.wait()

        @pl.when(n == nx + 1)
        def _():
            for copy in far_on:
                copy.wait()

        both = lambda buf: jnp.concatenate(
            [buf[j, :, :, p, c].reshape(features, cut) for c in range(CORES)], axis=1
        )
        up, down = both(up_buf), both(down_buf)
        bias = jnp.concatenate(
            [vec_ref[pl.ds(B_UP + p * CORES + c, 1), lanes] for c in range(CORES)], axis=1
        )
        hidden = dot(low_ref[...], up, 1, 0) + bias
        square = hidden * hidden
        bent = jnp.tanh(GELU_C * hidden * (1.0 + GELU_A * square))
        half = 0.5 * (1.0 + bent)
        active = (hidden * half).astype(BF16)
        slope = half + (0.5 * GELU_C) * hidden * (1.0 - bent * bent) * (
            1.0 + (3.0 * GELU_A) * square
        )
        acc_out[...] += dot(active, down, 1, 1)
        for m in range(1, nx):
            @pl.when(n == m)
            def _(m=m):
                ul[m - 1].advance(0)
                ul_x[nx - 1 - m].start()
                dl[m - 1].advance(0)
                dl_y[m - 1].start(0)

        @pl.when(n == nx)
        def _():
            ul[nx - 1].advance(0)
            dl[nx - 1].advance(0)
            dl_y[nx - 1].start(0)
            for copy in far_up + far_down:
                copy.wait()
            for copy in far_on:
                copy.start()

        grad_down = dot(dlt_ref[...], active, 1, 0).astype(BF16)
        d_hidden = (dot(dl_t_ref[...], down, 1, 0) * slope).astype(BF16)
        sums = sum_tokens(d_hidden.astype(F32))
        for c in range(CORES):
            stat_ref[pl.ds(S_B_UP + p * CORES + c, 1), lanes] = sums[:, c * cut : (c + 1) * cut]
        grad_up = dot(lowt_ref[...], d_hidden, 1, 0).astype(BF16)
        acc_in[...] += dot(d_hidden, up, 1, 1)
        for c in range(CORES):
            lanes_of = slice(c * cut, (c + 1) * cut)
            shape = up_buf.shape[1:3] + (-1, cut)
            down_buf[slot, :, :, p, c] = grad_down[:, lanes_of].reshape(shape)
            up_buf[slot, :, :, p, c] = grad_up[:, lanes_of].reshape(shape)

        for m in range(nx):
            @pl.when(n == m)
            def _(m=m):
                ul[m].start(0)
                dl[m].start(0)
                if m == 0:
                    for copy in near_down:
                        copy.wait()
                    for copy in near_on:
                        copy.start()

        return carry

    lax.fori_loop(0, 2 * nx, block, 0)
    uh.start(0)
    dh.start(0)
    middle = dmid_ref[...]
    mlp_out = acc_out[...] + vec(B_DOWN)
    mlp_branch = vec(GATE_M) * mlp_out
    result = middle + mlp_branch
    out_ref[...] = result.astype(BF16)
    cot = g_ref[...].astype(F32)
    stat_ref[S_SQ_M : S_SQ_M + 1] = sum_tokens(mlp_branch * mlp_branch)
    stat_ref[S_SQ_R : S_SQ_R + 1] = sum_tokens(result * result)
    stat_ref[S_GATE_M : S_GATE_M + 1] = sum_tokens(cot * mlp_out)
    e = acc_in[...]
    centred = middle - mean_rows(middle)
    inv = lax.rsqrt(mean_rows(centred * centred) + EPSILON)
    nhat = centred * inv
    gain, scale = vec(GAIN2), 1.0 + vec(SCALE_M)
    by_nhat = sum_tokens(e * nhat)
    stat_ref[S_SHIFT_M : S_SHIFT_M + 1] = sum_tokens(e)
    stat_ref[S_SCALE_M : S_SCALE_M + 1] = by_nhat * gain
    stat_ref[S_GAIN2 : S_GAIN2 + 1] = by_nhat * scale
    dn = e * (scale * gain)
    d_middle = cot + inv * (dn - mean_rows(dn) - nhat * mean_rows(dn * nhat))
    dmid_ref[...] = d_middle
    stat_ref[S_GATE_A : S_GATE_A + 1] = sum_tokens(d_middle * attn_ref[...])
    d_attn = (vec(GATE_A) * d_middle).astype(BF16)
    d_attn_t = d_attn.T
    for b in range(n_t):
        dmix_ref[b] = dot(d_attn, w_out(b), 1, 0).astype(BF16).T
        go_buf[b % CORES, :, :, b // CORES, :, :width] = (
            dot(d_attn_t, mix_ref[b], 1, 1).astype(BF16).reshape(go_buf.shape[1:3] + (-1, width))
        )
    keeps[0].start()
    uh.advance(0)
    keeps[1].start()
    dh.advance(0)
    keeps[2].start()
    for one in ul_x:
        one.wait()
    no = count["z"]

    def fold(n, carry):
        at = (n // INNER, lax.rem(n, INNER))
        value = rul[(nx - 1,) + at].astype(F32)
        for r in range(nx - 1):
            value += mul_x[(r,) + at].astype(F32)
        rul[(nx - 1,) + at] = value.astype(BF16)
        return carry

    lax.fori_loop(0, no * INNER, fold, 0)
    keeps[3].start()
    for one in dl_y:
        one.advance(0)
    keeps[4].start()
    for copy in keeps:
        copy.wait()


def middle_call(mix, x, g, vecs, w_ul, w_dl, w_uh, w_dh, w_out, stat_rows, n_d, n_t):
    rows, features = x.shape
    cut = w_ul.shape[-1]
    part, wide = w_out.shape[-2:]
    width = mix.shape[1]
    count = counts(n_d, n_t)
    no, nx = count["z"], count["x"]
    per = (3,) + w_ul.shape
    plane = (no, INNER, part, cut)
    tail = (part, cut)
    g_out = (CORES, no, INNER, nx, part, wide)
    return pl.pallas_call(
        partial(middle_kernel, n_d, n_t),
        name="middle",
        out_shape=[
            struct((rows, features), BF16),
            struct((rows, features), F32),
            struct((n_t, width, rows), BF16),
            struct((stat_rows, features), F32),
            struct((no, INNER) + tail, BF16),
            struct((no, nx) + tail, BF16),
            struct((no, INNER, nx) + tail, BF16),
            struct((no, INNER, nx) + tail, BF16),
            struct(g_out, BF16),
        ],
        in_specs=[VMEM] * 4 + [ANY] * 5,
        out_specs=[VMEM] * 4 + [ANY] * 5,
        scratch_shapes=[
            pltpu.VMEM(per, BF16), pltpu.VMEM(per, BF16), pltpu.VMEM(w_out.shape, BF16),
            pltpu.VMEM(g_out, BF16),
            pltpu.VMEM((rows, features), F32),
            pltpu.VMEM((rows, features), BF16),
            pltpu.VMEM((features, rows), BF16),
            pltpu.VMEM((rows, features), BF16),
            pltpu.VMEM((features, rows), BF16),
            pltpu.VMEM((rows, features), F32),
            pltpu.VMEM((rows, features), F32),
        ]
        + [
            pltpu.VMEM((nx, 1) + plane, BF16), pltpu.VMEM((nx,) + plane, BF16),
            pltpu.VMEM((nx - 1,) + plane, BF16),
            pltpu.VMEM((nx, 1) + plane, BF16), pltpu.VMEM((nx, INNER - 1, no) + tail, BF16),
            pltpu.VMEM((no, INNER, nx) + tail, BF16),
            pltpu.VMEM((1, no, INNER, nx) + tail, BF16),
            pltpu.VMEM((1, no, INNER, nx) + tail, BF16),
        ]
        + [
            DMA((2,)), DMA((2,)), DMA((6,)),
            DMA((2 + 2 * (INNER - 1 + nx - 1 + (INNER - 1) * (nx - 1)),)),
            DMA((2 + 2 * (INNER - 1 + nx - 1 + (INNER - 1) * (nx - 1)),)),
            DMA((4 * nx + 4, max(nx, INNER, CORES) - 1)), DMA((4 * nx + 4, max(nx, INNER, CORES) - 1)),
        ],
        compiler_params=params(1),
        cost_estimate=cost(2 * rows * features * features * (6 * n_t + 4), 30e6),
    )(mix, x, g, vecs, w_ul, w_dl, w_uh, w_dh, w_out)


def back_kernel(
    n_d, n_t, parts, heads,
    dmix_ref, proj_ref, mix_ref, lse_ref, cos_ref, sin_ref, in_hbm, wq_hbm, stat_ref,
    x_hbm, dmid_hbm, vec_ref, ada_ref,
    hul_ref, hdl_ref, huh_ref, hdh_ref, gout_ref,
    grad_in_ref, gq_ref, up_ref, down_ref, out_ref, table_ref, flat_ref, gain_ref, gcond_ref,
    dmix_all, key_ref, keyt_ref, val_ref, dkey_ref, dval_ref, dquery_ref, dproj_ref, in_ref, wq_ref,
    acc_ref, pair_ref, value_ref, rc, rx, pair_y, pair_z, pair_sum, value_z, value_y, value_mid,
    got_ref, mine_ref,
    x_ref, dmid_ref, late_ref, late_got, late_mine, late_all, rows_out, rows_in, *more,
):
    buffers, at = [], 0
    for size in (len(reduce_scratch(CODE, dims, path, (1, 1))) for dims, path in BACK_SUMS):
        buffers.append(more[at : at + size])
        at += size
    (
        s_a, r_a, s_l, s_g, r_g, s_t, r_t, s_d, r_d, s_c, r_c, s_x, r_x,
        s_v, r_v, s_e, r_e, s_p, r_p,
    ) = more[at:]
    places = Places(n_d, n_t)
    d, t, oi, ii, xi, ci = place(n_d, n_t)
    nx, no = n_t // CORES, n_d // INNER
    other = xi * CORES + (1 - ci)
    blocks, total, rows = proj_ref.shape
    width = total // 3
    half = HEAD_DIM // 2
    features = x_ref.shape[1]
    assert nx == 2 and CORES == 2

    cut = hul_ref.shape[-1]

    def put(target, lanes):
        def store(value):
            target[:, lanes] = value
        return store

    def put_out(value):
        out_ref[...] = value.T[:width]

    sinks = (
        put(up_ref, slice(0, cut)), put(down_ref, slice(0, cut)),
        put(up_ref, slice(cut, 2 * cut)), put(down_ref, slice(cut, 2 * cut)), put_out,
    )
    sums = []
    row = 0
    for n, ((dims, path), source) in enumerate(
        zip(BACK_SUMS, (hul_ref, hdl_ref, huh_ref, hdh_ref, gout_ref))
    ):
        steps = len(path)
        sums.append(
            Reduce(
                places, dims, path, source, buffers[n][0], buffers[n][1 : 1 + steps],
                list(buffers[n][1 + steps :]) + [sinks[n]], s_g, r_g, s_l.at[6 + n], row,
            )
        )
        row += steps
    flows = dict(zip(BACK_DIMS, sums))
    stage = dict.fromkeys(flows, 0)

    def at_point(point):
        for step in BACK_PLAN.get(point, ()):
            what, name = step.split()
            if what == "s":
                flows[name].start(0)
            else:
                flows[name].advance(stage[name])
                stage[name] += 1

    def put_low(value):
        gq_ref[0] = value[:, :width]
        gq_ref[1] = value[:, width:]

    def put_high(value):
        gq_ref[2] = value

    pair = Reduce(
        places, "zy", "yz", pair_ref, None, [pair_y, pair_z], [pair_sum, put_low], s_g, r_g, None, row
    )
    value_sum = Reduce(
        places, "zy", "zy", value_ref, None, [value_z, value_y], [value_mid, put_high],
        s_g, r_g, None, row + 2,
    )

    greet(n_d, n_t)
    a_copies = {}
    for m in range(1, n_t):
        b = order(m, xi, ci, nx)
        a_copies[mirror(m, nx)] = remote(
            dmix_ref.at[b], dmix_all.at[t], s_a.at[m - 1], r_a.at[mirror(m, nx) - 1], d, b
        )
    for m in range(n_t - 1, 0, -1):
        a_copies[mirror(m, nx)].start()
    at_point("0")
    loads = [
        pltpu.make_async_copy(dmix_ref.at[t], dmix_all.at[t], s_l.at[0]),
        pltpu.make_async_copy(in_hbm, in_ref, s_l.at[1]),
        pltpu.make_async_copy(wq_hbm, wq_ref, s_l.at[2]),
        pltpu.make_async_copy(x_hbm, x_ref, s_l.at[3]),
        pltpu.make_async_copy(dmid_hbm, dmid_ref, s_l.at[4]),
    ]
    for copy in loads:
        copy.start()
    t_copies = []
    for r in range(1, n_t):
        copy = remote(
            stat_ref, got_ref.at[r - 1], s_t.at[r - 1], r_t.at[r - 1], d, lax.rem(t + r, n_t)
        )
        copy.start()
        t_copies.append(copy)
    d_copies = [pltpu.make_async_copy(mine_ref, table_ref.at[d], s_l.at[5])]
    for r in range(1, n_d):
        d_copies.append(
            remote(mine_ref, table_ref.at[d], s_d.at[r - 1], r_d.at[r - 1], lax.rem(d + r, n_d), t)
        )

    def share_statistics():
        for copy in t_copies:
            copy.wait()
        value = stat_ref[...]
        for r in range(1, n_t):
            value += got_ref[r - 1]
        mine_ref[...] = value
        for copy in d_copies:
            copy.start()

    dkey_ref[...] = jnp.zeros_like(dkey_ref)
    dval_ref[...] = jnp.zeros_like(dval_ref)

    def turn(b, carry):
        lanes = pl.ds(pl.multiple_of(b * rows, rows), rows)
        keyt_ref[:, lanes] = proj_ref[b, width : 2 * width]
        for h in range(heads):
            at = h * HEAD_DIM
            key_ref[h, lanes] = proj_ref[b, width + at : width + at + HEAD_DIM].T
            val_ref[h, lanes] = proj_ref[b, 2 * width + at : 2 * width + at + HEAD_DIM].T
        return carry

    lax.fori_loop(0, blocks, turn, 0)
    loads[0].wait()

    loads[1].wait()
    loads[2].wait()
    dquery_ref[...] = jnp.zeros_like(dquery_ref)
    acc_ref[...] = jnp.zeros_like(acc_ref)
    part_ref = in_ref
    piece = rows // parts
    c_copies = {}
    for r in range(nx):
        block = lax.rem(xi + r, nx) * CORES + 1 - ci
        for p in range(parts):
            at = pl.ds(p * piece, piece)
            c_copies[r, p] = remote(
                part_ref.at[block, at], rc.at[r, at], s_c.at[r, p], r_c.at[r, p], d, other
            )
    x_copies = {}
    for p in range(parts):
        at = pl.ds(p * piece, piece)
        x_copies[p] = remote(
            part_ref.at[lax.rem(xi + 1, nx) * CORES + ci, at], rx.at[0, at],
            s_x.at[0, p], r_x.at[0, p], d, lax.rem(xi + 1, nx) * CORES + ci,
        )

    def unrotate(b, at, factor, first, last):
        lanes = pl.ds(pl.multiple_of(b * rows, rows), rows)
        cos, sin = cos_ref[:, lanes], sin_ref[:, lanes]
        dproj_ref[b, at : at + half] = ((first * cos + last * sin) * factor).astype(BF16)
        dproj_ref[b, at + half : at + HEAD_DIM] = ((last * cos - first * sin) * factor).astype(BF16)

    def close(b):
        lanes = pl.ds(pl.multiple_of(b * rows, rows), rows)
        for h in range(heads):
            at = h * HEAD_DIM
            d_query = dquery_ref[b, at : at + HEAD_DIM]
            unrotate(b, at, HEAD_DIM**-0.5, d_query[:half], d_query[half:])
            d_key = dkey_ref[h, lanes].T
            unrotate(b, width + at, 1.0, d_key[:half], d_key[half:])
            dproj_ref[b, 2 * width + at : 2 * width + at + HEAD_DIM] = (
                dval_ref[h, lanes].T.astype(BF16)
            )
        d_proj = dproj_ref[b]
        acc_ref[...] += dot(d_proj, in_ref[b], 1, 0)
        part_ref[b] = dot(d_proj.T, wq_ref[...], 1, 1).astype(BF16)

    def attend(n, carry):
        for m, at_step in ((1, 1), (2, 2), (3, 4)):
            @pl.when(n == at_step)
            def _(m=m):
                a_copies[m].wait()
        late_part, last_part = (n + 6) // 8, (n + 2) // 8
        q_other = late_part - last_part
        k_other = (1 - late_part) + q_other * lax.rem(n + 1, 2)
        offset = (1 - late_part) * n + q_other * (n // 2 - 1) + last_part * (n - 6)
        i = lax.rem(xi + q_other, nx) * CORES + lax.rem(ci + offset, CORES)
        span = CORES * rows
        keys = pl.ds(pl.multiple_of(lax.rem(xi + k_other, nx) * span, span), span)
        for h in range(heads):
            at = h * HEAD_DIM
            query_t = proj_ref[i, at : at + HEAD_DIM]
            dmix_t = dmix_all[i, at : at + HEAD_DIM]
            mix_t = mix_ref[i, at : at + HEAD_DIM]
            inner = jnp.sum(dmix_t.astype(F32) * mix_t.astype(F32), axis=0, keepdims=True)
            probs = jnp.exp(dot(key_ref[h, keys], query_t, 1, 0) - lse_ref[i, h : h + 1])
            d_probs = dot(val_ref[h, keys], dmix_t, 1, 0)
            d_scores = (probs * (d_probs - inner)).astype(BF16)
            dval_ref[h, keys] += dot(probs.astype(BF16), dmix_t.T, 1, 0)
            dkey_ref[h, keys] += dot(d_scores, query_t.T, 1, 0)
            dquery_ref[i, at : at + HEAD_DIM] += dot(keyt_ref[at : at + HEAD_DIM, keys], d_scores, 1, 0)

        @pl.when(n == 1)
        def _():
            share_statistics()

        @pl.when((n == 5) | (n == 7))
        def _():
            plane = lax.rem(xi + 1 - last_part, nx)

            def one(c, carry):
                close(plane * CORES + c)
                return carry

            lax.fori_loop(0, CORES, one, 0)

        @pl.when(n == 5)
        def _():
            for p in range(parts):
                c_copies[1, p].start()

        @pl.when(n == 6)
        def _():
            to = lax.rem(xi + 1, nx) * CORES + ci
            for p in range(parts):
                at = pl.ds(p * piece, piece)
                c_copies[1, p].wait()
                part_ref[to, at] = (part_ref[to, at].astype(F32) + rc[1, at].astype(F32)).astype(BF16)
                x_copies[p].start()

        for m in range(2 * n_t):
            if f"n{m}" in BACK_PLAN:
                @pl.when(n == m)
                def _(m=m):
                    at_point(f"n{m}")

        return carry

    lax.fori_loop(0, 2 * n_t, attend, 0)
    for p in range(parts):
        c_copies[0, p].start()
    grads = acc_ref[...].T.astype(BF16)
    pair_ref[...] = grads[:, : 2 * width].reshape(pair_ref.shape)
    value_ref[...] = grads[:, 2 * width :].reshape(value_ref.shape)
    pair.start(0)
    value_sum.start(0)
    at_point("t0")
    for copy in d_copies:
        copy.wait()
    loads[3].wait()
    loads[4].wait()
    pair.advance(0)
    at_point("t1")
    value_sum.advance(0)
    at_point("t2")

    gain, scale = vec_ref[GAIN1 : GAIN1 + 1], 1.0 + vec_ref[SCALE_A : SCALE_A + 1]
    shift_sum = jnp.zeros((1, features), F32)
    nhat_sum = jnp.zeros((1, features), F32)
    for p in range(parts):
        c_copies[0, p].wait()
        x_copies[p].wait()
        at = pl.ds(p * (rows // parts), rows // parts)
        e = part_ref[t, at].astype(F32) + rc[0, at].astype(F32)
        for r in range(1, nx):
            e += rx[r - 1, at].astype(F32)
        x = x_ref[at].astype(F32)
        centred = x - mean_rows(x)
        inv = lax.rsqrt(mean_rows(centred * centred) + EPSILON)
        nhat = centred * inv
        shift_sum += sum_tokens(e)
        nhat_sum += sum_tokens(e * nhat)
        dn = e * (scale * gain)
        grad_in_ref[at] = dmid_ref[at] + inv * (
            dn - mean_rows(dn) - nhat * mean_rows(dn * nhat)
        )
    at_point("t3")
    late_ref[:, :features] = shift_sum
    late_ref[:, features : 2 * features] = nhat_sum * gain
    late_ref[:, 2 * features :] = nhat_sum * scale

    copies = []
    for r in range(1, n_t):
        copy = remote(
            late_ref, late_got.at[r - 1], s_v.at[r - 1], r_v.at[r - 1], d, lax.rem(t + r, n_t)
        )
        copy.start()
        copies.append(copy)
    value = late_ref[...]
    for r in range(1, n_t):
        copies[r - 1].wait()
        value += late_got[r - 1]
    late_mine[...] = value
    copies = [pltpu.make_async_copy(late_mine, late_all.at[d], s_l.at[0])]
    for r in range(1, n_d):
        copies.append(
            remote(
                late_mine, late_all.at[d], s_e.at[r - 1], r_e.at[r - 1], lax.rem(d + r, n_d), t
            )
        )
    for copy in copies:
        copy.start()
    at_point("t4")
    for s in range(n_d):
        for block, row in EARLY:
            flat_ref[s : s + 1, block * features : (block + 1) * features] = table_ref[
                s, row : row + 1
            ]
    for copy in copies:
        copy.wait()
    value = late_all[0, :, 2 * features :]
    for s in range(1, n_d):
        value += late_all[s, :, 2 * features :]
    gain_ref[...] = value
    for s in range(n_d):
        flat_ref[s : s + 1, : 2 * features] = late_all[s, :, : 2 * features]
    columns = ada_ref.shape[0]
    moved = pltpu.roll(flat_ref[...], lax.rem(n_d - d, n_d) * columns, 1)[:, :columns]
    rows_out[:, 0, :] = lax.dot_general(
        moved, ada_ref[...].astype(F32), (((1,), (0,)), ((), ())),
        precision=lax.Precision.HIGHEST, preferred_element_type=F32,
    )
    copies = [pltpu.make_async_copy(rows_out.at[d], rows_in.at[d], s_l.at[1])]
    for r in range(1, n_d):
        peer = lax.rem(d + r, n_d)
        copies.append(remote(rows_out.at[peer], rows_in.at[d], s_p.at[r - 1], r_p.at[r - 1], peer, t))
    for copy in copies:
        copy.start()
    at_point("t5")
    pair.advance(1)
    value_sum.advance(1)
    at_point("t6")
    at_point("end")
    for name, flow in flows.items():
        assert stage[name] == len(flow.path), name
    for copy in copies:
        copy.wait()
    gcond_ref[...] = jnp.sum(rows_in[:, 0, :], axis=0, keepdims=True)


def back_call(
    dmix, proj, mix, lse, cos, sin, attn_in, w_qkv, stat, x, dmid, vecs, ada_t, partial_sums, n_d, n_t
):
    parts = 4
    count = counts(n_d, n_t)
    nx, no = count["x"], count["z"]
    blocks, total, rows = proj.shape
    width = total // 3
    heads = width // HEAD_DIM
    length = blocks * rows
    features = attn_in.shape[2]
    part = features // n_d
    cond_width = ada_t.shape[1]
    cut = partial_sums[0].shape[-1]
    buffers = []
    for (dims, path), source in zip(BACK_SUMS, partial_sums):
        buffers += reduce_scratch(count, dims, path, source.shape[-2:])
    stages = sum(len(path) for _, path in BACK_SUMS)
    widest = max(count.values()) - 1
    late = (1, 3 * features)
    return pl.pallas_call(
        partial(back_kernel, n_d, n_t, parts, heads),
        name="back",
        out_shape=[
            struct((rows, features), F32),
            struct((3, part, width), F32),
            struct((part, 2 * cut), F32),
            struct((part, 2 * cut), F32),
            struct((width, part), F32),
            struct((n_d,) + stat.shape, F32),
            struct((n_d, 6 * features), F32),
            struct((1, features), F32),
            struct((1, cond_width), F32),
        ],
        in_specs=[VMEM] * 6 + [ANY] * 2 + [VMEM] + [ANY] * 2 + [VMEM] * 2 + [ANY] * 5,
        out_specs=[VMEM] * 9,
        scratch_shapes=[
            pltpu.VMEM(dmix.shape, BF16),
            pltpu.VMEM((heads, length, HEAD_DIM), BF16),
            pltpu.VMEM((width, length), BF16),
            pltpu.VMEM((heads, length, HEAD_DIM), BF16),
            pltpu.VMEM((heads, length, HEAD_DIM), F32),
            pltpu.VMEM((heads, length, HEAD_DIM), F32),
            pltpu.VMEM((n_t, width, rows), F32),
            pltpu.VMEM(proj.shape, BF16),
            pltpu.VMEM(attn_in.shape, BF16),
            pltpu.VMEM(w_qkv.shape, BF16),
            pltpu.VMEM((total, features), F32),
            pltpu.VMEM((no, INNER, part, 2 * width), BF16),
            pltpu.VMEM((no, INNER, part, width), BF16),
            pltpu.VMEM((nx, rows, features), BF16),
            pltpu.VMEM((nx - 1, rows, features), BF16),
            *reduce_scratch(count, "zy", "yz", (part, 2 * width), own=False),
            *reduce_scratch(count, "zy", "zy", (part, width), own=False),
            pltpu.VMEM((n_t - 1,) + stat.shape, F32),
            pltpu.VMEM(stat.shape, F32),
            pltpu.VMEM(x.shape, BF16),
            pltpu.VMEM(x.shape, F32),
            pltpu.VMEM(late, F32),
            pltpu.VMEM((n_t - 1,) + late, F32),
            pltpu.VMEM(late, F32),
            pltpu.VMEM((n_d,) + late, F32),
            pltpu.VMEM((n_d, 1, cond_width), F32),
            pltpu.VMEM((n_d, 1, cond_width), F32),
        ]
        + buffers
        + [
            DMA((n_t - 1,)), DMA((n_t - 1,)), DMA((6 + len(BACK_SUMS),)),
            DMA((stages + 4, widest)), DMA((stages + 4, widest)),
            DMA((n_t - 1,)), DMA((n_t - 1,)), DMA((n_d - 1,)), DMA((n_d - 1,)),
            DMA((nx, parts)), DMA((nx, parts)), DMA((nx - 1, parts)), DMA((nx - 1, parts)),
            DMA((n_t - 1,)), DMA((n_t - 1,)), DMA((n_d - 1,)), DMA((n_d - 1,)),
            DMA((n_d - 1,)), DMA((n_d - 1,)),
        ],
        compiler_params=params(2),
        cost_estimate=cost(45 * heads * length * length * HEAD_DIM, 40e6, heads * length * length),
    )(dmix, proj, mix, lse, cos, sin, attn_in, w_qkv, stat, x, dmid, vecs, ada_t, *partial_sums)


def finish_kernel(
    count, n_units, n_moved, table_ref, flat_ref, cond_ref, gain_in, gcond_in, *more
):
    sources, more = more[:n_moved], more[n_moved:]
    ada_ref, bias_ref, gain1_ref, gain2_ref, bdown_ref, bup_ref, root_ref, gcond_ref = more[:8]
    for src, dst in zip(sources, more[8:]):
        if len(dst.shape) > len(src.shape):
            dst[:, 0, :] = src[...]
        else:
            dst[...] = src[...]
    n_d = table_ref.shape[0]
    features = table_ref.shape[2]
    total = table_ref[0]
    for s in range(1, n_d):
        total += table_ref[s]
    root_ref[...] = jnp.sqrt(jnp.sum(total[S_SQ_A : S_SQ_R + 1], axis=1) / count)
    gain2_ref[...] = total[S_GAIN2]
    bdown_ref[...] = total[S_B_DOWN]
    for u in range(n_units):
        bup_ref[u * features : (u + 1) * features] = total[S_B_UP + u]
    gain1_ref[...] = gain_in[0]
    gcond_ref[...] = gcond_in[...]
    for block in range(6):
        at = slice(block * features, (block + 1) * features)
        value = jnp.zeros((cond_ref.shape[0], features), F32)
        for s in range(n_d):
            value += cond_ref[:, s : s + 1] * flat_ref[s : s + 1, at]
        ada_ref[:, at] = value
        bias_ref[at] = jnp.sum(flat_ref[:, at], axis=0)


def finish_call(table, flat, cond_t, gain, gcond, moved, count, n_units):
    rows, wide = moved[1].shape
    shapes = [a.shape for a in moved]
    shapes[1] = (rows, 1, wide)
    features = table.shape[2]
    width = cond_t.shape[0]
    return pl.pallas_call(
        partial(finish_kernel, count, n_units, len(moved)),
        name="finish",
        out_shape=[
            struct((width, 6 * features), F32),
            struct((6 * features,), F32),
            struct((features,), F32),
            struct((features,), F32),
            struct((features,), F32),
            struct((n_units * features,), F32),
            struct((3,), F32),
            struct((1, width), F32),
        ]
        + [struct(shape, a.dtype) for a, shape in zip(moved, shapes)],
        in_specs=[VMEM] * (5 + len(moved)),
        out_specs=[VMEM] * (8 + len(moved)),
        compiler_params=params(),
        cost_estimate=cost(1e7, 4e6),
    )(table, flat, cond_t, gain, gcond, *moved)


def shards(
    block_input, condition, modulation_weight, modulation_bias, first_gain, qkv_weight, out_weight,
    second_gain, up_weight, up_bias, down_weight, down_bias, grad_output,
):
    n_t, n_d = lax.axis_size("tensor"), lax.axis_size("dp")
    rows, sequences, features = block_input.shape
    assert sequences == 1
    length = rows * n_t
    part, width = qkv_weight.shape[1:]
    units = up_weight.shape[1]
    assert units == features and n_t % CORES == 0 and n_d % INNER == 0
    x = block_input.reshape(rows, features)
    g = grad_output.reshape(rows, features)
    ada_t = modulation_weight.T

    smalls = (first_gain, second_gain, down_bias, up_bias, condition, modulation_bias)
    inverse = 10000.0 ** (-np.arange(HEAD_DIM // 2) * 2.0 / HEAD_DIM)
    angles = inverse[:, None] * np.arange(length)[None, :]
    cos, sin = jnp.asarray(np.cos(angles), F32), jnp.asarray(np.sin(angles), F32)

    attn_in, proj, mix, lse, mix_own, vecs, cond_t, w_qkv, w_ul, w_dl, w_uh, w_dh, w_out = front_call(
        x, qkv_weight, smalls, ada_t, up_weight, down_weight.T, out_weight, cos, sin, n_d, n_t
    )
    stat_rows = -(-(S_B_UP + n_t) // 8) * 8
    out, d_middle, d_mix, stat, *partial_sums = middle_call(
        mix_own, x, g, vecs, w_ul, w_dl, w_uh, w_dh, w_out, stat_rows, n_d, n_t
    )
    grad_input, g_qkv, g_up, g_down, g_out, table, flat, gain1, grad_cond = back_call(
        d_mix, proj, mix, lse, cos, sin, attn_in, w_qkv.reshape(features, 3 * width), stat,
        x, d_middle, vecs, ada_t, partial_sums, n_d, n_t,
    )
    moved = (out, grad_input, g_qkv, g_up, g_down, g_out)
    grad_ada, grad_ada_b, gain1, gain2, b_down, b_up, roots, grad_cond, *moved = finish_call(
        table, flat, cond_t, gain1, grad_cond, moved, float(length * n_d * features), n_t
    )
    out, grad_input, g_qkv, g_up, g_down, g_out = moved
    return (
        out.reshape(block_input.shape), grad_input, grad_cond, grad_ada, grad_ada_b, gain1, g_qkv,
        g_out, gain2, g_up, b_up, g_down.T, b_down, roots,
    )


def solution(mesh):
    in_specs = (
        P("tensor", "dp", None),
        P("dp", None),
        P(None, "dp"),
        P("dp"),
        P("dp"),
        P(None, "dp", "tensor"),
        P("tensor", "dp"),
        P("dp"),
        P("dp", "tensor"),
        P("dp"),
        P("tensor", "dp"),
        P("dp"),
        P("tensor", "dp", None),
    )
    out_specs = (
        P("tensor", "dp", None),
        P("tensor", "dp", None),
        P("dp", None),
        P(),
        P(),
        P(),
        P(None, "dp", "tensor"),
        P("tensor", "dp"),
        P(),
        P("dp", "tensor"),
        P(),
        P("tensor", "dp"),
        P(),
        P(),
    )
    return jax.shard_map(shards, mesh=mesh, in_specs=in_specs, out_specs=out_specs, check_vma=False)
```
